32 devices in a mesh: ctx: 8 (over z, y), fsdp: 4 (over x, core).
Axes of the slice: x: 2, y: 2, z: 4, core: 2. Of those that a mesh axis runs over, the one named last changes fastest.
Arguments:
- tokens: bfloat16 [4, 1024, 2048], P('fsdp', 'ctx'), may hold values from -6 to 6
- doc_lengths: int32 [4, 8], P('fsdp'), may hold values from 1 to 512, 1024 in all within a row
- cotangent: bfloat16 [4, 1024, 2048], P('fsdp', 'ctx'), may hold values from -6 to 6
- gain_attn: bfloat16 [2048], P(('ctx', 'fsdp')), may hold values from 0.099609375 to 1.8984375
- w_query: bfloat16 [2048, 2048], P(('ctx', 'fsdp')), may hold values from -0.5 to 0.5
- w_key: bfloat16 [2048, 512], P(('ctx', 'fsdp')), may hold values from -0.5 to 0.5
- w_value: bfloat16 [2048, 512], P(('ctx', 'fsdp')), may hold values from -0.125 to 0.125
- w_output: bfloat16 [2048, 2048], P(('ctx', 'fsdp')), may hold values from -3 to 3
- gain_mlp: bfloat16 [2048], P(('ctx', 'fsdp')), may hold values from 0.099609375 to 1.8984375
- w_gate: bfloat16 [2048, 8192], P(('ctx', 'fsdp')), may hold values from -0.125 to 0.125
- w_up: bfloat16 [2048, 8192], P(('ctx', 'fsdp')), may hold values from -0.125 to 0.125
- w_down: bfloat16 [8192, 2048], P(('ctx', 'fsdp')), may hold values from -0.5 to 0.5
Outputs:
- output: bfloat16 [4, 1024, 2048], P('fsdp', 'ctx')
- grad_tokens: float32 [4, 1024, 2048], P('fsdp', 'ctx')
- grad_gain_attn: float32 [2048], P(('ctx', 'fsdp'))
- grad_w_query: float32 [2048, 2048], P(('ctx', 'fsdp'))
- grad_w_key: float32 [2048, 512], P(('ctx', 'fsdp'))
- grad_w_value: float32 [2048, 512], P(('ctx', 'fsdp'))
- grad_w_output: float32 [2048, 2048], P(('ctx', 'fsdp'))
- grad_gain_mlp: float32 [2048], P(('ctx', 'fsdp'))
- grad_w_gate: float32 [2048, 8192], P(('ctx', 'fsdp'))
- grad_w_up: float32 [2048, 8192], P(('ctx', 'fsdp'))
- grad_w_down: float32 [8192, 2048], P(('ctx', 'fsdp'))
The draws below stay inside these ranges and needn't reach their ends.
Inputs may be any that keep to these rules, and one draw needn't show every extreme that they name: `doc_lengths`: each sequence's 8 lengths sum to 1024, and the longest is 512.
All inputs are finite; a program needn't handle non-finite values.
Results may differ from the reference program's by a relative error of at most 0.022.
Values may be sent and summed in bfloat16 or wider, within the bound.
A program may use at most 640 MiB of HBM per device.

```python
import math
import jax
import jax.numpy as jnp
import numpy as np
from jax import lax

D = 2048
H = 32
KVH = 8
HD = 64
FF = 8192
DOCS = 8
SEQ_TOKENS = 1024
DOC_MOST = 512
SEQS = 4


def block_scale(stream_key, dims, shards, smallest, high):
    factor_of, own = 1.0, jax.random.fold_in(stream_key, 6)
    for axis_at, parts in shards:
        steps = jnp.exp(jax.random.uniform(jax.random.fold_in(own, axis_at), (parts,), jnp.float32, smallest / len(shards), high / len(shards)))
        factor_of = factor_of * jnp.repeat(steps, dims[axis_at] // parts).reshape([-1 if axis == axis_at else 1 for axis in range(len(dims))])
    return factor_of


def profile(amount, total, limit, lean):
    weights = [(1 << 20) // math.isqrt(standing ** lean) + 1 for standing in range(2, amount + 1)]
    surplus, counts = total - limit - (amount - 1), [1] * (amount - 1)
    while surplus > 0:
        free = [i for i in range(amount - 1) if counts[i] < limit]
        pool, remaining = sum([weights[i] for i in free]), surplus
        for i in free:
            more = min(limit - counts[i], max(1, remaining * weights[i] // pool), surplus)
            counts[i] = counts[i] + more
            surplus = surplus - more
    return np.array([limit] + counts)


def ragged(stream_key, number_of, total, reach, skew):
    if number_of == 2:
        one = jax.random.randint(stream_key, (), max(1, total - reach), min(reach, total - 1) + 1)
        return jnp.stack([one, total - one])
    lengths = jnp.asarray(profile(number_of, total, reach, skew), jnp.int32)
    couples = (number_of - 1) // 2
    donor, receiver = lengths[1:1 + 2 * couples:2], lengths[2:2 + 2 * couples:2]
    room = jnp.minimum(donor - 1, reach - receiver)
    passed = jax.random.randint(jax.random.fold_in(stream_key, 1), (couples,), 0, 1 << 20) % (room + 1)
    lengths = lengths.at[1:1 + 2 * couples:2].set(donor - passed).at[2:2 + 2 * couples:2].set(receiver + passed)
    return lengths[jax.random.permutation(jax.random.fold_in(stream_key, 2), number_of)]


def bell_draw(stream_key, dims, width, bound, split=(), kind=jnp.bfloat16):
    values = width * jax.random.normal(stream_key, dims, jnp.float32)
    if split:
        values = values * block_scale(stream_key, dims, split, -0.22, 0.18)
    return jnp.clip(values, -bound, bound).astype(kind)


def setup_inputs(seed: int = 0) -> dict:
    keys = jax.random.split(jax.random.key(seed), 13)
    tokens = bell_draw(keys[0], (SEQS, SEQ_TOKENS, D), 1.0, 6.0, ((0, 4), (1, 8)))
    doc_lengths = jax.vmap(lambda own: ragged(own, DOCS, SEQ_TOKENS, DOC_MOST, 2))(jax.random.split(keys[1], SEQS)).reshape((SEQS, DOCS)).astype(jnp.int32)
    cotangent = bell_draw(keys[2], (SEQS, SEQ_TOKENS, D), 1.0, 6.0, ((0, 4), (1, 8)))
    gain_attn = jnp.clip(1.0 + 0.18 * jax.random.normal(keys[3], (D,), jnp.float32), 0.099609375, 1.8984375).astype(jnp.bfloat16)
    w_query = bell_draw(keys[4], (D, H * HD), (D // 16) ** -0.5, 0.5, ((0, 32),))
    w_key = bell_draw(keys[5], (D, KVH * HD), (D // 16) ** -0.5, 0.5, ((0, 32),))
    w_value = bell_draw(keys[6], (D, KVH * HD), D ** -0.5, 0.125, ((0, 32),))
    w_output = bell_draw(keys[7], (H * HD, D), 4 ** -0.5, 3.0, ((0, 32),))
    gain_mlp = jnp.clip(1.0 + 0.18 * jax.random.normal(keys[8], (D,), jnp.float32), 0.099609375, 1.8984375).astype(jnp.bfloat16)
    w_gate = bell_draw(keys[9], (D, FF), D ** -0.5, 0.125, ((0, 32),))
    w_up = bell_draw(keys[10], (D, FF), D ** -0.5, 0.125, ((0, 32),))
    w_down = bell_draw(keys[11], (FF, D), (FF // 64) ** -0.5, 0.5, ((0, 32),))
    return {"tokens": tokens, "doc_lengths": doc_lengths, "cotangent": cotangent, "gain_attn": gain_attn, "w_query": w_query, "w_key": w_key, "w_value": w_value, "w_output": w_output, "gain_mlp": gain_mlp, "w_gate": w_gate, "w_up": w_up, "w_down": w_down}


EPSILON = 1e-05
SCORE_SCALE = 1.0 / 64.0
RESIDUAL_MULT = 0.22
ROPE_BASE = 10000000.0
NEGATIVE = -1e+30
PRECISE = lax.Precision.HIGHEST

@jax.custom_vjp
def low(v):
    return lax.optimization_barrier(v.astype(jnp.bfloat16)).astype(jnp.float32)

@jax.custom_vjp
def low_back(v):
    return v

def low_keep(v):
    return (low(v), None)

def low_pass(kept, grad):
    return (grad,)

def back_keep(v):
    return (v, None)

def back_low(kept, grad):
    return (low(grad),)
low.defvjp(low_keep, low_pass)
low_back.defvjp(back_keep, back_low)

def matmul(left, right):
    return jnp.dot(left, right, precision=PRECISE, preferred_element_type=jnp.float32)

def normalize(values):
    return values * lax.rsqrt(lax.optimization_barrier(jnp.mean(values * values, axis=-1, keepdims=True)) + EPSILON)

def doc_index(positions, starts):
    return lax.optimization_barrier(jnp.sum((positions[:, None] >= starts[None, :]).astype(jnp.int32), axis=1)) - 1

def rope_tables(positions):
    half_size = HD // 2
    frequency = ROPE_BASE ** (-(jnp.arange(half_size, dtype=jnp.float32) * 2.0) / HD)
    angles = positions.astype(jnp.float32)[:, None] * frequency[None, :]
    return (jnp.cos(angles), jnp.sin(angles))

def rotate(tensor, cos_table, sin_table, head_count):
    row_count = tensor.shape[0]
    by_head = tensor.reshape(row_count, head_count, HD)
    half_size = HD // 2
    first_half = by_head[..., :half_size]
    second_half = by_head[..., half_size:]
    cos_rows = cos_table[:, None, :]
    sin_rows = sin_table[:, None, :]
    turned = jnp.concatenate([first_half * cos_rows - second_half * sin_rows, second_half * cos_rows + first_half * sin_rows], axis=-1)
    return turned.reshape(row_count, head_count * HD)

def attention(queries, key_rot, values, positions, doc_ids):
    length = queries.shape[0]
    block_rows = math.gcd(length, 512)
    block_count = length // block_rows
    grouped = queries.reshape(block_count, block_rows, KVH, H // KVH, HD)
    key_heads = key_rot.reshape(length, KVH, HD)
    value_heads = values.reshape(length, KVH, HD)
    query_pos = positions.reshape(block_count, block_rows)
    query_docs = doc_ids.reshape(block_count, block_rows)

    def block_attend(block_item):
        query_blk, pos_blk, doc_blk = block_item
        scores = low_back(SCORE_SCALE * jnp.einsum('qkgd,tkd->qkgt', query_blk, key_heads, precision=PRECISE))
        allowed = (doc_ids[None, :] == doc_blk[:, None]) & (positions[None, :] <= pos_blk[:, None])
        allowed = allowed[:, None, None, :]
        masked = jnp.where(allowed, scores, NEGATIVE)
        top_score = lax.optimization_barrier(jnp.max(masked, axis=-1, keepdims=True))
        weights_exp = jnp.where(allowed, jnp.exp(masked - top_score), 0.0)
        probs_low = low(weights_exp / lax.optimization_barrier(jnp.sum(weights_exp, axis=-1, keepdims=True)))
        return jnp.einsum('qkgt,tkd->qkgd', probs_low, value_heads, precision=PRECISE)
    attended = lax.map(jax.checkpoint(block_attend), (grouped, query_pos, query_docs))
    return attended.reshape(length, H * HD)

def one_sequence(seq_tokens, seq_lengths, gain_attn, w_query, w_key, w_value, w_output, gain_mlp, w_gate, w_up, w_down):
    length = seq_tokens.shape[0]
    positions = jnp.arange(length, dtype=jnp.int32)
    starts = (jnp.cumsum(seq_lengths) - seq_lengths).astype(jnp.int32)
    doc_ids = doc_index(positions, starts)
    cos_table, sin_table = rope_tables(positions)
    normed1 = low(normalize(seq_tokens) * gain_attn)
    queries = low(rotate(low_back(matmul(normed1, w_query)), cos_table, sin_table, H))
    key_rot = low(rotate(low_back(matmul(normed1, w_key)), cos_table, sin_table, KVH))
    values = low(low_back(matmul(normed1, w_value)))
    attended = attention(queries, key_rot, values, positions, doc_ids)
    mixed_heads = low(low_back(attended))
    attn_branch = low_back(matmul(mixed_heads, w_output))
    hidden = seq_tokens + RESIDUAL_MULT * attn_branch
    normed2 = low(normalize(hidden) * gain_mlp)
    gate_pre = low_back(matmul(normed2, w_gate))
    up_pre = low_back(matmul(normed2, w_up))
    activ = low(jax.nn.silu(gate_pre) * up_pre)
    mlp_branch = low_back(matmul(activ, w_down))
    return hidden + RESIDUAL_MULT * mlp_branch

def reference(tokens, doc_lengths, cotangent, gain_attn, w_query, w_key, w_value, w_output, gain_mlp, w_gate, w_up, w_down):
    weights = (gain_attn.astype(jnp.float32), w_query.astype(jnp.float32), w_key.astype(jnp.float32), w_value.astype(jnp.float32), w_output.astype(jnp.float32), gain_mlp.astype(jnp.float32), w_gate.astype(jnp.float32), w_up.astype(jnp.float32), w_down.astype(jnp.float32))
    inputs = tokens.astype(jnp.float32)

    def forward(stacked, params):

        def per_sequence(seq_item):
            seq_tokens, seq_lengths = seq_item
            return one_sequence(seq_tokens, seq_lengths, *params)
        return lax.map(jax.checkpoint(per_sequence), (stacked, doc_lengths))
    result, pullback = jax.vjp(forward, inputs, weights)
    grad_inputs, grad_params = pullback(cotangent.astype(jnp.float32))
    return (result.astype(jnp.bfloat16), grad_inputs, grad_params[0], grad_params[1], grad_params[2], grad_params[3], grad_params[4], grad_params[5], grad_params[6], grad_params[7], grad_params[8])
```

```python
import functools
import math

import jax
import jax.numpy as jnp
from jax import lax
from jax.experimental import pallas as pl
from jax.experimental.pallas import tpu as pltpu
from jax.sharding import PartitionSpec as P

H = 32
KVH = 8
HD = 64
FF = 8192


EPSILON = 1e-05
SCORE_SCALE = 1.0 / 64.0
RESIDUAL_MULT = 0.22
ROPE_BASE = 10000000.0
NEGATIVE = -1e30


def doc_index(positions, starts):
    return jnp.sum((positions[:, None] >= starts[None, :]).astype(jnp.int32), axis=1) - 1


def rope_tables(positions):
    half_size = HD // 2
    frequency = ROPE_BASE ** (-(jnp.arange(half_size, dtype=jnp.float32) * 2.0) / HD)
    angles = positions.astype(jnp.float32)[:, None] * frequency[None, :]
    return (jnp.cos(angles), jnp.sin(angles))


def rotate(tensor, cos_table, sin_table, head_count):
    row_count = tensor.shape[0]
    by_head = tensor.reshape(row_count, head_count, HD)
    half_size = HD // 2
    first_half = by_head[..., :half_size]
    second_half = by_head[..., half_size:]
    cos_rows = cos_table[:, None, :]
    sin_rows = sin_table[:, None, :]
    turned = jnp.concatenate(
        [
            first_half * cos_rows - second_half * sin_rows,
            second_half * cos_rows + first_half * sin_rows,
        ],
        axis=-1,
    )
    return turned.reshape(row_count, head_count * HD)


def dot_plain(left, right):
    return jnp.dot(left, right, preferred_element_type=jnp.float32)


def dot_back(left, right):
    return lax.dot_general(
        left, right, (((1,), (1,)), ((), ())), preferred_element_type=jnp.float32
    )


def dot_outer(left, right):
    return lax.dot_general(
        left, right, (((0,), (0,)), ((), ())), preferred_element_type=jnp.float32
    )


def norm_back(grad_normed, unit_rows, inv_scale, gain_full):
    scaled = grad_normed * gain_full
    return inv_scale * (scaled - unit_rows * jnp.mean(scaled * unit_rows, axis=-1, keepdims=True))


def general_device(
    tokens,
    doc_lengths,
    cotangent,
    gain_attn,
    w_query,
    w_key,
    w_value,
    w_output,
    gain_mlp,
    w_gate,
    w_up,
    w_down,
):
    local_rows = tokens.shape[1]
    ctx_size = lax.axis_size("ctx")
    length = local_rows * ctx_size
    group_size = H // KVH
    offset = lax.axis_index("ctx") * local_rows
    positions = offset + jnp.arange(local_rows, dtype=jnp.int32)
    seq_lengths = doc_lengths[0]
    starts = jnp.cumsum(seq_lengths) - seq_lengths
    doc_ids = doc_index(positions, starts)
    last_pos = offset + local_rows - 1
    first_doc = doc_ids[0]
    cos_table, sin_table = rope_tables(positions)
    gain1, gain2, wq_full, wk_full, wv_full, wo_full = (
        lax.all_gather(gain_attn, ("ctx", "fsdp"), axis=0, tiled=True),
        lax.all_gather(gain_mlp, ("ctx", "fsdp"), axis=0, tiled=True),
        lax.all_gather(w_query, ("ctx", "fsdp"), axis=0, tiled=True),
        lax.all_gather(w_key, ("ctx", "fsdp"), axis=0, tiled=True),
        lax.all_gather(w_value, ("ctx", "fsdp"), axis=0, tiled=True),
        lax.all_gather(w_output, ("ctx", "fsdp"), axis=0, tiled=True),
    )
    gain1_f = gain1.astype(jnp.float32)
    gain2_f = gain2.astype(jnp.float32)
    inputs = tokens[0].astype(jnp.float32)
    inv_one = lax.rsqrt(jnp.mean(inputs * inputs, axis=-1, keepdims=True) + EPSILON)
    unit_one = inputs * inv_one
    normed1 = (unit_one * gain1_f).astype(jnp.bfloat16)
    queries = rotate(dot_plain(normed1, wq_full), cos_table, sin_table, H).astype(jnp.bfloat16)
    key_rot = rotate(dot_plain(normed1, wk_full), cos_table, sin_table, KVH).astype(jnp.bfloat16)
    values = dot_plain(normed1, wv_full).astype(jnp.bfloat16)
    grouped = queries.reshape(local_rows, KVH, group_size, HD)
    start_state = (
        jnp.full((local_rows, KVH, group_size), NEGATIVE, jnp.float32),
        jnp.zeros((local_rows, KVH, group_size), jnp.float32),
        jnp.zeros((local_rows, KVH, group_size, HD), jnp.float32),
    )
    running = start_state
    key_piece = lax.all_gather(key_rot, "ctx", axis=0, tiled=True)
    value_piece = lax.all_gather(values, "ctx", axis=0, tiled=True)
    piece_rows = key_piece.shape[0]
    attend_key_width = math.gcd(piece_rows, 512)
    block_count = piece_rows // attend_key_width

    def one_block(carried, index_block):
        block_start = index_block * attend_key_width
        key_blk = lax.dynamic_slice_in_dim(key_piece, block_start, attend_key_width, 0).reshape(
            attend_key_width, KVH, HD
        )
        value_blk = lax.dynamic_slice_in_dim(value_piece, block_start, attend_key_width, 0).reshape(
            attend_key_width, KVH, HD
        )
        key_pos = block_start + jnp.arange(attend_key_width, dtype=jnp.int32)
        key_docs = doc_index(key_pos, starts)
        skip_block = (block_start > last_pos) | (key_docs[attend_key_width - 1] < first_doc)

        def update(current):
            run_max, run_sum, accumulated = current
            scores = (
                jnp.einsum("qkgd,tkd->qkgt", grouped, key_blk, preferred_element_type=jnp.float32)
                * SCORE_SCALE
            )
            allowed = (key_docs[None, :] == doc_ids[:, None]) & (
                key_pos[None, :] <= positions[:, None]
            )
            allowed = allowed[:, None, None, :]
            masked = jnp.where(allowed, scores, NEGATIVE)
            new_max = jnp.maximum(run_max, jnp.max(masked, axis=-1))
            weights_exp = jnp.where(allowed, jnp.exp(masked - new_max[..., None]), 0.0)
            factor = jnp.exp(run_max - new_max)
            new_sum = run_sum * factor + jnp.sum(weights_exp, axis=-1)
            new_acc = accumulated * factor[..., None] + jnp.einsum(
                "qkgt,tkd->qkgd",
                weights_exp.astype(jnp.bfloat16),
                value_blk,
                preferred_element_type=jnp.float32,
            )
            return (new_max, new_sum, new_acc)

        return (lax.cond(skip_block, lambda unchanged: unchanged, update, carried), None)

    running, _ = lax.scan(one_block, running, jnp.arange(block_count))
    run_max, run_sum, accumulated = running
    attended = accumulated / run_sum[..., None]
    log_sum = run_max + jnp.log(run_sum)
    mixed_heads = attended.reshape(local_rows, H * HD).astype(jnp.bfloat16)
    hidden = inputs + RESIDUAL_MULT * dot_plain(mixed_heads, wo_full)
    inv_two = lax.rsqrt(jnp.mean(hidden * hidden, axis=-1, keepdims=True) + EPSILON)
    unit_two = hidden * inv_two
    normed2 = (unit_two * gain2_f).astype(jnp.bfloat16)
    wg_full, wu_full, wd_full = (
        lax.all_gather(w_gate, ("ctx", "fsdp"), axis=0, tiled=True),
        lax.all_gather(w_up, ("ctx", "fsdp"), axis=0, tiled=True),
        lax.all_gather(w_down, ("ctx", "fsdp"), axis=0, tiled=True),
    )
    gate_pre = dot_plain(normed2, wg_full)
    up_pre = dot_plain(normed2, wu_full)
    sig_gate = jax.nn.sigmoid(gate_pre)
    silu_gate = gate_pre * sig_gate
    activ = (silu_gate * up_pre).astype(jnp.bfloat16)
    result = hidden + RESIDUAL_MULT * dot_plain(activ, wd_full)
    output = result.astype(jnp.bfloat16)[None]
    grad_out = cotangent[0].astype(jnp.float32)
    grad_mlp = (RESIDUAL_MULT * grad_out).astype(jnp.bfloat16)
    silu_slope = sig_gate * (1.0 + gate_pre * (1.0 - sig_gate))
    wg_back, wu_back, wd_back = (
        lax.all_gather(w_gate, ("ctx", "fsdp"), axis=0, tiled=True),
        lax.all_gather(w_up, ("ctx", "fsdp"), axis=0, tiled=True),
        lax.all_gather(w_down, ("ctx", "fsdp"), axis=0, tiled=True),
    )
    grad_act = dot_back(grad_mlp, wd_back)
    grad_gate = (grad_act * up_pre * silu_slope).astype(jnp.bfloat16)
    grad_up = (grad_act * silu_gate).astype(jnp.bfloat16)
    grad_norm2 = dot_back(grad_gate, wg_back) + dot_back(grad_up, wu_back)
    left_cols = normed2
    gate_up_shard = lax.psum_scatter(
        jnp.concatenate([dot_outer(left_cols, grad_gate), dot_outer(left_cols, grad_up)], axis=1),
        ("ctx", "fsdp"),
        scatter_dimension=0,
        tiled=True,
    )
    wg_shard = gate_up_shard[:, :FF]
    wu_shard = gate_up_shard[:, FF:]
    left_cols = activ
    wd_shard = lax.psum_scatter(
        dot_outer(left_cols, grad_mlp), ("ctx", "fsdp"), scatter_dimension=0, tiled=True
    )
    grad_g2 = jnp.sum(grad_norm2 * unit_two, axis=0)
    grad_hidden = grad_out + norm_back(grad_norm2, unit_two, inv_two, gain2_f)
    grad_attn = (RESIDUAL_MULT * grad_hidden).astype(jnp.bfloat16)
    wq_back, wk_back, wv_back, wo_back = (
        lax.all_gather(w_query, ("ctx", "fsdp"), axis=0, tiled=True),
        lax.all_gather(w_key, ("ctx", "fsdp"), axis=0, tiled=True),
        lax.all_gather(w_value, ("ctx", "fsdp"), axis=0, tiled=True),
        lax.all_gather(w_output, ("ctx", "fsdp"), axis=0, tiled=True),
    )
    grad_wo = dot_outer(mixed_heads, grad_attn)
    grad_att = (
        dot_back(grad_attn, wo_back).astype(jnp.bfloat16).reshape(local_rows, KVH, group_size, HD)
    )
    row_delta = jnp.sum(grad_att.astype(jnp.float32) * attended, axis=-1)
    key_all, value_all = (
        lax.all_gather(key_rot, "ctx", axis=0, tiled=True),
        lax.all_gather(values, "ctx", axis=0, tiled=True),
    )
    key_width = math.gcd(length, 512)
    block_count = length // key_width

    def back_block(grad_query, index_block):
        block_start = index_block * key_width
        key_blk = lax.dynamic_slice_in_dim(key_all, block_start, key_width, 0).reshape(
            key_width, KVH, HD
        )
        value_blk = lax.dynamic_slice_in_dim(value_all, block_start, key_width, 0).reshape(
            key_width, KVH, HD
        )
        key_pos = block_start + jnp.arange(key_width, dtype=jnp.int32)
        key_docs = doc_index(key_pos, starts)
        skip_block = (block_start > last_pos) | (key_docs[key_width - 1] < first_doc)

        def compute(current):
            scores = (
                jnp.einsum("qkgd,tkd->qkgt", grouped, key_blk, preferred_element_type=jnp.float32)
                * SCORE_SCALE
            )
            allowed = (key_docs[None, :] == doc_ids[:, None]) & (
                key_pos[None, :] <= positions[:, None]
            )
            allowed = allowed[:, None, None, :]
            probs_blk = jnp.where(
                allowed, jnp.exp(jnp.where(allowed, scores, NEGATIVE) - log_sum[..., None]), 0.0
            )
            grad_probs = jnp.einsum(
                "qkgd,tkd->qkgt", grad_att, value_blk, preferred_element_type=jnp.float32
            )
            grad_scores = (probs_blk * (grad_probs - row_delta[..., None])).astype(jnp.bfloat16)
            new_query = (
                current
                + jnp.einsum(
                    "qkgt,tkd->qkgd", grad_scores, key_blk, preferred_element_type=jnp.float32
                )
                * SCORE_SCALE
            )
            grad_key = (
                jnp.einsum(
                    "qkgt,qkgd->tkd", grad_scores, grouped, preferred_element_type=jnp.float32
                )
                * SCORE_SCALE
            )
            grad_value = jnp.einsum(
                "qkgt,qkgd->tkd",
                probs_blk.astype(jnp.bfloat16),
                grad_att,
                preferred_element_type=jnp.float32,
            )
            return (
                new_query,
                (grad_key.reshape(key_width, KVH * HD), grad_value.reshape(key_width, KVH * HD)),
            )

        def nothing(current):
            zero_rows = jnp.zeros((key_width, KVH * HD), jnp.float32)
            return (current, (zero_rows, zero_rows))

        return lax.cond(skip_block, nothing, compute, grad_query)

    grad_query, key_terms = lax.scan(
        back_block,
        jnp.zeros((local_rows, KVH, group_size, HD), jnp.float32),
        jnp.arange(block_count),
    )
    key_term_all = key_terms[0].reshape(length, KVH * HD)
    value_term_all = key_terms[1].reshape(length, KVH * HD)
    grad_keys, grad_values = (
        lax.psum_scatter(
            key_term_all.astype(jnp.bfloat16), "ctx", scatter_dimension=0, tiled=True
        ).astype(jnp.float32),
        lax.psum_scatter(
            value_term_all.astype(jnp.bfloat16), "ctx", scatter_dimension=0, tiled=True
        ).astype(jnp.float32),
    )
    grad_q_pre = rotate(grad_query.reshape(local_rows, H * HD), cos_table, -sin_table, H).astype(
        jnp.bfloat16
    )
    grad_k_pre = rotate(grad_keys, cos_table, -sin_table, KVH).astype(jnp.bfloat16)
    grad_v_pre = grad_values.astype(jnp.bfloat16)
    grad_norm1 = (
        dot_back(grad_q_pre, wq_back)
        + dot_back(grad_k_pre, wk_back)
        + dot_back(grad_v_pre, wv_back)
    )
    grad_wq = dot_outer(normed1, grad_q_pre)
    grad_wk = dot_outer(normed1, grad_k_pre)
    grad_wv = dot_outer(normed1, grad_v_pre)
    grad_g1 = jnp.sum(grad_norm1 * unit_one, axis=0)
    grad_inputs = grad_hidden + norm_back(grad_norm1, unit_one, inv_one, gain1_f)
    g1_shard, g2_shard, wq_shard, wk_shard, wv_shard, wo_shard = (
        lax.psum_scatter(grad_g1, ("ctx", "fsdp"), scatter_dimension=0, tiled=True),
        lax.psum_scatter(grad_g2, ("ctx", "fsdp"), scatter_dimension=0, tiled=True),
        lax.psum_scatter(grad_wq, ("ctx", "fsdp"), scatter_dimension=0, tiled=True),
        lax.psum_scatter(grad_wk, ("ctx", "fsdp"), scatter_dimension=0, tiled=True),
        lax.psum_scatter(grad_wv, ("ctx", "fsdp"), scatter_dimension=0, tiled=True),
        lax.psum_scatter(grad_wo, ("ctx", "fsdp"), scatter_dimension=0, tiled=True),
    )
    return (
        output,
        grad_inputs[None],
        g1_shard,
        wq_shard,
        wk_shard,
        wv_shard,
        wo_shard,
        g2_shard,
        wg_shard,
        wu_shard,
        wd_shard,
    )


def rows_of(blocks):
    return blocks.reshape((-1,) + blocks.shape[2:])


def gather_ctx(local):
    return lax.all_gather(local, "ctx", axis=0, tiled=True)


def scatter_ctx(partial):
    return lax.psum_scatter(partial, "ctx", scatter_dimension=0, tiled=True).astype(jnp.float32)


def swap_ctx(blocks):
    return lax.all_to_all(blocks, "ctx", split_axis=0, concat_axis=0, tiled=True)


def spread_columns(blocks):
    mine = swap_ctx(blocks)
    full = lax.all_gather(mine[:, None], "fsdp", axis=1, tiled=True)
    return full.reshape(-1, blocks.shape[-1])


def return_columns(grad, ctx_size, fsdp_size):
    by_owner = grad.reshape(ctx_size, fsdp_size, -1, grad.shape[-1]).transpose(1, 0, 2, 3)
    mine = lax.psum_scatter(rows_of(rows_of(by_owner)), "fsdp", scatter_dimension=0, tiled=True)
    return swap_ctx(mine.reshape(ctx_size, -1, grad.shape[-1]))


def half_turn(values, sign_table):
    lane = lax.broadcasted_iota(jnp.int32, values.shape, 1)
    width = values.shape[1]
    quarter = HD // 2
    ahead = pltpu.roll(values, width - quarter, 1)
    behind = pltpu.roll(values, quarter, 1)
    return jnp.where(lane % HD < quarter, ahead, behind) * sign_table


def turn(values, cos_table, sign_table):
    copies = values.shape[1] // cos_table.shape[1]
    if copies > 1:
        cos_table = jnp.concatenate([cos_table] * copies, axis=1)
        sign_table = jnp.concatenate([sign_table] * copies, axis=1)
    return values * cos_table + half_turn(values, sign_table)


def attention_forward_kernel(
    block_rows, qkv_ref, cos_ref, sin_ref, doc_col_ref, doc_row_ref, q_ref, kv_ref, out_ref, lse_ref
):
    length = qkv_ref.shape[0]
    group = H // KVH
    width = group * HD
    q_ref[...] = turn(qkv_ref[:, :width], cos_ref[...], sin_ref[...]).astype(jnp.bfloat16)
    pair = qkv_ref[:, width:]
    lane = lax.broadcasted_iota(jnp.int32, pair.shape, 1)
    turned = turn(pair, cos_ref[...], sin_ref[...])
    kv_ref[...] = jnp.where(lane < HD, turned, pair).astype(jnp.bfloat16)
    for block in range(length // block_rows):
        rows = slice(block * block_rows, (block + 1) * block_rows)
        reach = (block + 1) * block_rows
        keys = kv_ref[:reach, :HD]
        values = kv_ref[:reach, HD:]
        query_at = block * block_rows + lax.broadcasted_iota(jnp.int32, (block_rows, reach), 0)
        key_at = lax.broadcasted_iota(jnp.int32, (block_rows, reach), 1)
        allowed = (doc_col_ref[rows, :] == doc_row_ref[:, :reach]) & (key_at <= query_at)
        for head in range(group):
            cols = slice(head * HD, (head + 1) * HD)
            scores = dot_back(q_ref[rows, cols], keys) * SCORE_SCALE
            masked = jnp.where(allowed, scores, NEGATIVE)
            top = jnp.max(masked, axis=1, keepdims=True)
            weights = jnp.where(allowed, jnp.exp(masked - top), 0.0)
            total = jnp.sum(weights, axis=1, keepdims=True)
            mixed = dot_plain(weights.astype(jnp.bfloat16), values)
            out_ref[rows, cols] = (mixed / total).astype(jnp.bfloat16)
            lse_ref[rows, head : head + 1] = top + jnp.log(total)


def attention_backward_kernel(
    block_rows, q_ref, kv_ref, do_ref, lse_ref, cos_ref, sin_ref, doc_col_ref, doc_row_ref, grad_ref, dq_ref, dkv_ref
):
    length = q_ref.shape[0]
    group = H // KVH
    width = group * HD
    dkv_ref[...] = jnp.zeros_like(dkv_ref)
    for block in range(length // block_rows):
        rows = slice(block * block_rows, (block + 1) * block_rows)
        reach = (block + 1) * block_rows
        keys = kv_ref[:reach, :HD]
        values = kv_ref[:reach, HD:]
        query_at = block * block_rows + lax.broadcasted_iota(jnp.int32, (block_rows, reach), 0)
        key_at = lax.broadcasted_iota(jnp.int32, (block_rows, reach), 1)
        allowed = (doc_col_ref[rows, :] == doc_row_ref[:, :reach]) & (key_at <= query_at)
        for head in range(group):
            cols = slice(head * HD, (head + 1) * HD)
            query = q_ref[rows, cols]
            grad_out = do_ref[rows, cols]
            scores = dot_back(query, keys) * SCORE_SCALE
            probs = jnp.where(
                allowed,
                jnp.exp(jnp.where(allowed, scores, NEGATIVE) - lse_ref[rows, head : head + 1]),
                0.0,
            )
            grad_probs = dot_back(grad_out, values)
            delta = jnp.sum(probs * grad_probs, axis=1, keepdims=True)
            grad_scores = (probs * (grad_probs - delta)).astype(jnp.bfloat16)
            dq_ref[rows, cols] = dot_plain(grad_scores, keys) * SCORE_SCALE
            dkv_ref[:reach, :HD] += dot_outer(grad_scores, query) * SCORE_SCALE
            dkv_ref[:reach, HD:] += dot_outer(probs.astype(jnp.bfloat16), grad_out)
    grad_ref[:, :width] = turn(dq_ref[...], cos_ref[...], -sin_ref[...]).astype(jnp.bfloat16)
    pair = dkv_ref[...]
    lane = lax.broadcasted_iota(jnp.int32, pair.shape, 1)
    turned = turn(pair, cos_ref[...], -sin_ref[...])
    grad_ref[:, width:] = jnp.where(lane < HD, turned, pair).astype(jnp.bfloat16)


def in_vmem(count):
    return [pl.BlockSpec(memory_space=pltpu.VMEM)] * count


def attention_forward(qkv, tables, block_rows):
    length = qkv.shape[0]
    width = (H // KVH) * HD
    return pl.pallas_call(
        functools.partial(attention_forward_kernel, block_rows),
        out_shape=(
            jax.ShapeDtypeStruct((length, width), jnp.bfloat16),
            jax.ShapeDtypeStruct((length, 2 * HD), jnp.bfloat16),
            jax.ShapeDtypeStruct((length, width), jnp.bfloat16),
            jax.ShapeDtypeStruct((length, H // KVH), jnp.float32),
        ),
        in_specs=in_vmem(5),
        out_specs=tuple(in_vmem(4)),
        compiler_params=pltpu.CompilerParams(vmem_limit_bytes=48 * 2**20),
        name="attend",
    )(qkv, *tables)


def attention_backward(q, kv, grad_out, lse, tables, block_rows):
    length, width = q.shape
    return pl.pallas_call(
        functools.partial(attention_backward_kernel, block_rows),
        out_shape=jax.ShapeDtypeStruct((length, width + 2 * HD), jnp.bfloat16),
        in_specs=in_vmem(8),
        out_specs=in_vmem(1)[0],
        scratch_shapes=[
            pltpu.VMEM((length, width), jnp.float32),
            pltpu.VMEM((length, 2 * HD), jnp.float32),
        ],
        compiler_params=pltpu.CompilerParams(vmem_limit_bytes=48 * 2**20),
        name="attend_back",
    )(q, kv, grad_out, lse, *tables)


def on_device(
    tokens,
    doc_lengths,
    cotangent,
    gain_attn,
    w_query,
    w_key,
    w_value,
    w_output,
    gain_mlp,
    w_gate,
    w_up,
    w_down,
):
    local_rows, model = tokens.shape[1:]
    ctx_size = lax.axis_size("ctx")
    fsdp_size = lax.axis_size("fsdp")
    length = local_rows * ctx_size
    group_width = (H // KVH) * HD
    ff_slice = FF // ctx_size
    held_rows = w_query.shape[0]
    bf16 = jnp.bfloat16

    positions = jnp.arange(length, dtype=jnp.int32)
    seq_lengths = doc_lengths[0]
    starts = jnp.cumsum(seq_lengths) - seq_lengths
    doc_ids = doc_index(positions, starts)
    cos_half, sin_half = rope_tables(positions)
    cos_table = jnp.concatenate([cos_half] * 4, axis=1)
    sin_table = jnp.concatenate([-sin_half, sin_half] * 2, axis=1)
    tables = (cos_table, sin_table, doc_ids[:, None], doc_ids[None, :])

    gains = lax.all_gather(jnp.stack([gain_attn, gain_mlp]), ("ctx", "fsdp"), axis=1, tiled=True)
    gain1 = gains[0].astype(jnp.float32)
    gain2 = gains[1].astype(jnp.float32)

    def by_slice(weight):
        return weight.reshape(held_rows, ctx_size, -1)

    qkv_parts = jnp.concatenate([by_slice(w_query), by_slice(w_key), by_slice(w_value)], axis=2)
    w_qkv = spread_columns(qkv_parts.transpose(1, 0, 2))
    wo_mine = lax.all_gather(w_output, "fsdp", axis=0, tiled=True)
    gu_parts = jnp.concatenate([by_slice(w_gate), by_slice(w_up)], axis=2)
    w_gu = spread_columns(gu_parts.transpose(1, 0, 2))
    wd_mine = lax.all_gather(w_down, "fsdp", axis=0, tiled=True)

    inputs = tokens[0].astype(jnp.float32)
    inv_one = lax.rsqrt(jnp.mean(inputs * inputs, axis=-1, keepdims=True) + EPSILON)
    unit_one = inputs * inv_one
    normed1 = gather_ctx((unit_one * gain1).astype(bf16))
    grad_out = cotangent[0].astype(jnp.float32)
    grad_mlp = gather_ctx((RESIDUAL_MULT * grad_out).astype(bf16))

    block_rows = math.gcd(length, 256)
    qkv = dot_plain(normed1, w_qkv)
    q, kv, mixed_heads, log_sum = attention_forward(qkv, tables, block_rows)
    hidden = inputs + RESIDUAL_MULT * scatter_ctx(dot_plain(mixed_heads, wo_mine).astype(bf16))
    inv_two = lax.rsqrt(jnp.mean(hidden * hidden, axis=-1, keepdims=True) + EPSILON)
    unit_two = hidden * inv_two
    normed2 = gather_ctx((unit_two * gain2).astype(bf16))

    gate_up = dot_plain(normed2, w_gu)
    gate_pre, up_pre = gate_up[:, :ff_slice], gate_up[:, ff_slice:]
    sig_gate = jax.nn.sigmoid(gate_pre)
    silu_gate = gate_pre * sig_gate
    activ = (silu_gate * up_pre).astype(bf16)
    branch = scatter_ctx(dot_plain(activ, wd_mine).astype(bf16))
    output = (hidden + RESIDUAL_MULT * branch).astype(bf16)[None]

    silu_slope = sig_gate * (1.0 + gate_pre * (1.0 - sig_gate))
    grad_act = dot_back(grad_mlp, wd_mine)
    grad_gu = jnp.concatenate(
        [(grad_act * up_pre * silu_slope).astype(bf16), (grad_act * silu_gate).astype(bf16)], axis=1
    )
    grad_norm2 = scatter_ctx(dot_back(grad_gu, w_gu).astype(bf16))
    gu_back = return_columns(dot_outer(normed2, grad_gu).astype(bf16), ctx_size, fsdp_size)
    wd_back = lax.psum_scatter(
        dot_outer(activ, grad_mlp).astype(bf16), "fsdp", scatter_dimension=0, tiled=True
    )

    grad_g2 = jnp.sum(grad_norm2 * unit_two, axis=0)
    grad_hidden = grad_out + norm_back(grad_norm2, unit_two, inv_two, gain2)
    grad_attn = gather_ctx((RESIDUAL_MULT * grad_hidden).astype(bf16))
    grad_mixed = dot_back(grad_attn, wo_mine).astype(bf16)
    wo_back = lax.psum_scatter(
        dot_outer(mixed_heads, grad_attn).astype(bf16), "fsdp", scatter_dimension=0, tiled=True
    )
    grad_qkv = attention_backward(q, kv, grad_mixed, log_sum, tables, block_rows)
    grad_norm1 = scatter_ctx(dot_back(grad_qkv, w_qkv).astype(bf16))
    qkv_back = return_columns(dot_outer(normed1, grad_qkv).astype(bf16), ctx_size, fsdp_size)
    grad_g1 = jnp.sum(grad_norm1 * unit_one, axis=0)
    grad_inputs = grad_hidden + norm_back(grad_norm1, unit_one, inv_one, gain1)
    gain_back = lax.psum_scatter(
        jnp.stack([grad_g1, grad_g2]), ("ctx", "fsdp"), scatter_dimension=1, tiled=True
    )

    def joined(parts):
        return parts.transpose(1, 0, 2).reshape(held_rows, -1).astype(jnp.float32)

    key_end = group_width + HD
    return (
        output,
        grad_inputs[None],
        gain_back[0],
        joined(qkv_back[:, :, :group_width]),
        joined(qkv_back[:, :, group_width:key_end]),
        joined(qkv_back[:, :, key_end:]),
        wo_back.astype(jnp.float32),
        gain_back[1],
        joined(gu_back[:, :, :ff_slice]),
        joined(gu_back[:, :, ff_slice:]),
        wd_back.astype(jnp.float32),
    )


def solution(mesh):
    in_specs = (
        P("fsdp", "ctx", None),
        P("fsdp", None),
        P("fsdp", "ctx", None),
        P(("ctx", "fsdp")),
        P(("ctx", "fsdp"), None),
        P(("ctx", "fsdp"), None),
        P(("ctx", "fsdp"), None),
        P(("ctx", "fsdp"), None),
        P(("ctx", "fsdp")),
        P(("ctx", "fsdp"), None),
        P(("ctx", "fsdp"), None),
        P(("ctx", "fsdp"), None),
    )
    out_specs = (
        P("fsdp", "ctx", None),
        P("fsdp", "ctx", None),
        P(("ctx", "fsdp")),
        P(("ctx", "fsdp"), None),
        P(("ctx", "fsdp"), None),
        P(("ctx", "fsdp"), None),
        P(("ctx", "fsdp"), None),
        P(("ctx", "fsdp")),
        P(("ctx", "fsdp"), None),
        P(("ctx", "fsdp"), None),
        P(("ctx", "fsdp"), None),
    )
    split_heads = mesh.shape["ctx"] == KVH
    return jax.shard_map(
        on_device if split_heads else general_device, mesh=mesh, in_specs=in_specs, out_specs=out_specs, check_vma=False
    )
```

```python
import functools
import math

import jax
import jax.numpy as jnp
from jax import lax
from jax.experimental import pallas as pl
from jax.experimental.pallas import tpu as pltpu
from jax.sharding import PartitionSpec as P

H = 32
KVH = 8
HD = 64
FF = 8192


EPSILON = 1e-05
SCORE_SCALE = 1.0 / 64.0
RESIDUAL_MULT = 0.22
ROPE_BASE = 10000000.0
NEGATIVE = -1e30
MESH = pl.DeviceIdType.MESH
PAIR = 2
CHUNKS = 2


def doc_index(positions, starts):
    return jnp.sum((positions[:, None] >= starts[None, :]).astype(jnp.int32), axis=1) - 1


def rope_tables(positions):
    half_size = HD // 2
    frequency = ROPE_BASE ** (-(jnp.arange(half_size, dtype=jnp.float32) * 2.0) / HD)
    angles = positions.astype(jnp.float32)[:, None] * frequency[None, :]
    return (jnp.cos(angles), jnp.sin(angles))


def rotate(tensor, cos_table, sin_table, head_count):
    row_count = tensor.shape[0]
    by_head = tensor.reshape(row_count, head_count, HD)
    half_size = HD // 2
    first_half = by_head[..., :half_size]
    second_half = by_head[..., half_size:]
    cos_rows = cos_table[:, None, :]
    sin_rows = sin_table[:, None, :]
    turned = jnp.concatenate(
        [
            first_half * cos_rows - second_half * sin_rows,
            second_half * cos_rows + first_half * sin_rows,
        ],
        axis=-1,
    )
    return turned.reshape(row_count, head_count * HD)


def dot_plain(left, right):
    return jnp.dot(left, right, preferred_element_type=jnp.float32)


def dot_back(left, right):
    return lax.dot_general(
        left, right, (((1,), (1,)), ((), ())), preferred_element_type=jnp.float32
    )


def dot_outer(left, right):
    return lax.dot_general(
        left, right, (((0,), (0,)), ((), ())), preferred_element_type=jnp.float32
    )


def norm_back(grad_normed, unit_rows, inv_scale, gain_full):
    scaled = grad_normed * gain_full
    return inv_scale * (scaled - unit_rows * jnp.mean(scaled * unit_rows, axis=-1, keepdims=True))


def general_device(
    tokens,
    doc_lengths,
    cotangent,
    gain_attn,
    w_query,
    w_key,
    w_value,
    w_output,
    gain_mlp,
    w_gate,
    w_up,
    w_down,
):
    local_rows = tokens.shape[1]
    ctx_size = lax.axis_size("ctx")
    length = local_rows * ctx_size
    group_size = H // KVH
    offset = lax.axis_index("ctx") * local_rows
    positions = offset + jnp.arange(local_rows, dtype=jnp.int32)
    seq_lengths = doc_lengths[0]
    starts = jnp.cumsum(seq_lengths) - seq_lengths
    doc_ids = doc_index(positions, starts)
    last_pos = offset + local_rows - 1
    first_doc = doc_ids[0]
    cos_table, sin_table = rope_tables(positions)
    gain1, gain2, wq_full, wk_full, wv_full, wo_full = (
        lax.all_gather(gain_attn, ("ctx", "fsdp"), axis=0, tiled=True),
        lax.all_gather(gain_mlp, ("ctx", "fsdp"), axis=0, tiled=True),
        lax.all_gather(w_query, ("ctx", "fsdp"), axis=0, tiled=True),
        lax.all_gather(w_key, ("ctx", "fsdp"), axis=0, tiled=True),
        lax.all_gather(w_value, ("ctx", "fsdp"), axis=0, tiled=True),
        lax.all_gather(w_output, ("ctx", "fsdp"), axis=0, tiled=True),
    )
    gain1_f = gain1.astype(jnp.float32)
    gain2_f = gain2.astype(jnp.float32)
    inputs = tokens[0].astype(jnp.float32)
    inv_one = lax.rsqrt(jnp.mean(inputs * inputs, axis=-1, keepdims=True) + EPSILON)
    unit_one = inputs * inv_one
    normed1 = (unit_one * gain1_f).astype(jnp.bfloat16)
    queries = rotate(dot_plain(normed1, wq_full), cos_table, sin_table, H).astype(jnp.bfloat16)
    key_rot = rotate(dot_plain(normed1, wk_full), cos_table, sin_table, KVH).astype(jnp.bfloat16)
    values = dot_plain(normed1, wv_full).astype(jnp.bfloat16)
    grouped = queries.reshape(local_rows, KVH, group_size, HD)
    start_state = (
        jnp.full((local_rows, KVH, group_size), NEGATIVE, jnp.float32),
        jnp.zeros((local_rows, KVH, group_size), jnp.float32),
        jnp.zeros((local_rows, KVH, group_size, HD), jnp.float32),
    )
    running = start_state
    key_piece = lax.all_gather(key_rot, "ctx", axis=0, tiled=True)
    value_piece = lax.all_gather(values, "ctx", axis=0, tiled=True)
    piece_rows = key_piece.shape[0]
    attend_key_width = math.gcd(piece_rows, 512)
    block_count = piece_rows // attend_key_width

    def one_block(carried, index_block):
        block_start = index_block * attend_key_width
        key_blk = lax.dynamic_slice_in_dim(key_piece, block_start, attend_key_width, 0).reshape(
            attend_key_width, KVH, HD
        )
        value_blk = lax.dynamic_slice_in_dim(value_piece, block_start, attend_key_width, 0).reshape(
            attend_key_width, KVH, HD
        )
        key_pos = block_start + jnp.arange(attend_key_width, dtype=jnp.int32)
        key_docs = doc_index(key_pos, starts)
        skip_block = (block_start > last_pos) | (key_docs[attend_key_width - 1] < first_doc)

        def update(current):
            run_max, run_sum, accumulated = current
            scores = (
                jnp.einsum("qkgd,tkd->qkgt", grouped, key_blk, preferred_element_type=jnp.float32)
                * SCORE_SCALE
            )
            allowed = (key_docs[None, :] == doc_ids[:, None]) & (
                key_pos[None, :] <= positions[:, None]
            )
            allowed = allowed[:, None, None, :]
            masked = jnp.where(allowed, scores, NEGATIVE)
            new_max = jnp.maximum(run_max, jnp.max(masked, axis=-1))
            weights_exp = jnp.where(allowed, jnp.exp(masked - new_max[..., None]), 0.0)
            factor = jnp.exp(run_max - new_max)
            new_sum = run_sum * factor + jnp.sum(weights_exp, axis=-1)
            new_acc = accumulated * factor[..., None] + jnp.einsum(
                "qkgt,tkd->qkgd",
                weights_exp.astype(jnp.bfloat16),
                value_blk,
                preferred_element_type=jnp.float32,
            )
            return (new_max, new_sum, new_acc)

        return (lax.cond(skip_block, lambda unchanged: unchanged, update, carried), None)

    running, _ = lax.scan(one_block, running, jnp.arange(block_count))
    run_max, run_sum, accumulated = running
    attended = accumulated / run_sum[..., None]
    log_sum = run_max + jnp.log(run_sum)
    mixed_heads = attended.reshape(local_rows, H * HD).astype(jnp.bfloat16)
    hidden = inputs + RESIDUAL_MULT * dot_plain(mixed_heads, wo_full)
    inv_two = lax.rsqrt(jnp.mean(hidden * hidden, axis=-1, keepdims=True) + EPSILON)
    unit_two = hidden * inv_two
    normed2 = (unit_two * gain2_f).astype(jnp.bfloat16)
    wg_full, wu_full, wd_full = (
        lax.all_gather(w_gate, ("ctx", "fsdp"), axis=0, tiled=True),
        lax.all_gather(w_up, ("ctx", "fsdp"), axis=0, tiled=True),
        lax.all_gather(w_down, ("ctx", "fsdp"), axis=0, tiled=True),
    )
    gate_pre = dot_plain(normed2, wg_full)
    up_pre = dot_plain(normed2, wu_full)
    sig_gate = jax.nn.sigmoid(gate_pre)
    silu_gate = gate_pre * sig_gate
    activ = (silu_gate * up_pre).astype(jnp.bfloat16)
    result = hidden + RESIDUAL_MULT * dot_plain(activ, wd_full)
    output = result.astype(jnp.bfloat16)[None]
    grad_out = cotangent[0].astype(jnp.float32)
    grad_mlp = (RESIDUAL_MULT * grad_out).astype(jnp.bfloat16)
    silu_slope = sig_gate * (1.0 + gate_pre * (1.0 - sig_gate))
    wg_back, wu_back, wd_back = (
        lax.all_gather(w_gate, ("ctx", "fsdp"), axis=0, tiled=True),
        lax.all_gather(w_up, ("ctx", "fsdp"), axis=0, tiled=True),
        lax.all_gather(w_down, ("ctx", "fsdp"), axis=0, tiled=True),
    )
    grad_act = dot_back(grad_mlp, wd_back)
    grad_gate = (grad_act * up_pre * silu_slope).astype(jnp.bfloat16)
    grad_up = (grad_act * silu_gate).astype(jnp.bfloat16)
    grad_norm2 = dot_back(grad_gate, wg_back) + dot_back(grad_up, wu_back)
    left_cols = normed2
    gate_up_shard = lax.psum_scatter(
        jnp.concatenate([dot_outer(left_cols, grad_gate), dot_outer(left_cols, grad_up)], axis=1),
        ("ctx", "fsdp"),
        scatter_dimension=0,
        tiled=True,
    )
    wg_shard = gate_up_shard[:, :FF]
    wu_shard = gate_up_shard[:, FF:]
    left_cols = activ
    wd_shard = lax.psum_scatter(
        dot_outer(left_cols, grad_mlp), ("ctx", "fsdp"), scatter_dimension=0, tiled=True
    )
    grad_g2 = jnp.sum(grad_norm2 * unit_two, axis=0)
    grad_hidden = grad_out + norm_back(grad_norm2, unit_two, inv_two, gain2_f)
    grad_attn = (RESIDUAL_MULT * grad_hidden).astype(jnp.bfloat16)
    wq_back, wk_back, wv_back, wo_back = (
        lax.all_gather(w_query, ("ctx", "fsdp"), axis=0, tiled=True),
        lax.all_gather(w_key, ("ctx", "fsdp"), axis=0, tiled=True),
        lax.all_gather(w_value, ("ctx", "fsdp"), axis=0, tiled=True),
        lax.all_gather(w_output, ("ctx", "fsdp"), axis=0, tiled=True),
    )
    grad_wo = dot_outer(mixed_heads, grad_attn)
    grad_att = (
        dot_back(grad_attn, wo_back).astype(jnp.bfloat16).reshape(local_rows, KVH, group_size, HD)
    )
    row_delta = jnp.sum(grad_att.astype(jnp.float32) * attended, axis=-1)
    key_all, value_all = (
        lax.all_gather(key_rot, "ctx", axis=0, tiled=True),
        lax.all_gather(values, "ctx", axis=0, tiled=True),
    )
    key_width = math.gcd(length, 512)
    block_count = length // key_width

    def back_block(grad_query, index_block):
        block_start = index_block * key_width
        key_blk = lax.dynamic_slice_in_dim(key_all, block_start, key_width, 0).reshape(
            key_width, KVH, HD
        )
        value_blk = lax.dynamic_slice_in_dim(value_all, block_start, key_width, 0).reshape(
            key_width, KVH, HD
        )
        key_pos = block_start + jnp.arange(key_width, dtype=jnp.int32)
        key_docs = doc_index(key_pos, starts)
        skip_block = (block_start > last_pos) | (key_docs[key_width - 1] < first_doc)

        def compute(current):
            scores = (
                jnp.einsum("qkgd,tkd->qkgt", grouped, key_blk, preferred_element_type=jnp.float32)
                * SCORE_SCALE
            )
            allowed = (key_docs[None, :] == doc_ids[:, None]) & (
                key_pos[None, :] <= positions[:, None]
            )
            allowed = allowed[:, None, None, :]
            probs_blk = jnp.where(
                allowed, jnp.exp(jnp.where(allowed, scores, NEGATIVE) - log_sum[..., None]), 0.0
            )
            grad_probs = jnp.einsum(
                "qkgd,tkd->qkgt", grad_att, value_blk, preferred_element_type=jnp.float32
            )
            grad_scores = (probs_blk * (grad_probs - row_delta[..., None])).astype(jnp.bfloat16)
            new_query = (
                current
                + jnp.einsum(
                    "qkgt,tkd->qkgd", grad_scores, key_blk, preferred_element_type=jnp.float32
                )
                * SCORE_SCALE
            )
            grad_key = (
                jnp.einsum(
                    "qkgt,qkgd->tkd", grad_scores, grouped, preferred_element_type=jnp.float32
                )
                * SCORE_SCALE
            )
            grad_value = jnp.einsum(
                "qkgt,qkgd->tkd",
                probs_blk.astype(jnp.bfloat16),
                grad_att,
                preferred_element_type=jnp.float32,
            )
            return (
                new_query,
                (grad_key.reshape(key_width, KVH * HD), grad_value.reshape(key_width, KVH * HD)),
            )

        def nothing(current):
            zero_rows = jnp.zeros((key_width, KVH * HD), jnp.float32)
            return (current, (zero_rows, zero_rows))

        return lax.cond(skip_block, nothing, compute, grad_query)

    grad_query, key_terms = lax.scan(
        back_block,
        jnp.zeros((local_rows, KVH, group_size, HD), jnp.float32),
        jnp.arange(block_count),
    )
    key_term_all = key_terms[0].reshape(length, KVH * HD)
    value_term_all = key_terms[1].reshape(length, KVH * HD)
    grad_keys, grad_values = (
        lax.psum_scatter(
            key_term_all.astype(jnp.bfloat16), "ctx", scatter_dimension=0, tiled=True
        ).astype(jnp.float32),
        lax.psum_scatter(
            value_term_all.astype(jnp.bfloat16), "ctx", scatter_dimension=0, tiled=True
        ).astype(jnp.float32),
    )
    grad_q_pre = rotate(grad_query.reshape(local_rows, H * HD), cos_table, -sin_table, H).astype(
        jnp.bfloat16
    )
    grad_k_pre = rotate(grad_keys, cos_table, -sin_table, KVH).astype(jnp.bfloat16)
    grad_v_pre = grad_values.astype(jnp.bfloat16)
    grad_norm1 = (
        dot_back(grad_q_pre, wq_back)
        + dot_back(grad_k_pre, wk_back)
        + dot_back(grad_v_pre, wv_back)
    )
    grad_wq = dot_outer(normed1, grad_q_pre)
    grad_wk = dot_outer(normed1, grad_k_pre)
    grad_wv = dot_outer(normed1, grad_v_pre)
    grad_g1 = jnp.sum(grad_norm1 * unit_one, axis=0)
    grad_inputs = grad_hidden + norm_back(grad_norm1, unit_one, inv_one, gain1_f)
    g1_shard, g2_shard, wq_shard, wk_shard, wv_shard, wo_shard = (
        lax.psum_scatter(grad_g1, ("ctx", "fsdp"), scatter_dimension=0, tiled=True),
        lax.psum_scatter(grad_g2, ("ctx", "fsdp"), scatter_dimension=0, tiled=True),
        lax.psum_scatter(grad_wq, ("ctx", "fsdp"), scatter_dimension=0, tiled=True),
        lax.psum_scatter(grad_wk, ("ctx", "fsdp"), scatter_dimension=0, tiled=True),
        lax.psum_scatter(grad_wv, ("ctx", "fsdp"), scatter_dimension=0, tiled=True),
        lax.psum_scatter(grad_wo, ("ctx", "fsdp"), scatter_dimension=0, tiled=True),
    )
    return (
        output,
        grad_inputs[None],
        g1_shard,
        wq_shard,
        wk_shard,
        wv_shard,
        wo_shard,
        g2_shard,
        wg_shard,
        wu_shard,
        wd_shard,
    )


def rows_of(blocks):
    return blocks.reshape((-1,) + blocks.shape[2:])


def greet_line(barrier, ctx_at, line_at, line_size):
    other = ctx_at + 1 - 2 * (ctx_at % PAIR)
    pl.semaphore_signal(barrier, inc=1, device_id={"ctx": other}, device_id_type=MESH)

    @pl.when(line_at > 0)
    def _():
        pl.semaphore_signal(barrier, inc=1, device_id={"ctx": ctx_at - PAIR}, device_id_type=MESH)

    @pl.when(line_at < line_size - 1)
    def _():
        pl.semaphore_signal(barrier, inc=1, device_id={"ctx": ctx_at + PAIR}, device_id_type=MESH)

    last = line_size - 1
    neighbours = 1 + (line_at + last - 1) // last + (2 * last - 1 - line_at) // last
    pl.semaphore_wait(barrier, neighbours)


def gather_kernel(line_size, x_ref, out_ref, send_sem, recv_sem, own_sem):
    me = lax.axis_index("ctx")
    line_at, pair_at = me // PAIR, me % PAIR
    rows = x_ref.shape[0]
    step = rows // CHUNKS
    greet_line(pltpu.get_barrier_semaphore(), me, line_at, line_size)

    def piece(block, part):
        return out_ref.at[pl.ds(pl.multiple_of(block * rows + part * step, step), step), :]

    def copy(block, part, way, own):
        target = (me + 1 - 2 * pair_at, me + PAIR, me - PAIR)[way]
        slot = block * CHUNKS + part
        return pltpu.make_async_remote_copy(
            src_ref=x_ref.at[pl.ds(part * step, step), :] if own else piece(block, part),
            dst_ref=piece(block, part),
            send_sem=send_sem.at[way, slot],
            recv_sem=recv_sem.at[slot],
            device_id={"ctx": target},
            device_id_type=MESH,
        )

    def pass_on(block, part, upward, downward, own, act):
        if upward is not None:
            pl.when(upward)(lambda: act(copy(block, part, 1, own)))
        if downward is not None:
            pl.when(downward)(lambda: act(copy(block, part, 2, own)))
        act(copy(block, part, 0, own))

    def visit(act, arrive):
        for part in range(CHUNKS):
            pass_on(me, part, line_at < line_size - 1, line_at > 0, True, act)
        for distance in range(1, line_size):
            for part in range(CHUNKS):

                @pl.when(line_at >= distance)
                def _():
                    block = me - PAIR * distance
                    arrive(block, part)
                    pass_on(block, part, line_at < line_size - 1, None, False, act)

                @pl.when(line_at + distance < line_size)
                def _():
                    block = me + PAIR * distance
                    arrive(block, part)
                    pass_on(block, part, None, line_at > 0, False, act)

    keep = pltpu.make_async_copy(
        x_ref, out_ref.at[pl.ds(pl.multiple_of(me * rows, rows), rows), :], own_sem
    )
    keep.start()
    visit(lambda c: c.start(), lambda block, part: copy(block, part, 0, False).wait_recv())
    for place in range(line_size):
        for part in range(CHUNKS):
            copy(place * PAIR + 1 - pair_at, part, 0, False).wait_recv()
    visit(lambda c: c.wait_send(), lambda block, part: None)
    keep.wait()


def gather_ctx(local):
    ctx_size = lax.axis_size("ctx")
    rows, width = local.shape
    return pl.pallas_call(
        functools.partial(gather_kernel, ctx_size // PAIR),
        out_shape=jax.ShapeDtypeStruct((ctx_size * rows, width), local.dtype),
        in_specs=[pl.BlockSpec(memory_space=pl.ANY)],
        out_specs=pl.BlockSpec(memory_space=pl.ANY),
        scratch_shapes=[
            pltpu.SemaphoreType.DMA((3, ctx_size * CHUNKS)),
            pltpu.SemaphoreType.DMA((ctx_size * CHUNKS,)),
            pltpu.SemaphoreType.DMA,
        ],
        compiler_params=pltpu.CompilerParams(collective_id=0, has_side_effects=True),
        name="gather_ctx",
    )(local)


def scatter_kernel(line_size, x_ref, out_ref, near, below, above, send_sem, near_sem, line_sem, line_send):
    me = lax.axis_index("ctx")
    line_at, pair_at = me // PAIR, me % PAIR
    rows = out_ref.shape[0]
    step = rows // CHUNKS
    greet_line(pltpu.get_barrier_semaphore(), me, line_at, line_size)
    half = line_size // 2
    low = line_at // half
    last = line_size - 1
    order = [k + (last - 2 * k) * (1 - low) for k in range(half)]
    if line_size == 4:
        order += [line_at + 1 - 2 * (line_at % 2), line_at]

    def near_copy(place, part):
        start = (place * PAIR + 1 - pair_at) * rows + part * step
        return pltpu.make_async_remote_copy(
            src_ref=x_ref.at[pl.ds(pl.multiple_of(start, step), step), :],
            dst_ref=near.at[place, pl.ds(part * step, step), :],
            send_sem=send_sem.at[place, part],
            recv_sem=near_sem.at[place, part],
            device_id={"ctx": me + 1 - 2 * pair_at},
            device_id_type=MESH,
        )

    def line_copy(place, part, up):
        part_rows = pl.ds(part * step, step)
        return pltpu.make_async_remote_copy(
            src_ref=near.at[place, part_rows, :],
            dst_ref=(below if up else above).at[place, part_rows, :],
            send_sem=line_send.at[place, part],
            recv_sem=line_sem.at[0 if up else 1, place, part],
            device_id={"ctx": me + PAIR if up else me - PAIR},
            device_id_type=MESH,
        )

    for place in order:
        for part in range(CHUNKS):
            near_copy(place, part).start()

    for place in order[:-1]:
        for part in range(CHUNKS):
            part_rows = pl.ds(part * step, step)
            mine = x_ref.at[pl.ds(pl.multiple_of((place * PAIR + pair_at) * rows + part * step, step), step), :]
            near_copy(place, part).wait_recv()

            def send(up, waits, arrived):
                @pl.when(waits)
                def _():
                    line_copy(place, part, up).wait_recv()
                    near[place, part_rows, :] = (
                        mine[...].astype(jnp.float32)
                        + near[place, part_rows, :].astype(jnp.float32)
                        + arrived[place, part_rows, :].astype(jnp.float32)
                    ).astype(near.dtype)

                @pl.when(jnp.logical_not(waits))
                def _():
                    near[place, part_rows, :] = (
                        mine[...].astype(jnp.float32) + near[place, part_rows, :].astype(jnp.float32)
                    ).astype(near.dtype)

                line_copy(place, part, up).start()

            @pl.when(place > line_at)
            def _():
                send(True, line_at > 0, below)

            @pl.when(place < line_at)
            def _():
                send(False, line_at < last, above)

    for part in range(CHUNKS):
        part_rows = pl.ds(part * step, step)
        mine = x_ref.at[pl.ds(pl.multiple_of(me * rows + part * step, step), step), :]
        near_copy(line_at, part).wait_recv()
        out_ref[part_rows, :] = mine[...].astype(jnp.float32) + near[line_at, part_rows, :].astype(jnp.float32)

        @pl.when(line_at > 0)
        def _():
            line_copy(line_at, part, True).wait_recv()
            out_ref[part_rows, :] += below[line_at, part_rows, :].astype(jnp.float32)

        @pl.when(line_at < last)
        def _():
            line_copy(line_at, part, False).wait_recv()
            out_ref[part_rows, :] += above[line_at, part_rows, :].astype(jnp.float32)

    for place in order:
        for part in range(CHUNKS):
            near_copy(place, part).wait_send()
    for place in order[:-1]:
        for part in range(CHUNKS):
            line_copy(place, part, True).wait_send()


def scatter_ctx(partial):
    ctx_size = lax.axis_size("ctx")
    line_size = ctx_size // PAIR
    rows, width = partial.shape[0] // ctx_size, partial.shape[1]
    held = pltpu.VMEM((line_size, rows, width), partial.dtype)
    return pl.pallas_call(
        functools.partial(scatter_kernel, line_size),
        out_shape=jax.ShapeDtypeStruct((rows, width), jnp.float32),
        in_specs=[pl.BlockSpec(memory_space=pltpu.VMEM)],
        out_specs=pl.BlockSpec(memory_space=pltpu.VMEM),
        scratch_shapes=[
            held, held, held,
            pltpu.SemaphoreType.DMA((line_size, CHUNKS)),
            pltpu.SemaphoreType.DMA((line_size, CHUNKS)),
            pltpu.SemaphoreType.DMA((2, line_size, CHUNKS)),
            pltpu.SemaphoreType.DMA((line_size, CHUNKS)),
        ],
        compiler_params=pltpu.CompilerParams(
            collective_id=1, has_side_effects=True, vmem_limit_bytes=32 * 2**20
        ),
        name="scatter_ctx",
    )(partial)


def exchange_kernel(ctx_size, fsdp_size, x_ref, out_ref, send_sem, recv_sem):
    count = ctx_size * fsdp_size
    me = lax.axis_index("ctx") * fsdp_size + lax.axis_index("fsdp")
    barrier = pltpu.get_barrier_semaphore()

    def device(index):
        return (index // fsdp_size, index % fsdp_size)

    def greet(k, unused):
        pl.semaphore_signal(barrier, inc=1, device_id=device((me + k) % count), device_id_type=MESH)
        return unused

    lax.fori_loop(1, count, greet, 0)
    pl.semaphore_wait(barrier, count - 1)

    def copy(k):
        target = (me + k) % count
        return pltpu.make_async_remote_copy(
            src_ref=x_ref.at[target], dst_ref=out_ref.at[me],
            send_sem=send_sem.at[k], recv_sem=recv_sem.at[k],
            device_id=device(target), device_id_type=MESH,
        )

    def start(k, unused):
        copy(k).start()
        return unused

    def finish(k, unused):
        source = (me + count - k) % count
        pltpu.make_async_remote_copy(
            src_ref=x_ref.at[source], dst_ref=out_ref.at[source],
            send_sem=send_sem.at[k], recv_sem=recv_sem.at[k],
            device_id=device(source), device_id_type=MESH,
        ).wait_recv()
        copy(k).wait_send()
        return unused

    lax.fori_loop(1, count, start, 0)
    out_ref[pl.ds(me, 1)] = x_ref[pl.ds(me, 1)]
    lax.fori_loop(1, count, finish, 0)


def exchange(tiles):
    ctx_size, fsdp_size = lax.axis_size("ctx"), lax.axis_size("fsdp")
    count = ctx_size * fsdp_size
    return pl.pallas_call(
        functools.partial(exchange_kernel, ctx_size, fsdp_size),
        out_shape=jax.ShapeDtypeStruct(tiles.shape, tiles.dtype),
        in_specs=[pl.BlockSpec(memory_space=pltpu.VMEM)],
        out_specs=pl.BlockSpec(memory_space=pltpu.VMEM),
        scratch_shapes=[pltpu.SemaphoreType.DMA((count,)), pltpu.SemaphoreType.DMA((count,))],
        compiler_params=pltpu.CompilerParams(collective_id=2, has_side_effects=True),
        name="exchange",
    )(tiles)


def padded(rows):
    return jnp.pad(rows, ((0, 0), (0, 8 - rows.shape[1]), (0, 128 - rows.shape[2])))


def gather_rows(rows):
    count = lax.axis_size("ctx") * lax.axis_size("fsdp")
    tiles = jnp.broadcast_to(padded(rows[None]), (count, 8, 128))
    return exchange(tiles)[:, : rows.shape[0], : rows.shape[1]].transpose(1, 0, 2).reshape(rows.shape[0], -1)


def scatter_rows(rows):
    count = lax.axis_size("ctx") * lax.axis_size("fsdp")
    by_owner = rows.reshape(rows.shape[0], count, -1).transpose(1, 0, 2)
    return jnp.sum(exchange(padded(by_owner)), axis=0)[: rows.shape[0], : by_owner.shape[2]]


def swap_ctx(blocks):
    return lax.all_to_all(blocks, "ctx", split_axis=0, concat_axis=0, tiled=True)


def spread_columns(blocks):
    mine = swap_ctx(blocks)
    full = lax.all_gather(mine[:, None], "fsdp", axis=1, tiled=True)
    return full.reshape(-1, blocks.shape[-1])


def return_columns(grad, ctx_size, fsdp_size):
    by_owner = grad.reshape(ctx_size, fsdp_size, -1, grad.shape[-1]).transpose(1, 0, 2, 3)
    mine = lax.psum_scatter(rows_of(rows_of(by_owner)), "fsdp", scatter_dimension=0, tiled=True)
    return swap_ctx(mine.reshape(ctx_size, -1, grad.shape[-1]))


def half_turn(values, sign_table):
    lane = lax.broadcasted_iota(jnp.int32, values.shape, 1)
    width = values.shape[1]
    quarter = HD // 2
    ahead = pltpu.roll(values, width - quarter, 1)
    behind = pltpu.roll(values, quarter, 1)
    return jnp.where(lane % HD < quarter, ahead, behind) * sign_table


def turn(values, cos_table, sign_table):
    copies = values.shape[1] // cos_table.shape[1]
    if copies > 1:
        cos_table = jnp.concatenate([cos_table] * copies, axis=1)
        sign_table = jnp.concatenate([sign_table] * copies, axis=1)
    return values * cos_table + half_turn(values, sign_table)


def attention_forward_kernel(
    block_rows, qkv_ref, cos_ref, sin_ref, doc_col_ref, doc_row_ref, q_ref, kv_ref, out_ref, lse_ref
):
    length = qkv_ref.shape[0]
    group = H // KVH
    width = group * HD
    q_ref[...] = turn(qkv_ref[:, :width], cos_ref[...], sin_ref[...]).astype(jnp.bfloat16)
    pair = qkv_ref[:, width:]
    lane = lax.broadcasted_iota(jnp.int32, pair.shape, 1)
    turned = turn(pair, cos_ref[...], sin_ref[...])
    kv_ref[...] = jnp.where(lane < HD, turned, pair).astype(jnp.bfloat16)
    for block in range(length // block_rows):
        rows = slice(block * block_rows, (block + 1) * block_rows)
        reach = (block + 1) * block_rows
        keys = kv_ref[:reach, :HD]
        values = kv_ref[:reach, HD:]
        query_at = block * block_rows + lax.broadcasted_iota(jnp.int32, (block_rows, reach), 0)
        key_at = lax.broadcasted_iota(jnp.int32, (block_rows, reach), 1)
        allowed = (doc_col_ref[rows, :] == doc_row_ref[:, :reach]) & (key_at <= query_at)
        for head in range(group):
            cols = slice(head * HD, (head + 1) * HD)
            scores = dot_back(q_ref[rows, cols], keys) * SCORE_SCALE
            masked = jnp.where(allowed, scores, NEGATIVE)
            top = jnp.max(masked, axis=1, keepdims=True)
            weights = jnp.where(allowed, jnp.exp(masked - top), 0.0)
            total = jnp.sum(weights, axis=1, keepdims=True)
            mixed = dot_plain(weights.astype(jnp.bfloat16), values)
            out_ref[rows, cols] = (mixed / total).astype(jnp.bfloat16)
            lse_ref[rows, head : head + 1] = top + jnp.log(total)


def attention_backward_kernel(
    block_rows, q_ref, kv_ref, do_ref, lse_ref, cos_ref, sin_ref, doc_col_ref, doc_row_ref, grad_ref, dq_ref, dkv_ref
):
    length = q_ref.shape[0]
    group = H // KVH
    width = group * HD
    dkv_ref[...] = jnp.zeros_like(dkv_ref)
    for block in range(length // block_rows):
        rows = slice(block * block_rows, (block + 1) * block_rows)
        reach = (block + 1) * block_rows
        keys = kv_ref[:reach, :HD]
        values = kv_ref[:reach, HD:]
        query_at = block * block_rows + lax.broadcasted_iota(jnp.int32, (block_rows, reach), 0)
        key_at = lax.broadcasted_iota(jnp.int32, (block_rows, reach), 1)
        allowed = (doc_col_ref[rows, :] == doc_row_ref[:, :reach]) & (key_at <= query_at)
        for head in range(group):
            cols = slice(head * HD, (head + 1) * HD)
            query = q_ref[rows, cols]
            grad_out = do_ref[rows, cols]
            scores = dot_back(query, keys) * SCORE_SCALE
            probs = jnp.where(
                allowed,
                jnp.exp(jnp.where(allowed, scores, NEGATIVE) - lse_ref[rows, head : head + 1]),
                0.0,
            )
            grad_probs = dot_back(grad_out, values)
            delta = jnp.sum(probs * grad_probs, axis=1, keepdims=True)
            grad_scores = (probs * (grad_probs - delta)).astype(jnp.bfloat16)
            dq_ref[rows, cols] = dot_plain(grad_scores, keys) * SCORE_SCALE
            dkv_ref[:reach, :HD] += dot_outer(grad_scores, query) * SCORE_SCALE
            dkv_ref[:reach, HD:] += dot_outer(probs.astype(jnp.bfloat16), grad_out)
    grad_ref[:, :width] = turn(dq_ref[...], cos_ref[...], -sin_ref[...]).astype(jnp.bfloat16)
    pair = dkv_ref[...]
    lane = lax.broadcasted_iota(jnp.int32, pair.shape, 1)
    turned = turn(pair, cos_ref[...], -sin_ref[...])
    grad_ref[:, width:] = jnp.where(lane < HD, turned, pair).astype(jnp.bfloat16)


def in_vmem(count):
    return [pl.BlockSpec(memory_space=pltpu.VMEM)] * count


def attention_forward(qkv, tables, block_rows):
    length = qkv.shape[0]
    width = (H // KVH) * HD
    return pl.pallas_call(
        functools.partial(attention_forward_kernel, block_rows),
        out_shape=(
            jax.ShapeDtypeStruct((length, width), jnp.bfloat16),
            jax.ShapeDtypeStruct((length, 2 * HD), jnp.bfloat16),
            jax.ShapeDtypeStruct((length, width), jnp.bfloat16),
            jax.ShapeDtypeStruct((length, H // KVH), jnp.float32),
        ),
        in_specs=in_vmem(5),
        out_specs=tuple(in_vmem(4)),
        compiler_params=pltpu.CompilerParams(vmem_limit_bytes=48 * 2**20),
        name="attend",
    )(qkv, *tables)


def attention_backward(q, kv, grad_out, lse, tables, block_rows):
    length, width = q.shape
    return pl.pallas_call(
        functools.partial(attention_backward_kernel, block_rows),
        out_shape=jax.ShapeDtypeStruct((length, width + 2 * HD), jnp.bfloat16),
        in_specs=in_vmem(8),
        out_specs=in_vmem(1)[0],
        scratch_shapes=[
            pltpu.VMEM((length, width), jnp.float32),
            pltpu.VMEM((length, 2 * HD), jnp.float32),
        ],
        compiler_params=pltpu.CompilerParams(vmem_limit_bytes=48 * 2**20),
        name="attend_back",
    )(q, kv, grad_out, lse, *tables)


def on_device(
    tokens,
    doc_lengths,
    cotangent,
    gain_attn,
    w_query,
    w_key,
    w_value,
    w_output,
    gain_mlp,
    w_gate,
    w_up,
    w_down,
):
    local_rows, model = tokens.shape[1:]
    ctx_size = lax.axis_size("ctx")
    fsdp_size = lax.axis_size("fsdp")
    length = local_rows * ctx_size
    group_width = (H // KVH) * HD
    ff_slice = FF // ctx_size
    held_rows = w_query.shape[0]
    bf16 = jnp.bfloat16

    positions = jnp.arange(length, dtype=jnp.int32)
    seq_lengths = doc_lengths[0]
    starts = jnp.cumsum(seq_lengths) - seq_lengths
    doc_ids = doc_index(positions, starts)
    cos_half, sin_half = rope_tables(positions)
    cos_table = jnp.concatenate([cos_half] * 4, axis=1)
    sin_table = jnp.concatenate([-sin_half, sin_half] * 2, axis=1)
    tables = (cos_table, sin_table, doc_ids[:, None], doc_ids[None, :])

    gain1, gain2 = gather_rows(jnp.stack([gain_attn, gain_mlp]).astype(jnp.float32))

    def by_slice(weight):
        return weight.reshape(held_rows, ctx_size, -1)

    qkv_parts = jnp.concatenate([by_slice(w_query), by_slice(w_key), by_slice(w_value)], axis=2)
    w_qkv = spread_columns(qkv_parts.transpose(1, 0, 2))
    wo_mine = lax.all_gather(w_output, "fsdp", axis=0, tiled=True)
    gu_parts = jnp.concatenate([by_slice(w_gate), by_slice(w_up)], axis=2)
    w_gu = spread_columns(gu_parts.transpose(1, 0, 2))
    wd_mine = lax.all_gather(w_down, "fsdp", axis=0, tiled=True)

    inputs = tokens[0].astype(jnp.float32)
    inv_one = lax.rsqrt(jnp.mean(inputs * inputs, axis=-1, keepdims=True) + EPSILON)
    unit_one = inputs * inv_one
    normed1 = gather_ctx((unit_one * gain1).astype(bf16))
    grad_out = cotangent[0].astype(jnp.float32)
    grad_mlp = gather_ctx((RESIDUAL_MULT * grad_out).astype(bf16))

    block_rows = math.gcd(length, 256)
    qkv = dot_plain(normed1, w_qkv)
    q, kv, mixed_heads, log_sum = attention_forward(qkv, tables, block_rows)
    hidden = inputs + RESIDUAL_MULT * scatter_ctx(dot_plain(mixed_heads, wo_mine).astype(bf16))
    inv_two = lax.rsqrt(jnp.mean(hidden * hidden, axis=-1, keepdims=True) + EPSILON)
    unit_two = hidden * inv_two
    normed2 = gather_ctx((unit_two * gain2).astype(bf16))

    gate_up = dot_plain(normed2, w_gu)
    gate_pre, up_pre = gate_up[:, :ff_slice], gate_up[:, ff_slice:]
    sig_gate = jax.nn.sigmoid(gate_pre)
    silu_gate = gate_pre * sig_gate
    activ = (silu_gate * up_pre).astype(bf16)
    branch = scatter_ctx(dot_plain(activ, wd_mine).astype(bf16))
    output = (hidden + RESIDUAL_MULT * branch).astype(bf16)[None]

    silu_slope = sig_gate * (1.0 + gate_pre * (1.0 - sig_gate))
    grad_act = dot_back(grad_mlp, wd_mine)
    grad_gu = jnp.concatenate(
        [(grad_act * up_pre * silu_slope).astype(bf16), (grad_act * silu_gate).astype(bf16)], axis=1
    )
    grad_norm2 = scatter_ctx(dot_back(grad_gu, w_gu).astype(bf16))
    gu_back = return_columns(dot_outer(normed2, grad_gu).astype(bf16), ctx_size, fsdp_size)
    wd_back = lax.psum_scatter(
        dot_outer(activ, grad_mlp).astype(bf16), "fsdp", scatter_dimension=0, tiled=True
    )

    grad_g2 = jnp.sum(grad_norm2 * unit_two, axis=0)
    grad_hidden = grad_out + norm_back(grad_norm2, unit_two, inv_two, gain2)
    grad_attn = gather_ctx((RESIDUAL_MULT * grad_hidden).astype(bf16))
    grad_mixed = dot_back(grad_attn, wo_mine).astype(bf16)
    wo_back = lax.psum_scatter(
        dot_outer(mixed_heads, grad_attn).astype(bf16), "fsdp", scatter_dimension=0, tiled=True
    )
    grad_qkv = attention_backward(q, kv, grad_mixed, log_sum, tables, block_rows)
    grad_norm1 = scatter_ctx(dot_back(grad_qkv, w_qkv).astype(bf16))
    qkv_back = return_columns(dot_outer(normed1, grad_qkv).astype(bf16), ctx_size, fsdp_size)
    grad_g1 = jnp.sum(grad_norm1 * unit_one, axis=0)
    grad_inputs = grad_hidden + norm_back(grad_norm1, unit_one, inv_one, gain1)
    gain_back = scatter_rows(jnp.stack([grad_g1, grad_g2]))

    def joined(parts):
        return parts.transpose(1, 0, 2).reshape(held_rows, -1).astype(jnp.float32)

    key_end = group_width + HD
    return (
        output,
        grad_inputs[None],
        gain_back[0],
        joined(qkv_back[:, :, :group_width]),
        joined(qkv_back[:, :, group_width:key_end]),
        joined(qkv_back[:, :, key_end:]),
        wo_back.astype(jnp.float32),
        gain_back[1],
        joined(gu_back[:, :, :ff_slice]),
        joined(gu_back[:, :, ff_slice:]),
        wd_back.astype(jnp.float32),
    )


def solution(mesh):
    in_specs = (
        P("fsdp", "ctx", None),
        P("fsdp", None),
        P("fsdp", "ctx", None),
        P(("ctx", "fsdp")),
        P(("ctx", "fsdp"), None),
        P(("ctx", "fsdp"), None),
        P(("ctx", "fsdp"), None),
        P(("ctx", "fsdp"), None),
        P(("ctx", "fsdp")),
        P(("ctx", "fsdp"), None),
        P(("ctx", "fsdp"), None),
        P(("ctx", "fsdp"), None),
    )
    out_specs = (
        P("fsdp", "ctx", None),
        P("fsdp", "ctx", None),
        P(("ctx", "fsdp")),
        P(("ctx", "fsdp"), None),
        P(("ctx", "fsdp"), None),
        P(("ctx", "fsdp"), None),
        P(("ctx", "fsdp"), None),
        P(("ctx", "fsdp")),
        P(("ctx", "fsdp"), None),
        P(("ctx", "fsdp"), None),
        P(("ctx", "fsdp"), None),
    )
    split_heads = mesh.shape["ctx"] == KVH == 4 * PAIR
    return jax.shard_map(
        on_device if split_heads else general_device, mesh=mesh, in_specs=in_specs, out_specs=out_specs, check_vma=False
    )
```

```python
import functools
import math

import jax
import jax.numpy as jnp
from jax import lax
from jax.experimental import pallas as pl
from jax.experimental.pallas import tpu as pltpu
from jax.sharding import PartitionSpec as P

H = 32
KVH = 8
HD = 64
FF = 8192


EPSILON = 1e-05
SCORE_SCALE = 1.0 / 64.0
RESIDUAL_MULT = 0.22
ROPE_BASE = 10000000.0
NEGATIVE = -1e30
MESH = pl.DeviceIdType.MESH
PAIR = 2
CHUNKS = 2
LINK_COST = pl.CostEstimate(flops=0, bytes_accessed=150_000_000, transcendentals=0)


def doc_index(positions, starts):
    return jnp.sum((positions[:, None] >= starts[None, :]).astype(jnp.int32), axis=1) - 1


def rope_tables(positions):
    half_size = HD // 2
    frequency = ROPE_BASE ** (-(jnp.arange(half_size, dtype=jnp.float32) * 2.0) / HD)
    angles = positions.astype(jnp.float32)[:, None] * frequency[None, :]
    return (jnp.cos(angles), jnp.sin(angles))


def rotate(tensor, cos_table, sin_table, head_count):
    row_count = tensor.shape[0]
    by_head = tensor.reshape(row_count, head_count, HD)
    half_size = HD // 2
    first_half = by_head[..., :half_size]
    second_half = by_head[..., half_size:]
    cos_rows = cos_table[:, None, :]
    sin_rows = sin_table[:, None, :]
    turned = jnp.concatenate(
        [
            first_half * cos_rows - second_half * sin_rows,
            second_half * cos_rows + first_half * sin_rows,
        ],
        axis=-1,
    )
    return turned.reshape(row_count, head_count * HD)


def dot_plain(left, right):
    return jnp.dot(left, right, preferred_element_type=jnp.float32)


def dot_back(left, right):
    return lax.dot_general(
        left, right, (((1,), (1,)), ((), ())), preferred_element_type=jnp.float32
    )


def dot_outer(left, right):
    return lax.dot_general(
        left, right, (((0,), (0,)), ((), ())), preferred_element_type=jnp.float32
    )


def norm_back(grad_normed, unit_rows, inv_scale, gain_full):
    scaled = grad_normed * gain_full
    return inv_scale * (scaled - unit_rows * jnp.mean(scaled * unit_rows, axis=-1, keepdims=True))


def general_device(
    tokens,
    doc_lengths,
    cotangent,
    gain_attn,
    w_query,
    w_key,
    w_value,
    w_output,
    gain_mlp,
    w_gate,
    w_up,
    w_down,
):
    local_rows = tokens.shape[1]
    ctx_size = lax.axis_size("ctx")
    length = local_rows * ctx_size
    group_size = H // KVH
    offset = lax.axis_index("ctx") * local_rows
    positions = offset + jnp.arange(local_rows, dtype=jnp.int32)
    seq_lengths = doc_lengths[0]
    starts = jnp.cumsum(seq_lengths) - seq_lengths
    doc_ids = doc_index(positions, starts)
    last_pos = offset + local_rows - 1
    first_doc = doc_ids[0]
    cos_table, sin_table = rope_tables(positions)
    gain1, gain2, wq_full, wk_full, wv_full, wo_full = (
        lax.all_gather(gain_attn, ("ctx", "fsdp"), axis=0, tiled=True),
        lax.all_gather(gain_mlp, ("ctx", "fsdp"), axis=0, tiled=True),
        lax.all_gather(w_query, ("ctx", "fsdp"), axis=0, tiled=True),
        lax.all_gather(w_key, ("ctx", "fsdp"), axis=0, tiled=True),
        lax.all_gather(w_value, ("ctx", "fsdp"), axis=0, tiled=True),
        lax.all_gather(w_output, ("ctx", "fsdp"), axis=0, tiled=True),
    )
    gain1_f = gain1.astype(jnp.float32)
    gain2_f = gain2.astype(jnp.float32)
    inputs = tokens[0].astype(jnp.float32)
    inv_one = lax.rsqrt(jnp.mean(inputs * inputs, axis=-1, keepdims=True) + EPSILON)
    unit_one = inputs * inv_one
    normed1 = (unit_one * gain1_f).astype(jnp.bfloat16)
    queries = rotate(dot_plain(normed1, wq_full), cos_table, sin_table, H).astype(jnp.bfloat16)
    key_rot = rotate(dot_plain(normed1, wk_full), cos_table, sin_table, KVH).astype(jnp.bfloat16)
    values = dot_plain(normed1, wv_full).astype(jnp.bfloat16)
    grouped = queries.reshape(local_rows, KVH, group_size, HD)
    start_state = (
        jnp.full((local_rows, KVH, group_size), NEGATIVE, jnp.float32),
        jnp.zeros((local_rows, KVH, group_size), jnp.float32),
        jnp.zeros((local_rows, KVH, group_size, HD), jnp.float32),
    )
    running = start_state
    key_piece = lax.all_gather(key_rot, "ctx", axis=0, tiled=True)
    value_piece = lax.all_gather(values, "ctx", axis=0, tiled=True)
    piece_rows = key_piece.shape[0]
    attend_key_width = math.gcd(piece_rows, 512)
    block_count = piece_rows // attend_key_width

    def one_block(carried, index_block):
        block_start = index_block * attend_key_width
        key_blk = lax.dynamic_slice_in_dim(key_piece, block_start, attend_key_width, 0).reshape(
            attend_key_width, KVH, HD
        )
        value_blk = lax.dynamic_slice_in_dim(value_piece, block_start, attend_key_width, 0).reshape(
            attend_key_width, KVH, HD
        )
        key_pos = block_start + jnp.arange(attend_key_width, dtype=jnp.int32)
        key_docs = doc_index(key_pos, starts)
        skip_block = (block_start > last_pos) | (key_docs[attend_key_width - 1] < first_doc)

        def update(current):
            run_max, run_sum, accumulated = current
            scores = (
                jnp.einsum("qkgd,tkd->qkgt", grouped, key_blk, preferred_element_type=jnp.float32)
                * SCORE_SCALE
            )
            allowed = (key_docs[None, :] == doc_ids[:, None]) & (
                key_pos[None, :] <= positions[:, None]
            )
            allowed = allowed[:, None, None, :]
            masked = jnp.where(allowed, scores, NEGATIVE)
            new_max = jnp.maximum(run_max, jnp.max(masked, axis=-1))
            weights_exp = jnp.where(allowed, jnp.exp(masked - new_max[..., None]), 0.0)
            factor = jnp.exp(run_max - new_max)
            new_sum = run_sum * factor + jnp.sum(weights_exp, axis=-1)
            new_acc = accumulated * factor[..., None] + jnp.einsum(
                "qkgt,tkd->qkgd",
                weights_exp.astype(jnp.bfloat16),
                value_blk,
                preferred_element_type=jnp.float32,
            )
            return (new_max, new_sum, new_acc)

        return (lax.cond(skip_block, lambda unchanged: unchanged, update, carried), None)

    running, _ = lax.scan(one_block, running, jnp.arange(block_count))
    run_max, run_sum, accumulated = running
    attended = accumulated / run_sum[..., None]
    log_sum = run_max + jnp.log(run_sum)
    mixed_heads = attended.reshape(local_rows, H * HD).astype(jnp.bfloat16)
    hidden = inputs + RESIDUAL_MULT * dot_plain(mixed_heads, wo_full)
    inv_two = lax.rsqrt(jnp.mean(hidden * hidden, axis=-1, keepdims=True) + EPSILON)
    unit_two = hidden * inv_two
    normed2 = (unit_two * gain2_f).astype(jnp.bfloat16)
    wg_full, wu_full, wd_full = (
        lax.all_gather(w_gate, ("ctx", "fsdp"), axis=0, tiled=True),
        lax.all_gather(w_up, ("ctx", "fsdp"), axis=0, tiled=True),
        lax.all_gather(w_down, ("ctx", "fsdp"), axis=0, tiled=True),
    )
    gate_pre = dot_plain(normed2, wg_full)
    up_pre = dot_plain(normed2, wu_full)
    sig_gate = jax.nn.sigmoid(gate_pre)
    silu_gate = gate_pre * sig_gate
    activ = (silu_gate * up_pre).astype(jnp.bfloat16)
    result = hidden + RESIDUAL_MULT * dot_plain(activ, wd_full)
    output = result.astype(jnp.bfloat16)[None]
    grad_out = cotangent[0].astype(jnp.float32)
    grad_mlp = (RESIDUAL_MULT * grad_out).astype(jnp.bfloat16)
    silu_slope = sig_gate * (1.0 + gate_pre * (1.0 - sig_gate))
    wg_back, wu_back, wd_back = (
        lax.all_gather(w_gate, ("ctx", "fsdp"), axis=0, tiled=True),
        lax.all_gather(w_up, ("ctx", "fsdp"), axis=0, tiled=True),
        lax.all_gather(w_down, ("ctx", "fsdp"), axis=0, tiled=True),
    )
    grad_act = dot_back(grad_mlp, wd_back)
    grad_gate = (grad_act * up_pre * silu_slope).astype(jnp.bfloat16)
    grad_up = (grad_act * silu_gate).astype(jnp.bfloat16)
    grad_norm2 = dot_back(grad_gate, wg_back) + dot_back(grad_up, wu_back)
    left_cols = normed2
    gate_up_shard = lax.psum_scatter(
        jnp.concatenate([dot_outer(left_cols, grad_gate), dot_outer(left_cols, grad_up)], axis=1),
        ("ctx", "fsdp"),
        scatter_dimension=0,
        tiled=True,
    )
    wg_shard = gate_up_shard[:, :FF]
    wu_shard = gate_up_shard[:, FF:]
    left_cols = activ
    wd_shard = lax.psum_scatter(
        dot_outer(left_cols, grad_mlp), ("ctx", "fsdp"), scatter_dimension=0, tiled=True
    )
    grad_g2 = jnp.sum(grad_norm2 * unit_two, axis=0)
    grad_hidden = grad_out + norm_back(grad_norm2, unit_two, inv_two, gain2_f)
    grad_attn = (RESIDUAL_MULT * grad_hidden).astype(jnp.bfloat16)
    wq_back, wk_back, wv_back, wo_back = (
        lax.all_gather(w_query, ("ctx", "fsdp"), axis=0, tiled=True),
        lax.all_gather(w_key, ("ctx", "fsdp"), axis=0, tiled=True),
        lax.all_gather(w_value, ("ctx", "fsdp"), axis=0, tiled=True),
        lax.all_gather(w_output, ("ctx", "fsdp"), axis=0, tiled=True),
    )
    grad_wo = dot_outer(mixed_heads, grad_attn)
    grad_att = (
        dot_back(grad_attn, wo_back).astype(jnp.bfloat16).reshape(local_rows, KVH, group_size, HD)
    )
    row_delta = jnp.sum(grad_att.astype(jnp.float32) * attended, axis=-1)
    key_all, value_all = (
        lax.all_gather(key_rot, "ctx", axis=0, tiled=True),
        lax.all_gather(values, "ctx", axis=0, tiled=True),
    )
    key_width = math.gcd(length, 512)
    block_count = length // key_width

    def back_block(grad_query, index_block):
        block_start = index_block * key_width
        key_blk = lax.dynamic_slice_in_dim(key_all, block_start, key_width, 0).reshape(
            key_width, KVH, HD
        )
        value_blk = lax.dynamic_slice_in_dim(value_all, block_start, key_width, 0).reshape(
            key_width, KVH, HD
        )
        key_pos = block_start + jnp.arange(key_width, dtype=jnp.int32)
        key_docs = doc_index(key_pos, starts)
        skip_block = (block_start > last_pos) | (key_docs[key_width - 1] < first_doc)

        def compute(current):
            scores = (
                jnp.einsum("qkgd,tkd->qkgt", grouped, key_blk, preferred_element_type=jnp.float32)
                * SCORE_SCALE
            )
            allowed = (key_docs[None, :] == doc_ids[:, None]) & (
                key_pos[None, :] <= positions[:, None]
            )
            allowed = allowed[:, None, None, :]
            probs_blk = jnp.where(
                allowed, jnp.exp(jnp.where(allowed, scores, NEGATIVE) - log_sum[..., None]), 0.0
            )
            grad_probs = jnp.einsum(
                "qkgd,tkd->qkgt", grad_att, value_blk, preferred_element_type=jnp.float32
            )
            grad_scores = (probs_blk * (grad_probs - row_delta[..., None])).astype(jnp.bfloat16)
            new_query = (
                current
                + jnp.einsum(
                    "qkgt,tkd->qkgd", grad_scores, key_blk, preferred_element_type=jnp.float32
                )
                * SCORE_SCALE
            )
            grad_key = (
                jnp.einsum(
                    "qkgt,qkgd->tkd", grad_scores, grouped, preferred_element_type=jnp.float32
                )
                * SCORE_SCALE
            )
            grad_value = jnp.einsum(
                "qkgt,qkgd->tkd",
                probs_blk.astype(jnp.bfloat16),
                grad_att,
                preferred_element_type=jnp.float32,
            )
            return (
                new_query,
                (grad_key.reshape(key_width, KVH * HD), grad_value.reshape(key_width, KVH * HD)),
            )

        def nothing(current):
            zero_rows = jnp.zeros((key_width, KVH * HD), jnp.float32)
            return (current, (zero_rows, zero_rows))

        return lax.cond(skip_block, nothing, compute, grad_query)

    grad_query, key_terms = lax.scan(
        back_block,
        jnp.zeros((local_rows, KVH, group_size, HD), jnp.float32),
        jnp.arange(block_count),
    )
    key_term_all = key_terms[0].reshape(length, KVH * HD)
    value_term_all = key_terms[1].reshape(length, KVH * HD)
    grad_keys, grad_values = (
        lax.psum_scatter(
            key_term_all.astype(jnp.bfloat16), "ctx", scatter_dimension=0, tiled=True
        ).astype(jnp.float32),
        lax.psum_scatter(
            value_term_all.astype(jnp.bfloat16), "ctx", scatter_dimension=0, tiled=True
        ).astype(jnp.float32),
    )
    grad_q_pre = rotate(grad_query.reshape(local_rows, H * HD), cos_table, -sin_table, H).astype(
        jnp.bfloat16
    )
    grad_k_pre = rotate(grad_keys, cos_table, -sin_table, KVH).astype(jnp.bfloat16)
    grad_v_pre = grad_values.astype(jnp.bfloat16)
    grad_norm1 = (
        dot_back(grad_q_pre, wq_back)
        + dot_back(grad_k_pre, wk_back)
        + dot_back(grad_v_pre, wv_back)
    )
    grad_wq = dot_outer(normed1, grad_q_pre)
    grad_wk = dot_outer(normed1, grad_k_pre)
    grad_wv = dot_outer(normed1, grad_v_pre)
    grad_g1 = jnp.sum(grad_norm1 * unit_one, axis=0)
    grad_inputs = grad_hidden + norm_back(grad_norm1, unit_one, inv_one, gain1_f)
    g1_shard, g2_shard, wq_shard, wk_shard, wv_shard, wo_shard = (
        lax.psum_scatter(grad_g1, ("ctx", "fsdp"), scatter_dimension=0, tiled=True),
        lax.psum_scatter(grad_g2, ("ctx", "fsdp"), scatter_dimension=0, tiled=True),
        lax.psum_scatter(grad_wq, ("ctx", "fsdp"), scatter_dimension=0, tiled=True),
        lax.psum_scatter(grad_wk, ("ctx", "fsdp"), scatter_dimension=0, tiled=True),
        lax.psum_scatter(grad_wv, ("ctx", "fsdp"), scatter_dimension=0, tiled=True),
        lax.psum_scatter(grad_wo, ("ctx", "fsdp"), scatter_dimension=0, tiled=True),
    )
    return (
        output,
        grad_inputs[None],
        g1_shard,
        wq_shard,
        wk_shard,
        wv_shard,
        wo_shard,
        g2_shard,
        wg_shard,
        wu_shard,
        wd_shard,
    )


def rows_of(blocks):
    return blocks.reshape((-1,) + blocks.shape[2:])


def greet_line(barrier, ctx_at, line_at, line_size):
    other = ctx_at + 1 - 2 * (ctx_at % PAIR)
    pl.semaphore_signal(barrier, inc=1, device_id={"ctx": other}, device_id_type=MESH)

    @pl.when(line_at > 0)
    def _():
        pl.semaphore_signal(barrier, inc=1, device_id={"ctx": ctx_at - PAIR}, device_id_type=MESH)

    @pl.when(line_at < line_size - 1)
    def _():
        pl.semaphore_signal(barrier, inc=1, device_id={"ctx": ctx_at + PAIR}, device_id_type=MESH)

    last = line_size - 1
    neighbours = 1 + (line_at + last - 1) // last + (2 * last - 1 - line_at) // last
    pl.semaphore_wait(barrier, neighbours)


def gather_kernel(line_size, x_ref, out_ref, send_sem, recv_sem, own_sem):
    me = lax.axis_index("ctx")
    line_at, pair_at = me // PAIR, me % PAIR
    rows = x_ref.shape[0]
    step = rows // CHUNKS
    greet_line(pltpu.get_barrier_semaphore(), me, line_at, line_size)

    def piece(block, part):
        return out_ref.at[pl.ds(pl.multiple_of(block * rows + part * step, step), step), :]

    def copy(block, part, way, own):
        target = (me + 1 - 2 * pair_at, me + PAIR, me - PAIR)[way]
        slot = block * CHUNKS + part
        return pltpu.make_async_remote_copy(
            src_ref=x_ref.at[pl.ds(part * step, step), :] if own else piece(block, part),
            dst_ref=piece(block, part),
            send_sem=send_sem.at[way, slot],
            recv_sem=recv_sem.at[slot],
            device_id={"ctx": target},
            device_id_type=MESH,
        )

    def pass_on(block, part, upward, downward, own, act):
        if upward is not None:
            pl.when(upward)(lambda: act(copy(block, part, 1, own)))
        if downward is not None:
            pl.when(downward)(lambda: act(copy(block, part, 2, own)))
        act(copy(block, part, 0, own))

    def visit(act, arrive):
        for part in range(CHUNKS):
            pass_on(me, part, line_at < line_size - 1, line_at > 0, True, act)
        for distance in range(1, line_size):
            for part in range(CHUNKS):

                @pl.when(line_at >= distance)
                def _():
                    block = me - PAIR * distance
                    arrive(block, part)
                    pass_on(block, part, line_at < line_size - 1, None, False, act)

                @pl.when(line_at + distance < line_size)
                def _():
                    block = me + PAIR * distance
                    arrive(block, part)
                    pass_on(block, part, None, line_at > 0, False, act)

    keep = pltpu.make_async_copy(
        x_ref, out_ref.at[pl.ds(pl.multiple_of(me * rows, rows), rows), :], own_sem
    )
    keep.start()
    visit(lambda c: c.start(), lambda block, part: copy(block, part, 0, False).wait_recv())
    for place in range(line_size):
        for part in range(CHUNKS):
            copy(place * PAIR + 1 - pair_at, part, 0, False).wait_recv()
    visit(lambda c: c.wait_send(), lambda block, part: None)
    keep.wait()


def gather_ctx(local):
    ctx_size = lax.axis_size("ctx")
    rows, width = local.shape
    return pl.pallas_call(
        functools.partial(gather_kernel, ctx_size // PAIR),
        out_shape=jax.ShapeDtypeStruct((ctx_size * rows, width), local.dtype),
        in_specs=[pl.BlockSpec(memory_space=pl.ANY)],
        out_specs=pl.BlockSpec(memory_space=pl.ANY),
        scratch_shapes=[
            pltpu.SemaphoreType.DMA((3, ctx_size * CHUNKS)),
            pltpu.SemaphoreType.DMA((ctx_size * CHUNKS,)),
            pltpu.SemaphoreType.DMA,
        ],
        compiler_params=pltpu.CompilerParams(collective_id=0, has_side_effects=True),
        cost_estimate=LINK_COST,
        name="gather_ctx",
    )(local)


def scatter_kernel(line_size, x_ref, out_ref, near, below, above, send_sem, near_sem, line_sem, line_send):
    me = lax.axis_index("ctx")
    line_at, pair_at = me // PAIR, me % PAIR
    rows = out_ref.shape[0]
    step = rows // CHUNKS
    greet_line(pltpu.get_barrier_semaphore(), me, line_at, line_size)
    half = line_size // 2
    low = line_at // half
    last = line_size - 1
    order = [k + (last - 2 * k) * (1 - low) for k in range(half)]
    if line_size == 4:
        order += [line_at + 1 - 2 * (line_at % 2), line_at]

    def near_copy(place, part):
        start = (place * PAIR + 1 - pair_at) * rows + part * step
        return pltpu.make_async_remote_copy(
            src_ref=x_ref.at[pl.ds(pl.multiple_of(start, step), step), :],
            dst_ref=near.at[place, pl.ds(part * step, step), :],
            send_sem=send_sem.at[place, part],
            recv_sem=near_sem.at[place, part],
            device_id={"ctx": me + 1 - 2 * pair_at},
            device_id_type=MESH,
        )

    def line_copy(place, part, up):
        part_rows = pl.ds(part * step, step)
        return pltpu.make_async_remote_copy(
            src_ref=near.at[place, part_rows, :],
            dst_ref=(below if up else above).at[place, part_rows, :],
            send_sem=line_send.at[place, part],
            recv_sem=line_sem.at[0 if up else 1, place, part],
            device_id={"ctx": me + PAIR if up else me - PAIR},
            device_id_type=MESH,
        )

    for place in order:
        for part in range(CHUNKS):
            near_copy(place, part).start()

    for place in order[:-1]:
        for part in range(CHUNKS):
            part_rows = pl.ds(part * step, step)
            mine = x_ref.at[pl.ds(pl.multiple_of((place * PAIR + pair_at) * rows + part * step, step), step), :]
            near_copy(place, part).wait_recv()

            def send(up, waits, arrived):
                @pl.when(waits)
                def _():
                    line_copy(place, part, up).wait_recv()
                    near[place, part_rows, :] = (
                        mine[...].astype(jnp.float32)
                        + near[place, part_rows, :].astype(jnp.float32)
                        + arrived[place, part_rows, :].astype(jnp.float32)
                    ).astype(near.dtype)

                @pl.when(jnp.logical_not(waits))
                def _():
                    near[place, part_rows, :] = (
                        mine[...].astype(jnp.float32) + near[place, part_rows, :].astype(jnp.float32)
                    ).astype(near.dtype)

                line_copy(place, part, up).start()

            @pl.when(place > line_at)
            def _():
                send(True, line_at > 0, below)

            @pl.when(place < line_at)
            def _():
                send(False, line_at < last, above)

    for part in range(CHUNKS):
        part_rows = pl.ds(part * step, step)
        mine = x_ref.at[pl.ds(pl.multiple_of(me * rows + part * step, step), step), :]
        near_copy(line_at, part).wait_recv()
        out_ref[part_rows, :] = mine[...].astype(jnp.float32) + near[line_at, part_rows, :].astype(jnp.float32)

        @pl.when(line_at > 0)
        def _():
            line_copy(line_at, part, True).wait_recv()
            out_ref[part_rows, :] += below[line_at, part_rows, :].astype(jnp.float32)

        @pl.when(line_at < last)
        def _():
            line_copy(line_at, part, False).wait_recv()
            out_ref[part_rows, :] += above[line_at, part_rows, :].astype(jnp.float32)

    for place in order:
        for part in range(CHUNKS):
            near_copy(place, part).wait_send()
    for place in order[:-1]:
        for part in range(CHUNKS):
            line_copy(place, part, True).wait_send()


def scatter_ctx(partial):
    ctx_size = lax.axis_size("ctx")
    line_size = ctx_size // PAIR
    rows, width = partial.shape[0] // ctx_size, partial.shape[1]
    held = pltpu.VMEM((line_size, rows, width), partial.dtype)
    return pl.pallas_call(
        functools.partial(scatter_kernel, line_size),
        out_shape=jax.ShapeDtypeStruct((rows, width), jnp.float32),
        in_specs=[pl.BlockSpec(memory_space=pltpu.VMEM)],
        out_specs=pl.BlockSpec(memory_space=pltpu.VMEM),
        scratch_shapes=[
            held, held, held,
            pltpu.SemaphoreType.DMA((line_size, CHUNKS)),
            pltpu.SemaphoreType.DMA((line_size, CHUNKS)),
            pltpu.SemaphoreType.DMA((2, line_size, CHUNKS)),
            pltpu.SemaphoreType.DMA((line_size, CHUNKS)),
        ],
        compiler_params=pltpu.CompilerParams(
            collective_id=1, has_side_effects=True, vmem_limit_bytes=32 * 2**20
        ),
        cost_estimate=LINK_COST,
        name="scatter_ctx",
    )(partial)


def exchange_kernel(ctx_size, fsdp_size, x_ref, out_ref, send_sem, recv_sem):
    count = ctx_size * fsdp_size
    me = lax.axis_index("ctx") * fsdp_size + lax.axis_index("fsdp")
    barrier = pltpu.get_barrier_semaphore()

    def device(index):
        return (index // fsdp_size, index % fsdp_size)

    def greet(k, unused):
        pl.semaphore_signal(barrier, inc=1, device_id=device((me + k) % count), device_id_type=MESH)
        return unused

    lax.fori_loop(1, count, greet, 0)
    pl.semaphore_wait(barrier, count - 1)

    def copy(k):
        target = (me + k) % count
        return pltpu.make_async_remote_copy(
            src_ref=x_ref.at[target], dst_ref=out_ref.at[me],
            send_sem=send_sem.at[k], recv_sem=recv_sem.at[k],
            device_id=device(target), device_id_type=MESH,
        )

    def start(k, unused):
        copy(k).start()
        return unused

    def finish(k, unused):
        source = (me + count - k) % count
        pltpu.make_async_remote_copy(
            src_ref=x_ref.at[source], dst_ref=out_ref.at[source],
            send_sem=send_sem.at[k], recv_sem=recv_sem.at[k],
            device_id=device(source), device_id_type=MESH,
        ).wait_recv()
        copy(k).wait_send()
        return unused

    lax.fori_loop(1, count, start, 0)
    out_ref[pl.ds(me, 1)] = x_ref[pl.ds(me, 1)]
    lax.fori_loop(1, count, finish, 0)


def exchange(tiles):
    ctx_size, fsdp_size = lax.axis_size("ctx"), lax.axis_size("fsdp")
    count = ctx_size * fsdp_size
    return pl.pallas_call(
        functools.partial(exchange_kernel, ctx_size, fsdp_size),
        out_shape=jax.ShapeDtypeStruct(tiles.shape, tiles.dtype),
        in_specs=[pl.BlockSpec(memory_space=pltpu.VMEM)],
        out_specs=pl.BlockSpec(memory_space=pltpu.VMEM),
        scratch_shapes=[pltpu.SemaphoreType.DMA((count,)), pltpu.SemaphoreType.DMA((count,))],
        compiler_params=pltpu.CompilerParams(collective_id=2, has_side_effects=True),
        cost_estimate=pl.CostEstimate(flops=0, bytes_accessed=25_000_000, transcendentals=0),
        name="exchange",
    )(tiles)


def padded(rows):
    return jnp.pad(rows, ((0, 0), (0, 8 - rows.shape[1]), (0, 128 - rows.shape[2])))


def gather_rows(rows):
    count = lax.axis_size("ctx") * lax.axis_size("fsdp")
    tiles = jnp.broadcast_to(padded(rows[None]), (count, 8, 128))
    return exchange(tiles)[:, : rows.shape[0], : rows.shape[1]].transpose(1, 0, 2).reshape(rows.shape[0], -1)


def scatter_rows(rows):
    count = lax.axis_size("ctx") * lax.axis_size("fsdp")
    by_owner = rows.reshape(rows.shape[0], count, -1).transpose(1, 0, 2)
    return jnp.sum(exchange(padded(by_owner)), axis=0)[: rows.shape[0], : by_owner.shape[2]]


def swap_ctx(blocks):
    return lax.all_to_all(blocks, "ctx", split_axis=0, concat_axis=0, tiled=True)


def spread_columns(mine):
    full = lax.all_gather(mine[:, None], "fsdp", axis=1, tiled=True)
    return full.reshape(-1, mine.shape[-1])


def by_fsdp(grad, ctx_size, fsdp_size):
    parts = grad.reshape(ctx_size, fsdp_size, -1, grad.shape[-1]).transpose(1, 0, 2, 3)
    return rows_of(rows_of(parts))


def return_columns(terms, ctx_size):
    return swap_ctx(terms.reshape(ctx_size, -1, terms.shape[-1]))


def half_turn(values, sign_table):
    lane = lax.broadcasted_iota(jnp.int32, values.shape, 1)
    width = values.shape[1]
    quarter = HD // 2
    ahead = pltpu.roll(values, width - quarter, 1)
    behind = pltpu.roll(values, quarter, 1)
    return jnp.where(lane % HD < quarter, ahead, behind) * sign_table


def turn(values, cos_table, sign_table):
    copies = values.shape[1] // cos_table.shape[1]
    if copies > 1:
        cos_table = jnp.concatenate([cos_table] * copies, axis=1)
        sign_table = jnp.concatenate([sign_table] * copies, axis=1)
    return values * cos_table + half_turn(values, sign_table)


def attention_forward_kernel(
    block_rows, qkv_ref, cos_ref, sin_ref, doc_col_ref, doc_row_ref, q_ref, kv_ref, out_ref, lse_ref
):
    length = qkv_ref.shape[0]
    group = H // KVH
    width = group * HD
    q_ref[...] = turn(qkv_ref[:, :width], cos_ref[...], sin_ref[...]).astype(jnp.bfloat16)
    pair = qkv_ref[:, width:]
    lane = lax.broadcasted_iota(jnp.int32, pair.shape, 1)
    turned = turn(pair, cos_ref[...], sin_ref[...])
    kv_ref[...] = jnp.where(lane < HD, turned, pair).astype(jnp.bfloat16)
    for block in range(length // block_rows):
        rows = slice(block * block_rows, (block + 1) * block_rows)
        reach = (block + 1) * block_rows
        keys = kv_ref[:reach, :HD]
        values = kv_ref[:reach, HD:]
        query_at = block * block_rows + lax.broadcasted_iota(jnp.int32, (block_rows, reach), 0)
        key_at = lax.broadcasted_iota(jnp.int32, (block_rows, reach), 1)
        allowed = (doc_col_ref[rows, :] == doc_row_ref[:, :reach]) & (key_at <= query_at)
        for head in range(group):
            cols = slice(head * HD, (head + 1) * HD)
            scores = dot_back(q_ref[rows, cols], keys) * SCORE_SCALE
            masked = jnp.where(allowed, scores, NEGATIVE)
            top = jnp.max(masked, axis=1, keepdims=True)
            weights = jnp.where(allowed, jnp.exp(masked - top), 0.0)
            total = jnp.sum(weights, axis=1, keepdims=True)
            mixed = dot_plain(weights.astype(jnp.bfloat16), values)
            out_ref[rows, cols] = (mixed / total).astype(jnp.bfloat16)
            lse_ref[rows, head : head + 1] = top + jnp.log(total)


def attention_backward_kernel(
    block_rows, q_ref, kv_ref, do_ref, lse_ref, cos_ref, sin_ref, doc_col_ref, doc_row_ref, grad_ref, dq_ref, dkv_ref
):
    length = q_ref.shape[0]
    group = H // KVH
    width = group * HD
    dkv_ref[...] = jnp.zeros_like(dkv_ref)
    for block in range(length // block_rows):
        rows = slice(block * block_rows, (block + 1) * block_rows)
        reach = (block + 1) * block_rows
        keys = kv_ref[:reach, :HD]
        values = kv_ref[:reach, HD:]
        query_at = block * block_rows + lax.broadcasted_iota(jnp.int32, (block_rows, reach), 0)
        key_at = lax.broadcasted_iota(jnp.int32, (block_rows, reach), 1)
        allowed = (doc_col_ref[rows, :] == doc_row_ref[:, :reach]) & (key_at <= query_at)
        for head in range(group):
            cols = slice(head * HD, (head + 1) * HD)
            query = q_ref[rows, cols]
            grad_out = do_ref[rows, cols]
            scores = dot_back(query, keys) * SCORE_SCALE
            probs = jnp.where(
                allowed,
                jnp.exp(jnp.where(allowed, scores, NEGATIVE) - lse_ref[rows, head : head + 1]),
                0.0,
            )
            grad_probs = dot_back(grad_out, values)
            delta = jnp.sum(probs * grad_probs, axis=1, keepdims=True)
            grad_scores = (probs * (grad_probs - delta)).astype(jnp.bfloat16)
            dq_ref[rows, cols] = dot_plain(grad_scores, keys) * SCORE_SCALE
            dkv_ref[:reach, :HD] += dot_outer(grad_scores, query) * SCORE_SCALE
            dkv_ref[:reach, HD:] += dot_outer(probs.astype(jnp.bfloat16), grad_out)
    grad_ref[:, :width] = turn(dq_ref[...], cos_ref[...], -sin_ref[...]).astype(jnp.bfloat16)
    pair = dkv_ref[...]
    lane = lax.broadcasted_iota(jnp.int32, pair.shape, 1)
    turned = turn(pair, cos_ref[...], -sin_ref[...])
    grad_ref[:, width:] = jnp.where(lane < HD, turned, pair).astype(jnp.bfloat16)


def in_vmem(count):
    return [pl.BlockSpec(memory_space=pltpu.VMEM)] * count


def attention_forward(qkv, tables, block_rows):
    length = qkv.shape[0]
    width = (H // KVH) * HD
    return pl.pallas_call(
        functools.partial(attention_forward_kernel, block_rows),
        out_shape=(
            jax.ShapeDtypeStruct((length, width), jnp.bfloat16),
            jax.ShapeDtypeStruct((length, 2 * HD), jnp.bfloat16),
            jax.ShapeDtypeStruct((length, width), jnp.bfloat16),
            jax.ShapeDtypeStruct((length, H // KVH), jnp.float32),
        ),
        in_specs=in_vmem(5),
        out_specs=tuple(in_vmem(4)),
        compiler_params=pltpu.CompilerParams(vmem_limit_bytes=48 * 2**20),
        name="attend",
    )(qkv, *tables)


def attention_backward(q, kv, grad_out, lse, tables, block_rows):
    length, width = q.shape
    return pl.pallas_call(
        functools.partial(attention_backward_kernel, block_rows),
        out_shape=jax.ShapeDtypeStruct((length, width + 2 * HD), jnp.bfloat16),
        in_specs=in_vmem(8),
        out_specs=in_vmem(1)[0],
        scratch_shapes=[
            pltpu.VMEM((length, width), jnp.float32),
            pltpu.VMEM((length, 2 * HD), jnp.float32),
        ],
        compiler_params=pltpu.CompilerParams(vmem_limit_bytes=48 * 2**20),
        name="attend_back",
    )(q, kv, grad_out, lse, *tables)


def on_device(
    tokens,
    doc_lengths,
    cotangent,
    gain_attn,
    w_query,
    w_key,
    w_value,
    w_output,
    gain_mlp,
    w_gate,
    w_up,
    w_down,
):
    local_rows, _ = tokens.shape[1:]
    ctx_size = lax.axis_size("ctx")
    fsdp_size = lax.axis_size("fsdp")
    length = local_rows * ctx_size
    group_width = (H // KVH) * HD
    ff_slice = FF // ctx_size
    held_rows = w_query.shape[0]
    bf16 = jnp.bfloat16

    positions = jnp.arange(length, dtype=jnp.int32)
    seq_lengths = doc_lengths[0]
    starts = jnp.cumsum(seq_lengths) - seq_lengths
    doc_ids = doc_index(positions, starts)
    cos_half, sin_half = rope_tables(positions)
    cos_table = jnp.concatenate([cos_half] * 4, axis=1)
    sin_table = jnp.concatenate([-sin_half, sin_half] * 2, axis=1)
    tables = (cos_table, sin_table, doc_ids[:, None], doc_ids[None, :])

    gain1, gain2 = gather_rows(jnp.stack([gain_attn, gain_mlp]).astype(jnp.float32))

    def by_slice(weight):
        return weight.reshape(held_rows, ctx_size, -1)

    qkv_parts = jnp.concatenate([by_slice(w_query), by_slice(w_key), by_slice(w_value)], axis=2)
    w_qkv = spread_columns(swap_ctx(qkv_parts.transpose(1, 0, 2)))
    wo_mine = lax.all_gather(w_output, "fsdp", axis=0, tiled=True)
    gu_parts = jnp.concatenate([by_slice(w_gate), by_slice(w_up)], axis=2)
    gu_mine = swap_ctx(gu_parts.transpose(1, 0, 2))

    inputs = tokens[0].astype(jnp.float32)
    inv_one = lax.rsqrt(jnp.mean(inputs * inputs, axis=-1, keepdims=True) + EPSILON)
    unit_one = inputs * inv_one
    normed1 = gather_ctx((unit_one * gain1).astype(bf16))
    normed1, gu_mine = lax.optimization_barrier((normed1, gu_mine))
    w_gu = spread_columns(gu_mine)
    wd_mine = lax.all_gather(w_down, "fsdp", axis=0, tiled=True)
    grad_out = cotangent[0].astype(jnp.float32)
    grad_mlp = (RESIDUAL_MULT * grad_out).astype(bf16)

    block_rows = math.gcd(length, 256)
    qkv = dot_plain(normed1, w_qkv)
    qkv, grad_mlp = lax.optimization_barrier((qkv, grad_mlp))
    grad_mlp = lax.all_gather(grad_mlp, "ctx", axis=0, tiled=True)
    q, kv, mixed_heads, log_sum = attention_forward(qkv, tables, block_rows)
    hidden = inputs + RESIDUAL_MULT * scatter_ctx(dot_plain(mixed_heads, wo_mine).astype(bf16))
    inv_two = lax.rsqrt(jnp.mean(hidden * hidden, axis=-1, keepdims=True) + EPSILON)
    unit_two = hidden * inv_two
    normed2 = gather_ctx((unit_two * gain2).astype(bf16))

    gate_up = dot_plain(normed2, w_gu)
    gate_pre, up_pre = gate_up[:, :ff_slice], gate_up[:, ff_slice:]
    sig_gate = jax.nn.sigmoid(gate_pre)
    silu_gate = gate_pre * sig_gate
    activ = (silu_gate * up_pre).astype(bf16)
    out_terms = dot_plain(activ, wd_mine).astype(bf16)

    silu_slope = sig_gate * (1.0 + gate_pre * (1.0 - sig_gate))
    grad_act = dot_back(grad_mlp, wd_mine)
    grad_gu = jnp.concatenate(
        [(grad_act * up_pre * silu_slope).astype(bf16), (grad_act * silu_gate).astype(bf16)], axis=1
    )
    out_terms, partial2, gu_terms, wd_terms = lax.optimization_barrier(
        (
            out_terms,
            dot_back(grad_gu, w_gu).astype(bf16),
            by_fsdp(dot_outer(normed2, grad_gu).astype(bf16), ctx_size, fsdp_size),
            dot_outer(activ, grad_mlp).astype(bf16),
        )
    )
    branch = lax.psum_scatter(out_terms, "ctx", scatter_dimension=0, tiled=True)
    output = (hidden + RESIDUAL_MULT * branch.astype(jnp.float32)).astype(bf16)[None]
    grad_norm2 = scatter_ctx(partial2)
    gu_back = lax.psum_scatter(gu_terms, "fsdp", scatter_dimension=0, tiled=True)
    wd_back = lax.psum_scatter(wd_terms, "fsdp", scatter_dimension=0, tiled=True)

    grad_g2 = jnp.sum(grad_norm2 * unit_two, axis=0)
    grad_hidden = grad_out + norm_back(grad_norm2, unit_two, inv_two, gain2)
    grad_attn = gather_ctx((RESIDUAL_MULT * grad_hidden).astype(bf16))
    grad_mixed, wo_terms = lax.optimization_barrier(
        (
            dot_back(grad_attn, wo_mine).astype(bf16),
            dot_outer(mixed_heads, grad_attn).astype(bf16),
        )
    )
    wo_back = lax.psum_scatter(wo_terms, "fsdp", scatter_dimension=0, tiled=True)
    grad_qkv = attention_backward(q, kv, grad_mixed, log_sum, tables, block_rows)
    grad_qkv, gu_back = lax.optimization_barrier((grad_qkv, gu_back))
    gu_back = return_columns(gu_back, ctx_size)
    partial1, qkv_terms = lax.optimization_barrier(
        (
            dot_back(grad_qkv, w_qkv).astype(bf16),
            by_fsdp(dot_outer(normed1, grad_qkv).astype(bf16), ctx_size, fsdp_size),
        )
    )
    grad_norm1 = scatter_ctx(partial1)
    qkv_back = lax.psum_scatter(qkv_terms, "fsdp", scatter_dimension=0, tiled=True)
    grad_norm1, qkv_back = lax.optimization_barrier((grad_norm1, qkv_back))
    qkv_back = return_columns(qkv_back, ctx_size)
    grad_g1 = jnp.sum(grad_norm1 * unit_one, axis=0)
    grad_inputs = grad_hidden + norm_back(grad_norm1, unit_one, inv_one, gain1)
    gain_back = scatter_rows(jnp.stack([grad_g1, grad_g2]))

    def joined(parts):
        return parts.transpose(1, 0, 2).reshape(held_rows, -1).astype(jnp.float32)

    key_end = group_width + HD
    return (
        output,
        grad_inputs[None],
        gain_back[0],
        joined(qkv_back[:, :, :group_width]),
        joined(qkv_back[:, :, group_width:key_end]),
        joined(qkv_back[:, :, key_end:]),
        wo_back.astype(jnp.float32),
        gain_back[1],
        joined(gu_back[:, :, :ff_slice]),
        joined(gu_back[:, :, ff_slice:]),
        wd_back.astype(jnp.float32),
    )


def solution(mesh):
    in_specs = (
        P("fsdp", "ctx", None),
        P("fsdp", None),
        P("fsdp", "ctx", None),
        P(("ctx", "fsdp")),
        P(("ctx", "fsdp"), None),
        P(("ctx", "fsdp"), None),
        P(("ctx", "fsdp"), None),
        P(("ctx", "fsdp"), None),
        P(("ctx", "fsdp")),
        P(("ctx", "fsdp"), None),
        P(("ctx", "fsdp"), None),
        P(("ctx", "fsdp"), None),
    )
    out_specs = (
        P("fsdp", "ctx", None),
        P("fsdp", "ctx", None),
        P(("ctx", "fsdp")),
        P(("ctx", "fsdp"), None),
        P(("ctx", "fsdp"), None),
        P(("ctx", "fsdp"), None),
        P(("ctx", "fsdp"), None),
        P(("ctx", "fsdp")),
        P(("ctx", "fsdp"), None),
        P(("ctx", "fsdp"), None),
        P(("ctx", "fsdp"), None),
    )
    if mesh.shape["ctx"] != KVH or KVH != 4 * PAIR:
        return jax.shard_map(
            general_device, mesh=mesh, in_specs=in_specs, out_specs=out_specs, check_vma=False
        )

    return jax.shard_map(
        on_device, mesh=mesh, in_specs=in_specs, out_specs=out_specs, check_vma=False
    )
```

```python
import functools
import math

import jax
import jax.numpy as jnp
from jax import lax
from jax.experimental import pallas as pl
from jax.experimental.pallas import tpu as pltpu
from jax.sharding import PartitionSpec as P

H = 32
KVH = 8
HD = 64
FF = 8192


EPSILON = 1e-05
SCORE_SCALE = 1.0 / 64.0
RESIDUAL_MULT = 0.22
ROPE_BASE = 10000000.0
NEGATIVE = -1e30
MESH = pl.DeviceIdType.MESH
PAIR = 2
CHUNKS = 2
LINK_COST = pl.CostEstimate(flops=0, bytes_accessed=150_000_000, transcendentals=0)


def doc_index(positions, starts):
    return jnp.sum((positions[:, None] >= starts[None, :]).astype(jnp.int32), axis=1) - 1


def rope_tables(positions):
    half_size = HD // 2
    frequency = ROPE_BASE ** (-(jnp.arange(half_size, dtype=jnp.float32) * 2.0) / HD)
    angles = positions.astype(jnp.float32)[:, None] * frequency[None, :]
    return (jnp.cos(angles), jnp.sin(angles))


def rotate(tensor, cos_table, sin_table, head_count):
    row_count = tensor.shape[0]
    by_head = tensor.reshape(row_count, head_count, HD)
    half_size = HD // 2
    first_half = by_head[..., :half_size]
    second_half = by_head[..., half_size:]
    cos_rows = cos_table[:, None, :]
    sin_rows = sin_table[:, None, :]
    turned = jnp.concatenate(
        [
            first_half * cos_rows - second_half * sin_rows,
            second_half * cos_rows + first_half * sin_rows,
        ],
        axis=-1,
    )
    return turned.reshape(row_count, head_count * HD)


def dot_plain(left, right):
    return jnp.dot(left, right, preferred_element_type=jnp.float32)


def dot_back(left, right):
    return lax.dot_general(
        left, right, (((1,), (1,)), ((), ())), preferred_element_type=jnp.float32
    )


def dot_outer(left, right):
    return lax.dot_general(
        left, right, (((0,), (0,)), ((), ())), preferred_element_type=jnp.float32
    )


def norm_back(grad_normed, unit_rows, inv_scale, gain_full):
    scaled = grad_normed * gain_full
    return inv_scale * (scaled - unit_rows * jnp.mean(scaled * unit_rows, axis=-1, keepdims=True))


def general_device(
    tokens,
    doc_lengths,
    cotangent,
    gain_attn,
    w_query,
    w_key,
    w_value,
    w_output,
    gain_mlp,
    w_gate,
    w_up,
    w_down,
):
    local_rows = tokens.shape[1]
    ctx_size = lax.axis_size("ctx")
    length = local_rows * ctx_size
    group_size = H // KVH
    offset = lax.axis_index("ctx") * local_rows
    positions = offset + jnp.arange(local_rows, dtype=jnp.int32)
    seq_lengths = doc_lengths[0]
    starts = jnp.cumsum(seq_lengths) - seq_lengths
    doc_ids = doc_index(positions, starts)
    last_pos = offset + local_rows - 1
    first_doc = doc_ids[0]
    cos_table, sin_table = rope_tables(positions)
    gain1, gain2, wq_full, wk_full, wv_full, wo_full = (
        lax.all_gather(gain_attn, ("ctx", "fsdp"), axis=0, tiled=True),
        lax.all_gather(gain_mlp, ("ctx", "fsdp"), axis=0, tiled=True),
        lax.all_gather(w_query, ("ctx", "fsdp"), axis=0, tiled=True),
        lax.all_gather(w_key, ("ctx", "fsdp"), axis=0, tiled=True),
        lax.all_gather(w_value, ("ctx", "fsdp"), axis=0, tiled=True),
        lax.all_gather(w_output, ("ctx", "fsdp"), axis=0, tiled=True),
    )
    gain1_f = gain1.astype(jnp.float32)
    gain2_f = gain2.astype(jnp.float32)
    inputs = tokens[0].astype(jnp.float32)
    inv_one = lax.rsqrt(jnp.mean(inputs * inputs, axis=-1, keepdims=True) + EPSILON)
    unit_one = inputs * inv_one
    normed1 = (unit_one * gain1_f).astype(jnp.bfloat16)
    queries = rotate(dot_plain(normed1, wq_full), cos_table, sin_table, H).astype(jnp.bfloat16)
    key_rot = rotate(dot_plain(normed1, wk_full), cos_table, sin_table, KVH).astype(jnp.bfloat16)
    values = dot_plain(normed1, wv_full).astype(jnp.bfloat16)
    grouped = queries.reshape(local_rows, KVH, group_size, HD)
    start_state = (
        jnp.full((local_rows, KVH, group_size), NEGATIVE, jnp.float32),
        jnp.zeros((local_rows, KVH, group_size), jnp.float32),
        jnp.zeros((local_rows, KVH, group_size, HD), jnp.float32),
    )
    running = start_state
    key_piece = lax.all_gather(key_rot, "ctx", axis=0, tiled=True)
    value_piece = lax.all_gather(values, "ctx", axis=0, tiled=True)
    piece_rows = key_piece.shape[0]
    attend_key_width = math.gcd(piece_rows, 512)
    block_count = piece_rows // attend_key_width

    def one_block(carried, index_block):
        block_start = index_block * attend_key_width
        key_blk = lax.dynamic_slice_in_dim(key_piece, block_start, attend_key_width, 0).reshape(
            attend_key_width, KVH, HD
        )
        value_blk = lax.dynamic_slice_in_dim(value_piece, block_start, attend_key_width, 0).reshape(
            attend_key_width, KVH, HD
        )
        key_pos = block_start + jnp.arange(attend_key_width, dtype=jnp.int32)
        key_docs = doc_index(key_pos, starts)
        skip_block = (block_start > last_pos) | (key_docs[attend_key_width - 1] < first_doc)

        def update(current):
            run_max, run_sum, accumulated = current
            scores = (
                jnp.einsum("qkgd,tkd->qkgt", grouped, key_blk, preferred_element_type=jnp.float32)
                * SCORE_SCALE
            )
            allowed = (key_docs[None, :] == doc_ids[:, None]) & (
                key_pos[None, :] <= positions[:, None]
            )
            allowed = allowed[:, None, None, :]
            masked = jnp.where(allowed, scores, NEGATIVE)
            new_max = jnp.maximum(run_max, jnp.max(masked, axis=-1))
            weights_exp = jnp.where(allowed, jnp.exp(masked - new_max[..., None]), 0.0)
            factor = jnp.exp(run_max - new_max)
            new_sum = run_sum * factor + jnp.sum(weights_exp, axis=-1)
            new_acc = accumulated * factor[..., None] + jnp.einsum(
                "qkgt,tkd->qkgd",
                weights_exp.astype(jnp.bfloat16),
                value_blk,
                preferred_element_type=jnp.float32,
            )
            return (new_max, new_sum, new_acc)

        return (lax.cond(skip_block, lambda unchanged: unchanged, update, carried), None)

    running, _ = lax.scan(one_block, running, jnp.arange(block_count))
    run_max, run_sum, accumulated = running
    attended = accumulated / run_sum[..., None]
    log_sum = run_max + jnp.log(run_sum)
    mixed_heads = attended.reshape(local_rows, H * HD).astype(jnp.bfloat16)
    hidden = inputs + RESIDUAL_MULT * dot_plain(mixed_heads, wo_full)
    inv_two = lax.rsqrt(jnp.mean(hidden * hidden, axis=-1, keepdims=True) + EPSILON)
    unit_two = hidden * inv_two
    normed2 = (unit_two * gain2_f).astype(jnp.bfloat16)
    wg_full, wu_full, wd_full = (
        lax.all_gather(w_gate, ("ctx", "fsdp"), axis=0, tiled=True),
        lax.all_gather(w_up, ("ctx", "fsdp"), axis=0, tiled=True),
        lax.all_gather(w_down, ("ctx", "fsdp"), axis=0, tiled=True),
    )
    gate_pre = dot_plain(normed2, wg_full)
    up_pre = dot_plain(normed2, wu_full)
    sig_gate = jax.nn.sigmoid(gate_pre)
    silu_gate = gate_pre * sig_gate
    activ = (silu_gate * up_pre).astype(jnp.bfloat16)
    result = hidden + RESIDUAL_MULT * dot_plain(activ, wd_full)
    output = result.astype(jnp.bfloat16)[None]
    grad_out = cotangent[0].astype(jnp.float32)
    grad_mlp = (RESIDUAL_MULT * grad_out).astype(jnp.bfloat16)
    silu_slope = sig_gate * (1.0 + gate_pre * (1.0 - sig_gate))
    wg_back, wu_back, wd_back = (
        lax.all_gather(w_gate, ("ctx", "fsdp"), axis=0, tiled=True),
        lax.all_gather(w_up, ("ctx", "fsdp"), axis=0, tiled=True),
        lax.all_gather(w_down, ("ctx", "fsdp"), axis=0, tiled=True),
    )
    grad_act = dot_back(grad_mlp, wd_back)
    grad_gate = (grad_act * up_pre * silu_slope).astype(jnp.bfloat16)
    grad_up = (grad_act * silu_gate).astype(jnp.bfloat16)
    grad_norm2 = dot_back(grad_gate, wg_back) + dot_back(grad_up, wu_back)
    left_cols = normed2
    gate_up_shard = lax.psum_scatter(
        jnp.concatenate([dot_outer(left_cols, grad_gate), dot_outer(left_cols, grad_up)], axis=1),
        ("ctx", "fsdp"),
        scatter_dimension=0,
        tiled=True,
    )
    wg_shard = gate_up_shard[:, :FF]
    wu_shard = gate_up_shard[:, FF:]
    left_cols = activ
    wd_shard = lax.psum_scatter(
        dot_outer(left_cols, grad_mlp), ("ctx", "fsdp"), scatter_dimension=0, tiled=True
    )
    grad_g2 = jnp.sum(grad_norm2 * unit_two, axis=0)
    grad_hidden = grad_out + norm_back(grad_norm2, unit_two, inv_two, gain2_f)
    grad_attn = (RESIDUAL_MULT * grad_hidden).astype(jnp.bfloat16)
    wq_back, wk_back, wv_back, wo_back = (
        lax.all_gather(w_query, ("ctx", "fsdp"), axis=0, tiled=True),
        lax.all_gather(w_key, ("ctx", "fsdp"), axis=0, tiled=True),
        lax.all_gather(w_value, ("ctx", "fsdp"), axis=0, tiled=True),
        lax.all_gather(w_output, ("ctx", "fsdp"), axis=0, tiled=True),
    )
    grad_wo = dot_outer(mixed_heads, grad_attn)
    grad_att = (
        dot_back(grad_attn, wo_back).astype(jnp.bfloat16).reshape(local_rows, KVH, group_size, HD)
    )
    row_delta = jnp.sum(grad_att.astype(jnp.float32) * attended, axis=-1)
    key_all, value_all = (
        lax.all_gather(key_rot, "ctx", axis=0, tiled=True),
        lax.all_gather(values, "ctx", axis=0, tiled=True),
    )
    key_width = math.gcd(length, 512)
    block_count = length // key_width

    def back_block(grad_query, index_block):
        block_start = index_block * key_width
        key_blk = lax.dynamic_slice_in_dim(key_all, block_start, key_width, 0).reshape(
            key_width, KVH, HD
        )
        value_blk = lax.dynamic_slice_in_dim(value_all, block_start, key_width, 0).reshape(
            key_width, KVH, HD
        )
        key_pos = block_start + jnp.arange(key_width, dtype=jnp.int32)
        key_docs = doc_index(key_pos, starts)
        skip_block = (block_start > last_pos) | (key_docs[key_width - 1] < first_doc)

        def compute(current):
            scores = (
                jnp.einsum("qkgd,tkd->qkgt", grouped, key_blk, preferred_element_type=jnp.float32)
                * SCORE_SCALE
            )
            allowed = (key_docs[None, :] == doc_ids[:, None]) & (
                key_pos[None, :] <= positions[:, None]
            )
            allowed = allowed[:, None, None, :]
            probs_blk = jnp.where(
                allowed, jnp.exp(jnp.where(allowed, scores, NEGATIVE) - log_sum[..., None]), 0.0
            )
            grad_probs = jnp.einsum(
                "qkgd,tkd->qkgt", grad_att, value_blk, preferred_element_type=jnp.float32
            )
            grad_scores = (probs_blk * (grad_probs - row_delta[..., None])).astype(jnp.bfloat16)
            new_query = (
                current
                + jnp.einsum(
                    "qkgt,tkd->qkgd", grad_scores, key_blk, preferred_element_type=jnp.float32
                )
                * SCORE_SCALE
            )
            grad_key = (
                jnp.einsum(
                    "qkgt,qkgd->tkd", grad_scores, grouped, preferred_element_type=jnp.float32
                )
                * SCORE_SCALE
            )
            grad_value = jnp.einsum(
                "qkgt,qkgd->tkd",
                probs_blk.astype(jnp.bfloat16),
                grad_att,
                preferred_element_type=jnp.float32,
            )
            return (
                new_query,
                (grad_key.reshape(key_width, KVH * HD), grad_value.reshape(key_width, KVH * HD)),
            )

        def nothing(current):
            zero_rows = jnp.zeros((key_width, KVH * HD), jnp.float32)
            return (current, (zero_rows, zero_rows))

        return lax.cond(skip_block, nothing, compute, grad_query)

    grad_query, key_terms = lax.scan(
        back_block,
        jnp.zeros((local_rows, KVH, group_size, HD), jnp.float32),
        jnp.arange(block_count),
    )
    key_term_all = key_terms[0].reshape(length, KVH * HD)
    value_term_all = key_terms[1].reshape(length, KVH * HD)
    grad_keys, grad_values = (
        lax.psum_scatter(
            key_term_all.astype(jnp.bfloat16), "ctx", scatter_dimension=0, tiled=True
        ).astype(jnp.float32),
        lax.psum_scatter(
            value_term_all.astype(jnp.bfloat16), "ctx", scatter_dimension=0, tiled=True
        ).astype(jnp.float32),
    )
    grad_q_pre = rotate(grad_query.reshape(local_rows, H * HD), cos_table, -sin_table, H).astype(
        jnp.bfloat16
    )
    grad_k_pre = rotate(grad_keys, cos_table, -sin_table, KVH).astype(jnp.bfloat16)
    grad_v_pre = grad_values.astype(jnp.bfloat16)
    grad_norm1 = (
        dot_back(grad_q_pre, wq_back)
        + dot_back(grad_k_pre, wk_back)
        + dot_back(grad_v_pre, wv_back)
    )
    grad_wq = dot_outer(normed1, grad_q_pre)
    grad_wk = dot_outer(normed1, grad_k_pre)
    grad_wv = dot_outer(normed1, grad_v_pre)
    grad_g1 = jnp.sum(grad_norm1 * unit_one, axis=0)
    grad_inputs = grad_hidden + norm_back(grad_norm1, unit_one, inv_one, gain1_f)
    g1_shard, g2_shard, wq_shard, wk_shard, wv_shard, wo_shard = (
        lax.psum_scatter(grad_g1, ("ctx", "fsdp"), scatter_dimension=0, tiled=True),
        lax.psum_scatter(grad_g2, ("ctx", "fsdp"), scatter_dimension=0, tiled=True),
        lax.psum_scatter(grad_wq, ("ctx", "fsdp"), scatter_dimension=0, tiled=True),
        lax.psum_scatter(grad_wk, ("ctx", "fsdp"), scatter_dimension=0, tiled=True),
        lax.psum_scatter(grad_wv, ("ctx", "fsdp"), scatter_dimension=0, tiled=True),
        lax.psum_scatter(grad_wo, ("ctx", "fsdp"), scatter_dimension=0, tiled=True),
    )
    return (
        output,
        grad_inputs[None],
        g1_shard,
        wq_shard,
        wk_shard,
        wv_shard,
        wo_shard,
        g2_shard,
        wg_shard,
        wu_shard,
        wd_shard,
    )


def rows_of(blocks):
    return blocks.reshape((-1,) + blocks.shape[2:])


def greet_line(barrier, ctx_at, line_at, line_size):
    other = ctx_at + 1 - 2 * (ctx_at % PAIR)
    pl.semaphore_signal(barrier, inc=1, device_id={"ctx": other}, device_id_type=MESH)

    @pl.when(line_at > 0)
    def _():
        pl.semaphore_signal(barrier, inc=1, device_id={"ctx": ctx_at - PAIR}, device_id_type=MESH)

    @pl.when(line_at < line_size - 1)
    def _():
        pl.semaphore_signal(barrier, inc=1, device_id={"ctx": ctx_at + PAIR}, device_id_type=MESH)

    last = line_size - 1
    neighbours = 1 + (line_at + last - 1) // last + (2 * last - 1 - line_at) // last
    pl.semaphore_wait(barrier, neighbours)


def gather_kernel(line_size, x_ref, out_ref, send_sem, recv_sem, own_sem):
    me = lax.axis_index("ctx")
    line_at, pair_at = me // PAIR, me % PAIR
    rows = x_ref.shape[0]
    step = rows // CHUNKS
    greet_line(pltpu.get_barrier_semaphore(), me, line_at, line_size)

    def piece(block, part):
        return out_ref.at[pl.ds(pl.multiple_of(block * rows + part * step, step), step), :]

    def copy(block, part, way, own):
        target = (me + 1 - 2 * pair_at, me + PAIR, me - PAIR)[way]
        slot = block * CHUNKS + part
        return pltpu.make_async_remote_copy(
            src_ref=x_ref.at[pl.ds(part * step, step), :] if own else piece(block, part),
            dst_ref=piece(block, part),
            send_sem=send_sem.at[way, slot],
            recv_sem=recv_sem.at[slot],
            device_id={"ctx": target},
            device_id_type=MESH,
        )

    def pass_on(block, part, upward, downward, own, act):
        if upward is not None:
            pl.when(upward)(lambda: act(copy(block, part, 1, own)))
        if downward is not None:
            pl.when(downward)(lambda: act(copy(block, part, 2, own)))
        act(copy(block, part, 0, own))

    def visit(act, arrive):
        for part in range(CHUNKS):
            pass_on(me, part, line_at < line_size - 1, line_at > 0, True, act)
        for distance in range(1, line_size):
            for part in range(CHUNKS):

                @pl.when(line_at >= distance)
                def _():
                    block = me - PAIR * distance
                    arrive(block, part)
                    pass_on(block, part, line_at < line_size - 1, None, False, act)

                @pl.when(line_at + distance < line_size)
                def _():
                    block = me + PAIR * distance
                    arrive(block, part)
                    pass_on(block, part, None, line_at > 0, False, act)

    keep = pltpu.make_async_copy(
        x_ref, out_ref.at[pl.ds(pl.multiple_of(me * rows, rows), rows), :], own_sem
    )
    keep.start()
    visit(lambda c: c.start(), lambda block, part: copy(block, part, 0, False).wait_recv())
    for place in range(line_size):
        for part in range(CHUNKS):
            copy(place * PAIR + 1 - pair_at, part, 0, False).wait_recv()
    visit(lambda c: c.wait_send(), lambda block, part: None)
    keep.wait()


def gather_ctx(local):
    ctx_size = lax.axis_size("ctx")
    rows, width = local.shape
    return pl.pallas_call(
        functools.partial(gather_kernel, ctx_size // PAIR),
        out_shape=jax.ShapeDtypeStruct((ctx_size * rows, width), local.dtype),
        in_specs=[pl.BlockSpec(memory_space=pl.ANY)],
        out_specs=pl.BlockSpec(memory_space=pl.ANY),
        scratch_shapes=[
            pltpu.SemaphoreType.DMA((3, ctx_size * CHUNKS)),
            pltpu.SemaphoreType.DMA((ctx_size * CHUNKS,)),
            pltpu.SemaphoreType.DMA,
        ],
        compiler_params=pltpu.CompilerParams(collective_id=0, has_side_effects=True),
        cost_estimate=LINK_COST,
        name="gather_ctx",
    )(local)


def scatter_kernel(line_size, x_ref, out_ref, near, below, above, send_sem, near_sem, line_sem, line_send):
    me = lax.axis_index("ctx")
    line_at, pair_at = me // PAIR, me % PAIR
    rows = out_ref.shape[0]
    step = rows // CHUNKS
    greet_line(pltpu.get_barrier_semaphore(), me, line_at, line_size)
    half = line_size // 2
    low = line_at // half
    last = line_size - 1
    order = [k + (last - 2 * k) * (1 - low) for k in range(half)]
    if line_size == 4:
        order += [line_at + 1 - 2 * (line_at % 2), line_at]

    def near_copy(place, part):
        start = (place * PAIR + 1 - pair_at) * rows + part * step
        return pltpu.make_async_remote_copy(
            src_ref=x_ref.at[pl.ds(pl.multiple_of(start, step), step), :],
            dst_ref=near.at[place, pl.ds(part * step, step), :],
            send_sem=send_sem.at[place, part],
            recv_sem=near_sem.at[place, part],
            device_id={"ctx": me + 1 - 2 * pair_at},
            device_id_type=MESH,
        )

    def line_copy(place, part, up):
        part_rows = pl.ds(part * step, step)
        return pltpu.make_async_remote_copy(
            src_ref=near.at[place, part_rows, :],
            dst_ref=(below if up else above).at[place, part_rows, :],
            send_sem=line_send.at[place, part],
            recv_sem=line_sem.at[0 if up else 1, place, part],
            device_id={"ctx": me + PAIR if up else me - PAIR},
            device_id_type=MESH,
        )

    for place in order:
        for part in range(CHUNKS):
            near_copy(place, part).start()

    for place in order[:-1]:
        for part in range(CHUNKS):
            part_rows = pl.ds(part * step, step)
            mine = x_ref.at[pl.ds(pl.multiple_of((place * PAIR + pair_at) * rows + part * step, step), step), :]
            near_copy(place, part).wait_recv()

            def send(up, waits, arrived):
                @pl.when(waits)
                def _():
                    line_copy(place, part, up).wait_recv()
                    near[place, part_rows, :] = (
                        mine[...].astype(jnp.float32)
                        + near[place, part_rows, :].astype(jnp.float32)
                        + arrived[place, part_rows, :].astype(jnp.float32)
                    ).astype(near.dtype)

                @pl.when(jnp.logical_not(waits))
                def _():
                    near[place, part_rows, :] = (
                        mine[...].astype(jnp.float32) + near[place, part_rows, :].astype(jnp.float32)
                    ).astype(near.dtype)

                line_copy(place, part, up).start()

            @pl.when(place > line_at)
            def _():
                send(True, line_at > 0, below)

            @pl.when(place < line_at)
            def _():
                send(False, line_at < last, above)

    for part in range(CHUNKS):
        part_rows = pl.ds(part * step, step)
        mine = x_ref.at[pl.ds(pl.multiple_of(me * rows + part * step, step), step), :]
        near_copy(line_at, part).wait_recv()
        out_ref[part_rows, :] = mine[...].astype(jnp.float32) + near[line_at, part_rows, :].astype(jnp.float32)

        @pl.when(line_at > 0)
        def _():
            line_copy(line_at, part, True).wait_recv()
            out_ref[part_rows, :] += below[line_at, part_rows, :].astype(jnp.float32)

        @pl.when(line_at < last)
        def _():
            line_copy(line_at, part, False).wait_recv()
            out_ref[part_rows, :] += above[line_at, part_rows, :].astype(jnp.float32)

    for place in order:
        for part in range(CHUNKS):
            near_copy(place, part).wait_send()
    for place in order[:-1]:
        for part in range(CHUNKS):
            line_copy(place, part, True).wait_send()


def scatter_ctx(partial):
    ctx_size = lax.axis_size("ctx")
    line_size = ctx_size // PAIR
    rows, width = partial.shape[0] // ctx_size, partial.shape[1]
    held = pltpu.VMEM((line_size, rows, width), partial.dtype)
    return pl.pallas_call(
        functools.partial(scatter_kernel, line_size),
        out_shape=jax.ShapeDtypeStruct((rows, width), jnp.float32),
        in_specs=[pl.BlockSpec(memory_space=pltpu.VMEM)],
        out_specs=pl.BlockSpec(memory_space=pltpu.VMEM),
        scratch_shapes=[
            held, held, held,
            pltpu.SemaphoreType.DMA((line_size, CHUNKS)),
            pltpu.SemaphoreType.DMA((line_size, CHUNKS)),
            pltpu.SemaphoreType.DMA((2, line_size, CHUNKS)),
            pltpu.SemaphoreType.DMA((line_size, CHUNKS)),
        ],
        compiler_params=pltpu.CompilerParams(
            collective_id=1, has_side_effects=True, vmem_limit_bytes=32 * 2**20
        ),
        cost_estimate=LINK_COST,
        name="scatter_ctx",
    )(partial)


def exchange_kernel(ctx_size, fsdp_size, x_ref, out_ref, send_sem, recv_sem):
    count = ctx_size * fsdp_size
    me = lax.axis_index("ctx") * fsdp_size + lax.axis_index("fsdp")
    barrier = pltpu.get_barrier_semaphore()

    def device(index):
        return (index // fsdp_size, index % fsdp_size)

    def greet(k, unused):
        pl.semaphore_signal(barrier, inc=1, device_id=device((me + k) % count), device_id_type=MESH)
        return unused

    lax.fori_loop(1, count, greet, 0)
    pl.semaphore_wait(barrier, count - 1)

    def copy(k):
        target = (me + k) % count
        return pltpu.make_async_remote_copy(
            src_ref=x_ref.at[target], dst_ref=out_ref.at[me],
            send_sem=send_sem.at[k], recv_sem=recv_sem.at[k],
            device_id=device(target), device_id_type=MESH,
        )

    def start(k, unused):
        copy(k).start()
        return unused

    def finish(k, unused):
        source = (me + count - k) % count
        pltpu.make_async_remote_copy(
            src_ref=x_ref.at[source], dst_ref=out_ref.at[source],
            send_sem=send_sem.at[k], recv_sem=recv_sem.at[k],
            device_id=device(source), device_id_type=MESH,
        ).wait_recv()
        copy(k).wait_send()
        return unused

    lax.fori_loop(1, count, start, 0)
    out_ref[pl.ds(me, 1)] = x_ref[pl.ds(me, 1)]
    lax.fori_loop(1, count, finish, 0)


def exchange(tiles):
    ctx_size, fsdp_size = lax.axis_size("ctx"), lax.axis_size("fsdp")
    count = ctx_size * fsdp_size
    return pl.pallas_call(
        functools.partial(exchange_kernel, ctx_size, fsdp_size),
        out_shape=jax.ShapeDtypeStruct(tiles.shape, tiles.dtype),
        in_specs=[pl.BlockSpec(memory_space=pltpu.VMEM)],
        out_specs=pl.BlockSpec(memory_space=pltpu.VMEM),
        scratch_shapes=[pltpu.SemaphoreType.DMA((count,)), pltpu.SemaphoreType.DMA((count,))],
        compiler_params=pltpu.CompilerParams(collective_id=2, has_side_effects=True),
        cost_estimate=pl.CostEstimate(flops=0, bytes_accessed=25_000_000, transcendentals=0),
        name="exchange",
    )(tiles)


def padded(rows):
    return jnp.pad(rows, ((0, 0), (0, 8 - rows.shape[1]), (0, 128 - rows.shape[2])))


def gather_rows(rows):
    count = lax.axis_size("ctx") * lax.axis_size("fsdp")
    tiles = jnp.broadcast_to(padded(rows[None]), (count, 8, 128))
    return exchange(tiles)[:, : rows.shape[0], : rows.shape[1]].transpose(1, 0, 2).reshape(rows.shape[0], -1)


def scatter_rows(rows):
    count = lax.axis_size("ctx") * lax.axis_size("fsdp")
    by_owner = rows.reshape(rows.shape[0], count, -1).transpose(1, 0, 2)
    return jnp.sum(exchange(padded(by_owner)), axis=0)[: rows.shape[0], : by_owner.shape[2]]


def swap_ctx(blocks):
    return lax.all_to_all(blocks, "ctx", split_axis=0, concat_axis=0, tiled=True)


def spread_columns(mine):
    full = lax.all_gather(mine[:, None], "fsdp", axis=1, tiled=True)
    return full.reshape(-1, mine.shape[-1])


def by_fsdp(grad, ctx_size, fsdp_size):
    parts = grad.reshape(ctx_size, fsdp_size, -1, grad.shape[-1]).transpose(1, 0, 2, 3)
    return rows_of(rows_of(parts))


def return_columns(terms, ctx_size):
    return swap_ctx(terms.reshape(ctx_size, -1, terms.shape[-1]))


def swap_groups(values, outer, inner):
    parts = values.reshape(values.shape[0], outer, inner, -1)
    return parts.transpose(0, 2, 1, 3).reshape(values.shape)


def half_turn(values, sign_table):
    lane = lax.broadcasted_iota(jnp.int32, values.shape, 1)
    width = values.shape[1]
    quarter = HD // 2
    ahead = pltpu.roll(values, width - quarter, 1)
    behind = pltpu.roll(values, quarter, 1)
    return jnp.where(lane % HD < quarter, ahead, behind) * sign_table


def turn(values, cos_table, sign_table):
    copies = values.shape[1] // cos_table.shape[1]
    if copies > 1:
        cos_table = jnp.concatenate([cos_table] * copies, axis=1)
        sign_table = jnp.concatenate([sign_table] * copies, axis=1)
    return values * cos_table + half_turn(values, sign_table)


def attention_forward_kernel(
    block_rows, qkv_ref, cos_ref, sin_ref, doc_col_ref, doc_row_ref, q_ref, kv_ref, out_ref, lse_ref
):
    length = qkv_ref.shape[0]
    group = H // KVH
    width = group * HD
    q_ref[...] = turn(qkv_ref[:, :width], cos_ref[...], sin_ref[...]).astype(jnp.bfloat16)
    pair = qkv_ref[:, width:]
    lane = lax.broadcasted_iota(jnp.int32, pair.shape, 1)
    turned = turn(pair, cos_ref[...], sin_ref[...])
    kv_ref[...] = jnp.where(lane < HD, turned, pair).astype(jnp.bfloat16)
    for block in range(length // block_rows):
        rows = slice(block * block_rows, (block + 1) * block_rows)
        reach = (block + 1) * block_rows
        keys = kv_ref[:reach, :HD]
        values = kv_ref[:reach, HD:]
        query_at = block * block_rows + lax.broadcasted_iota(jnp.int32, (block_rows, reach), 0)
        key_at = lax.broadcasted_iota(jnp.int32, (block_rows, reach), 1)
        allowed = (doc_col_ref[rows, :] == doc_row_ref[:, :reach]) & (key_at <= query_at)
        for head in range(group):
            cols = slice(head * HD, (head + 1) * HD)
            scores = dot_back(q_ref[rows, cols], keys) * SCORE_SCALE
            masked = jnp.where(allowed, scores, NEGATIVE)
            top = jnp.max(masked, axis=1, keepdims=True)
            weights = jnp.where(allowed, jnp.exp(masked - top), 0.0)
            total = jnp.sum(weights, axis=1, keepdims=True)
            mixed = dot_plain(weights.astype(jnp.bfloat16), values)
            out_ref[rows, cols] = (mixed / total).astype(jnp.bfloat16)
            lse_ref[rows, head : head + 1] = top + jnp.log(total)


def attention_backward_kernel(
    block_rows, q_ref, kv_ref, do_ref, lse_ref, cos_ref, sin_ref, doc_col_ref, doc_row_ref, grad_ref, dq_ref, dkv_ref
):
    length = q_ref.shape[0]
    group = H // KVH
    width = group * HD
    dkv_ref[...] = jnp.zeros_like(dkv_ref)
    for block in range(length // block_rows):
        rows = slice(block * block_rows, (block + 1) * block_rows)
        reach = (block + 1) * block_rows
        keys = kv_ref[:reach, :HD]
        values = kv_ref[:reach, HD:]
        query_at = block * block_rows + lax.broadcasted_iota(jnp.int32, (block_rows, reach), 0)
        key_at = lax.broadcasted_iota(jnp.int32, (block_rows, reach), 1)
        allowed = (doc_col_ref[rows, :] == doc_row_ref[:, :reach]) & (key_at <= query_at)
        for head in range(group):
            cols = slice(head * HD, (head + 1) * HD)
            query = q_ref[rows, cols]
            grad_out = do_ref[rows, cols]
            scores = dot_back(query, keys) * SCORE_SCALE
            probs = jnp.where(
                allowed,
                jnp.exp(jnp.where(allowed, scores, NEGATIVE) - lse_ref[rows, head : head + 1]),
                0.0,
            )
            grad_probs = dot_back(grad_out, values)
            delta = jnp.sum(probs * grad_probs, axis=1, keepdims=True)
            grad_scores = (probs * (grad_probs - delta)).astype(jnp.bfloat16)
            dq_ref[rows, cols] = dot_plain(grad_scores, keys) * SCORE_SCALE
            dkv_ref[:reach, :HD] += dot_outer(grad_scores, query) * SCORE_SCALE
            dkv_ref[:reach, HD:] += dot_outer(probs.astype(jnp.bfloat16), grad_out)
    grad_ref[:, :width] = turn(dq_ref[...], cos_ref[...], -sin_ref[...]).astype(jnp.bfloat16)
    pair = dkv_ref[...]
    lane = lax.broadcasted_iota(jnp.int32, pair.shape, 1)
    turned = turn(pair, cos_ref[...], -sin_ref[...])
    grad_ref[:, width:] = jnp.where(lane < HD, turned, pair).astype(jnp.bfloat16)


def in_vmem(count):
    return [pl.BlockSpec(memory_space=pltpu.VMEM)] * count


def attention_forward(qkv, tables, block_rows):
    length = qkv.shape[0]
    width = (H // KVH) * HD
    return pl.pallas_call(
        functools.partial(attention_forward_kernel, block_rows),
        out_shape=(
            jax.ShapeDtypeStruct((length, width), jnp.bfloat16),
            jax.ShapeDtypeStruct((length, 2 * HD), jnp.bfloat16),
            jax.ShapeDtypeStruct((length, width), jnp.bfloat16),
            jax.ShapeDtypeStruct((length, H // KVH), jnp.float32),
        ),
        in_specs=in_vmem(5),
        out_specs=tuple(in_vmem(4)),
        compiler_params=pltpu.CompilerParams(vmem_limit_bytes=48 * 2**20),
        name="attend",
    )(qkv, *tables)


def attention_backward(q, kv, grad_out, lse, tables, block_rows):
    length, width = q.shape
    return pl.pallas_call(
        functools.partial(attention_backward_kernel, block_rows),
        out_shape=jax.ShapeDtypeStruct((length, width + 2 * HD), jnp.bfloat16),
        in_specs=in_vmem(8),
        out_specs=in_vmem(1)[0],
        scratch_shapes=[
            pltpu.VMEM((length, width), jnp.float32),
            pltpu.VMEM((length, 2 * HD), jnp.float32),
        ],
        compiler_params=pltpu.CompilerParams(vmem_limit_bytes=48 * 2**20),
        name="attend_back",
    )(q, kv, grad_out, lse, *tables)


def on_device(
    tokens,
    doc_lengths,
    cotangent,
    gain_attn,
    w_query,
    w_key,
    w_value,
    w_output,
    gain_mlp,
    w_gate,
    w_up,
    w_down,
):
    local_rows, _ = tokens.shape[1:]
    ctx_size = lax.axis_size("ctx")
    fsdp_size = lax.axis_size("fsdp")
    length = local_rows * ctx_size
    group_width = (H // KVH) * HD
    ff_slice = FF // ctx_size
    held_rows = w_query.shape[0]
    bf16 = jnp.bfloat16

    positions = jnp.arange(length, dtype=jnp.int32)
    seq_lengths = doc_lengths[0]
    starts = jnp.cumsum(seq_lengths) - seq_lengths
    doc_ids = doc_index(positions, starts)
    cos_half, sin_half = rope_tables(positions)
    cos_table = jnp.concatenate([cos_half] * 4, axis=1)
    sin_table = jnp.concatenate([-sin_half, sin_half] * 2, axis=1)
    tables = (cos_table, sin_table, doc_ids[:, None], doc_ids[None, :])

    gain1, gain2 = gather_rows(jnp.stack([gain_attn, gain_mlp]).astype(jnp.float32))

    def by_slice(weight):
        return weight.reshape(held_rows, ctx_size, -1)

    qkv_parts = jnp.concatenate([by_slice(w_query), by_slice(w_key), by_slice(w_value)], axis=2)
    w_qkv = spread_columns(swap_ctx(qkv_parts.transpose(1, 0, 2)))
    wo_mine = lax.all_gather(w_output, "fsdp", axis=0, tiled=True)
    gu_parts = jnp.concatenate([by_slice(w_gate), by_slice(w_up)], axis=2)
    gu_mine = swap_ctx(gu_parts.transpose(1, 0, 2))

    inputs = tokens[0].astype(jnp.float32)
    inv_one = lax.rsqrt(jnp.mean(inputs * inputs, axis=-1, keepdims=True) + EPSILON)
    unit_one = inputs * inv_one
    normed1 = gather_ctx((unit_one * gain1).astype(bf16))
    normed1, gu_mine = lax.optimization_barrier((normed1, gu_mine))
    w_gu = lax.all_gather(rows_of(gu_mine), "fsdp", axis=0, tiled=True)
    wd_mine = lax.all_gather(w_down, "fsdp", axis=0, tiled=True)
    grad_out = cotangent[0].astype(jnp.float32)
    grad_mlp = (RESIDUAL_MULT * grad_out).astype(bf16)

    block_rows = math.gcd(length, 256)
    qkv = dot_plain(normed1, w_qkv)
    qkv, grad_mlp = lax.optimization_barrier((qkv, grad_mlp))
    grad_mlp = lax.all_gather(grad_mlp, "ctx", axis=0, tiled=True)
    q, kv, mixed_heads, log_sum = attention_forward(qkv, tables, block_rows)
    hidden = inputs + RESIDUAL_MULT * scatter_ctx(dot_plain(mixed_heads, wo_mine).astype(bf16))
    inv_two = lax.rsqrt(jnp.mean(hidden * hidden, axis=-1, keepdims=True) + EPSILON)
    unit_two = hidden * inv_two
    normed2 = gather_ctx(swap_groups((unit_two * gain2).astype(bf16), ctx_size, fsdp_size))

    gate_up = dot_plain(normed2, w_gu)
    gate_pre, up_pre = gate_up[:, :ff_slice], gate_up[:, ff_slice:]
    sig_gate = jax.nn.sigmoid(gate_pre)
    silu_gate = gate_pre * sig_gate
    activ = (silu_gate * up_pre).astype(bf16)
    activ, gate_up = lax.optimization_barrier((activ, gate_up))
    gate_pre, up_pre = gate_up[:, :ff_slice], gate_up[:, ff_slice:]
    sig_gate = jax.nn.sigmoid(gate_pre)
    silu_gate = gate_pre * sig_gate
    out_terms, grad_mlp = lax.optimization_barrier(
        (dot_plain(activ, wd_mine).astype(bf16), grad_mlp)
    )
    branch = lax.psum_scatter(out_terms, "ctx", scatter_dimension=0, tiled=True)
    output = (hidden + RESIDUAL_MULT * branch.astype(jnp.float32)).astype(bf16)[None]

    silu_slope = sig_gate * (1.0 + gate_pre * (1.0 - sig_gate))
    grad_act = dot_back(grad_mlp, wd_mine)
    grad_gu = jnp.concatenate(
        [(grad_act * up_pre * silu_slope).astype(bf16), (grad_act * silu_gate).astype(bf16)], axis=1
    )
    partial2, gu_terms, wd_terms = lax.optimization_barrier(
        (
            dot_back(grad_gu, w_gu).astype(bf16),
            dot_outer(normed2, grad_gu).astype(bf16),
            dot_outer(activ, grad_mlp).astype(bf16),
        )
    )
    grad_norm2 = swap_groups(scatter_ctx(partial2), fsdp_size, ctx_size)
    gu_back = lax.psum_scatter(gu_terms, "fsdp", scatter_dimension=0, tiled=True)
    wd_back = lax.psum_scatter(wd_terms, "fsdp", scatter_dimension=0, tiled=True)

    grad_g2 = jnp.sum(grad_norm2 * unit_two, axis=0)
    grad_hidden = grad_out + norm_back(grad_norm2, unit_two, inv_two, gain2)
    grad_attn = gather_ctx((RESIDUAL_MULT * grad_hidden).astype(bf16))
    grad_mixed, wo_terms = lax.optimization_barrier(
        (
            dot_back(grad_attn, wo_mine).astype(bf16),
            dot_outer(mixed_heads, grad_attn).astype(bf16),
        )
    )
    wo_back = lax.psum_scatter(wo_terms, "fsdp", scatter_dimension=0, tiled=True)
    grad_qkv = attention_backward(q, kv, grad_mixed, log_sum, tables, block_rows)
    grad_qkv, gu_back = lax.optimization_barrier((grad_qkv, gu_back))
    gu_back = return_columns(gu_back, ctx_size)
    partial1, qkv_terms = lax.optimization_barrier(
        (
            dot_back(grad_qkv, w_qkv).astype(bf16),
            by_fsdp(dot_outer(normed1, grad_qkv).astype(bf16), ctx_size, fsdp_size),
        )
    )
    grad_norm1 = scatter_ctx(partial1)
    qkv_back = lax.psum_scatter(qkv_terms, "fsdp", scatter_dimension=0, tiled=True)
    grad_norm1, qkv_back = lax.optimization_barrier((grad_norm1, qkv_back))
    qkv_back = return_columns(qkv_back, ctx_size)
    grad_g1 = jnp.sum(grad_norm1 * unit_one, axis=0)
    grad_inputs = grad_hidden + norm_back(grad_norm1, unit_one, inv_one, gain1)
    gain_back = scatter_rows(jnp.stack([grad_g1, grad_g2]))

    def joined(parts):
        return parts.transpose(1, 0, 2).reshape(held_rows, -1).astype(jnp.float32)

    key_end = group_width + HD
    return (
        output,
        grad_inputs[None],
        gain_back[0],
        joined(qkv_back[:, :, :group_width]),
        joined(qkv_back[:, :, group_width:key_end]),
        joined(qkv_back[:, :, key_end:]),
        wo_back.astype(jnp.float32),
        gain_back[1],
        joined(gu_back[:, :, :ff_slice]),
        joined(gu_back[:, :, ff_slice:]),
        wd_back.astype(jnp.float32),
    )


def solution(mesh):
    in_specs = (
        P("fsdp", "ctx", None),
        P("fsdp", None),
        P("fsdp", "ctx", None),
        P(("ctx", "fsdp")),
        P(("ctx", "fsdp"), None),
        P(("ctx", "fsdp"), None),
        P(("ctx", "fsdp"), None),
        P(("ctx", "fsdp"), None),
        P(("ctx", "fsdp")),
        P(("ctx", "fsdp"), None),
        P(("ctx", "fsdp"), None),
        P(("ctx", "fsdp"), None),
    )
    out_specs = (
        P("fsdp", "ctx", None),
        P("fsdp", "ctx", None),
        P(("ctx", "fsdp")),
        P(("ctx", "fsdp"), None),
        P(("ctx", "fsdp"), None),
        P(("ctx", "fsdp"), None),
        P(("ctx", "fsdp"), None),
        P(("ctx", "fsdp")),
        P(("ctx", "fsdp"), None),
        P(("ctx", "fsdp"), None),
        P(("ctx", "fsdp"), None),
    )
    if mesh.shape["ctx"] != KVH or KVH != 4 * PAIR:
        return jax.shard_map(
            general_device, mesh=mesh, in_specs=in_specs, out_specs=out_specs, check_vma=False
        )

    return jax.shard_map(
        on_device, mesh=mesh, in_specs=in_specs, out_specs=out_specs, check_vma=False
    )
```

```python
import functools
import math

import jax
import jax.numpy as jnp
from jax import lax
from jax.experimental import pallas as pl
from jax.experimental.pallas import tpu as pltpu
from jax.sharding import PartitionSpec as P

H = 32
KVH = 8
HD = 64
FF = 8192


EPSILON = 1e-05
SCORE_SCALE = 1.0 / 64.0
RESIDUAL_MULT = 0.22
ROPE_BASE = 10000000.0
NEGATIVE = -1e30
MESH = pl.DeviceIdType.MESH
PAIR = 2
CHUNKS = 2
ANYWHERE = pl.BlockSpec(memory_space=pl.ANY)
LINK_COST = pl.CostEstimate(flops=0, bytes_accessed=150_000_000, transcendentals=0)


def doc_index(positions, starts):
    return jnp.sum((positions[:, None] >= starts[None, :]).astype(jnp.int32), axis=1) - 1


def rope_tables(positions):
    half_size = HD // 2
    frequency = ROPE_BASE ** (-(jnp.arange(half_size, dtype=jnp.float32) * 2.0) / HD)
    angles = positions.astype(jnp.float32)[:, None] * frequency[None, :]
    return (jnp.cos(angles), jnp.sin(angles))


def rotate(tensor, cos_table, sin_table, head_count):
    row_count = tensor.shape[0]
    by_head = tensor.reshape(row_count, head_count, HD)
    half_size = HD // 2
    first_half = by_head[..., :half_size]
    second_half = by_head[..., half_size:]
    cos_rows = cos_table[:, None, :]
    sin_rows = sin_table[:, None, :]
    turned = jnp.concatenate(
        [
            first_half * cos_rows - second_half * sin_rows,
            second_half * cos_rows + first_half * sin_rows,
        ],
        axis=-1,
    )
    return turned.reshape(row_count, head_count * HD)


def dot_plain(left, right):
    return jnp.dot(left, right, preferred_element_type=jnp.float32)


def dot_back(left, right):
    return lax.dot_general(
        left, right, (((1,), (1,)), ((), ())), preferred_element_type=jnp.float32
    )


def dot_outer(left, right):
    return lax.dot_general(
        left, right, (((0,), (0,)), ((), ())), preferred_element_type=jnp.float32
    )


def norm_back(grad_normed, unit_rows, inv_scale, gain_full):
    scaled = grad_normed * gain_full
    return inv_scale * (scaled - unit_rows * jnp.mean(scaled * unit_rows, axis=-1, keepdims=True))


def general_device(
    tokens,
    doc_lengths,
    cotangent,
    gain_attn,
    w_query,
    w_key,
    w_value,
    w_output,
    gain_mlp,
    w_gate,
    w_up,
    w_down,
):
    local_rows = tokens.shape[1]
    ctx_size = lax.axis_size("ctx")
    length = local_rows * ctx_size
    group_size = H // KVH
    offset = lax.axis_index("ctx") * local_rows
    positions = offset + jnp.arange(local_rows, dtype=jnp.int32)
    seq_lengths = doc_lengths[0]
    starts = jnp.cumsum(seq_lengths) - seq_lengths
    doc_ids = doc_index(positions, starts)
    last_pos = offset + local_rows - 1
    first_doc = doc_ids[0]
    cos_table, sin_table = rope_tables(positions)
    gain1, gain2, wq_full, wk_full, wv_full, wo_full = (
        lax.all_gather(gain_attn, ("ctx", "fsdp"), axis=0, tiled=True),
        lax.all_gather(gain_mlp, ("ctx", "fsdp"), axis=0, tiled=True),
        lax.all_gather(w_query, ("ctx", "fsdp"), axis=0, tiled=True),
        lax.all_gather(w_key, ("ctx", "fsdp"), axis=0, tiled=True),
        lax.all_gather(w_value, ("ctx", "fsdp"), axis=0, tiled=True),
        lax.all_gather(w_output, ("ctx", "fsdp"), axis=0, tiled=True),
    )
    gain1_f = gain1.astype(jnp.float32)
    gain2_f = gain2.astype(jnp.float32)
    inputs = tokens[0].astype(jnp.float32)
    inv_one = lax.rsqrt(jnp.mean(inputs * inputs, axis=-1, keepdims=True) + EPSILON)
    unit_one = inputs * inv_one
    normed1 = (unit_one * gain1_f).astype(jnp.bfloat16)
    queries = rotate(dot_plain(normed1, wq_full), cos_table, sin_table, H).astype(jnp.bfloat16)
    key_rot = rotate(dot_plain(normed1, wk_full), cos_table, sin_table, KVH).astype(jnp.bfloat16)
    values = dot_plain(normed1, wv_full).astype(jnp.bfloat16)
    grouped = queries.reshape(local_rows, KVH, group_size, HD)
    start_state = (
        jnp.full((local_rows, KVH, group_size), NEGATIVE, jnp.float32),
        jnp.zeros((local_rows, KVH, group_size), jnp.float32),
        jnp.zeros((local_rows, KVH, group_size, HD), jnp.float32),
    )
    running = start_state
    key_piece = lax.all_gather(key_rot, "ctx", axis=0, tiled=True)
    value_piece = lax.all_gather(values, "ctx", axis=0, tiled=True)
    piece_rows = key_piece.shape[0]
    attend_key_width = math.gcd(piece_rows, 512)
    block_count = piece_rows // attend_key_width

    def one_block(carried, index_block):
        block_start = index_block * attend_key_width
        key_blk = lax.dynamic_slice_in_dim(key_piece, block_start, attend_key_width, 0).reshape(
            attend_key_width, KVH, HD
        )
        value_blk = lax.dynamic_slice_in_dim(value_piece, block_start, attend_key_width, 0).reshape(
            attend_key_width, KVH, HD
        )
        key_pos = block_start + jnp.arange(attend_key_width, dtype=jnp.int32)
        key_docs = doc_index(key_pos, starts)
        skip_block = (block_start > last_pos) | (key_docs[attend_key_width - 1] < first_doc)

        def update(current):
            run_max, run_sum, accumulated = current
            scores = (
                jnp.einsum("qkgd,tkd->qkgt", grouped, key_blk, preferred_element_type=jnp.float32)
                * SCORE_SCALE
            )
            allowed = (key_docs[None, :] == doc_ids[:, None]) & (
                key_pos[None, :] <= positions[:, None]
            )
            allowed = allowed[:, None, None, :]
            masked = jnp.where(allowed, scores, NEGATIVE)
            new_max = jnp.maximum(run_max, jnp.max(masked, axis=-1))
            weights_exp = jnp.where(allowed, jnp.exp(masked - new_max[..., None]), 0.0)
            factor = jnp.exp(run_max - new_max)
            new_sum = run_sum * factor + jnp.sum(weights_exp, axis=-1)
            new_acc = accumulated * factor[..., None] + jnp.einsum(
                "qkgt,tkd->qkgd",
                weights_exp.astype(jnp.bfloat16),
                value_blk,
                preferred_element_type=jnp.float32,
            )
            return (new_max, new_sum, new_acc)

        return (lax.cond(skip_block, lambda unchanged: unchanged, update, carried), None)

    running, _ = lax.scan(one_block, running, jnp.arange(block_count))
    run_max, run_sum, accumulated = running
    attended = accumulated / run_sum[..., None]
    log_sum = run_max + jnp.log(run_sum)
    mixed_heads = attended.reshape(local_rows, H * HD).astype(jnp.bfloat16)
    hidden = inputs + RESIDUAL_MULT * dot_plain(mixed_heads, wo_full)
    inv_two = lax.rsqrt(jnp.mean(hidden * hidden, axis=-1, keepdims=True) + EPSILON)
    unit_two = hidden * inv_two
    normed2 = (unit_two * gain2_f).astype(jnp.bfloat16)
    wg_full, wu_full, wd_full = (
        lax.all_gather(w_gate, ("ctx", "fsdp"), axis=0, tiled=True),
        lax.all_gather(w_up, ("ctx", "fsdp"), axis=0, tiled=True),
        lax.all_gather(w_down, ("ctx", "fsdp"), axis=0, tiled=True),
    )
    gate_pre = dot_plain(normed2, wg_full)
    up_pre = dot_plain(normed2, wu_full)
    sig_gate = jax.nn.sigmoid(gate_pre)
    silu_gate = gate_pre * sig_gate
    activ = (silu_gate * up_pre).astype(jnp.bfloat16)
    result = hidden + RESIDUAL_MULT * dot_plain(activ, wd_full)
    output = result.astype(jnp.bfloat16)[None]
    grad_out = cotangent[0].astype(jnp.float32)
    grad_mlp = (RESIDUAL_MULT * grad_out).astype(jnp.bfloat16)
    silu_slope = sig_gate * (1.0 + gate_pre * (1.0 - sig_gate))
    wg_back, wu_back, wd_back = (
        lax.all_gather(w_gate, ("ctx", "fsdp"), axis=0, tiled=True),
        lax.all_gather(w_up, ("ctx", "fsdp"), axis=0, tiled=True),
        lax.all_gather(w_down, ("ctx", "fsdp"), axis=0, tiled=True),
    )
    grad_act = dot_back(grad_mlp, wd_back)
    grad_gate = (grad_act * up_pre * silu_slope).astype(jnp.bfloat16)
    grad_up = (grad_act * silu_gate).astype(jnp.bfloat16)
    grad_norm2 = dot_back(grad_gate, wg_back) + dot_back(grad_up, wu_back)
    left_cols = normed2
    gate_up_shard = lax.psum_scatter(
        jnp.concatenate([dot_outer(left_cols, grad_gate), dot_outer(left_cols, grad_up)], axis=1),
        ("ctx", "fsdp"),
        scatter_dimension=0,
        tiled=True,
    )
    wg_shard = gate_up_shard[:, :FF]
    wu_shard = gate_up_shard[:, FF:]
    left_cols = activ
    wd_shard = lax.psum_scatter(
        dot_outer(left_cols, grad_mlp), ("ctx", "fsdp"), scatter_dimension=0, tiled=True
    )
    grad_g2 = jnp.sum(grad_norm2 * unit_two, axis=0)
    grad_hidden = grad_out + norm_back(grad_norm2, unit_two, inv_two, gain2_f)
    grad_attn = (RESIDUAL_MULT * grad_hidden).astype(jnp.bfloat16)
    wq_back, wk_back, wv_back, wo_back = (
        lax.all_gather(w_query, ("ctx", "fsdp"), axis=0, tiled=True),
        lax.all_gather(w_key, ("ctx", "fsdp"), axis=0, tiled=True),
        lax.all_gather(w_value, ("ctx", "fsdp"), axis=0, tiled=True),
        lax.all_gather(w_output, ("ctx", "fsdp"), axis=0, tiled=True),
    )
    grad_wo = dot_outer(mixed_heads, grad_attn)
    grad_att = (
        dot_back(grad_attn, wo_back).astype(jnp.bfloat16).reshape(local_rows, KVH, group_size, HD)
    )
    row_delta = jnp.sum(grad_att.astype(jnp.float32) * attended, axis=-1)
    key_all, value_all = (
        lax.all_gather(key_rot, "ctx", axis=0, tiled=True),
        lax.all_gather(values, "ctx", axis=0, tiled=True),
    )
    key_width = math.gcd(length, 512)
    block_count = length // key_width

    def back_block(grad_query, index_block):
        block_start = index_block * key_width
        key_blk = lax.dynamic_slice_in_dim(key_all, block_start, key_width, 0).reshape(
            key_width, KVH, HD
        )
        value_blk = lax.dynamic_slice_in_dim(value_all, block_start, key_width, 0).reshape(
            key_width, KVH, HD
        )
        key_pos = block_start + jnp.arange(key_width, dtype=jnp.int32)
        key_docs = doc_index(key_pos, starts)
        skip_block = (block_start > last_pos) | (key_docs[key_width - 1] < first_doc)

        def compute(current):
            scores = (
                jnp.einsum("qkgd,tkd->qkgt", grouped, key_blk, preferred_element_type=jnp.float32)
                * SCORE_SCALE
            )
            allowed = (key_docs[None, :] == doc_ids[:, None]) & (
                key_pos[None, :] <= positions[:, None]
            )
            allowed = allowed[:, None, None, :]
            probs_blk = jnp.where(
                allowed, jnp.exp(jnp.where(allowed, scores, NEGATIVE) - log_sum[..., None]), 0.0
            )
            grad_probs = jnp.einsum(
                "qkgd,tkd->qkgt", grad_att, value_blk, preferred_element_type=jnp.float32
            )
            grad_scores = (probs_blk * (grad_probs - row_delta[..., None])).astype(jnp.bfloat16)
            new_query = (
                current
                + jnp.einsum(
                    "qkgt,tkd->qkgd", grad_scores, key_blk, preferred_element_type=jnp.float32
                )
                * SCORE_SCALE
            )
            grad_key = (
                jnp.einsum(
                    "qkgt,qkgd->tkd", grad_scores, grouped, preferred_element_type=jnp.float32
                )
                * SCORE_SCALE
            )
            grad_value = jnp.einsum(
                "qkgt,qkgd->tkd",
                probs_blk.astype(jnp.bfloat16),
                grad_att,
                preferred_element_type=jnp.float32,
            )
            return (
                new_query,
                (grad_key.reshape(key_width, KVH * HD), grad_value.reshape(key_width, KVH * HD)),
            )

        def nothing(current):
            zero_rows = jnp.zeros((key_width, KVH * HD), jnp.float32)
            return (current, (zero_rows, zero_rows))

        return lax.cond(skip_block, nothing, compute, grad_query)

    grad_query, key_terms = lax.scan(
        back_block,
        jnp.zeros((local_rows, KVH, group_size, HD), jnp.float32),
        jnp.arange(block_count),
    )
    key_term_all = key_terms[0].reshape(length, KVH * HD)
    value_term_all = key_terms[1].reshape(length, KVH * HD)
    grad_keys, grad_values = (
        lax.psum_scatter(
            key_term_all.astype(jnp.bfloat16), "ctx", scatter_dimension=0, tiled=True
        ).astype(jnp.float32),
        lax.psum_scatter(
            value_term_all.astype(jnp.bfloat16), "ctx", scatter_dimension=0, tiled=True
        ).astype(jnp.float32),
    )
    grad_q_pre = rotate(grad_query.reshape(local_rows, H * HD), cos_table, -sin_table, H).astype(
        jnp.bfloat16
    )
    grad_k_pre = rotate(grad_keys, cos_table, -sin_table, KVH).astype(jnp.bfloat16)
    grad_v_pre = grad_values.astype(jnp.bfloat16)
    grad_norm1 = (
        dot_back(grad_q_pre, wq_back)
        + dot_back(grad_k_pre, wk_back)
        + dot_back(grad_v_pre, wv_back)
    )
    grad_wq = dot_outer(normed1, grad_q_pre)
    grad_wk = dot_outer(normed1, grad_k_pre)
    grad_wv = dot_outer(normed1, grad_v_pre)
    grad_g1 = jnp.sum(grad_norm1 * unit_one, axis=0)
    grad_inputs = grad_hidden + norm_back(grad_norm1, unit_one, inv_one, gain1_f)
    g1_shard, g2_shard, wq_shard, wk_shard, wv_shard, wo_shard = (
        lax.psum_scatter(grad_g1, ("ctx", "fsdp"), scatter_dimension=0, tiled=True),
        lax.psum_scatter(grad_g2, ("ctx", "fsdp"), scatter_dimension=0, tiled=True),
        lax.psum_scatter(grad_wq, ("ctx", "fsdp"), scatter_dimension=0, tiled=True),
        lax.psum_scatter(grad_wk, ("ctx", "fsdp"), scatter_dimension=0, tiled=True),
        lax.psum_scatter(grad_wv, ("ctx", "fsdp"), scatter_dimension=0, tiled=True),
        lax.psum_scatter(grad_wo, ("ctx", "fsdp"), scatter_dimension=0, tiled=True),
    )
    return (
        output,
        grad_inputs[None],
        g1_shard,
        wq_shard,
        wk_shard,
        wv_shard,
        wo_shard,
        g2_shard,
        wg_shard,
        wu_shard,
        wd_shard,
    )


def rows_of(blocks):
    return blocks.reshape((-1,) + blocks.shape[2:])


def in_vmem(count):
    return [pl.BlockSpec(memory_space=pltpu.VMEM)] * count


def greet_line(barrier, ctx_at, line_at, line_size):
    other = ctx_at + 1 - 2 * (ctx_at % PAIR)
    pl.semaphore_signal(barrier, inc=1, device_id={"ctx": other}, device_id_type=MESH)

    @pl.when(line_at > 0)
    def _():
        pl.semaphore_signal(barrier, inc=1, device_id={"ctx": ctx_at - PAIR}, device_id_type=MESH)

    @pl.when(line_at < line_size - 1)
    def _():
        pl.semaphore_signal(barrier, inc=1, device_id={"ctx": ctx_at + PAIR}, device_id_type=MESH)

    last = line_size - 1
    neighbours = 1 + (line_at + last - 1) // last + (2 * last - 1 - line_at) // last
    pl.semaphore_wait(barrier, neighbours)


def greet_all(barrier, me, count, fsdp_size):
    def greet(k, unused):
        target = (me + k) % count
        pl.semaphore_signal(
            barrier, inc=1, device_id=(target // fsdp_size, target % fsdp_size), device_id_type=MESH
        )
        return unused

    lax.fori_loop(1, count, greet, 0)
    pl.semaphore_wait(barrier, count - 1)


def gather_phase(line_size, x_ref, out_ref, send_sem, recv_sem, own_sem):
    me = lax.axis_index("ctx")
    line_at, pair_at = me // PAIR, me % PAIR
    rows = x_ref.shape[0]
    step = rows // CHUNKS

    def piece(block, part):
        return out_ref.at[pl.ds(pl.multiple_of(block * rows + part * step, step), step), :]

    def copy(block, part, way, own):
        slot = block * CHUNKS + part
        return pltpu.make_async_remote_copy(
            src_ref=x_ref.at[pl.ds(part * step, step), :] if own else piece(block, part),
            dst_ref=piece(block, part),
            send_sem=send_sem.at[way, slot],
            recv_sem=recv_sem.at[slot],
            device_id={"ctx": (me + 1 - 2 * pair_at, me + PAIR, me - PAIR)[way]},
            device_id_type=MESH,
        )

    def pass_on(block, part, upward, downward, own, act):
        if upward is not None:
            pl.when(upward)(lambda: act(copy(block, part, 1, own)))
        if downward is not None:
            pl.when(downward)(lambda: act(copy(block, part, 2, own)))
        act(copy(block, part, 0, own))

    def own_part(part, act):
        pass_on(me, part, line_at < line_size - 1, line_at > 0, True, act)

    def others(act, arrive):
        for distance in range(1, line_size):
            for part in range(CHUNKS):

                @pl.when(line_at >= distance)
                def _():
                    block = me - PAIR * distance
                    arrive(block, part)
                    pass_on(block, part, line_at < line_size - 1, None, False, act)

                @pl.when(line_at + distance < line_size)
                def _():
                    block = me + PAIR * distance
                    arrive(block, part)
                    pass_on(block, part, None, line_at > 0, False, act)

    def start_own(part):
        own_part(part, lambda c: c.start())

    def finish():
        keep = pltpu.make_async_copy(
            x_ref, out_ref.at[pl.ds(pl.multiple_of(me * rows, rows), rows), :], own_sem
        )
        keep.start()
        others(lambda c: c.start(), lambda block, part: copy(block, part, 0, False).wait_recv())
        for place in range(line_size):
            for part in range(CHUNKS):
                copy(place * PAIR + 1 - pair_at, part, 0, False).wait_recv()
        for part in range(CHUNKS):
            own_part(part, lambda c: c.wait_send())
        others(lambda c: c.wait_send(), lambda block, part: None)
        keep.wait()

    return start_own, finish


def gather_scratch(ctx_size):
    return [
        pltpu.SemaphoreType.DMA((3, ctx_size * CHUNKS)),
        pltpu.SemaphoreType.DMA((ctx_size * CHUNKS,)),
        pltpu.SemaphoreType.DMA,
    ]


def scatter_phase(line_size, x_ref, sum_ref, near, below, above, near_send, near_sem, line_send, line_sem, emit):
    me = lax.axis_index("ctx")
    line_at, pair_at = me // PAIR, me % PAIR
    rows = sum_ref.shape[0]
    step = rows // CHUNKS
    last = line_size - 1
    low = line_at // (line_size // 2)
    order = [k + (last - 2 * k) * (1 - low) for k in range(line_size // 2)]
    order += [line_at + 1 - 2 * (line_at % 2), line_at]

    def near_copy(place, part):
        start = (place * PAIR + 1 - pair_at) * rows + part * step
        return pltpu.make_async_remote_copy(
            src_ref=x_ref.at[pl.ds(pl.multiple_of(start, step), step), :],
            dst_ref=near.at[place, pl.ds(part * step, step), :],
            send_sem=near_send.at[place, part],
            recv_sem=near_sem.at[place, part],
            device_id={"ctx": me + 1 - 2 * pair_at},
            device_id_type=MESH,
        )

    def line_copy(place, part, up):
        part_rows = pl.ds(part * step, step)
        return pltpu.make_async_remote_copy(
            src_ref=near.at[place, part_rows, :],
            dst_ref=(below if up else above).at[place, part_rows, :],
            send_sem=line_send.at[place, part],
            recv_sem=line_sem.at[0 if up else 1, place, part],
            device_id={"ctx": me + PAIR if up else me - PAIR},
            device_id_type=MESH,
        )

    def mine(place, part):
        start = (place * PAIR + pair_at) * rows + part * step
        return x_ref[pl.ds(pl.multiple_of(start, step), step), :].astype(jnp.float32)

    for place in order:
        for part in range(CHUNKS):
            near_copy(place, part).start()

    for place in order[:-1]:
        for part in range(CHUNKS):
            part_rows = pl.ds(part * step, step)
            near_copy(place, part).wait_recv()

            def send(up, waits, arrived):
                @pl.when(waits)
                def _():
                    line_copy(place, part, up).wait_recv()
                    near[place, part_rows, :] = (
                        mine(place, part)
                        + near[place, part_rows, :].astype(jnp.float32)
                        + arrived[place, part_rows, :].astype(jnp.float32)
                    ).astype(near.dtype)

                @pl.when(jnp.logical_not(waits))
                def _():
                    near[place, part_rows, :] = (
                        mine(place, part) + near[place, part_rows, :].astype(jnp.float32)
                    ).astype(near.dtype)

                line_copy(place, part, up).start()

            pl.when(place > line_at)(lambda: send(True, line_at > 0, below))
            pl.when(place < line_at)(lambda: send(False, line_at < last, above))

    for part in range(CHUNKS):
        part_rows = pl.ds(part * step, step)
        near_copy(line_at, part).wait_recv()
        sum_ref[part_rows, :] = mine(line_at, part) + near[line_at, part_rows, :].astype(jnp.float32)

        @pl.when(line_at > 0)
        def _():
            line_copy(line_at, part, True).wait_recv()
            sum_ref[part_rows, :] += below[line_at, part_rows, :].astype(jnp.float32)

        @pl.when(line_at < last)
        def _():
            line_copy(line_at, part, False).wait_recv()
            sum_ref[part_rows, :] += above[line_at, part_rows, :].astype(jnp.float32)

        emit(part, slice(part * step, (part + 1) * step))

    def finish():
        for place in order:
            for part in range(CHUNKS):
                near_copy(place, part).wait_send()
        for place in order[:-1]:
            for part in range(CHUNKS):
                line_copy(place, part, True).wait_send()

    return finish


def scatter_scratch(ctx_size, rows, width):
    line_size = ctx_size // PAIR
    held = pltpu.VMEM((line_size, rows, width), jnp.bfloat16)
    return [
        held,
        held,
        held,
        pltpu.SemaphoreType.DMA((line_size, CHUNKS)),
        pltpu.SemaphoreType.DMA((line_size, CHUNKS)),
        pltpu.SemaphoreType.DMA((line_size, CHUNKS)),
        pltpu.SemaphoreType.DMA((2, line_size, CHUNKS)),
    ]


def swap_lanes(values, outer, inner):
    tile = 128
    half = tile // 2
    low = lax.broadcasted_iota(jnp.int32, (values.shape[0], tile), 1) < half
    placed = [None] * (outer * inner // 2)
    for first in range(0, outer, 2):
        for second in range(0, inner, 2):
            at = (first * inner + second) // 2
            one = values[:, at * tile : (at + 1) * tile]
            at += inner // 2
            two = values[:, at * tile : (at + 1) * tile]
            at = (second * outer + first) // 2
            placed[at] = jnp.where(low, one, pltpu.roll(two, half, 1))
            placed[at + outer // 2] = jnp.where(low, pltpu.roll(one, half, 1), two)
    return jnp.concatenate(placed, axis=1)


def start_kernel(
    ctx_size, fsdp_size, tokens_ref, tile_ref, parts_ref, out_ref, gains_ref, weight_ref,
    tiles, normed, tile_send, tile_recv, far_send, far_recv, near_send, near_recv, kept, *sems
):
    me_ctx, me_fsdp = lax.axis_index("ctx"), lax.axis_index("fsdp")
    count = ctx_size * fsdp_size
    me = me_ctx * fsdp_size + me_fsdp
    greet_all(pltpu.get_barrier_semaphore(), me, count, fsdp_size)

    def tile_copy(k, source):
        target = (me + k) % count
        return pltpu.make_async_remote_copy(
            src_ref=tile_ref,
            dst_ref=tiles.at[source],
            send_sem=tile_send.at[k],
            recv_sem=tile_recv.at[k],
            device_id=(target // fsdp_size, target % fsdp_size),
            device_id_type=MESH,
        )

    def start_tile(k, unused):
        tile_copy(k, me).start()
        return unused

    def finish_tile(k, unused):
        tile_copy(k, (me + count - k) % count).wait_recv()
        return unused

    lax.fori_loop(1, count, start_tile, 0)
    tiles[pl.ds(me, 1)] = tile_ref[...][None]

    def far_copy(k, source):
        target = (me_ctx + k) % ctx_size
        return pltpu.make_async_remote_copy(
            src_ref=parts_ref.at[target],
            dst_ref=weight_ref.at[source * fsdp_size + me_fsdp],
            send_sem=far_send.at[k],
            recv_sem=far_recv.at[k],
            device_id={"ctx": target},
            device_id_type=MESH,
        )

    def near_copy(k, j, fsdp_source):
        block = (me_ctx + ctx_size - k) % ctx_size * fsdp_size + fsdp_source
        return pltpu.make_async_remote_copy(
            src_ref=parts_ref.at[me_ctx] if k == 0 else weight_ref.at[block],
            dst_ref=weight_ref.at[block],
            send_sem=near_send.at[k, j],
            recv_sem=near_recv.at[k, j],
            device_id={"fsdp": (me_fsdp + j) % fsdp_size},
            device_id_type=MESH,
        )

    for k in range(1, ctx_size):
        far_copy(k, me_ctx).start()
    for j in range(1, fsdp_size):
        near_copy(0, j, me_fsdp).start()
    keep = pltpu.make_async_copy(parts_ref.at[me_ctx], weight_ref.at[me], kept)
    keep.start()

    rows, model = tokens_ref.shape
    lax.fori_loop(1, count, finish_tile, 0)
    held = model // count
    for pair in range(count // 2):
        cols = slice(pair * 2 * held, (pair + 1) * 2 * held)
        gains_ref[:, cols] = tiles[2 * pair] + tiles[2 * pair + 1]
    start_own, finish_gather = gather_phase(ctx_size // PAIR, normed, out_ref, *sems)
    step = rows // CHUNKS
    for part in range(CHUNKS):
        part_rows = slice(part * step, (part + 1) * step)
        values = tokens_ref[part_rows, :].astype(jnp.float32)
        scale = lax.rsqrt(jnp.mean(values * values, axis=-1, keepdims=True) + EPSILON)
        normed[part_rows, :] = (values * scale * gains_ref[0:1, :]).astype(normed.dtype)
        start_own(part)
    for k in range(1, ctx_size):
        far_copy(k, (me_ctx + ctx_size - k) % ctx_size).wait_recv()
        for j in range(1, fsdp_size):
            near_copy(k, j, me_fsdp).start()
    finish_gather()
    for k in range(ctx_size):
        for j in range(1, fsdp_size):
            near_copy(k, j, (me_fsdp + fsdp_size - j) % fsdp_size).wait_recv()
    for k in range(ctx_size):
        for j in range(1, fsdp_size):
            near_copy(k, j, me_fsdp).wait_send()
    for k in range(1, ctx_size):
        far_copy(k, me_ctx).wait_send()

    def sent_tile(k, unused):
        tile_copy(k, me).wait_send()
        return unused

    lax.fori_loop(1, count, sent_tile, 0)
    keep.wait()


def start_layer(tokens, tile, parts):
    ctx_size, fsdp_size = lax.axis_size("ctx"), lax.axis_size("fsdp")
    count = ctx_size * fsdp_size
    rows, model = tokens.shape
    dma = pltpu.SemaphoreType.DMA
    normed1, gains, weight = pl.pallas_call(
        functools.partial(start_kernel, ctx_size, fsdp_size),
        out_shape=(
            jax.ShapeDtypeStruct((ctx_size * rows, model), jnp.bfloat16),
            jax.ShapeDtypeStruct((8, model), jnp.float32),
            jax.ShapeDtypeStruct((count,) + parts.shape[1:], parts.dtype),
        ),
        in_specs=in_vmem(3),
        out_specs=(ANYWHERE, in_vmem(1)[0], ANYWHERE),
        scratch_shapes=[
            pltpu.VMEM((count, 8, 128), jnp.float32),
            pltpu.VMEM((rows, model), jnp.bfloat16),
            dma((count,)),
            dma((count,)),
            dma((ctx_size,)),
            dma((ctx_size,)),
            dma((ctx_size, fsdp_size)),
            dma((ctx_size, fsdp_size)),
            dma,
        ]
        + gather_scratch(ctx_size),
        compiler_params=pltpu.CompilerParams(
            collective_id=0, has_side_effects=True, vmem_limit_bytes=32 * 2**20
        ),
        cost_estimate=LINK_COST,
        name="start_layer",
    )(tokens, tile, parts)
    return normed1, gains, rows_of(weight)


def mlp_forward_kernel(
    ctx_size, fsdp_size, x_ref, tokens_ref, gains_ref, hidden_ref, out_ref, sums, normed, *sems
):
    line_size = ctx_size // PAIR
    me = lax.axis_index("ctx")
    greet_line(pltpu.get_barrier_semaphore(), me, me // PAIR, line_size)
    start_own, finish_gather = gather_phase(line_size, normed, out_ref, *sems[7:])

    def emit(part, rows):
        hidden = tokens_ref[rows, :].astype(jnp.float32) + RESIDUAL_MULT * sums[rows, :]
        hidden_ref[rows, :] = hidden
        scale = lax.rsqrt(jnp.mean(hidden * hidden, axis=-1, keepdims=True) + EPSILON)
        scaled = hidden * scale * gains_ref[1:2, :]
        normed[rows, :] = swap_lanes(scaled, ctx_size, fsdp_size).astype(normed.dtype)
        start_own(part)

    finish_scatter = scatter_phase(line_size, x_ref, sums, *sems[:7], emit)
    finish_gather()
    finish_scatter()


def mlp_backward_kernel(
    ctx_size, fsdp_size, x_ref, hidden_ref, grad_ref, gains_ref, grad_hidden_ref, grad_gain_ref, out_ref,
    sums, normed, *sems
):
    line_size = ctx_size // PAIR
    me = lax.axis_index("ctx")
    greet_line(pltpu.get_barrier_semaphore(), me, me // PAIR, line_size)
    start_own, finish_gather = gather_phase(line_size, normed, out_ref, *sems[7:])

    def emit(part, rows):
        grad_norm = swap_lanes(sums[rows, :], fsdp_size, ctx_size)
        hidden = hidden_ref[rows, :]
        scale = lax.rsqrt(jnp.mean(hidden * hidden, axis=-1, keepdims=True) + EPSILON)
        unit = hidden * scale
        grad_gain_ref[part : part + 1, :] = jnp.sum(grad_norm * unit, axis=0, keepdims=True)
        grad_hidden = grad_ref[rows, :].astype(jnp.float32) + norm_back(
            grad_norm, unit, scale, gains_ref[1:2, :]
        )
        grad_hidden_ref[rows, :] = grad_hidden
        normed[rows, :] = (RESIDUAL_MULT * grad_hidden).astype(normed.dtype)
        start_own(part)

    finish_scatter = scatter_phase(line_size, x_ref, sums, *sems[:7], emit)
    finish_gather()
    finish_scatter()


def scatter_gather(kernel, collective_id, extra_shapes, partial, *others):
    ctx_size, fsdp_size = lax.axis_size("ctx"), lax.axis_size("fsdp")
    rows, model = partial.shape[0] // ctx_size, partial.shape[1]
    return pl.pallas_call(
        functools.partial(kernel, ctx_size, fsdp_size),
        out_shape=extra_shapes + (jax.ShapeDtypeStruct(partial.shape, jnp.bfloat16),),
        in_specs=in_vmem(1 + len(others)),
        out_specs=tuple(in_vmem(len(extra_shapes))) + (ANYWHERE,),
        scratch_shapes=[pltpu.VMEM((rows, model), jnp.float32), pltpu.VMEM((rows, model), jnp.bfloat16)]
        + scatter_scratch(ctx_size, rows, model)
        + gather_scratch(ctx_size),
        compiler_params=pltpu.CompilerParams(
            collective_id=collective_id, has_side_effects=True, vmem_limit_bytes=40 * 2**20
        ),
        cost_estimate=LINK_COST,
    )(partial, *others)


def mlp_forward(partial, tokens, gains):
    hidden = jax.ShapeDtypeStruct(tokens.shape, jnp.float32)
    return scatter_gather(mlp_forward_kernel, 1, (hidden,), partial, tokens, gains)


def mlp_backward(partial, hidden, grad_out, gains):
    like = jax.ShapeDtypeStruct(hidden.shape, jnp.float32)
    gain = jax.ShapeDtypeStruct((CHUNKS, hidden.shape[1]), jnp.float32)
    return scatter_gather(mlp_backward_kernel, 2, (like, gain), partial, hidden, grad_out, gains)


def scatter_kernel(ctx_size, x_ref, out_ref, *sems):
    line_size = ctx_size // PAIR
    me = lax.axis_index("ctx")
    greet_line(pltpu.get_barrier_semaphore(), me, me // PAIR, line_size)
    scatter_phase(line_size, x_ref, out_ref, *sems, lambda part, rows: None)()


def scatter_ctx(partial):
    ctx_size = lax.axis_size("ctx")
    rows, model = partial.shape[0] // ctx_size, partial.shape[1]
    return pl.pallas_call(
        functools.partial(scatter_kernel, ctx_size),
        out_shape=jax.ShapeDtypeStruct((rows, model), jnp.float32),
        in_specs=in_vmem(1),
        out_specs=in_vmem(1)[0],
        scratch_shapes=scatter_scratch(ctx_size, rows, model),
        compiler_params=pltpu.CompilerParams(
            collective_id=3, has_side_effects=True, vmem_limit_bytes=32 * 2**20
        ),
        cost_estimate=LINK_COST,
        name="scatter_ctx",
    )(partial)


def exchange_kernel(ctx_size, fsdp_size, x_ref, out_ref, send_sem, recv_sem):
    count = ctx_size * fsdp_size
    me = lax.axis_index("ctx") * fsdp_size + lax.axis_index("fsdp")
    barrier = pltpu.get_barrier_semaphore()

    def device(index):
        return (index // fsdp_size, index % fsdp_size)

    def greet(k, unused):
        pl.semaphore_signal(barrier, inc=1, device_id=device((me + k) % count), device_id_type=MESH)
        return unused

    lax.fori_loop(1, count, greet, 0)
    pl.semaphore_wait(barrier, count - 1)

    def copy(k):
        target = (me + k) % count
        return pltpu.make_async_remote_copy(
            src_ref=x_ref.at[target], dst_ref=out_ref.at[me],
            send_sem=send_sem.at[k], recv_sem=recv_sem.at[k],
            device_id=device(target), device_id_type=MESH,
        )

    def start(k, unused):
        copy(k).start()
        return unused

    def finish(k, unused):
        source = (me + count - k) % count
        pltpu.make_async_remote_copy(
            src_ref=x_ref.at[source], dst_ref=out_ref.at[source],
            send_sem=send_sem.at[k], recv_sem=recv_sem.at[k],
            device_id=device(source), device_id_type=MESH,
        ).wait_recv()
        copy(k).wait_send()
        return unused

    lax.fori_loop(1, count, start, 0)
    out_ref[pl.ds(me, 1)] = x_ref[pl.ds(me, 1)]
    lax.fori_loop(1, count, finish, 0)


def exchange(tiles):
    ctx_size, fsdp_size = lax.axis_size("ctx"), lax.axis_size("fsdp")
    count = ctx_size * fsdp_size
    return pl.pallas_call(
        functools.partial(exchange_kernel, ctx_size, fsdp_size),
        out_shape=jax.ShapeDtypeStruct(tiles.shape, tiles.dtype),
        in_specs=[pl.BlockSpec(memory_space=pltpu.VMEM)],
        out_specs=pl.BlockSpec(memory_space=pltpu.VMEM),
        scratch_shapes=[pltpu.SemaphoreType.DMA((count,)), pltpu.SemaphoreType.DMA((count,))],
        compiler_params=pltpu.CompilerParams(collective_id=4, has_side_effects=True),
        cost_estimate=pl.CostEstimate(flops=0, bytes_accessed=25_000_000, transcendentals=0),
        name="exchange",
    )(tiles)


def padded(rows):
    return jnp.pad(rows, ((0, 0), (0, 8 - rows.shape[1]), (0, 128 - rows.shape[2])))


def scatter_rows(rows):
    count = lax.axis_size("ctx") * lax.axis_size("fsdp")
    by_owner = rows.reshape(rows.shape[0], count, -1).transpose(1, 0, 2)
    return jnp.sum(exchange(padded(by_owner)), axis=0)[: rows.shape[0], : by_owner.shape[2]]


def swap_ctx(blocks):
    return lax.all_to_all(blocks, "ctx", split_axis=0, concat_axis=0, tiled=True)


def by_fsdp(grad, ctx_size, fsdp_size):
    parts = grad.reshape(ctx_size, fsdp_size, -1, grad.shape[-1]).transpose(1, 0, 2, 3)
    return rows_of(rows_of(parts))


def return_columns(terms, ctx_size):
    return swap_ctx(terms.reshape(ctx_size, -1, terms.shape[-1]))


def half_turn(values, sign_table):
    lane = lax.broadcasted_iota(jnp.int32, values.shape, 1)
    width = values.shape[1]
    quarter = HD // 2
    ahead = pltpu.roll(values, width - quarter, 1)
    behind = pltpu.roll(values, quarter, 1)
    return jnp.where(lane % HD < quarter, ahead, behind) * sign_table


def turn(values, cos_table, sign_table):
    copies = values.shape[1] // cos_table.shape[1]
    if copies > 1:
        cos_table = jnp.concatenate([cos_table] * copies, axis=1)
        sign_table = jnp.concatenate([sign_table] * copies, axis=1)
    return values * cos_table + half_turn(values, sign_table)


def attention_forward_kernel(
    block_rows, qkv_ref, cos_ref, sin_ref, doc_col_ref, doc_row_ref, q_ref, kv_ref, out_ref, lse_ref
):
    length = qkv_ref.shape[0]
    group = H // KVH
    width = group * HD
    q_ref[...] = turn(qkv_ref[:, :width], cos_ref[...], sin_ref[...]).astype(jnp.bfloat16)
    pair = qkv_ref[:, width:]
    lane = lax.broadcasted_iota(jnp.int32, pair.shape, 1)
    turned = turn(pair, cos_ref[...], sin_ref[...])
    kv_ref[...] = jnp.where(lane < HD, turned, pair).astype(jnp.bfloat16)
    for block in range(length // block_rows):
        rows = slice(block * block_rows, (block + 1) * block_rows)
        reach = (block + 1) * block_rows
        keys = kv_ref[:reach, :HD]
        values = kv_ref[:reach, HD:]
        query_at = block * block_rows + lax.broadcasted_iota(jnp.int32, (block_rows, reach), 0)
        key_at = lax.broadcasted_iota(jnp.int32, (block_rows, reach), 1)
        allowed = (doc_col_ref[rows, :] == doc_row_ref[:, :reach]) & (key_at <= query_at)
        for head in range(group):
            cols = slice(head * HD, (head + 1) * HD)
            scores = dot_back(q_ref[rows, cols], keys) * SCORE_SCALE
            masked = jnp.where(allowed, scores, NEGATIVE)
            top = jnp.max(masked, axis=1, keepdims=True)
            weights = jnp.where(allowed, jnp.exp(masked - top), 0.0)
            total = jnp.sum(weights, axis=1, keepdims=True)
            mixed = dot_plain(weights.astype(jnp.bfloat16), values)
            out_ref[rows, cols] = (mixed / total).astype(jnp.bfloat16)
            lse_ref[rows, head : head + 1] = top + jnp.log(total)


def attention_backward_kernel(
    block_rows, q_ref, kv_ref, do_ref, lse_ref, cos_ref, sin_ref, doc_col_ref, doc_row_ref, grad_ref, dq_ref, dkv_ref
):
    length = q_ref.shape[0]
    group = H // KVH
    width = group * HD
    dkv_ref[...] = jnp.zeros_like(dkv_ref)
    for block in range(length // block_rows):
        rows = slice(block * block_rows, (block + 1) * block_rows)
        reach = (block + 1) * block_rows
        keys = kv_ref[:reach, :HD]
        values = kv_ref[:reach, HD:]
        query_at = block * block_rows + lax.broadcasted_iota(jnp.int32, (block_rows, reach), 0)
        key_at = lax.broadcasted_iota(jnp.int32, (block_rows, reach), 1)
        allowed = (doc_col_ref[rows, :] == doc_row_ref[:, :reach]) & (key_at <= query_at)
        for head in range(group):
            cols = slice(head * HD, (head + 1) * HD)
            query = q_ref[rows, cols]
            grad_out = do_ref[rows, cols]
            scores = dot_back(query, keys) * SCORE_SCALE
            probs = jnp.where(
                allowed,
                jnp.exp(jnp.where(allowed, scores, NEGATIVE) - lse_ref[rows, head : head + 1]),
                0.0,
            )
            grad_probs = dot_back(grad_out, values)
            delta = jnp.sum(probs * grad_probs, axis=1, keepdims=True)
            grad_scores = (probs * (grad_probs - delta)).astype(jnp.bfloat16)
            dq_ref[rows, cols] = dot_plain(grad_scores, keys) * SCORE_SCALE
            dkv_ref[:reach, :HD] += dot_outer(grad_scores, query) * SCORE_SCALE
            dkv_ref[:reach, HD:] += dot_outer(probs.astype(jnp.bfloat16), grad_out)
    grad_ref[:, :width] = turn(dq_ref[...], cos_ref[...], -sin_ref[...]).astype(jnp.bfloat16)
    pair = dkv_ref[...]
    lane = lax.broadcasted_iota(jnp.int32, pair.shape, 1)
    turned = turn(pair, cos_ref[...], -sin_ref[...])
    grad_ref[:, width:] = jnp.where(lane < HD, turned, pair).astype(jnp.bfloat16)


def attention_forward(qkv, tables, block_rows):
    length = qkv.shape[0]
    width = (H // KVH) * HD
    return pl.pallas_call(
        functools.partial(attention_forward_kernel, block_rows),
        out_shape=(
            jax.ShapeDtypeStruct((length, width), jnp.bfloat16),
            jax.ShapeDtypeStruct((length, 2 * HD), jnp.bfloat16),
            jax.ShapeDtypeStruct((length, width), jnp.bfloat16),
            jax.ShapeDtypeStruct((length, H // KVH), jnp.float32),
        ),
        in_specs=in_vmem(5),
        out_specs=tuple(in_vmem(4)),
        compiler_params=pltpu.CompilerParams(vmem_limit_bytes=48 * 2**20),
        name="attend",
    )(qkv, *tables)


def attention_backward(q, kv, grad_out, lse, tables, block_rows):
    length, width = q.shape
    return pl.pallas_call(
        functools.partial(attention_backward_kernel, block_rows),
        out_shape=jax.ShapeDtypeStruct((length, width + 2 * HD), jnp.bfloat16),
        in_specs=in_vmem(8),
        out_specs=in_vmem(1)[0],
        scratch_shapes=[
            pltpu.VMEM((length, width), jnp.float32),
            pltpu.VMEM((length, 2 * HD), jnp.float32),
        ],
        compiler_params=pltpu.CompilerParams(vmem_limit_bytes=48 * 2**20),
        name="attend_back",
    )(q, kv, grad_out, lse, *tables)


def on_device(
    tokens,
    doc_lengths,
    cotangent,
    gain_attn,
    w_query,
    w_key,
    w_value,
    w_output,
    gain_mlp,
    w_gate,
    w_up,
    w_down,
):
    local_rows, _ = tokens.shape[1:]
    ctx_size = lax.axis_size("ctx")
    fsdp_size = lax.axis_size("fsdp")
    length = local_rows * ctx_size
    group_width = (H // KVH) * HD
    ff_slice = FF // ctx_size
    held_rows = w_query.shape[0]
    bf16 = jnp.bfloat16

    positions = jnp.arange(length, dtype=jnp.int32)
    seq_lengths = doc_lengths[0]
    starts = jnp.cumsum(seq_lengths) - seq_lengths
    doc_ids = doc_index(positions, starts)
    cos_half, sin_half = rope_tables(positions)
    cos_table = jnp.concatenate([cos_half] * 4, axis=1)
    sin_table = jnp.concatenate([-sin_half, sin_half] * 2, axis=1)
    tables = (cos_table, sin_table, doc_ids[:, None], doc_ids[None, :])


    def by_slice(weight):
        return weight.reshape(held_rows, ctx_size, -1)

    qkv_parts = jnp.concatenate([by_slice(w_query), by_slice(w_key), by_slice(w_value)], axis=2)
    wo_mine = lax.all_gather(w_output, "fsdp", axis=0, tiled=True)
    gain_rows = jnp.stack([gain_attn, gain_mlp]).astype(jnp.float32)
    odd = lax.axis_index("fsdp") % 2
    gain_tile = jnp.concatenate([gain_rows * (1 - odd), gain_rows * odd], axis=1)
    gain_tile = jnp.pad(gain_tile, ((0, 8 - gain_tile.shape[0]), (0, 128 - gain_tile.shape[1])))
    normed1, gains, w_qkv = start_layer(tokens[0], gain_tile, qkv_parts.transpose(1, 0, 2))
    gu_parts = jnp.concatenate([by_slice(w_gate), by_slice(w_up)], axis=2).transpose(1, 0, 2)
    normed1, gu_parts = lax.optimization_barrier((normed1, gu_parts))
    w_gu = lax.all_gather(rows_of(swap_ctx(gu_parts)), "fsdp", axis=0, tiled=True)
    wd_mine = lax.all_gather(w_down, "fsdp", axis=0, tiled=True)
    inputs = tokens[0].astype(jnp.float32)
    inv_one = lax.rsqrt(jnp.mean(inputs * inputs, axis=-1, keepdims=True) + EPSILON)
    unit_one = inputs * inv_one
    grad_out = cotangent[0].astype(jnp.float32)
    grad_mlp = (RESIDUAL_MULT * grad_out).astype(bf16)

    block_rows = math.gcd(length, 256)
    qkv = dot_plain(normed1, w_qkv)
    qkv, grad_mlp = lax.optimization_barrier((qkv, grad_mlp))
    grad_mlp = lax.all_gather(grad_mlp, "ctx", axis=0, tiled=True)
    q, kv, mixed_heads, log_sum = attention_forward(qkv, tables, block_rows)
    hidden, normed2 = mlp_forward(dot_plain(mixed_heads, wo_mine).astype(bf16), tokens[0], gains)

    gate_up = dot_plain(normed2, w_gu)
    gate_pre, up_pre = gate_up[:, :ff_slice], gate_up[:, ff_slice:]
    sig_gate = jax.nn.sigmoid(gate_pre)
    silu_gate = gate_pre * sig_gate
    activ = (silu_gate * up_pre).astype(bf16)
    activ, gate_up = lax.optimization_barrier((activ, gate_up))
    gate_pre, up_pre = gate_up[:, :ff_slice], gate_up[:, ff_slice:]
    sig_gate = jax.nn.sigmoid(gate_pre)
    silu_gate = gate_pre * sig_gate
    out_terms, grad_mlp = lax.optimization_barrier(
        (dot_plain(activ, wd_mine).astype(bf16), grad_mlp)
    )
    branch = lax.psum_scatter(out_terms, "ctx", scatter_dimension=0, tiled=True)
    output = (hidden + RESIDUAL_MULT * branch.astype(jnp.float32)).astype(bf16)[None]

    silu_slope = sig_gate * (1.0 + gate_pre * (1.0 - sig_gate))
    grad_act = dot_back(grad_mlp, wd_mine)
    grad_gu = jnp.concatenate(
        [(grad_act * up_pre * silu_slope).astype(bf16), (grad_act * silu_gate).astype(bf16)], axis=1
    )
    partial2, gu_terms, wd_terms = lax.optimization_barrier(
        (
            dot_back(grad_gu, w_gu).astype(bf16),
            dot_outer(normed2, grad_gu).astype(bf16),
            dot_outer(activ, grad_mlp).astype(bf16),
        )
    )
    grad_hidden, grad_g2, grad_attn = mlp_backward(partial2, hidden, cotangent[0], gains)
    gu_back = lax.psum_scatter(gu_terms, "fsdp", scatter_dimension=0, tiled=True)
    wd_back = lax.psum_scatter(wd_terms, "fsdp", scatter_dimension=0, tiled=True)

    grad_mixed, wo_terms = lax.optimization_barrier(
        (
            dot_back(grad_attn, wo_mine).astype(bf16),
            dot_outer(mixed_heads, grad_attn).astype(bf16),
        )
    )
    wo_back = lax.psum_scatter(wo_terms, "fsdp", scatter_dimension=0, tiled=True)
    grad_qkv = attention_backward(q, kv, grad_mixed, log_sum, tables, block_rows)
    grad_qkv, gu_back = lax.optimization_barrier((grad_qkv, gu_back))
    gu_back = return_columns(gu_back, ctx_size)
    partial1, qkv_terms = lax.optimization_barrier(
        (
            dot_back(grad_qkv, w_qkv).astype(bf16),
            by_fsdp(dot_outer(normed1, grad_qkv).astype(bf16), ctx_size, fsdp_size),
        )
    )
    grad_norm1 = scatter_ctx(partial1)
    qkv_back = lax.psum_scatter(qkv_terms, "fsdp", scatter_dimension=0, tiled=True)
    grad_norm1, qkv_back = lax.optimization_barrier((grad_norm1, qkv_back))
    qkv_back = return_columns(qkv_back, ctx_size)
    grad_g1 = jnp.sum(grad_norm1 * unit_one, axis=0)
    grad_inputs = grad_hidden + norm_back(grad_norm1, unit_one, inv_one, gains[0])
    gain_back = scatter_rows(jnp.stack([grad_g1, jnp.sum(grad_g2, axis=0)]))

    def joined(parts):
        return parts.transpose(1, 0, 2).reshape(held_rows, -1).astype(jnp.float32)

    key_end = group_width + HD
    return (
        output,
        grad_inputs[None],
        gain_back[0],
        joined(qkv_back[:, :, :group_width]),
        joined(qkv_back[:, :, group_width:key_end]),
        joined(qkv_back[:, :, key_end:]),
        wo_back.astype(jnp.float32),
        gain_back[1],
        joined(gu_back[:, :, :ff_slice]),
        joined(gu_back[:, :, ff_slice:]),
        wd_back.astype(jnp.float32),
    )


def solution(mesh):
    in_specs = (
        P("fsdp", "ctx", None),
        P("fsdp", None),
        P("fsdp", "ctx", None),
        P(("ctx", "fsdp")),
        P(("ctx", "fsdp"), None),
        P(("ctx", "fsdp"), None),
        P(("ctx", "fsdp"), None),
        P(("ctx", "fsdp"), None),
        P(("ctx", "fsdp")),
        P(("ctx", "fsdp"), None),
        P(("ctx", "fsdp"), None),
        P(("ctx", "fsdp"), None),
    )
    out_specs = (
        P("fsdp", "ctx", None),
        P("fsdp", "ctx", None),
        P(("ctx", "fsdp")),
        P(("ctx", "fsdp"), None),
        P(("ctx", "fsdp"), None),
        P(("ctx", "fsdp"), None),
        P(("ctx", "fsdp"), None),
        P(("ctx", "fsdp")),
        P(("ctx", "fsdp"), None),
        P(("ctx", "fsdp"), None),
        P(("ctx", "fsdp"), None),
    )
    if mesh.shape["ctx"] != KVH or KVH != 4 * PAIR:
        return jax.shard_map(
            general_device, mesh=mesh, in_specs=in_specs, out_specs=out_specs, check_vma=False
        )

    return jax.shard_map(
        on_device, mesh=mesh, in_specs=in_specs, out_specs=out_specs, check_vma=False
    )
```

```python
import functools
import math

import jax
import jax.numpy as jnp
from jax import lax
from jax.experimental import pallas as pl
from jax.experimental.pallas import tpu as pltpu
from jax.sharding import PartitionSpec as P

H = 32
KVH = 8
HD = 64
FF = 8192


EPSILON = 1e-05
SCORE_SCALE = 1.0 / 64.0
RESIDUAL_MULT = 0.22
ROPE_BASE = 10000000.0
NEGATIVE = -1e30
MESH = pl.DeviceIdType.MESH
PAIR = 2
CHUNKS = 2
ANYWHERE = pl.BlockSpec(memory_space=pl.ANY)
LINK_COST = pl.CostEstimate(flops=0, bytes_accessed=150_000_000, transcendentals=0)


def doc_index(positions, starts):
    return jnp.sum((positions[:, None] >= starts[None, :]).astype(jnp.int32), axis=1) - 1


def rope_tables(positions):
    half_size = HD // 2
    frequency = ROPE_BASE ** (-(jnp.arange(half_size, dtype=jnp.float32) * 2.0) / HD)
    angles = positions.astype(jnp.float32)[:, None] * frequency[None, :]
    return (jnp.cos(angles), jnp.sin(angles))


def rotate(tensor, cos_table, sin_table, head_count):
    row_count = tensor.shape[0]
    by_head = tensor.reshape(row_count, head_count, HD)
    half_size = HD // 2
    first_half = by_head[..., :half_size]
    second_half = by_head[..., half_size:]
    cos_rows = cos_table[:, None, :]
    sin_rows = sin_table[:, None, :]
    turned = jnp.concatenate(
        [
            first_half * cos_rows - second_half * sin_rows,
            second_half * cos_rows + first_half * sin_rows,
        ],
        axis=-1,
    )
    return turned.reshape(row_count, head_count * HD)


def dot_plain(left, right):
    return jnp.dot(left, right, preferred_element_type=jnp.float32)


def dot_back(left, right):
    return lax.dot_general(
        left, right, (((1,), (1,)), ((), ())), preferred_element_type=jnp.float32
    )


def dot_outer(left, right):
    return lax.dot_general(
        left, right, (((0,), (0,)), ((), ())), preferred_element_type=jnp.float32
    )


def norm_back(grad_normed, unit_rows, inv_scale, gain_full):
    scaled = grad_normed * gain_full
    return inv_scale * (scaled - unit_rows * jnp.mean(scaled * unit_rows, axis=-1, keepdims=True))


def general_device(
    tokens,
    doc_lengths,
    cotangent,
    gain_attn,
    w_query,
    w_key,
    w_value,
    w_output,
    gain_mlp,
    w_gate,
    w_up,
    w_down,
):
    local_rows = tokens.shape[1]
    ctx_size = lax.axis_size("ctx")
    length = local_rows * ctx_size
    group_size = H // KVH
    offset = lax.axis_index("ctx") * local_rows
    positions = offset + jnp.arange(local_rows, dtype=jnp.int32)
    seq_lengths = doc_lengths[0]
    starts = jnp.cumsum(seq_lengths) - seq_lengths
    doc_ids = doc_index(positions, starts)
    last_pos = offset + local_rows - 1
    first_doc = doc_ids[0]
    cos_table, sin_table = rope_tables(positions)
    gain1, gain2, wq_full, wk_full, wv_full, wo_full = (
        lax.all_gather(gain_attn, ("ctx", "fsdp"), axis=0, tiled=True),
        lax.all_gather(gain_mlp, ("ctx", "fsdp"), axis=0, tiled=True),
        lax.all_gather(w_query, ("ctx", "fsdp"), axis=0, tiled=True),
        lax.all_gather(w_key, ("ctx", "fsdp"), axis=0, tiled=True),
        lax.all_gather(w_value, ("ctx", "fsdp"), axis=0, tiled=True),
        lax.all_gather(w_output, ("ctx", "fsdp"), axis=0, tiled=True),
    )
    gain1_f = gain1.astype(jnp.float32)
    gain2_f = gain2.astype(jnp.float32)
    inputs = tokens[0].astype(jnp.float32)
    inv_one = lax.rsqrt(jnp.mean(inputs * inputs, axis=-1, keepdims=True) + EPSILON)
    unit_one = inputs * inv_one
    normed1 = (unit_one * gain1_f).astype(jnp.bfloat16)
    queries = rotate(dot_plain(normed1, wq_full), cos_table, sin_table, H).astype(jnp.bfloat16)
    key_rot = rotate(dot_plain(normed1, wk_full), cos_table, sin_table, KVH).astype(jnp.bfloat16)
    values = dot_plain(normed1, wv_full).astype(jnp.bfloat16)
    grouped = queries.reshape(local_rows, KVH, group_size, HD)
    start_state = (
        jnp.full((local_rows, KVH, group_size), NEGATIVE, jnp.float32),
        jnp.zeros((local_rows, KVH, group_size), jnp.float32),
        jnp.zeros((local_rows, KVH, group_size, HD), jnp.float32),
    )
    running = start_state
    key_piece = lax.all_gather(key_rot, "ctx", axis=0, tiled=True)
    value_piece = lax.all_gather(values, "ctx", axis=0, tiled=True)
    piece_rows = key_piece.shape[0]
    attend_key_width = math.gcd(piece_rows, 512)
    block_count = piece_rows // attend_key_width

    def one_block(carried, index_block):
        block_start = index_block * attend_key_width
        key_blk = lax.dynamic_slice_in_dim(key_piece, block_start, attend_key_width, 0).reshape(
            attend_key_width, KVH, HD
        )
        value_blk = lax.dynamic_slice_in_dim(value_piece, block_start, attend_key_width, 0).reshape(
            attend_key_width, KVH, HD
        )
        key_pos = block_start + jnp.arange(attend_key_width, dtype=jnp.int32)
        key_docs = doc_index(key_pos, starts)
        skip_block = (block_start > last_pos) | (key_docs[attend_key_width - 1] < first_doc)

        def update(current):
            run_max, run_sum, accumulated = current
            scores = (
                jnp.einsum("qkgd,tkd->qkgt", grouped, key_blk, preferred_element_type=jnp.float32)
                * SCORE_SCALE
            )
            allowed = (key_docs[None, :] == doc_ids[:, None]) & (
                key_pos[None, :] <= positions[:, None]
            )
            allowed = allowed[:, None, None, :]
            masked = jnp.where(allowed, scores, NEGATIVE)
            new_max = jnp.maximum(run_max, jnp.max(masked, axis=-1))
            weights_exp = jnp.where(allowed, jnp.exp(masked - new_max[..., None]), 0.0)
            factor = jnp.exp(run_max - new_max)
            new_sum = run_sum * factor + jnp.sum(weights_exp, axis=-1)
            new_acc = accumulated * factor[..., None] + jnp.einsum(
                "qkgt,tkd->qkgd",
                weights_exp.astype(jnp.bfloat16),
                value_blk,
                preferred_element_type=jnp.float32,
            )
            return (new_max, new_sum, new_acc)

        return (lax.cond(skip_block, lambda unchanged: unchanged, update, carried), None)

    running, _ = lax.scan(one_block, running, jnp.arange(block_count))
    run_max, run_sum, accumulated = running
    attended = accumulated / run_sum[..., None]
    log_sum = run_max + jnp.log(run_sum)
    mixed_heads = attended.reshape(local_rows, H * HD).astype(jnp.bfloat16)
    hidden = inputs + RESIDUAL_MULT * dot_plain(mixed_heads, wo_full)
    inv_two = lax.rsqrt(jnp.mean(hidden * hidden, axis=-1, keepdims=True) + EPSILON)
    unit_two = hidden * inv_two
    normed2 = (unit_two * gain2_f).astype(jnp.bfloat16)
    wg_full, wu_full, wd_full = (
        lax.all_gather(w_gate, ("ctx", "fsdp"), axis=0, tiled=True),
        lax.all_gather(w_up, ("ctx", "fsdp"), axis=0, tiled=True),
        lax.all_gather(w_down, ("ctx", "fsdp"), axis=0, tiled=True),
    )
    gate_pre = dot_plain(normed2, wg_full)
    up_pre = dot_plain(normed2, wu_full)
    sig_gate = jax.nn.sigmoid(gate_pre)
    silu_gate = gate_pre * sig_gate
    activ = (silu_gate * up_pre).astype(jnp.bfloat16)
    result = hidden + RESIDUAL_MULT * dot_plain(activ, wd_full)
    output = result.astype(jnp.bfloat16)[None]
    grad_out = cotangent[0].astype(jnp.float32)
    grad_mlp = (RESIDUAL_MULT * grad_out).astype(jnp.bfloat16)
    silu_slope = sig_gate * (1.0 + gate_pre * (1.0 - sig_gate))
    wg_back, wu_back, wd_back = (
        lax.all_gather(w_gate, ("ctx", "fsdp"), axis=0, tiled=True),
        lax.all_gather(w_up, ("ctx", "fsdp"), axis=0, tiled=True),
        lax.all_gather(w_down, ("ctx", "fsdp"), axis=0, tiled=True),
    )
    grad_act = dot_back(grad_mlp, wd_back)
    grad_gate = (grad_act * up_pre * silu_slope).astype(jnp.bfloat16)
    grad_up = (grad_act * silu_gate).astype(jnp.bfloat16)
    grad_norm2 = dot_back(grad_gate, wg_back) + dot_back(grad_up, wu_back)
    left_cols = normed2
    gate_up_shard = lax.psum_scatter(
        jnp.concatenate([dot_outer(left_cols, grad_gate), dot_outer(left_cols, grad_up)], axis=1),
        ("ctx", "fsdp"),
        scatter_dimension=0,
        tiled=True,
    )
    wg_shard = gate_up_shard[:, :FF]
    wu_shard = gate_up_shard[:, FF:]
    left_cols = activ
    wd_shard = lax.psum_scatter(
        dot_outer(left_cols, grad_mlp), ("ctx", "fsdp"), scatter_dimension=0, tiled=True
    )
    grad_g2 = jnp.sum(grad_norm2 * unit_two, axis=0)
    grad_hidden = grad_out + norm_back(grad_norm2, unit_two, inv_two, gain2_f)
    grad_attn = (RESIDUAL_MULT * grad_hidden).astype(jnp.bfloat16)
    wq_back, wk_back, wv_back, wo_back = (
        lax.all_gather(w_query, ("ctx", "fsdp"), axis=0, tiled=True),
        lax.all_gather(w_key, ("ctx", "fsdp"), axis=0, tiled=True),
        lax.all_gather(w_value, ("ctx", "fsdp"), axis=0, tiled=True),
        lax.all_gather(w_output, ("ctx", "fsdp"), axis=0, tiled=True),
    )
    grad_wo = dot_outer(mixed_heads, grad_attn)
    grad_att = (
        dot_back(grad_attn, wo_back).astype(jnp.bfloat16).reshape(local_rows, KVH, group_size, HD)
    )
    row_delta = jnp.sum(grad_att.astype(jnp.float32) * attended, axis=-1)
    key_all, value_all = (
        lax.all_gather(key_rot, "ctx", axis=0, tiled=True),
        lax.all_gather(values, "ctx", axis=0, tiled=True),
    )
    key_width = math.gcd(length, 512)
    block_count = length // key_width

    def back_block(grad_query, index_block):
        block_start = index_block * key_width
        key_blk = lax.dynamic_slice_in_dim(key_all, block_start, key_width, 0).reshape(
            key_width, KVH, HD
        )
        value_blk = lax.dynamic_slice_in_dim(value_all, block_start, key_width, 0).reshape(
            key_width, KVH, HD
        )
        key_pos = block_start + jnp.arange(key_width, dtype=jnp.int32)
        key_docs = doc_index(key_pos, starts)
        skip_block = (block_start > last_pos) | (key_docs[key_width - 1] < first_doc)

        def compute(current):
            scores = (
                jnp.einsum("qkgd,tkd->qkgt", grouped, key_blk, preferred_element_type=jnp.float32)
                * SCORE_SCALE
            )
            allowed = (key_docs[None, :] == doc_ids[:, None]) & (
                key_pos[None, :] <= positions[:, None]
            )
            allowed = allowed[:, None, None, :]
            probs_blk = jnp.where(
                allowed, jnp.exp(jnp.where(allowed, scores, NEGATIVE) - log_sum[..., None]), 0.0
            )
            grad_probs = jnp.einsum(
                "qkgd,tkd->qkgt", grad_att, value_blk, preferred_element_type=jnp.float32
            )
            grad_scores = (probs_blk * (grad_probs - row_delta[..., None])).astype(jnp.bfloat16)
            new_query = (
                current
                + jnp.einsum(
                    "qkgt,tkd->qkgd", grad_scores, key_blk, preferred_element_type=jnp.float32
                )
                * SCORE_SCALE
            )
            grad_key = (
                jnp.einsum(
                    "qkgt,qkgd->tkd", grad_scores, grouped, preferred_element_type=jnp.float32
                )
                * SCORE_SCALE
            )
            grad_value = jnp.einsum(
                "qkgt,qkgd->tkd",
                probs_blk.astype(jnp.bfloat16),
                grad_att,
                preferred_element_type=jnp.float32,
            )
            return (
                new_query,
                (grad_key.reshape(key_width, KVH * HD), grad_value.reshape(key_width, KVH * HD)),
            )

        def nothing(current):
            zero_rows = jnp.zeros((key_width, KVH * HD), jnp.float32)
            return (current, (zero_rows, zero_rows))

        return lax.cond(skip_block, nothing, compute, grad_query)

    grad_query, key_terms = lax.scan(
        back_block,
        jnp.zeros((local_rows, KVH, group_size, HD), jnp.float32),
        jnp.arange(block_count),
    )
    key_term_all = key_terms[0].reshape(length, KVH * HD)
    value_term_all = key_terms[1].reshape(length, KVH * HD)
    grad_keys, grad_values = (
        lax.psum_scatter(
            key_term_all.astype(jnp.bfloat16), "ctx", scatter_dimension=0, tiled=True
        ).astype(jnp.float32),
        lax.psum_scatter(
            value_term_all.astype(jnp.bfloat16), "ctx", scatter_dimension=0, tiled=True
        ).astype(jnp.float32),
    )
    grad_q_pre = rotate(grad_query.reshape(local_rows, H * HD), cos_table, -sin_table, H).astype(
        jnp.bfloat16
    )
    grad_k_pre = rotate(grad_keys, cos_table, -sin_table, KVH).astype(jnp.bfloat16)
    grad_v_pre = grad_values.astype(jnp.bfloat16)
    grad_norm1 = (
        dot_back(grad_q_pre, wq_back)
        + dot_back(grad_k_pre, wk_back)
        + dot_back(grad_v_pre, wv_back)
    )
    grad_wq = dot_outer(normed1, grad_q_pre)
    grad_wk = dot_outer(normed1, grad_k_pre)
    grad_wv = dot_outer(normed1, grad_v_pre)
    grad_g1 = jnp.sum(grad_norm1 * unit_one, axis=0)
    grad_inputs = grad_hidden + norm_back(grad_norm1, unit_one, inv_one, gain1_f)
    g1_shard, g2_shard, wq_shard, wk_shard, wv_shard, wo_shard = (
        lax.psum_scatter(grad_g1, ("ctx", "fsdp"), scatter_dimension=0, tiled=True),
        lax.psum_scatter(grad_g2, ("ctx", "fsdp"), scatter_dimension=0, tiled=True),
        lax.psum_scatter(grad_wq, ("ctx", "fsdp"), scatter_dimension=0, tiled=True),
        lax.psum_scatter(grad_wk, ("ctx", "fsdp"), scatter_dimension=0, tiled=True),
        lax.psum_scatter(grad_wv, ("ctx", "fsdp"), scatter_dimension=0, tiled=True),
        lax.psum_scatter(grad_wo, ("ctx", "fsdp"), scatter_dimension=0, tiled=True),
    )
    return (
        output,
        grad_inputs[None],
        g1_shard,
        wq_shard,
        wk_shard,
        wv_shard,
        wo_shard,
        g2_shard,
        wg_shard,
        wu_shard,
        wd_shard,
    )


def rows_of(blocks):
    return blocks.reshape((-1,) + blocks.shape[2:])


def in_vmem(count):
    return [pl.BlockSpec(memory_space=pltpu.VMEM)] * count


def greet_line(barrier, ctx_at, line_at, line_size):
    other = ctx_at + 1 - 2 * (ctx_at % PAIR)
    pl.semaphore_signal(barrier, inc=1, device_id={"ctx": other}, device_id_type=MESH)

    @pl.when(line_at > 0)
    def _():
        pl.semaphore_signal(barrier, inc=1, device_id={"ctx": ctx_at - PAIR}, device_id_type=MESH)

    @pl.when(line_at < line_size - 1)
    def _():
        pl.semaphore_signal(barrier, inc=1, device_id={"ctx": ctx_at + PAIR}, device_id_type=MESH)

    last = line_size - 1
    neighbours = 1 + (line_at + last - 1) // last + (2 * last - 1 - line_at) // last
    pl.semaphore_wait(barrier, neighbours)


def greet_all(barrier, me, count, fsdp_size):
    def greet(k, unused):
        target = (me + k) % count
        pl.semaphore_signal(
            barrier, inc=1, device_id=(target // fsdp_size, target % fsdp_size), device_id_type=MESH
        )
        return unused

    lax.fori_loop(1, count, greet, 0)
    pl.semaphore_wait(barrier, count - 1)


def gather_phase(line_size, x_ref, out_ref, send_sem, recv_sem, own_sem):
    me = lax.axis_index("ctx")
    line_at, pair_at = me // PAIR, me % PAIR
    rows = x_ref.shape[0]
    step = rows // CHUNKS

    def piece(block, part):
        return out_ref.at[pl.ds(pl.multiple_of(block * rows + part * step, step), step), :]

    def copy(block, part, way, own):
        slot = block * CHUNKS + part
        return pltpu.make_async_remote_copy(
            src_ref=x_ref.at[pl.ds(part * step, step), :] if own else piece(block, part),
            dst_ref=piece(block, part),
            send_sem=send_sem.at[way, slot],
            recv_sem=recv_sem.at[slot],
            device_id={"ctx": (me + 1 - 2 * pair_at, me + PAIR, me - PAIR)[way]},
            device_id_type=MESH,
        )

    def pass_on(block, part, upward, downward, own, act):
        if upward is not None:
            pl.when(upward)(lambda: act(copy(block, part, 1, own)))
        if downward is not None:
            pl.when(downward)(lambda: act(copy(block, part, 2, own)))
        act(copy(block, part, 0, own))

    def own_part(part, act):
        pass_on(me, part, line_at < line_size - 1, line_at > 0, True, act)

    def others(act, arrive, between):
        for distance in range(1, line_size):
            between(distance)
            for part in range(CHUNKS):

                @pl.when(line_at >= distance)
                def _():
                    block = me - PAIR * distance
                    arrive(block, part)
                    pass_on(block, part, line_at < line_size - 1, None, False, act)

                @pl.when(line_at + distance < line_size)
                def _():
                    block = me + PAIR * distance
                    arrive(block, part)
                    pass_on(block, part, None, line_at > 0, False, act)

    def start_own(part):
        own_part(part, lambda c: c.start())

    def finish(between=lambda distance: None):
        keep = pltpu.make_async_copy(
            x_ref, out_ref.at[pl.ds(pl.multiple_of(me * rows, rows), rows), :], own_sem
        )
        keep.start()
        others(
            lambda c: c.start(),
            lambda block, part: copy(block, part, 0, False).wait_recv(),
            between,
        )
        for place in range(line_size):
            for part in range(CHUNKS):
                copy(place * PAIR + 1 - pair_at, part, 0, False).wait_recv()
        for part in range(CHUNKS):
            own_part(part, lambda c: c.wait_send())
        others(lambda c: c.wait_send(), lambda block, part: None, lambda distance: None)
        keep.wait()

    return start_own, finish


def gather_scratch(ctx_size):
    return [
        pltpu.SemaphoreType.DMA((3, ctx_size * CHUNKS)),
        pltpu.SemaphoreType.DMA((ctx_size * CHUNKS,)),
        pltpu.SemaphoreType.DMA,
    ]


def scatter_phase(line_size, x_ref, sum_ref, near, below, above, near_send, near_sem, line_send, line_sem, emit, midway=lambda: None):
    me = lax.axis_index("ctx")
    line_at, pair_at = me // PAIR, me % PAIR
    rows = sum_ref.shape[0]
    step = rows // CHUNKS
    last = line_size - 1
    low = line_at // (line_size // 2)
    order = [k + (last - 2 * k) * (1 - low) for k in range(line_size // 2)]
    order += [line_at + 1 - 2 * (line_at % 2), line_at]

    def near_copy(place, part):
        start = (place * PAIR + 1 - pair_at) * rows + part * step
        return pltpu.make_async_remote_copy(
            src_ref=x_ref.at[pl.ds(pl.multiple_of(start, step), step), :],
            dst_ref=near.at[place, pl.ds(part * step, step), :],
            send_sem=near_send.at[place, part],
            recv_sem=near_sem.at[place, part],
            device_id={"ctx": me + 1 - 2 * pair_at},
            device_id_type=MESH,
        )

    def line_copy(place, part, up):
        part_rows = pl.ds(part * step, step)
        return pltpu.make_async_remote_copy(
            src_ref=near.at[place, part_rows, :],
            dst_ref=(below if up else above).at[place, part_rows, :],
            send_sem=line_send.at[place, part],
            recv_sem=line_sem.at[0 if up else 1, place, part],
            device_id={"ctx": me + PAIR if up else me - PAIR},
            device_id_type=MESH,
        )

    def mine(place, part):
        start = (place * PAIR + pair_at) * rows + part * step
        return x_ref[pl.ds(pl.multiple_of(start, step), step), :].astype(jnp.float32)

    for place in order:
        for part in range(CHUNKS):
            near_copy(place, part).start()

    for place in order[:-1]:
        for part in range(CHUNKS):
            part_rows = pl.ds(part * step, step)
            near_copy(place, part).wait_recv()

            def send(up, waits, arrived):
                @pl.when(waits)
                def _():
                    line_copy(place, part, up).wait_recv()
                    near[place, part_rows, :] = (
                        mine(place, part)
                        + near[place, part_rows, :].astype(jnp.float32)
                        + arrived[place, part_rows, :].astype(jnp.float32)
                    ).astype(near.dtype)

                @pl.when(jnp.logical_not(waits))
                def _():
                    near[place, part_rows, :] = (
                        mine(place, part) + near[place, part_rows, :].astype(jnp.float32)
                    ).astype(near.dtype)

                line_copy(place, part, up).start()

            pl.when(place > line_at)(lambda: send(True, line_at > 0, below))
            pl.when(place < line_at)(lambda: send(False, line_at < last, above))

    midway()
    for part in range(CHUNKS):
        part_rows = pl.ds(part * step, step)
        near_copy(line_at, part).wait_recv()
        sum_ref[part_rows, :] = mine(line_at, part) + near[line_at, part_rows, :].astype(jnp.float32)

        @pl.when(line_at > 0)
        def _():
            line_copy(line_at, part, True).wait_recv()
            sum_ref[part_rows, :] += below[line_at, part_rows, :].astype(jnp.float32)

        @pl.when(line_at < last)
        def _():
            line_copy(line_at, part, False).wait_recv()
            sum_ref[part_rows, :] += above[line_at, part_rows, :].astype(jnp.float32)

        emit(part, slice(part * step, (part + 1) * step))

    def finish():
        for place in order:
            for part in range(CHUNKS):
                near_copy(place, part).wait_send()
        for place in order[:-1]:
            for part in range(CHUNKS):
                line_copy(place, part, True).wait_send()

    return finish


def scatter_scratch(ctx_size, rows, width):
    line_size = ctx_size // PAIR
    held = pltpu.VMEM((line_size, rows, width), jnp.bfloat16)
    return [
        held,
        held,
        held,
        pltpu.SemaphoreType.DMA((line_size, CHUNKS)),
        pltpu.SemaphoreType.DMA((line_size, CHUNKS)),
        pltpu.SemaphoreType.DMA((line_size, CHUNKS)),
        pltpu.SemaphoreType.DMA((2, line_size, CHUNKS)),
    ]


def swap_lanes(values, outer, inner):
    tile = 128
    half = tile // 2
    low = lax.broadcasted_iota(jnp.int32, (values.shape[0], tile), 1) < half
    placed = [None] * (outer * inner // 2)
    for first in range(0, outer, 2):
        for second in range(0, inner, 2):
            at = (first * inner + second) // 2
            one = values[:, at * tile : (at + 1) * tile]
            at += inner // 2
            two = values[:, at * tile : (at + 1) * tile]
            at = (second * outer + first) // 2
            placed[at] = jnp.where(low, one, pltpu.roll(two, half, 1))
            placed[at + outer // 2] = jnp.where(low, pltpu.roll(one, half, 1), two)
    return jnp.concatenate(placed, axis=1)


def start_kernel(
    ctx_size, fsdp_size, tokens_ref, tile_ref, parts_ref, gate_ref, up_ref, out_ref, gains_ref, weight_ref,
    wide_ref, tiles, normed, tile_send, tile_recv, far_send, far_recv, near_send, near_recv, wide_send,
    wide_recv, kept, wide_kept, *sems
):
    me_ctx, me_fsdp = lax.axis_index("ctx"), lax.axis_index("fsdp")
    count = ctx_size * fsdp_size
    me = me_ctx * fsdp_size + me_fsdp
    greet_all(pltpu.get_barrier_semaphore(), me, count, fsdp_size)

    def tile_copy(k, source):
        target = (me + k) % count
        return pltpu.make_async_remote_copy(
            src_ref=tile_ref,
            dst_ref=tiles.at[source],
            send_sem=tile_send.at[k],
            recv_sem=tile_recv.at[k],
            device_id=(target // fsdp_size, target % fsdp_size),
            device_id_type=MESH,
        )

    def start_tile(k, unused):
        tile_copy(k, me).start()
        return unused

    def finish_tile(k, unused):
        tile_copy(k, (me + count - k) % count).wait_recv()
        return unused

    lax.fori_loop(1, count, start_tile, 0)
    tiles[pl.ds(me, 1)] = tile_ref[...][None]

    def far_copy(k, source):
        target = (me_ctx + k) % ctx_size
        return pltpu.make_async_remote_copy(
            src_ref=parts_ref.at[target],
            dst_ref=weight_ref.at[source * fsdp_size + me_fsdp],
            send_sem=far_send.at[k],
            recv_sem=far_recv.at[k],
            device_id={"ctx": target},
            device_id_type=MESH,
        )

    def near_copy(k, j, fsdp_source):
        block = (me_ctx + ctx_size - k) % ctx_size * fsdp_size + fsdp_source
        return pltpu.make_async_remote_copy(
            src_ref=parts_ref.at[me_ctx] if k == 0 else weight_ref.at[block],
            dst_ref=weight_ref.at[block],
            send_sem=near_send.at[k, j],
            recv_sem=near_recv.at[k, j],
            device_id={"fsdp": (me_fsdp + j) % fsdp_size},
            device_id_type=MESH,
        )

    wide = gate_ref.shape[1] // ctx_size

    def wide_part(which, target, source):
        cols = pl.ds(pl.multiple_of(target * wide, wide), wide)
        return (
            (gate_ref, up_ref)[which].at[:, cols],
            wide_ref.at[source, :, which * wide : (which + 1) * wide],
        )

    def wide_copy(which, k, source):
        target = (me_ctx + k) % ctx_size
        src, dst = wide_part(which, target, source)
        return pltpu.make_async_remote_copy(
            src_ref=src,
            dst_ref=dst,
            send_sem=wide_send.at[which, k],
            recv_sem=wide_recv.at[which, k],
            device_id={"ctx": target},
            device_id_type=MESH,
        )

    def wide_keep(which):
        return pltpu.make_async_copy(*wide_part(which, me_ctx, me_ctx), wide_kept.at[which])

    def wide_start(distance):
        for k in range(2 * distance - 1, min(2 * distance + 1, ctx_size)):
            for which in range(2):
                wide_copy(which, k, me_ctx).start()
        if distance == ctx_size // PAIR - 1:
            for which in range(2):
                wide_copy(which, ctx_size - 1, me_ctx).start()

    for k in range(1, ctx_size):
        far_copy(k, me_ctx).start()
    for j in range(1, fsdp_size):
        near_copy(0, j, me_fsdp).start()
    for which in range(2):
        wide_keep(which).start()
    keep = pltpu.make_async_copy(parts_ref.at[me_ctx], weight_ref.at[me], kept)
    keep.start()

    rows, model = tokens_ref.shape
    lax.fori_loop(1, count, finish_tile, 0)
    held = model // count
    for pair in range(count // 2):
        cols = slice(pair * 2 * held, (pair + 1) * 2 * held)
        gains_ref[:, cols] = tiles[2 * pair] + tiles[2 * pair + 1]
    start_own, finish_gather = gather_phase(ctx_size // PAIR, normed, out_ref, *sems)
    step = rows // CHUNKS
    for part in range(CHUNKS):
        part_rows = slice(part * step, (part + 1) * step)
        values = tokens_ref[part_rows, :].astype(jnp.float32)
        scale = lax.rsqrt(jnp.mean(values * values, axis=-1, keepdims=True) + EPSILON)
        normed[part_rows, :] = (values * scale * gains_ref[0:1, :]).astype(normed.dtype)
        start_own(part)
    for k in range(1, ctx_size):
        far_copy(k, (me_ctx + ctx_size - k) % ctx_size).wait_recv()
        for j in range(1, fsdp_size):
            near_copy(k, j, me_fsdp).start()
    finish_gather(wide_start)
    for which in range(2):
        for k in range(1, ctx_size):
            wide_copy(which, k, (me_ctx + ctx_size - k) % ctx_size).wait_recv()
        for k in range(1, ctx_size):
            wide_copy(which, k, me_ctx).wait_send()
        wide_keep(which).wait()
    for k in range(ctx_size):
        for j in range(1, fsdp_size):
            near_copy(k, j, (me_fsdp + fsdp_size - j) % fsdp_size).wait_recv()
    for k in range(ctx_size):
        for j in range(1, fsdp_size):
            near_copy(k, j, me_fsdp).wait_send()
    for k in range(1, ctx_size):
        far_copy(k, me_ctx).wait_send()

    def sent_tile(k, unused):
        tile_copy(k, me).wait_send()
        return unused

    lax.fori_loop(1, count, sent_tile, 0)
    keep.wait()


def start_layer(tokens, tile, parts, w_gate, w_up):
    ctx_size, fsdp_size = lax.axis_size("ctx"), lax.axis_size("fsdp")
    count = ctx_size * fsdp_size
    rows, model = tokens.shape
    dma = pltpu.SemaphoreType.DMA
    held = w_gate.shape[0]
    normed1, gains, weight, wide = pl.pallas_call(
        functools.partial(start_kernel, ctx_size, fsdp_size),
        out_shape=(
            jax.ShapeDtypeStruct((ctx_size * rows, model), jnp.bfloat16),
            jax.ShapeDtypeStruct((8, model), jnp.float32),
            jax.ShapeDtypeStruct((count,) + parts.shape[1:], parts.dtype),
            jax.ShapeDtypeStruct((ctx_size, held, 2 * w_gate.shape[1] // ctx_size), w_gate.dtype),
        ),
        in_specs=in_vmem(5),
        out_specs=(ANYWHERE, in_vmem(1)[0], ANYWHERE, ANYWHERE),
        scratch_shapes=[
            pltpu.VMEM((count, 8, 128), jnp.float32),
            pltpu.VMEM((rows, model), jnp.bfloat16),
            dma((count,)),
            dma((count,)),
            dma((ctx_size,)),
            dma((ctx_size,)),
            dma((ctx_size, fsdp_size)),
            dma((ctx_size, fsdp_size)),
            dma((2, ctx_size)),
            dma((2, ctx_size)),
            dma,
            dma((2,)),
        ]
        + gather_scratch(ctx_size),
        compiler_params=pltpu.CompilerParams(
            collective_id=0, has_side_effects=True, vmem_limit_bytes=32 * 2**20
        ),
        cost_estimate=LINK_COST,
        name="start_layer",
    )(tokens, tile, parts, w_gate, w_up)
    return normed1, gains, rows_of(weight), rows_of(wide)


def mlp_forward_kernel(
    ctx_size, fsdp_size, x_ref, tokens_ref, gains_ref, hidden_ref, out_ref, sums, normed, *sems
):
    line_size = ctx_size // PAIR
    me = lax.axis_index("ctx")
    greet_line(pltpu.get_barrier_semaphore(), me, me // PAIR, line_size)
    start_own, finish_gather = gather_phase(line_size, normed, out_ref, *sems[7:])

    def emit(part, rows):
        hidden = tokens_ref[rows, :].astype(jnp.float32) + RESIDUAL_MULT * sums[rows, :]
        hidden_ref[rows, :] = hidden
        scale = lax.rsqrt(jnp.mean(hidden * hidden, axis=-1, keepdims=True) + EPSILON)
        scaled = hidden * scale * gains_ref[1:2, :]
        normed[rows, :] = swap_lanes(scaled, ctx_size, fsdp_size).astype(normed.dtype)
        start_own(part)

    finish_scatter = scatter_phase(line_size, x_ref, sums, *sems[:7], emit)
    finish_gather()
    finish_scatter()


def mlp_backward_kernel(
    ctx_size, fsdp_size, x_ref, hidden_ref, grad_ref, gains_ref, grad_hidden_ref, grad_gain_ref, out_ref,
    sums, normed, *sems
):
    line_size = ctx_size // PAIR
    me = lax.axis_index("ctx")
    greet_line(pltpu.get_barrier_semaphore(), me, me // PAIR, line_size)
    start_own, finish_gather = gather_phase(line_size, normed, out_ref, *sems[7:])

    def emit(part, rows):
        grad_norm = swap_lanes(sums[rows, :], fsdp_size, ctx_size)
        hidden = hidden_ref[rows, :]
        scale = lax.rsqrt(jnp.mean(hidden * hidden, axis=-1, keepdims=True) + EPSILON)
        unit = hidden * scale
        grad_gain_ref[part : part + 1, :] = jnp.sum(grad_norm * unit, axis=0, keepdims=True)
        grad_hidden = grad_ref[rows, :].astype(jnp.float32) + norm_back(
            grad_norm, unit, scale, gains_ref[1:2, :]
        )
        grad_hidden_ref[rows, :] = grad_hidden
        normed[rows, :] = (RESIDUAL_MULT * grad_hidden).astype(normed.dtype)
        start_own(part)

    finish_scatter = scatter_phase(line_size, x_ref, sums, *sems[:7], emit)
    finish_gather()
    finish_scatter()


def scatter_gather(kernel, collective_id, extra_shapes, partial, *others):
    ctx_size, fsdp_size = lax.axis_size("ctx"), lax.axis_size("fsdp")
    rows, model = partial.shape[0] // ctx_size, partial.shape[1]
    return pl.pallas_call(
        functools.partial(kernel, ctx_size, fsdp_size),
        out_shape=extra_shapes + (jax.ShapeDtypeStruct(partial.shape, jnp.bfloat16),),
        in_specs=in_vmem(1 + len(others)),
        out_specs=tuple(in_vmem(len(extra_shapes))) + (ANYWHERE,),
        scratch_shapes=[pltpu.VMEM((rows, model), jnp.float32), pltpu.VMEM((rows, model), jnp.bfloat16)]
        + scatter_scratch(ctx_size, rows, model)
        + gather_scratch(ctx_size),
        compiler_params=pltpu.CompilerParams(
            collective_id=collective_id, has_side_effects=True, vmem_limit_bytes=40 * 2**20
        ),
        cost_estimate=LINK_COST,
    )(partial, *others)


def mlp_forward(partial, tokens, gains):
    hidden = jax.ShapeDtypeStruct(tokens.shape, jnp.float32)
    return scatter_gather(mlp_forward_kernel, 1, (hidden,), partial, tokens, gains)


def mlp_backward(partial, hidden, grad_out, gains):
    like = jax.ShapeDtypeStruct(hidden.shape, jnp.float32)
    gain = jax.ShapeDtypeStruct((CHUNKS, hidden.shape[1]), jnp.float32)
    return scatter_gather(mlp_backward_kernel, 2, (like, gain), partial, hidden, grad_out, gains)


def finish_kernel(
    ctx_size, fsdp_size, x_ref, tokens_ref, grad_ref, gains_ref, gain2_ref, wo_ref, qkv_ref,
    grad_tokens_ref, gain_out_ref, wo_out_ref, qkv_out_ref,
    sums, gain1, tiles, arrived, wo_in, qkv_in, qkv_sum, tile_send, tile_recv, near_send, near_recv,
    far_send, far_recv, *sems
):
    line_size = ctx_size // PAIR
    me_ctx, me_fsdp = lax.axis_index("ctx"), lax.axis_index("fsdp")
    count = ctx_size * fsdp_size
    me = me_ctx * fsdp_size + me_fsdp
    greet_all(pltpu.get_barrier_semaphore(), me, count, fsdp_size)

    def near_copy(which, j):
        target = (me_fsdp + j) % fsdp_size
        terms, landing = ((wo_ref, wo_in), (qkv_ref, qkv_in))[which]
        return pltpu.make_async_remote_copy(
            src_ref=terms.at[target],
            dst_ref=landing.at[j],
            send_sem=near_send.at[which, j],
            recv_sem=near_recv.at[which, j],
            device_id={"fsdp": target},
            device_id_type=MESH,
        )

    def far_copy(k, source):
        target = (me_ctx + k) % ctx_size
        return pltpu.make_async_remote_copy(
            src_ref=qkv_sum.at[target],
            dst_ref=qkv_out_ref.at[source],
            send_sem=far_send.at[k],
            recv_sem=far_recv.at[k],
            device_id={"ctx": target},
            device_id_type=MESH,
        )

    def tile_copy(k, source):
        target = (me + k) % count
        return pltpu.make_async_remote_copy(
            src_ref=tiles.at[target // 2],
            dst_ref=arrived.at[source],
            send_sem=tile_send.at[k],
            recv_sem=tile_recv.at[k],
            device_id=(target // fsdp_size, target % fsdp_size),
            device_id_type=MESH,
        )

    def midway():
        for which, own, landing in ((1, qkv_ref, qkv_in), (0, wo_ref, wo_in)):
            for j in range(1, fsdp_size):
                near_copy(which, j).wait_recv()
            total = own[pl.ds(me_fsdp, 1)][0].astype(jnp.float32)
            for j in range(1, fsdp_size):
                total += landing[j].astype(jnp.float32)
            if which:
                qkv_sum[...] = total.astype(qkv_sum.dtype)
                for k in range(1, ctx_size):
                    far_copy(k, me_ctx).start()
                qkv_out_ref[pl.ds(me_ctx, 1)] = qkv_sum[pl.ds(me_ctx, 1)]
            else:
                wo_out_ref[...] = total

    def emit(part, rows):
        grad_norm = sums[rows, :]
        values = tokens_ref[rows, :].astype(jnp.float32)
        scale = lax.rsqrt(jnp.mean(values * values, axis=-1, keepdims=True) + EPSILON)
        unit = values * scale
        gain1[part : part + 1, :] = jnp.sum(grad_norm * unit, axis=0, keepdims=True)
        grad_tokens_ref[rows, :] = grad_ref[rows, :] + norm_back(
            grad_norm, unit, scale, gains_ref[0:1, :]
        )

    for which in (1, 0):
        for j in range(1, fsdp_size):
            near_copy(which, j).start()
    finish_scatter = scatter_phase(line_size, x_ref, sums, *sems, emit, midway)
    row = lax.broadcasted_iota(jnp.int32, (8, 128), 0)
    for pair in range(count // 2):
        cols = slice(pair * 128, (pair + 1) * 128)
        first = jnp.sum(gain1[:, cols], axis=0, keepdims=True)
        second = jnp.sum(gain2_ref[:, cols], axis=0, keepdims=True)
        tiles[pair] = jnp.where(row == 0, first, jnp.where(row == 1, second, 0.0))

    def start_tile(k, unused):
        tile_copy(k, me).start()
        return unused

    def finish_tile(k, unused):
        tile_copy(k, (me + count - k) % count).wait_recv()
        return unused

    def sent_tile(k, unused):
        tile_copy(k, me).wait_send()
        return unused

    lax.fori_loop(1, count, start_tile, 0)
    arrived[pl.ds(me, 1)] = tiles[pl.ds(me // 2, 1)]
    for k in range(1, ctx_size):
        far_copy(k, (me_ctx + ctx_size - k) % ctx_size).wait_recv()
    lax.fori_loop(1, count, finish_tile, 0)
    gain_out_ref[...] = jnp.sum(arrived[...], axis=0)
    finish_scatter()
    for which in range(2):
        for j in range(1, fsdp_size):
            near_copy(which, j).wait_send()
    for k in range(1, ctx_size):
        far_copy(k, me_ctx).wait_send()
    lax.fori_loop(1, count, sent_tile, 0)


def finish_layer(partial, tokens, grad_hidden, gains, grad_gain2, wo_terms, qkv_terms):
    ctx_size, fsdp_size = lax.axis_size("ctx"), lax.axis_size("fsdp")
    count = ctx_size * fsdp_size
    rows, model = tokens.shape
    dma = pltpu.SemaphoreType.DMA
    f32, bf16 = jnp.float32, jnp.bfloat16
    held, width = qkv_terms.shape[2:]
    return pl.pallas_call(
        functools.partial(finish_kernel, ctx_size, fsdp_size),
        out_shape=(
            jax.ShapeDtypeStruct((rows, model), f32),
            jax.ShapeDtypeStruct((8, 128), f32),
            jax.ShapeDtypeStruct(wo_terms.shape[1:], f32),
            jax.ShapeDtypeStruct((ctx_size, held, width), bf16),
        ),
        in_specs=in_vmem(7),
        out_specs=tuple(in_vmem(4)),
        scratch_shapes=[
            pltpu.VMEM((rows, model), f32),
            pltpu.VMEM((CHUNKS, model), f32),
            pltpu.VMEM((count // 2, 8, 128), f32),
            pltpu.VMEM((count, 8, 128), f32),
            pltpu.VMEM(wo_terms.shape, bf16),
            pltpu.VMEM(qkv_terms.shape, bf16),
            pltpu.VMEM((ctx_size, held, width), bf16),
            dma((count,)),
            dma((count,)),
            dma((2, fsdp_size)),
            dma((2, fsdp_size)),
            dma((ctx_size,)),
            dma((ctx_size,)),
        ]
        + scatter_scratch(ctx_size, rows, model),
        compiler_params=pltpu.CompilerParams(
            collective_id=3, has_side_effects=True, vmem_limit_bytes=40 * 2**20
        ),
        cost_estimate=LINK_COST,
        name="finish_layer",
    )(partial, tokens, grad_hidden, gains, grad_gain2, wo_terms, qkv_terms)


def swap_ctx(blocks):
    return lax.all_to_all(blocks, "ctx", split_axis=0, concat_axis=0, tiled=True)


def by_fsdp(grad, ctx_size, fsdp_size):
    parts = grad.reshape(ctx_size, fsdp_size, -1, grad.shape[-1]).transpose(1, 0, 2, 3)
    return rows_of(rows_of(parts))


def return_columns(terms, ctx_size):
    return swap_ctx(terms.reshape(ctx_size, -1, terms.shape[-1]))


def half_turn(values, sign_table):
    lane = lax.broadcasted_iota(jnp.int32, values.shape, 1)
    width = values.shape[1]
    quarter = HD // 2
    ahead = pltpu.roll(values, width - quarter, 1)
    behind = pltpu.roll(values, quarter, 1)
    return jnp.where(lane % HD < quarter, ahead, behind) * sign_table


def turn(values, cos_table, sign_table):
    copies = values.shape[1] // cos_table.shape[1]
    if copies > 1:
        cos_table = jnp.concatenate([cos_table] * copies, axis=1)
        sign_table = jnp.concatenate([sign_table] * copies, axis=1)
    return values * cos_table + half_turn(values, sign_table)


def attention_forward_kernel(
    block_rows, qkv_ref, cos_ref, sin_ref, doc_col_ref, doc_row_ref, q_ref, kv_ref, out_ref, lse_ref
):
    length = qkv_ref.shape[0]
    group = H // KVH
    width = group * HD
    q_ref[...] = turn(qkv_ref[:, :width], cos_ref[...], sin_ref[...]).astype(jnp.bfloat16)
    pair = qkv_ref[:, width:]
    lane = lax.broadcasted_iota(jnp.int32, pair.shape, 1)
    turned = turn(pair, cos_ref[...], sin_ref[...])
    kv_ref[...] = jnp.where(lane < HD, turned, pair).astype(jnp.bfloat16)
    for block in range(length // block_rows):
        rows = slice(block * block_rows, (block + 1) * block_rows)
        reach = (block + 1) * block_rows
        keys = kv_ref[:reach, :HD]
        values = kv_ref[:reach, HD:]
        query_at = block * block_rows + lax.broadcasted_iota(jnp.int32, (block_rows, reach), 0)
        key_at = lax.broadcasted_iota(jnp.int32, (block_rows, reach), 1)
        allowed = (doc_col_ref[rows, :] == doc_row_ref[:, :reach]) & (key_at <= query_at)
        for head in range(group):
            cols = slice(head * HD, (head + 1) * HD)
            scores = dot_back(q_ref[rows, cols], keys) * SCORE_SCALE
            masked = jnp.where(allowed, scores, NEGATIVE)
            top = jnp.max(masked, axis=1, keepdims=True)
            weights = jnp.where(allowed, jnp.exp(masked - top), 0.0)
            total = jnp.sum(weights, axis=1, keepdims=True)
            mixed = dot_plain(weights.astype(jnp.bfloat16), values)
            out_ref[rows, cols] = (mixed / total).astype(jnp.bfloat16)
            lse_ref[rows, head : head + 1] = top + jnp.log(total)


def attention_backward_kernel(
    block_rows, q_ref, kv_ref, do_ref, lse_ref, cos_ref, sin_ref, doc_col_ref, doc_row_ref, grad_ref, dq_ref, dkv_ref
):
    length = q_ref.shape[0]
    group = H // KVH
    width = group * HD
    dkv_ref[...] = jnp.zeros_like(dkv_ref)
    for block in range(length // block_rows):
        rows = slice(block * block_rows, (block + 1) * block_rows)
        reach = (block + 1) * block_rows
        keys = kv_ref[:reach, :HD]
        values = kv_ref[:reach, HD:]
        query_at = block * block_rows + lax.broadcasted_iota(jnp.int32, (block_rows, reach), 0)
        key_at = lax.broadcasted_iota(jnp.int32, (block_rows, reach), 1)
        allowed = (doc_col_ref[rows, :] == doc_row_ref[:, :reach]) & (key_at <= query_at)
        for head in range(group):
            cols = slice(head * HD, (head + 1) * HD)
            query = q_ref[rows, cols]
            grad_out = do_ref[rows, cols]
            scores = dot_back(query, keys) * SCORE_SCALE
            probs = jnp.where(
                allowed,
                jnp.exp(jnp.where(allowed, scores, NEGATIVE) - lse_ref[rows, head : head + 1]),
                0.0,
            )
            grad_probs = dot_back(grad_out, values)
            delta = jnp.sum(probs * grad_probs, axis=1, keepdims=True)
            grad_scores = (probs * (grad_probs - delta)).astype(jnp.bfloat16)
            dq_ref[rows, cols] = dot_plain(grad_scores, keys) * SCORE_SCALE
            dkv_ref[:reach, :HD] += dot_outer(grad_scores, query) * SCORE_SCALE
            dkv_ref[:reach, HD:] += dot_outer(probs.astype(jnp.bfloat16), grad_out)
    grad_ref[:, :width] = turn(dq_ref[...], cos_ref[...], -sin_ref[...]).astype(jnp.bfloat16)
    pair = dkv_ref[...]
    lane = lax.broadcasted_iota(jnp.int32, pair.shape, 1)
    turned = turn(pair, cos_ref[...], -sin_ref[...])
    grad_ref[:, width:] = jnp.where(lane < HD, turned, pair).astype(jnp.bfloat16)


def attention_forward(qkv, tables, block_rows):
    length = qkv.shape[0]
    width = (H // KVH) * HD
    return pl.pallas_call(
        functools.partial(attention_forward_kernel, block_rows),
        out_shape=(
            jax.ShapeDtypeStruct((length, width), jnp.bfloat16),
            jax.ShapeDtypeStruct((length, 2 * HD), jnp.bfloat16),
            jax.ShapeDtypeStruct((length, width), jnp.bfloat16),
            jax.ShapeDtypeStruct((length, H // KVH), jnp.float32),
        ),
        in_specs=in_vmem(5),
        out_specs=tuple(in_vmem(4)),
        compiler_params=pltpu.CompilerParams(vmem_limit_bytes=48 * 2**20),
        name="attend",
    )(qkv, *tables)


def attention_backward(q, kv, grad_out, lse, tables, block_rows):
    length, width = q.shape
    return pl.pallas_call(
        functools.partial(attention_backward_kernel, block_rows),
        out_shape=jax.ShapeDtypeStruct((length, width + 2 * HD), jnp.bfloat16),
        in_specs=in_vmem(8),
        out_specs=in_vmem(1)[0],
        scratch_shapes=[
            pltpu.VMEM((length, width), jnp.float32),
            pltpu.VMEM((length, 2 * HD), jnp.float32),
        ],
        compiler_params=pltpu.CompilerParams(vmem_limit_bytes=48 * 2**20),
        name="attend_back",
    )(q, kv, grad_out, lse, *tables)


def on_device(
    tokens,
    doc_lengths,
    cotangent,
    gain_attn,
    w_query,
    w_key,
    w_value,
    w_output,
    gain_mlp,
    w_gate,
    w_up,
    w_down,
):
    local_rows, model = tokens.shape[1:]
    ctx_size = lax.axis_size("ctx")
    fsdp_size = lax.axis_size("fsdp")
    length = local_rows * ctx_size
    group_width = (H // KVH) * HD
    ff_slice = FF // ctx_size
    held_rows = w_query.shape[0]
    bf16 = jnp.bfloat16

    positions = jnp.arange(length, dtype=jnp.int32)
    seq_lengths = doc_lengths[0]
    starts = jnp.cumsum(seq_lengths) - seq_lengths
    doc_ids = doc_index(positions, starts)
    cos_half, sin_half = rope_tables(positions)
    cos_table = jnp.concatenate([cos_half] * 4, axis=1)
    sin_table = jnp.concatenate([-sin_half, sin_half] * 2, axis=1)
    tables = (cos_table, sin_table, doc_ids[:, None], doc_ids[None, :])


    def by_slice(weight):
        return weight.reshape(held_rows, ctx_size, -1)

    qkv_parts = jnp.concatenate([by_slice(w_query), by_slice(w_key), by_slice(w_value)], axis=2)
    wo_mine = lax.all_gather(w_output, "fsdp", axis=0, tiled=True)
    wd_mine = lax.all_gather(w_down, "fsdp", axis=0, tiled=True)
    gain_rows = jnp.stack([gain_attn, gain_mlp]).astype(jnp.float32)
    odd = lax.axis_index("fsdp") % 2
    gain_tile = jnp.concatenate([gain_rows * (1 - odd), gain_rows * odd], axis=1)
    gain_tile = jnp.pad(gain_tile, ((0, 8 - gain_tile.shape[0]), (0, 128 - gain_tile.shape[1])))
    normed1, gains, w_qkv, gu_mine = start_layer(
        tokens[0], gain_tile, qkv_parts.transpose(1, 0, 2), w_gate, w_up
    )
    w_gu = lax.all_gather(gu_mine, "fsdp", axis=0, tiled=True)
    grad_out = cotangent[0].astype(jnp.float32)
    grad_mlp = (RESIDUAL_MULT * grad_out).astype(bf16)

    block_rows = math.gcd(length, 256)
    qkv = dot_plain(normed1, w_qkv)
    qkv, grad_mlp = lax.optimization_barrier((qkv, grad_mlp))
    grad_mlp = lax.all_gather(grad_mlp, "ctx", axis=0, tiled=True)
    q, kv, mixed_heads, log_sum = attention_forward(qkv, tables, block_rows)
    hidden, normed2 = mlp_forward(dot_plain(mixed_heads, wo_mine).astype(bf16), tokens[0], gains)

    gate_up = dot_plain(normed2, w_gu)
    gate_pre, up_pre = gate_up[:, :ff_slice], gate_up[:, ff_slice:]
    sig_gate = jax.nn.sigmoid(gate_pre)
    silu_gate = gate_pre * sig_gate
    activ = (silu_gate * up_pre).astype(bf16)
    activ, gate_up = lax.optimization_barrier((activ, gate_up))
    gate_pre, up_pre = gate_up[:, :ff_slice], gate_up[:, ff_slice:]
    sig_gate = jax.nn.sigmoid(gate_pre)
    silu_gate = gate_pre * sig_gate
    out_terms, grad_mlp = lax.optimization_barrier(
        (dot_plain(activ, wd_mine).astype(bf16), grad_mlp)
    )
    branch = lax.psum_scatter(out_terms, "ctx", scatter_dimension=0, tiled=True)
    output = (hidden + RESIDUAL_MULT * branch.astype(jnp.float32)).astype(bf16)[None]

    silu_slope = sig_gate * (1.0 + gate_pre * (1.0 - sig_gate))
    grad_act = dot_back(grad_mlp, wd_mine)
    grad_gu = jnp.concatenate(
        [(grad_act * up_pre * silu_slope).astype(bf16), (grad_act * silu_gate).astype(bf16)], axis=1
    )
    partial2, gu_terms, wd_terms = lax.optimization_barrier(
        (
            dot_back(grad_gu, w_gu).astype(bf16),
            dot_outer(normed2, grad_gu).astype(bf16),
            dot_outer(activ, grad_mlp).astype(bf16),
        )
    )
    grad_hidden, grad_g2, grad_attn = mlp_backward(partial2, hidden, cotangent[0], gains)
    gu_back = lax.psum_scatter(gu_terms, "fsdp", scatter_dimension=0, tiled=True)
    wd_back = lax.psum_scatter(wd_terms, "fsdp", scatter_dimension=0, tiled=True)

    grad_mixed = dot_back(grad_attn, wo_mine).astype(bf16)
    wo_terms = dot_outer(mixed_heads, grad_attn).astype(bf16)
    grad_qkv = attention_backward(q, kv, grad_mixed, log_sum, tables, block_rows)
    grad_qkv, gu_back = lax.optimization_barrier((grad_qkv, gu_back))
    gu_back = return_columns(gu_back, ctx_size)
    partial1 = dot_back(grad_qkv, w_qkv).astype(bf16)
    qkv_terms = by_fsdp(dot_outer(normed1, grad_qkv).astype(bf16), ctx_size, fsdp_size)
    grad_inputs, gain_back, wo_back, qkv_back = finish_layer(
        partial1,
        tokens[0],
        grad_hidden,
        gains,
        grad_g2,
        wo_terms.reshape(fsdp_size, held_rows, model),
        qkv_terms.reshape(fsdp_size, ctx_size, held_rows, -1),
    )
    grad_inputs, wd_back = lax.optimization_barrier((grad_inputs, wd_back))
    gain_back = jnp.where(odd == 0, gain_back[:2, :held_rows], gain_back[:2, held_rows:])

    def joined(parts):
        return parts.transpose(1, 0, 2).reshape(held_rows, -1).astype(jnp.float32)

    key_end = group_width + HD
    return (
        output,
        grad_inputs[None],
        gain_back[0],
        joined(qkv_back[:, :, :group_width]),
        joined(qkv_back[:, :, group_width:key_end]),
        joined(qkv_back[:, :, key_end:]),
        wo_back,
        gain_back[1],
        joined(gu_back[:, :, :ff_slice]),
        joined(gu_back[:, :, ff_slice:]),
        wd_back.astype(jnp.float32),
    )


def solution(mesh):
    in_specs = (
        P("fsdp", "ctx", None),
        P("fsdp", None),
        P("fsdp", "ctx", None),
        P(("ctx", "fsdp")),
        P(("ctx", "fsdp"), None),
        P(("ctx", "fsdp"), None),
        P(("ctx", "fsdp"), None),
        P(("ctx", "fsdp"), None),
        P(("ctx", "fsdp")),
        P(("ctx", "fsdp"), None),
        P(("ctx", "fsdp"), None),
        P(("ctx", "fsdp"), None),
    )
    out_specs = (
        P("fsdp", "ctx", None),
        P("fsdp", "ctx", None),
        P(("ctx", "fsdp")),
        P(("ctx", "fsdp"), None),
        P(("ctx", "fsdp"), None),
        P(("ctx", "fsdp"), None),
        P(("ctx", "fsdp"), None),
        P(("ctx", "fsdp")),
        P(("ctx", "fsdp"), None),
        P(("ctx", "fsdp"), None),
        P(("ctx", "fsdp"), None),
    )
    if mesh.shape["ctx"] != KVH or KVH != 4 * PAIR:
        return jax.shard_map(
            general_device, mesh=mesh, in_specs=in_specs, out_specs=out_specs, check_vma=False
        )

    return jax.shard_map(
        on_device, mesh=mesh, in_specs=in_specs, out_specs=out_specs, check_vma=False
    )
```

```python
import functools
import math

import jax
import jax.numpy as jnp
from jax import lax
from jax.experimental import pallas as pl
from jax.experimental.pallas import tpu as pltpu
from jax.sharding import PartitionSpec as P

H = 32
KVH = 8
HD = 64
FF = 8192


EPSILON = 1e-05
SCORE_SCALE = 1.0 / 64.0
RESIDUAL_MULT = 0.22
ROPE_BASE = 10000000.0
NEGATIVE = -1e30
MESH = pl.DeviceIdType.MESH
PAIR = 2
CHUNKS = 2
EVEN = 384
EVEN_LAST = 0
ANYWHERE = pl.BlockSpec(memory_space=pl.ANY)
LINK_COST = pl.CostEstimate(flops=0, bytes_accessed=150_000_000, transcendentals=0)


def doc_index(positions, starts):
    return jnp.sum((positions[:, None] >= starts[None, :]).astype(jnp.int32), axis=1) - 1


def rope_tables(positions):
    half_size = HD // 2
    frequency = ROPE_BASE ** (-(jnp.arange(half_size, dtype=jnp.float32) * 2.0) / HD)
    angles = positions.astype(jnp.float32)[:, None] * frequency[None, :]
    return (jnp.cos(angles), jnp.sin(angles))


def rotate(tensor, cos_table, sin_table, head_count):
    row_count = tensor.shape[0]
    by_head = tensor.reshape(row_count, head_count, HD)
    half_size = HD // 2
    first_half = by_head[..., :half_size]
    second_half = by_head[..., half_size:]
    cos_rows = cos_table[:, None, :]
    sin_rows = sin_table[:, None, :]
    turned = jnp.concatenate(
        [
            first_half * cos_rows - second_half * sin_rows,
            second_half * cos_rows + first_half * sin_rows,
        ],
        axis=-1,
    )
    return turned.reshape(row_count, head_count * HD)


def dot_plain(left, right):
    return jnp.dot(left, right, preferred_element_type=jnp.float32)


def dot_back(left, right):
    return lax.dot_general(
        left, right, (((1,), (1,)), ((), ())), preferred_element_type=jnp.float32
    )


def dot_outer(left, right):
    return lax.dot_general(
        left, right, (((0,), (0,)), ((), ())), preferred_element_type=jnp.float32
    )


def norm_back(grad_normed, unit_rows, inv_scale, gain_full):
    scaled = grad_normed * gain_full
    return inv_scale * (scaled - unit_rows * jnp.mean(scaled * unit_rows, axis=-1, keepdims=True))


def general_device(
    tokens,
    doc_lengths,
    cotangent,
    gain_attn,
    w_query,
    w_key,
    w_value,
    w_output,
    gain_mlp,
    w_gate,
    w_up,
    w_down,
):
    local_rows = tokens.shape[1]
    ctx_size = lax.axis_size("ctx")
    length = local_rows * ctx_size
    group_size = H // KVH
    offset = lax.axis_index("ctx") * local_rows
    positions = offset + jnp.arange(local_rows, dtype=jnp.int32)
    seq_lengths = doc_lengths[0]
    starts = jnp.cumsum(seq_lengths) - seq_lengths
    doc_ids = doc_index(positions, starts)
    last_pos = offset + local_rows - 1
    first_doc = doc_ids[0]
    cos_table, sin_table = rope_tables(positions)
    gain1, gain2, wq_full, wk_full, wv_full, wo_full = (
        lax.all_gather(gain_attn, ("ctx", "fsdp"), axis=0, tiled=True),
        lax.all_gather(gain_mlp, ("ctx", "fsdp"), axis=0, tiled=True),
        lax.all_gather(w_query, ("ctx", "fsdp"), axis=0, tiled=True),
        lax.all_gather(w_key, ("ctx", "fsdp"), axis=0, tiled=True),
        lax.all_gather(w_value, ("ctx", "fsdp"), axis=0, tiled=True),
        lax.all_gather(w_output, ("ctx", "fsdp"), axis=0, tiled=True),
    )
    gain1_f = gain1.astype(jnp.float32)
    gain2_f = gain2.astype(jnp.float32)
    inputs = tokens[0].astype(jnp.float32)
    inv_one = lax.rsqrt(jnp.mean(inputs * inputs, axis=-1, keepdims=True) + EPSILON)
    unit_one = inputs * inv_one
    normed1 = (unit_one * gain1_f).astype(jnp.bfloat16)
    queries = rotate(dot_plain(normed1, wq_full), cos_table, sin_table, H).astype(jnp.bfloat16)
    key_rot = rotate(dot_plain(normed1, wk_full), cos_table, sin_table, KVH).astype(jnp.bfloat16)
    values = dot_plain(normed1, wv_full).astype(jnp.bfloat16)
    grouped = queries.reshape(local_rows, KVH, group_size, HD)
    start_state = (
        jnp.full((local_rows, KVH, group_size), NEGATIVE, jnp.float32),
        jnp.zeros((local_rows, KVH, group_size), jnp.float32),
        jnp.zeros((local_rows, KVH, group_size, HD), jnp.float32),
    )
    running = start_state
    key_piece = lax.all_gather(key_rot, "ctx", axis=0, tiled=True)
    value_piece = lax.all_gather(values, "ctx", axis=0, tiled=True)
    piece_rows = key_piece.shape[0]
    attend_key_width = math.gcd(piece_rows, 512)
    block_count = piece_rows // attend_key_width

    def one_block(carried, index_block):
        block_start = index_block * attend_key_width
        key_blk = lax.dynamic_slice_in_dim(key_piece, block_start, attend_key_width, 0).reshape(
            attend_key_width, KVH, HD
        )
        value_blk = lax.dynamic_slice_in_dim(value_piece, block_start, attend_key_width, 0).reshape(
            attend_key_width, KVH, HD
        )
        key_pos = block_start + jnp.arange(attend_key_width, dtype=jnp.int32)
        key_docs = doc_index(key_pos, starts)
        skip_block = (block_start > last_pos) | (key_docs[attend_key_width - 1] < first_doc)

        def update(current):
            run_max, run_sum, accumulated = current
            scores = (
                jnp.einsum("qkgd,tkd->qkgt", grouped, key_blk, preferred_element_type=jnp.float32)
                * SCORE_SCALE
            )
            allowed = (key_docs[None, :] == doc_ids[:, None]) & (
                key_pos[None, :] <= positions[:, None]
            )
            allowed = allowed[:, None, None, :]
            masked = jnp.where(allowed, scores, NEGATIVE)
            new_max = jnp.maximum(run_max, jnp.max(masked, axis=-1))
            weights_exp = jnp.where(allowed, jnp.exp(masked - new_max[..., None]), 0.0)
            factor = jnp.exp(run_max - new_max)
            new_sum = run_sum * factor + jnp.sum(weights_exp, axis=-1)
            new_acc = accumulated * factor[..., None] + jnp.einsum(
                "qkgt,tkd->qkgd",
                weights_exp.astype(jnp.bfloat16),
                value_blk,
                preferred_element_type=jnp.float32,
            )
            return (new_max, new_sum, new_acc)

        return (lax.cond(skip_block, lambda unchanged: unchanged, update, carried), None)

    running, _ = lax.scan(one_block, running, jnp.arange(block_count))
    run_max, run_sum, accumulated = running
    attended = accumulated / run_sum[..., None]
    log_sum = run_max + jnp.log(run_sum)
    mixed_heads = attended.reshape(local_rows, H * HD).astype(jnp.bfloat16)
    hidden = inputs + RESIDUAL_MULT * dot_plain(mixed_heads, wo_full)
    inv_two = lax.rsqrt(jnp.mean(hidden * hidden, axis=-1, keepdims=True) + EPSILON)
    unit_two = hidden * inv_two
    normed2 = (unit_two * gain2_f).astype(jnp.bfloat16)
    wg_full, wu_full, wd_full = (
        lax.all_gather(w_gate, ("ctx", "fsdp"), axis=0, tiled=True),
        lax.all_gather(w_up, ("ctx", "fsdp"), axis=0, tiled=True),
        lax.all_gather(w_down, ("ctx", "fsdp"), axis=0, tiled=True),
    )
    gate_pre = dot_plain(normed2, wg_full)
    up_pre = dot_plain(normed2, wu_full)
    sig_gate = jax.nn.sigmoid(gate_pre)
    silu_gate = gate_pre * sig_gate
    activ = (silu_gate * up_pre).astype(jnp.bfloat16)
    result = hidden + RESIDUAL_MULT * dot_plain(activ, wd_full)
    output = result.astype(jnp.bfloat16)[None]
    grad_out = cotangent[0].astype(jnp.float32)
    grad_mlp = (RESIDUAL_MULT * grad_out).astype(jnp.bfloat16)
    silu_slope = sig_gate * (1.0 + gate_pre * (1.0 - sig_gate))
    wg_back, wu_back, wd_back = (
        lax.all_gather(w_gate, ("ctx", "fsdp"), axis=0, tiled=True),
        lax.all_gather(w_up, ("ctx", "fsdp"), axis=0, tiled=True),
        lax.all_gather(w_down, ("ctx", "fsdp"), axis=0, tiled=True),
    )
    grad_act = dot_back(grad_mlp, wd_back)
    grad_gate = (grad_act * up_pre * silu_slope).astype(jnp.bfloat16)
    grad_up = (grad_act * silu_gate).astype(jnp.bfloat16)
    grad_norm2 = dot_back(grad_gate, wg_back) + dot_back(grad_up, wu_back)
    left_cols = normed2
    gate_up_shard = lax.psum_scatter(
        jnp.concatenate([dot_outer(left_cols, grad_gate), dot_outer(left_cols, grad_up)], axis=1),
        ("ctx", "fsdp"),
        scatter_dimension=0,
        tiled=True,
    )
    wg_shard = gate_up_shard[:, :FF]
    wu_shard = gate_up_shard[:, FF:]
    left_cols = activ
    wd_shard = lax.psum_scatter(
        dot_outer(left_cols, grad_mlp), ("ctx", "fsdp"), scatter_dimension=0, tiled=True
    )
    grad_g2 = jnp.sum(grad_norm2 * unit_two, axis=0)
    grad_hidden = grad_out + norm_back(grad_norm2, unit_two, inv_two, gain2_f)
    grad_attn = (RESIDUAL_MULT * grad_hidden).astype(jnp.bfloat16)
    wq_back, wk_back, wv_back, wo_back = (
        lax.all_gather(w_query, ("ctx", "fsdp"), axis=0, tiled=True),
        lax.all_gather(w_key, ("ctx", "fsdp"), axis=0, tiled=True),
        lax.all_gather(w_value, ("ctx", "fsdp"), axis=0, tiled=True),
        lax.all_gather(w_output, ("ctx", "fsdp"), axis=0, tiled=True),
    )
    grad_wo = dot_outer(mixed_heads, grad_attn)
    grad_att = (
        dot_back(grad_attn, wo_back).astype(jnp.bfloat16).reshape(local_rows, KVH, group_size, HD)
    )
    row_delta = jnp.sum(grad_att.astype(jnp.float32) * attended, axis=-1)
    key_all, value_all = (
        lax.all_gather(key_rot, "ctx", axis=0, tiled=True),
        lax.all_gather(values, "ctx", axis=0, tiled=True),
    )
    key_width = math.gcd(length, 512)
    block_count = length // key_width

    def back_block(grad_query, index_block):
        block_start = index_block * key_width
        key_blk = lax.dynamic_slice_in_dim(key_all, block_start, key_width, 0).reshape(
            key_width, KVH, HD
        )
        value_blk = lax.dynamic_slice_in_dim(value_all, block_start, key_width, 0).reshape(
            key_width, KVH, HD
        )
        key_pos = block_start + jnp.arange(key_width, dtype=jnp.int32)
        key_docs = doc_index(key_pos, starts)
        skip_block = (block_start > last_pos) | (key_docs[key_width - 1] < first_doc)

        def compute(current):
            scores = (
                jnp.einsum("qkgd,tkd->qkgt", grouped, key_blk, preferred_element_type=jnp.float32)
                * SCORE_SCALE
            )
            allowed = (key_docs[None, :] == doc_ids[:, None]) & (
                key_pos[None, :] <= positions[:, None]
            )
            allowed = allowed[:, None, None, :]
            probs_blk = jnp.where(
                allowed, jnp.exp(jnp.where(allowed, scores, NEGATIVE) - log_sum[..., None]), 0.0
            )
            grad_probs = jnp.einsum(
                "qkgd,tkd->qkgt", grad_att, value_blk, preferred_element_type=jnp.float32
            )
            grad_scores = (probs_blk * (grad_probs - row_delta[..., None])).astype(jnp.bfloat16)
            new_query = (
                current
                + jnp.einsum(
                    "qkgt,tkd->qkgd", grad_scores, key_blk, preferred_element_type=jnp.float32
                )
                * SCORE_SCALE
            )
            grad_key = (
                jnp.einsum(
                    "qkgt,qkgd->tkd", grad_scores, grouped, preferred_element_type=jnp.float32
                )
                * SCORE_SCALE
            )
            grad_value = jnp.einsum(
                "qkgt,qkgd->tkd",
                probs_blk.astype(jnp.bfloat16),
                grad_att,
                preferred_element_type=jnp.float32,
            )
            return (
                new_query,
                (grad_key.reshape(key_width, KVH * HD), grad_value.reshape(key_width, KVH * HD)),
            )

        def nothing(current):
            zero_rows = jnp.zeros((key_width, KVH * HD), jnp.float32)
            return (current, (zero_rows, zero_rows))

        return lax.cond(skip_block, nothing, compute, grad_query)

    grad_query, key_terms = lax.scan(
        back_block,
        jnp.zeros((local_rows, KVH, group_size, HD), jnp.float32),
        jnp.arange(block_count),
    )
    key_term_all = key_terms[0].reshape(length, KVH * HD)
    value_term_all = key_terms[1].reshape(length, KVH * HD)
    grad_keys, grad_values = (
        lax.psum_scatter(
            key_term_all.astype(jnp.bfloat16), "ctx", scatter_dimension=0, tiled=True
        ).astype(jnp.float32),
        lax.psum_scatter(
            value_term_all.astype(jnp.bfloat16), "ctx", scatter_dimension=0, tiled=True
        ).astype(jnp.float32),
    )
    grad_q_pre = rotate(grad_query.reshape(local_rows, H * HD), cos_table, -sin_table, H).astype(
        jnp.bfloat16
    )
    grad_k_pre = rotate(grad_keys, cos_table, -sin_table, KVH).astype(jnp.bfloat16)
    grad_v_pre = grad_values.astype(jnp.bfloat16)
    grad_norm1 = (
        dot_back(grad_q_pre, wq_back)
        + dot_back(grad_k_pre, wk_back)
        + dot_back(grad_v_pre, wv_back)
    )
    grad_wq = dot_outer(normed1, grad_q_pre)
    grad_wk = dot_outer(normed1, grad_k_pre)
    grad_wv = dot_outer(normed1, grad_v_pre)
    grad_g1 = jnp.sum(grad_norm1 * unit_one, axis=0)
    grad_inputs = grad_hidden + norm_back(grad_norm1, unit_one, inv_one, gain1_f)
    g1_shard, g2_shard, wq_shard, wk_shard, wv_shard, wo_shard = (
        lax.psum_scatter(grad_g1, ("ctx", "fsdp"), scatter_dimension=0, tiled=True),
        lax.psum_scatter(grad_g2, ("ctx", "fsdp"), scatter_dimension=0, tiled=True),
        lax.psum_scatter(grad_wq, ("ctx", "fsdp"), scatter_dimension=0, tiled=True),
        lax.psum_scatter(grad_wk, ("ctx", "fsdp"), scatter_dimension=0, tiled=True),
        lax.psum_scatter(grad_wv, ("ctx", "fsdp"), scatter_dimension=0, tiled=True),
        lax.psum_scatter(grad_wo, ("ctx", "fsdp"), scatter_dimension=0, tiled=True),
    )
    return (
        output,
        grad_inputs[None],
        g1_shard,
        wq_shard,
        wk_shard,
        wv_shard,
        wo_shard,
        g2_shard,
        wg_shard,
        wu_shard,
        wd_shard,
    )


def rows_of(blocks):
    return blocks.reshape((-1,) + blocks.shape[2:])


def in_vmem(count):
    return [pl.BlockSpec(memory_space=pltpu.VMEM)] * count


def greet_line(barrier, ctx_at, line_at, line_size):
    other = ctx_at + 1 - 2 * (ctx_at % PAIR)
    pl.semaphore_signal(barrier, inc=1, device_id={"ctx": other}, device_id_type=MESH)

    @pl.when(line_at > 0)
    def _():
        pl.semaphore_signal(barrier, inc=1, device_id={"ctx": ctx_at - PAIR}, device_id_type=MESH)

    @pl.when(line_at < line_size - 1)
    def _():
        pl.semaphore_signal(barrier, inc=1, device_id={"ctx": ctx_at + PAIR}, device_id_type=MESH)

    last = line_size - 1
    neighbours = 1 + (line_at + last - 1) // last + (2 * last - 1 - line_at) // last
    pl.semaphore_wait(barrier, neighbours)


def greet_all(barrier, me, count, fsdp_size):
    def greet(k, unused):
        target = (me + k) % count
        pl.semaphore_signal(
            barrier, inc=1, device_id=(target // fsdp_size, target % fsdp_size), device_id_type=MESH
        )
        return unused

    lax.fori_loop(1, count, greet, 0)
    pl.semaphore_wait(barrier, count - 1)


def gather_phase(line_size, across_first, x_ref, out_ref, send_sem, recv_sem, own_sem):
    me = lax.axis_index("ctx")
    line_at, pair_at = me // PAIR, me % PAIR
    other = me + 1 - 2 * pair_at
    rows, width = x_ref.shape
    step = rows // CHUNKS
    split = width - across_first
    columns = (slice(0, split), slice(split, width))
    sides = (0, 1) if across_first else (0,)

    def piece(block, part, side):
        start = pl.multiple_of(block * rows + part * step, step)
        return out_ref.at[pl.ds(start, step), columns[side]]

    def copy(block, part, side, way, own=False):
        slot = (block * CHUNKS + part) * 2 + side
        return pltpu.make_async_remote_copy(
            src_ref=x_ref.at[pl.ds(part * step, step), columns[side]] if own else piece(block, part, side),
            dst_ref=piece(block, part, side),
            send_sem=send_sem.at[way, slot],
            recv_sem=recv_sem.at[slot],
            device_id={"ctx": (other, me + PAIR, me - PAIR)[way]},
            device_id_type=MESH,
        )

    up, down = line_at < line_size - 1, line_at > 0

    def own_part(part, act):
        for side in reversed(sides):
            pl.when(up)(lambda: act(copy(me, part, side, 1, True)))
            pl.when(down)(lambda: act(copy(me, part, side, 2, True)))
            act(copy(me, part, side, 0, True))

    def others(act, arrive, between):
        if across_first:
            for part in range(CHUNKS):
                arrive(other, part, 1)
                pl.when(up)(lambda: act(copy(other, part, 1, 1)))
                pl.when(down)(lambda: act(copy(other, part, 1, 2)))
        for distance in range(1, line_size):
            between(distance)
            for part in range(CHUNKS):

                def relay(sign, way, more):
                    block = me + sign * PAIR * distance
                    arrive(block, part, 0)
                    pl.when(more)(lambda: act(copy(block, part, 0, way)))
                    act(copy(block, part, 0, 0))
                    if across_first:
                        for passing in (block, other + sign * PAIR * distance):
                            arrive(passing, part, 1)
                            pl.when(more)(lambda: act(copy(passing, part, 1, way)))

                pl.when(line_at >= distance)(lambda: relay(-1, 1, up))
                pl.when(line_at + distance < line_size)(lambda: relay(1, 2, down))

    def start_own(part):
        own_part(part, lambda c: c.start())

    def finish(between=lambda distance: None):
        keep = pltpu.make_async_copy(
            x_ref, out_ref.at[pl.ds(pl.multiple_of(me * rows, rows), rows), :], own_sem
        )
        keep.start()
        others(
            lambda c: c.start(),
            lambda block, part, side: copy(block, part, side, 0).wait_recv(),
            between,
        )
        for place in range(line_size):
            for part in range(CHUNKS):
                copy(place * PAIR + 1 - pair_at, part, 0, 0).wait_recv()
        for part in range(CHUNKS):
            own_part(part, lambda c: c.wait_send())
        others(lambda c: c.wait_send(), lambda block, part, side: None, lambda distance: None)
        keep.wait()

    return start_own, finish


def gather_scratch(ctx_size):
    return [
        pltpu.SemaphoreType.DMA((3, ctx_size * CHUNKS * 2)),
        pltpu.SemaphoreType.DMA((ctx_size * CHUNKS * 2,)),
        pltpu.SemaphoreType.DMA,
    ]


def scatter_phase(
    line_size, along_first, x_ref, sum_ref, near, below, above, pass_far, below_far, above_far, across,
    near_send, near_sem, line_send, line_sem, far_send, far_sem, across_send, across_sem, emit,
    midway=lambda: None,
):
    me = lax.axis_index("ctx")
    line_at, pair_at = me // PAIR, me % PAIR
    other = me + 1 - 2 * pair_at
    rows, width = sum_ref.shape
    step = rows // CHUNKS
    split = width - along_first
    head, tail = slice(0, split), slice(split, width)
    last = line_size - 1
    up, down = line_at < last, line_at > 0
    low = line_at // (line_size // 2)
    order = [k + (last - 2 * k) * (1 - low) for k in range(line_size // 2)]
    order += [line_at + 1 - 2 * (line_at % 2), line_at]
    wide = lambda ref: ref.astype(jnp.float32)

    def near_copy(place, part):
        start = (place * PAIR + 1 - pair_at) * rows + part * step
        return pltpu.make_async_remote_copy(
            src_ref=x_ref.at[pl.ds(pl.multiple_of(start, step), step), head],
            dst_ref=near.at[place, pl.ds(part * step, step), :],
            send_sem=near_send.at[place, part],
            recv_sem=near_sem.at[place, part],
            device_id={"ctx": other},
            device_id_type=MESH,
        )

    def line_copy(place, part, upward):
        part_rows = pl.ds(part * step, step)
        return pltpu.make_async_remote_copy(
            src_ref=near.at[place, part_rows, :],
            dst_ref=(below if upward else above).at[place, part_rows, :],
            send_sem=line_send.at[place, part],
            recv_sem=line_sem.at[0 if upward else 1, place, part],
            device_id={"ctx": me + PAIR if upward else me - PAIR},
            device_id_type=MESH,
        )

    def far_copy(block, part, upward):
        part_rows = pl.ds(part * step, step)
        return pltpu.make_async_remote_copy(
            src_ref=pass_far.at[block, part_rows, :],
            dst_ref=(below_far if upward else above_far).at[block, part_rows, :],
            send_sem=far_send.at[block, part],
            recv_sem=far_sem.at[0 if upward else 1, block, part],
            device_id={"ctx": me + PAIR if upward else me - PAIR},
            device_id_type=MESH,
        )

    def across_copy(part):
        part_rows = pl.ds(part * step, step)
        return pltpu.make_async_remote_copy(
            src_ref=pass_far.at[other, part_rows, :],
            dst_ref=across.at[part_rows, :],
            send_sem=across_send.at[part],
            recv_sem=across_sem.at[part],
            device_id={"ctx": other},
            device_id_type=MESH,
        )

    def mine(block, part, columns):
        start = block * rows + part * step
        return wide(x_ref[pl.ds(pl.multiple_of(start, step), step), columns])

    for place in order:
        for part in range(CHUNKS):
            near_copy(place, part).start()

    def send(place, part, upward):
        part_rows = pl.ds(part * step, step)
        waits = down if upward else up
        if along_first:
            arrived = below_far if upward else above_far
            for pair in range(PAIR):
                block = place * PAIR + pair
                pass_far[block, part_rows, :] = mine(block, part, tail).astype(pass_far.dtype)

                @pl.when(waits)
                def _():
                    far_copy(block, part, upward).wait_recv()
                    pass_far[block, part_rows, :] = (
                        mine(block, part, tail) + wide(arrived[block, part_rows, :])
                    ).astype(pass_far.dtype)

                far_copy(block, part, upward).start()
        near_copy(place, part).wait_recv()
        total = mine(place * PAIR + pair_at, part, head) + wide(near[place, part_rows, :])
        arrived_near = below if upward else above

        @pl.when(waits)
        def _():
            line_copy(place, part, upward).wait_recv()
            near[place, part_rows, :] = (total + wide(arrived_near[place, part_rows, :])).astype(near.dtype)

        @pl.when(jnp.logical_not(waits))
        def _():
            near[place, part_rows, :] = total.astype(near.dtype)

        line_copy(place, part, upward).start()

    for place in order[:-1]:
        for part in range(CHUNKS):
            pl.when(place > line_at)(lambda: send(place, part, True))
            pl.when(place < line_at)(lambda: send(place, part, False))

    def add_far(block, part, total_ref, total_rows, total_columns):
        part_rows = pl.ds(part * step, step)
        for there, arrived, upward in ((down, below_far, True), (up, above_far, False)):

            @pl.when(there)
            def _():
                far_copy(block, part, upward).wait_recv()
                total_ref[total_rows, total_columns] += wide(arrived[block, part_rows, :])

    if along_first:
        for part in range(CHUNKS):
            part_rows = pl.ds(part * step, step)
            sum_ref[part_rows, tail] = mine(other, part, tail)
            add_far(other, part, sum_ref, part_rows, tail)
            pass_far[pl.ds(other, 1), part_rows, :] = sum_ref[part_rows, tail].astype(pass_far.dtype)[None]
            across_copy(part).start()
    midway()
    for part in range(CHUNKS):
        part_rows = pl.ds(part * step, step)
        if along_first:
            sum_ref[part_rows, tail] = mine(me, part, tail)
            add_far(me, part, sum_ref, part_rows, tail)
        near_copy(line_at, part).wait_recv()
        sum_ref[part_rows, head] = mine(me, part, head) + wide(near[line_at, part_rows, :])
        for there, arrived, upward in ((down, below, True), (up, above, False)):

            @pl.when(there)
            def _():
                line_copy(line_at, part, upward).wait_recv()
                sum_ref[part_rows, head] += wide(arrived[line_at, part_rows, :])

        if along_first:
            across_copy(part).wait_recv()
            sum_ref[part_rows, tail] += wide(across[part_rows, :])
        emit(part, slice(part * step, (part + 1) * step))

    def finish():
        for place in order:
            for part in range(CHUNKS):
                near_copy(place, part).wait_send()
        for place in order[:-1]:
            for part in range(CHUNKS):
                line_copy(place, part, True).wait_send()
                if along_first:
                    for pair in range(PAIR):
                        far_copy(place * PAIR + pair, part, True).wait_send()
        if along_first:
            for part in range(CHUNKS):
                across_copy(part).wait_send()

    return finish


def scatter_scratch(ctx_size, rows, width, along_first):
    line_size = ctx_size // PAIR
    dma = pltpu.SemaphoreType.DMA
    held = pltpu.VMEM((line_size, rows, width - along_first), jnp.bfloat16)
    far_blocks, far_width = (ctx_size, along_first) if along_first else (1, 128)
    far = pltpu.VMEM((far_blocks, rows, far_width), jnp.bfloat16)
    return [
        held,
        held,
        held,
        far,
        far,
        far,
        pltpu.VMEM((rows, far_width), jnp.bfloat16),
        dma((line_size, CHUNKS)),
        dma((line_size, CHUNKS)),
        dma((line_size, CHUNKS)),
        dma((2, line_size, CHUNKS)),
        dma((ctx_size, CHUNKS)),
        dma((2, ctx_size, CHUNKS)),
        dma((CHUNKS,)),
        dma((CHUNKS,)),
    ]


def swap_lanes(values, outer, inner):
    tile = 128
    half = tile // 2
    low = lax.broadcasted_iota(jnp.int32, (values.shape[0], tile), 1) < half
    placed = [None] * (outer * inner // 2)
    for first in range(0, outer, 2):
        for second in range(0, inner, 2):
            at = (first * inner + second) // 2
            one = values[:, at * tile : (at + 1) * tile]
            at += inner // 2
            two = values[:, at * tile : (at + 1) * tile]
            at = (second * outer + first) // 2
            placed[at] = jnp.where(low, one, pltpu.roll(two, half, 1))
            placed[at + outer // 2] = jnp.where(low, pltpu.roll(one, half, 1), two)
    return jnp.concatenate(placed, axis=1)


def start_kernel(
    ctx_size, fsdp_size, tokens_ref, tile_ref, parts_ref, gate_ref, up_ref, out_ref, gains_ref, weight_ref,
    wide_ref, tiles, normed, tile_send, tile_recv, far_send, far_recv, near_send, near_recv, wide_send,
    wide_recv, kept, wide_kept, *sems
):
    me_ctx, me_fsdp = lax.axis_index("ctx"), lax.axis_index("fsdp")
    count = ctx_size * fsdp_size
    me = me_ctx * fsdp_size + me_fsdp
    greet_all(pltpu.get_barrier_semaphore(), me, count, fsdp_size)

    def tile_copy(k, source):
        target = (me + k) % count
        return pltpu.make_async_remote_copy(
            src_ref=tile_ref,
            dst_ref=tiles.at[source],
            send_sem=tile_send.at[k],
            recv_sem=tile_recv.at[k],
            device_id=(target // fsdp_size, target % fsdp_size),
            device_id_type=MESH,
        )

    def start_tile(k, unused):
        tile_copy(k, me).start()
        return unused

    def finish_tile(k, unused):
        tile_copy(k, (me + count - k) % count).wait_recv()
        return unused

    lax.fori_loop(1, count, start_tile, 0)
    tiles[pl.ds(me, 1)] = tile_ref[...][None]

    def far_copy(k, source):
        target = (me_ctx + k) % ctx_size
        return pltpu.make_async_remote_copy(
            src_ref=parts_ref.at[target],
            dst_ref=weight_ref.at[source * fsdp_size + me_fsdp],
            send_sem=far_send.at[k],
            recv_sem=far_recv.at[k],
            device_id={"ctx": target},
            device_id_type=MESH,
        )

    def near_copy(k, j, fsdp_source):
        block = (me_ctx + ctx_size - k) % ctx_size * fsdp_size + fsdp_source
        return pltpu.make_async_remote_copy(
            src_ref=parts_ref.at[me_ctx] if k == 0 else weight_ref.at[block],
            dst_ref=weight_ref.at[block],
            send_sem=near_send.at[k, j],
            recv_sem=near_recv.at[k, j],
            device_id={"fsdp": (me_fsdp + j) % fsdp_size},
            device_id_type=MESH,
        )

    wide = gate_ref.shape[1] // ctx_size

    def wide_part(which, target, source):
        cols = pl.ds(pl.multiple_of(target * wide, wide), wide)
        return (
            (gate_ref, up_ref)[which].at[:, cols],
            wide_ref.at[source, :, which * wide : (which + 1) * wide],
        )

    def wide_copy(which, k, source):
        target = (me_ctx + k) % ctx_size
        src, dst = wide_part(which, target, source)
        return pltpu.make_async_remote_copy(
            src_ref=src,
            dst_ref=dst,
            send_sem=wide_send.at[which, k],
            recv_sem=wide_recv.at[which, k],
            device_id={"ctx": target},
            device_id_type=MESH,
        )

    def wide_keep(which):
        return pltpu.make_async_copy(*wide_part(which, me_ctx, me_ctx), wide_kept.at[which])

    def wide_start(distance):
        for k in range(2 * distance - 1, min(2 * distance + 1, ctx_size)):
            for which in range(2):
                wide_copy(which, k, me_ctx).start()
        if distance == ctx_size // PAIR - 1:
            for which in range(2):
                wide_copy(which, ctx_size - 1, me_ctx).start()

    for k in range(1, ctx_size):
        far_copy(k, me_ctx).start()
    for j in range(1, fsdp_size):
        near_copy(0, j, me_fsdp).start()
    for which in range(2):
        wide_keep(which).start()
    keep = pltpu.make_async_copy(parts_ref.at[me_ctx], weight_ref.at[me], kept)
    keep.start()

    rows, model = tokens_ref.shape
    lax.fori_loop(1, count, finish_tile, 0)
    held = model // count
    for pair in range(count // 2):
        cols = slice(pair * 2 * held, (pair + 1) * 2 * held)
        gains_ref[:, cols] = tiles[2 * pair] + tiles[2 * pair + 1]
    start_own, finish_gather = gather_phase(ctx_size // PAIR, 0, normed, out_ref, *sems)
    step = rows // CHUNKS
    for part in range(CHUNKS):
        part_rows = slice(part * step, (part + 1) * step)
        values = tokens_ref[part_rows, :].astype(jnp.float32)
        scale = lax.rsqrt(jnp.mean(values * values, axis=-1, keepdims=True) + EPSILON)
        normed[part_rows, :] = (values * scale * gains_ref[0:1, :]).astype(normed.dtype)
        start_own(part)
    for k in range(1, ctx_size):
        far_copy(k, (me_ctx + ctx_size - k) % ctx_size).wait_recv()
        for j in range(1, fsdp_size):
            near_copy(k, j, me_fsdp).start()
    finish_gather(wide_start)
    for which in range(2):
        for k in range(1, ctx_size):
            wide_copy(which, k, (me_ctx + ctx_size - k) % ctx_size).wait_recv()
        for k in range(1, ctx_size):
            wide_copy(which, k, me_ctx).wait_send()
        wide_keep(which).wait()
    for k in range(ctx_size):
        for j in range(1, fsdp_size):
            near_copy(k, j, (me_fsdp + fsdp_size - j) % fsdp_size).wait_recv()
    for k in range(ctx_size):
        for j in range(1, fsdp_size):
            near_copy(k, j, me_fsdp).wait_send()
    for k in range(1, ctx_size):
        far_copy(k, me_ctx).wait_send()

    def sent_tile(k, unused):
        tile_copy(k, me).wait_send()
        return unused

    lax.fori_loop(1, count, sent_tile, 0)
    keep.wait()


def start_layer(tokens, tile, parts, w_gate, w_up):
    ctx_size, fsdp_size = lax.axis_size("ctx"), lax.axis_size("fsdp")
    count = ctx_size * fsdp_size
    rows, model = tokens.shape
    dma = pltpu.SemaphoreType.DMA
    held = w_gate.shape[0]
    normed1, gains, weight, wide = pl.pallas_call(
        functools.partial(start_kernel, ctx_size, fsdp_size),
        out_shape=(
            jax.ShapeDtypeStruct((ctx_size * rows, model), jnp.bfloat16),
            jax.ShapeDtypeStruct((8, model), jnp.float32),
            jax.ShapeDtypeStruct((count,) + parts.shape[1:], parts.dtype),
            jax.ShapeDtypeStruct((ctx_size, held, 2 * w_gate.shape[1] // ctx_size), w_gate.dtype),
        ),
        in_specs=in_vmem(5),
        out_specs=(ANYWHERE, in_vmem(1)[0], ANYWHERE, ANYWHERE),
        scratch_shapes=[
            pltpu.VMEM((count, 8, 128), jnp.float32),
            pltpu.VMEM((rows, model), jnp.bfloat16),
            dma((count,)),
            dma((count,)),
            dma((ctx_size,)),
            dma((ctx_size,)),
            dma((ctx_size, fsdp_size)),
            dma((ctx_size, fsdp_size)),
            dma((2, ctx_size)),
            dma((2, ctx_size)),
            dma,
            dma((2,)),
        ]
        + gather_scratch(ctx_size),
        compiler_params=pltpu.CompilerParams(
            collective_id=0, has_side_effects=True, vmem_limit_bytes=32 * 2**20
        ),
        cost_estimate=LINK_COST,
        name="start_layer",
    )(tokens, tile, parts, w_gate, w_up)
    return normed1, gains, rows_of(weight), rows_of(wide)


def mlp_forward_kernel(
    ctx_size, fsdp_size, x_ref, tokens_ref, gains_ref, hidden_ref, out_ref, sums, normed, *sems
):
    line_size = ctx_size // PAIR
    me = lax.axis_index("ctx")
    greet_line(pltpu.get_barrier_semaphore(), me, me // PAIR, line_size)
    start_own, finish_gather = gather_phase(line_size, EVEN, normed, out_ref, *sems[15:])

    def emit(part, rows):
        hidden = tokens_ref[rows, :].astype(jnp.float32) + RESIDUAL_MULT * sums[rows, :]
        hidden_ref[rows, :] = hidden
        scale = lax.rsqrt(jnp.mean(hidden * hidden, axis=-1, keepdims=True) + EPSILON)
        scaled = hidden * scale * gains_ref[1:2, :]
        normed[rows, :] = swap_lanes(scaled, ctx_size, fsdp_size).astype(normed.dtype)
        start_own(part)

    finish_scatter = scatter_phase(line_size, EVEN, x_ref, sums, *sems[:15], emit)
    finish_gather()
    finish_scatter()


def mlp_backward_kernel(
    ctx_size, fsdp_size, x_ref, hidden_ref, grad_ref, gains_ref, grad_hidden_ref, grad_gain_ref, out_ref,
    sums, normed, *sems
):
    line_size = ctx_size // PAIR
    me = lax.axis_index("ctx")
    greet_line(pltpu.get_barrier_semaphore(), me, me // PAIR, line_size)
    start_own, finish_gather = gather_phase(line_size, EVEN, normed, out_ref, *sems[15:])

    def emit(part, rows):
        grad_norm = swap_lanes(sums[rows, :], fsdp_size, ctx_size)
        hidden = hidden_ref[rows, :]
        scale = lax.rsqrt(jnp.mean(hidden * hidden, axis=-1, keepdims=True) + EPSILON)
        unit = hidden * scale
        grad_gain_ref[part : part + 1, :] = jnp.sum(grad_norm * unit, axis=0, keepdims=True)
        grad_hidden = grad_ref[rows, :].astype(jnp.float32) + norm_back(
            grad_norm, unit, scale, gains_ref[1:2, :]
        )
        grad_hidden_ref[rows, :] = grad_hidden
        normed[rows, :] = (RESIDUAL_MULT * grad_hidden).astype(normed.dtype)
        start_own(part)

    finish_scatter = scatter_phase(line_size, EVEN, x_ref, sums, *sems[:15], emit)
    finish_gather()
    finish_scatter()


def scatter_gather(kernel, collective_id, extra_shapes, partial, *others):
    ctx_size, fsdp_size = lax.axis_size("ctx"), lax.axis_size("fsdp")
    rows, model = partial.shape[0] // ctx_size, partial.shape[1]
    return pl.pallas_call(
        functools.partial(kernel, ctx_size, fsdp_size),
        out_shape=extra_shapes + (jax.ShapeDtypeStruct(partial.shape, jnp.bfloat16),),
        in_specs=in_vmem(1 + len(others)),
        out_specs=tuple(in_vmem(len(extra_shapes))) + (ANYWHERE,),
        scratch_shapes=[pltpu.VMEM((rows, model), jnp.float32), pltpu.VMEM((rows, model), jnp.bfloat16)]
        + scatter_scratch(ctx_size, rows, model, EVEN)
        + gather_scratch(ctx_size),
        compiler_params=pltpu.CompilerParams(
            collective_id=collective_id, has_side_effects=True, vmem_limit_bytes=40 * 2**20
        ),
        cost_estimate=LINK_COST,
    )(partial, *others)


def mlp_forward(partial, tokens, gains):
    hidden = jax.ShapeDtypeStruct(tokens.shape, jnp.float32)
    return scatter_gather(mlp_forward_kernel, 1, (hidden,), partial, tokens, gains)


def mlp_backward(partial, hidden, grad_out, gains):
    like = jax.ShapeDtypeStruct(hidden.shape, jnp.float32)
    gain = jax.ShapeDtypeStruct((CHUNKS, hidden.shape[1]), jnp.float32)
    return scatter_gather(mlp_backward_kernel, 2, (like, gain), partial, hidden, grad_out, gains)


def finish_kernel(
    ctx_size, fsdp_size, x_ref, tokens_ref, grad_ref, gains_ref, gain2_ref, wo_ref, qkv_ref,
    grad_tokens_ref, gain_out_ref, wo_out_ref, qkv_out_ref,
    sums, gain1, tiles, arrived, wo_in, qkv_in, qkv_sum, tile_send, tile_recv, near_send, near_recv,
    far_send, far_recv, *sems
):
    line_size = ctx_size // PAIR
    me_ctx, me_fsdp = lax.axis_index("ctx"), lax.axis_index("fsdp")
    count = ctx_size * fsdp_size
    me = me_ctx * fsdp_size + me_fsdp
    greet_all(pltpu.get_barrier_semaphore(), me, count, fsdp_size)

    def near_copy(which, j):
        target = (me_fsdp + j) % fsdp_size
        terms, landing = ((wo_ref, wo_in), (qkv_ref, qkv_in))[which]
        return pltpu.make_async_remote_copy(
            src_ref=terms.at[target],
            dst_ref=landing.at[j],
            send_sem=near_send.at[which, j],
            recv_sem=near_recv.at[which, j],
            device_id={"fsdp": target},
            device_id_type=MESH,
        )

    def far_copy(k, source):
        target = (me_ctx + k) % ctx_size
        return pltpu.make_async_remote_copy(
            src_ref=qkv_sum.at[target],
            dst_ref=qkv_out_ref.at[source],
            send_sem=far_send.at[k],
            recv_sem=far_recv.at[k],
            device_id={"ctx": target},
            device_id_type=MESH,
        )

    def tile_copy(k, source):
        target = (me + k) % count
        return pltpu.make_async_remote_copy(
            src_ref=tiles.at[target // 2],
            dst_ref=arrived.at[source],
            send_sem=tile_send.at[k],
            recv_sem=tile_recv.at[k],
            device_id=(target // fsdp_size, target % fsdp_size),
            device_id_type=MESH,
        )

    def midway():
        for which, own, landing in ((1, qkv_ref, qkv_in), (0, wo_ref, wo_in)):
            for j in range(1, fsdp_size):
                near_copy(which, j).wait_recv()
            total = own[pl.ds(me_fsdp, 1)][0].astype(jnp.float32)
            for j in range(1, fsdp_size):
                total += landing[j].astype(jnp.float32)
            if which:
                qkv_sum[...] = total.astype(qkv_sum.dtype)
                for k in range(1, ctx_size):
                    far_copy(k, me_ctx).start()
                qkv_out_ref[pl.ds(me_ctx, 1)] = qkv_sum[pl.ds(me_ctx, 1)]
            else:
                wo_out_ref[...] = total

    def emit(part, rows):
        grad_norm = sums[rows, :]
        values = tokens_ref[rows, :].astype(jnp.float32)
        scale = lax.rsqrt(jnp.mean(values * values, axis=-1, keepdims=True) + EPSILON)
        unit = values * scale
        gain1[part : part + 1, :] = jnp.sum(grad_norm * unit, axis=0, keepdims=True)
        grad_tokens_ref[rows, :] = grad_ref[rows, :] + norm_back(
            grad_norm, unit, scale, gains_ref[0:1, :]
        )

    for which in (1, 0):
        for j in range(1, fsdp_size):
            near_copy(which, j).start()
    finish_scatter = scatter_phase(line_size, EVEN_LAST, x_ref, sums, *sems, emit, midway)
    row = lax.broadcasted_iota(jnp.int32, (8, 128), 0)
    for pair in range(count // 2):
        cols = slice(pair * 128, (pair + 1) * 128)
        first = jnp.sum(gain1[:, cols], axis=0, keepdims=True)
        second = jnp.sum(gain2_ref[:, cols], axis=0, keepdims=True)
        tiles[pair] = jnp.where(row == 0, first, jnp.where(row == 1, second, 0.0))

    def start_tile(k, unused):
        tile_copy(k, me).start()
        return unused

    def finish_tile(k, unused):
        tile_copy(k, (me + count - k) % count).wait_recv()
        return unused

    def sent_tile(k, unused):
        tile_copy(k, me).wait_send()
        return unused

    lax.fori_loop(1, count, start_tile, 0)
    arrived[pl.ds(me, 1)] = tiles[pl.ds(me // 2, 1)]
    for k in range(1, ctx_size):
        far_copy(k, (me_ctx + ctx_size - k) % ctx_size).wait_recv()
    lax.fori_loop(1, count, finish_tile, 0)
    gain_out_ref[...] = jnp.sum(arrived[...], axis=0)
    finish_scatter()
    for which in range(2):
        for j in range(1, fsdp_size):
            near_copy(which, j).wait_send()
    for k in range(1, ctx_size):
        far_copy(k, me_ctx).wait_send()
    lax.fori_loop(1, count, sent_tile, 0)


def finish_layer(partial, tokens, grad_hidden, gains, grad_gain2, wo_terms, qkv_terms):
    ctx_size, fsdp_size = lax.axis_size("ctx"), lax.axis_size("fsdp")
    count = ctx_size * fsdp_size
    rows, model = tokens.shape
    dma = pltpu.SemaphoreType.DMA
    f32, bf16 = jnp.float32, jnp.bfloat16
    held, width = qkv_terms.shape[2:]
    return pl.pallas_call(
        functools.partial(finish_kernel, ctx_size, fsdp_size),
        out_shape=(
            jax.ShapeDtypeStruct((rows, model), f32),
            jax.ShapeDtypeStruct((8, 128), f32),
            jax.ShapeDtypeStruct(wo_terms.shape[1:], f32),
            jax.ShapeDtypeStruct((ctx_size, held, width), bf16),
        ),
        in_specs=in_vmem(7),
        out_specs=tuple(in_vmem(4)),
        scratch_shapes=[
            pltpu.VMEM((rows, model), f32),
            pltpu.VMEM((CHUNKS, model), f32),
            pltpu.VMEM((count // 2, 8, 128), f32),
            pltpu.VMEM((count, 8, 128), f32),
            pltpu.VMEM(wo_terms.shape, bf16),
            pltpu.VMEM(qkv_terms.shape, bf16),
            pltpu.VMEM((ctx_size, held, width), bf16),
            dma((count,)),
            dma((count,)),
            dma((2, fsdp_size)),
            dma((2, fsdp_size)),
            dma((ctx_size,)),
            dma((ctx_size,)),
        ]
        + scatter_scratch(ctx_size, rows, model, EVEN_LAST),
        compiler_params=pltpu.CompilerParams(
            collective_id=3, has_side_effects=True, vmem_limit_bytes=40 * 2**20
        ),
        cost_estimate=LINK_COST,
        name="finish_layer",
    )(partial, tokens, grad_hidden, gains, grad_gain2, wo_terms, qkv_terms)


def swap_ctx(blocks):
    return lax.all_to_all(blocks, "ctx", split_axis=0, concat_axis=0, tiled=True)


def by_fsdp(grad, ctx_size, fsdp_size):
    parts = grad.reshape(ctx_size, fsdp_size, -1, grad.shape[-1]).transpose(1, 0, 2, 3)
    return rows_of(rows_of(parts))


def return_columns(terms, ctx_size):
    return swap_ctx(terms.reshape(ctx_size, -1, terms.shape[-1]))


def half_turn(values, sign_table):
    lane = lax.broadcasted_iota(jnp.int32, values.shape, 1)
    width = values.shape[1]
    quarter = HD // 2
    ahead = pltpu.roll(values, width - quarter, 1)
    behind = pltpu.roll(values, quarter, 1)
    return jnp.where(lane % HD < quarter, ahead, behind) * sign_table


def turn(values, cos_table, sign_table):
    copies = values.shape[1] // cos_table.shape[1]
    if copies > 1:
        cos_table = jnp.concatenate([cos_table] * copies, axis=1)
        sign_table = jnp.concatenate([sign_table] * copies, axis=1)
    return values * cos_table + half_turn(values, sign_table)


def attention_forward_kernel(
    block_rows, qkv_ref, cos_ref, sin_ref, doc_col_ref, doc_row_ref, q_ref, kv_ref, out_ref, lse_ref
):
    length = qkv_ref.shape[0]
    group = H // KVH
    width = group * HD
    q_ref[...] = turn(qkv_ref[:, :width], cos_ref[...], sin_ref[...]).astype(jnp.bfloat16)
    pair = qkv_ref[:, width:]
    lane = lax.broadcasted_iota(jnp.int32, pair.shape, 1)
    turned = turn(pair, cos_ref[...], sin_ref[...])
    kv_ref[...] = jnp.where(lane < HD, turned, pair).astype(jnp.bfloat16)
    for block in range(length // block_rows):
        rows = slice(block * block_rows, (block + 1) * block_rows)
        reach = (block + 1) * block_rows
        keys = kv_ref[:reach, :HD]
        values = kv_ref[:reach, HD:]
        query_at = block * block_rows + lax.broadcasted_iota(jnp.int32, (block_rows, reach), 0)
        key_at = lax.broadcasted_iota(jnp.int32, (block_rows, reach), 1)
        allowed = (doc_col_ref[rows, :] == doc_row_ref[:, :reach]) & (key_at <= query_at)
        for head in range(group):
            cols = slice(head * HD, (head + 1) * HD)
            scores = dot_back(q_ref[rows, cols], keys) * SCORE_SCALE
            masked = jnp.where(allowed, scores, NEGATIVE)
            top = jnp.max(masked, axis=1, keepdims=True)
            weights = jnp.where(allowed, jnp.exp(masked - top), 0.0)
            total = jnp.sum(weights, axis=1, keepdims=True)
            mixed = dot_plain(weights.astype(jnp.bfloat16), values)
            out_ref[rows, cols] = (mixed / total).astype(jnp.bfloat16)
            lse_ref[rows, head : head + 1] = top + jnp.log(total)


def attention_backward_kernel(
    block_rows, q_ref, kv_ref, do_ref, lse_ref, cos_ref, sin_ref, doc_col_ref, doc_row_ref, grad_ref, dq_ref, dkv_ref
):
    length = q_ref.shape[0]
    group = H // KVH
    width = group * HD
    dkv_ref[...] = jnp.zeros_like(dkv_ref)
    for block in range(length // block_rows):
        rows = slice(block * block_rows, (block + 1) * block_rows)
        reach = (block + 1) * block_rows
        keys = kv_ref[:reach, :HD]
        values = kv_ref[:reach, HD:]
        query_at = block * block_rows + lax.broadcasted_iota(jnp.int32, (block_rows, reach), 0)
        key_at = lax.broadcasted_iota(jnp.int32, (block_rows, reach), 1)
        allowed = (doc_col_ref[rows, :] == doc_row_ref[:, :reach]) & (key_at <= query_at)
        for head in range(group):
            cols = slice(head * HD, (head + 1) * HD)
            query = q_ref[rows, cols]
            grad_out = do_ref[rows, cols]
            scores = dot_back(query, keys) * SCORE_SCALE
            probs = jnp.where(
                allowed,
                jnp.exp(jnp.where(allowed, scores, NEGATIVE) - lse_ref[rows, head : head + 1]),
                0.0,
            )
            grad_probs = dot_back(grad_out, values)
            delta = jnp.sum(probs * grad_probs, axis=1, keepdims=True)
            grad_scores = (probs * (grad_probs - delta)).astype(jnp.bfloat16)
            dq_ref[rows, cols] = dot_plain(grad_scores, keys) * SCORE_SCALE
            dkv_ref[:reach, :HD] += dot_outer(grad_scores, query) * SCORE_SCALE
            dkv_ref[:reach, HD:] += dot_outer(probs.astype(jnp.bfloat16), grad_out)
    grad_ref[:, :width] = turn(dq_ref[...], cos_ref[...], -sin_ref[...]).astype(jnp.bfloat16)
    pair = dkv_ref[...]
    lane = lax.broadcasted_iota(jnp.int32, pair.shape, 1)
    turned = turn(pair, cos_ref[...], -sin_ref[...])
    grad_ref[:, width:] = jnp.where(lane < HD, turned, pair).astype(jnp.bfloat16)


def attention_forward(qkv, tables, block_rows):
    length = qkv.shape[0]
    width = (H // KVH) * HD
    return pl.pallas_call(
        functools.partial(attention_forward_kernel, block_rows),
        out_shape=(
            jax.ShapeDtypeStruct((length, width), jnp.bfloat16),
            jax.ShapeDtypeStruct((length, 2 * HD), jnp.bfloat16),
            jax.ShapeDtypeStruct((length, width), jnp.bfloat16),
            jax.ShapeDtypeStruct((length, H // KVH), jnp.float32),
        ),
        in_specs=in_vmem(5),
        out_specs=tuple(in_vmem(4)),
        compiler_params=pltpu.CompilerParams(vmem_limit_bytes=48 * 2**20),
        name="attend",
    )(qkv, *tables)


def attention_backward(q, kv, grad_out, lse, tables, block_rows):
    length, width = q.shape
    return pl.pallas_call(
        functools.partial(attention_backward_kernel, block_rows),
        out_shape=jax.ShapeDtypeStruct((length, width + 2 * HD), jnp.bfloat16),
        in_specs=in_vmem(8),
        out_specs=in_vmem(1)[0],
        scratch_shapes=[
            pltpu.VMEM((length, width), jnp.float32),
            pltpu.VMEM((length, 2 * HD), jnp.float32),
        ],
        compiler_params=pltpu.CompilerParams(vmem_limit_bytes=48 * 2**20),
        name="attend_back",
    )(q, kv, grad_out, lse, *tables)


def on_device(
    tokens,
    doc_lengths,
    cotangent,
    gain_attn,
    w_query,
    w_key,
    w_value,
    w_output,
    gain_mlp,
    w_gate,
    w_up,
    w_down,
):
    local_rows, model = tokens.shape[1:]
    ctx_size = lax.axis_size("ctx")
    fsdp_size = lax.axis_size("fsdp")
    length = local_rows * ctx_size
    group_width = (H // KVH) * HD
    ff_slice = FF // ctx_size
    held_rows = w_query.shape[0]
    bf16 = jnp.bfloat16

    positions = jnp.arange(length, dtype=jnp.int32)
    seq_lengths = doc_lengths[0]
    starts = jnp.cumsum(seq_lengths) - seq_lengths
    doc_ids = doc_index(positions, starts)
    cos_half, sin_half = rope_tables(positions)
    cos_table = jnp.concatenate([cos_half] * 4, axis=1)
    sin_table = jnp.concatenate([-sin_half, sin_half] * 2, axis=1)
    tables = (cos_table, sin_table, doc_ids[:, None], doc_ids[None, :])


    def by_slice(weight):
        return weight.reshape(held_rows, ctx_size, -1)

    qkv_parts = jnp.concatenate([by_slice(w_query), by_slice(w_key), by_slice(w_value)], axis=2)
    wo_mine = lax.all_gather(w_output, "fsdp", axis=0, tiled=True)
    wd_mine = lax.all_gather(w_down, "fsdp", axis=0, tiled=True)
    gain_rows = jnp.stack([gain_attn, gain_mlp]).astype(jnp.float32)
    odd = lax.axis_index("fsdp") % 2
    gain_tile = jnp.concatenate([gain_rows * (1 - odd), gain_rows * odd], axis=1)
    gain_tile = jnp.pad(gain_tile, ((0, 8 - gain_tile.shape[0]), (0, 128 - gain_tile.shape[1])))
    normed1, gains, w_qkv, gu_mine = start_layer(
        tokens[0], gain_tile, qkv_parts.transpose(1, 0, 2), w_gate, w_up
    )
    normed1, grad_mlp = lax.optimization_barrier(
        (normed1, (RESIDUAL_MULT * cotangent[0].astype(jnp.float32)).astype(bf16))
    )
    w_gu = lax.all_gather(gu_mine, "fsdp", axis=0, tiled=True)

    block_rows = math.gcd(length, 256)
    qkv = dot_plain(normed1, w_qkv)
    grad_mlp = lax.all_gather(grad_mlp, "ctx", axis=0, tiled=True)
    q, kv, mixed_heads, log_sum = attention_forward(qkv, tables, block_rows)
    hidden, normed2 = mlp_forward(dot_plain(mixed_heads, wo_mine).astype(bf16), tokens[0], gains)

    gate_up = dot_plain(normed2, w_gu)
    gate_pre, up_pre = gate_up[:, :ff_slice], gate_up[:, ff_slice:]
    sig_gate = jax.nn.sigmoid(gate_pre)
    silu_gate = gate_pre * sig_gate
    activ = (silu_gate * up_pre).astype(bf16)
    activ, gate_up = lax.optimization_barrier((activ, gate_up))
    gate_pre, up_pre = gate_up[:, :ff_slice], gate_up[:, ff_slice:]
    sig_gate = jax.nn.sigmoid(gate_pre)
    silu_gate = gate_pre * sig_gate
    out_terms, grad_mlp = lax.optimization_barrier(
        (dot_plain(activ, wd_mine).astype(bf16), grad_mlp)
    )
    branch = lax.psum_scatter(out_terms, "ctx", scatter_dimension=0, tiled=True)
    output = (hidden + RESIDUAL_MULT * branch.astype(jnp.float32)).astype(bf16)[None]

    silu_slope = sig_gate * (1.0 + gate_pre * (1.0 - sig_gate))
    grad_act = dot_back(grad_mlp, wd_mine)
    grad_gu = jnp.concatenate(
        [(grad_act * up_pre * silu_slope).astype(bf16), (grad_act * silu_gate).astype(bf16)], axis=1
    )
    partial2, gu_terms, wd_terms = lax.optimization_barrier(
        (
            dot_back(grad_gu, w_gu).astype(bf16),
            dot_outer(normed2, grad_gu).astype(bf16),
            dot_outer(activ, grad_mlp).astype(bf16),
        )
    )
    grad_hidden, grad_g2, grad_attn = mlp_backward(partial2, hidden, cotangent[0], gains)
    gu_back = lax.psum_scatter(gu_terms, "fsdp", scatter_dimension=0, tiled=True)
    wd_back = lax.psum_scatter(wd_terms, "fsdp", scatter_dimension=0, tiled=True)

    grad_mixed = dot_back(grad_attn, wo_mine).astype(bf16)
    wo_terms = dot_outer(mixed_heads, grad_attn).astype(bf16)
    grad_qkv = attention_backward(q, kv, grad_mixed, log_sum, tables, block_rows)
    grad_qkv, gu_back = lax.optimization_barrier((grad_qkv, gu_back))
    gu_back = return_columns(gu_back, ctx_size)
    partial1 = dot_back(grad_qkv, w_qkv).astype(bf16)
    qkv_terms = by_fsdp(dot_outer(normed1, grad_qkv).astype(bf16), ctx_size, fsdp_size)
    grad_inputs, gain_back, wo_back, qkv_back = finish_layer(
        partial1,
        tokens[0],
        grad_hidden,
        gains,
        grad_g2,
        wo_terms.reshape(fsdp_size, held_rows, model),
        qkv_terms.reshape(fsdp_size, ctx_size, held_rows, -1),
    )
    grad_inputs, wd_back = lax.optimization_barrier((grad_inputs, wd_back))
    gain_back = jnp.where(odd == 0, gain_back[:2, :held_rows], gain_back[:2, held_rows:])

    def joined(parts):
        return parts.transpose(1, 0, 2).reshape(held_rows, -1).astype(jnp.float32)

    key_end = group_width + HD
    return (
        output,
        grad_inputs[None],
        gain_back[0],
        joined(qkv_back[:, :, :group_width]),
        joined(qkv_back[:, :, group_width:key_end]),
        joined(qkv_back[:, :, key_end:]),
        wo_back,
        gain_back[1],
        joined(gu_back[:, :, :ff_slice]),
        joined(gu_back[:, :, ff_slice:]),
        wd_back.astype(jnp.float32),
    )


def solution(mesh):
    in_specs = (
        P("fsdp", "ctx", None),
        P("fsdp", None),
        P("fsdp", "ctx", None),
        P(("ctx", "fsdp")),
        P(("ctx", "fsdp"), None),
        P(("ctx", "fsdp"), None),
        P(("ctx", "fsdp"), None),
        P(("ctx", "fsdp"), None),
        P(("ctx", "fsdp")),
        P(("ctx", "fsdp"), None),
        P(("ctx", "fsdp"), None),
        P(("ctx", "fsdp"), None),
    )
    out_specs = (
        P("fsdp", "ctx", None),
        P("fsdp", "ctx", None),
        P(("ctx", "fsdp")),
        P(("ctx", "fsdp"), None),
        P(("ctx", "fsdp"), None),
        P(("ctx", "fsdp"), None),
        P(("ctx", "fsdp"), None),
        P(("ctx", "fsdp")),
        P(("ctx", "fsdp"), None),
        P(("ctx", "fsdp"), None),
        P(("ctx", "fsdp"), None),
    )
    if mesh.shape["ctx"] != KVH or KVH != 4 * PAIR:
        return jax.shard_map(
            general_device, mesh=mesh, in_specs=in_specs, out_specs=out_specs, check_vma=False
        )

    return jax.shard_map(
        on_device, mesh=mesh, in_specs=in_specs, out_specs=out_specs, check_vma=False
    )
```

```python
import functools
import math

import jax
import jax.numpy as jnp
from jax import lax
from jax.experimental import pallas as pl
from jax.experimental.pallas import tpu as pltpu
from jax.sharding import PartitionSpec as P

H = 32
KVH = 8
HD = 64
FF = 8192


EPSILON = 1e-05
SCORE_SCALE = 1.0 / 64.0
RESIDUAL_MULT = 0.22
ROPE_BASE = 10000000.0
NEGATIVE = -1e30
MESH = pl.DeviceIdType.MESH
PAIR = 2
CHUNKS = 2
ANYWHERE = pl.BlockSpec(memory_space=pl.ANY)
LINK_COST = pl.CostEstimate(flops=0, bytes_accessed=150_000_000, transcendentals=0)


def doc_index(positions, starts):
    return jnp.sum((positions[:, None] >= starts[None, :]).astype(jnp.int32), axis=1) - 1


def rope_tables(positions):
    half_size = HD // 2
    frequency = ROPE_BASE ** (-(jnp.arange(half_size, dtype=jnp.float32) * 2.0) / HD)
    angles = positions.astype(jnp.float32)[:, None] * frequency[None, :]
    return (jnp.cos(angles), jnp.sin(angles))


def rotate(tensor, cos_table, sin_table, head_count):
    row_count = tensor.shape[0]
    by_head = tensor.reshape(row_count, head_count, HD)
    half_size = HD // 2
    first_half = by_head[..., :half_size]
    second_half = by_head[..., half_size:]
    cos_rows = cos_table[:, None, :]
    sin_rows = sin_table[:, None, :]
    turned = jnp.concatenate(
        [
            first_half * cos_rows - second_half * sin_rows,
            second_half * cos_rows + first_half * sin_rows,
        ],
        axis=-1,
    )
    return turned.reshape(row_count, head_count * HD)


def dot_plain(left, right):
    return jnp.dot(left, right, preferred_element_type=jnp.float32)


def dot_back(left, right):
    return lax.dot_general(
        left, right, (((1,), (1,)), ((), ())), preferred_element_type=jnp.float32
    )


def dot_outer(left, right):
    return lax.dot_general(
        left, right, (((0,), (0,)), ((), ())), preferred_element_type=jnp.float32
    )


def norm_back(grad_normed, unit_rows, inv_scale, gain_full):
    scaled = grad_normed * gain_full
    return inv_scale * (scaled - unit_rows * jnp.mean(scaled * unit_rows, axis=-1, keepdims=True))


def general_device(
    tokens,
    doc_lengths,
    cotangent,
    gain_attn,
    w_query,
    w_key,
    w_value,
    w_output,
    gain_mlp,
    w_gate,
    w_up,
    w_down,
):
    local_rows = tokens.shape[1]
    ctx_size = lax.axis_size("ctx")
    length = local_rows * ctx_size
    group_size = H // KVH
    offset = lax.axis_index("ctx") * local_rows
    positions = offset + jnp.arange(local_rows, dtype=jnp.int32)
    seq_lengths = doc_lengths[0]
    starts = jnp.cumsum(seq_lengths) - seq_lengths
    doc_ids = doc_index(positions, starts)
    last_pos = offset + local_rows - 1
    first_doc = doc_ids[0]
    cos_table, sin_table = rope_tables(positions)
    gain1, gain2, wq_full, wk_full, wv_full, wo_full = (
        lax.all_gather(gain_attn, ("ctx", "fsdp"), axis=0, tiled=True),
        lax.all_gather(gain_mlp, ("ctx", "fsdp"), axis=0, tiled=True),
        lax.all_gather(w_query, ("ctx", "fsdp"), axis=0, tiled=True),
        lax.all_gather(w_key, ("ctx", "fsdp"), axis=0, tiled=True),
        lax.all_gather(w_value, ("ctx", "fsdp"), axis=0, tiled=True),
        lax.all_gather(w_output, ("ctx", "fsdp"), axis=0, tiled=True),
    )
    gain1_f = gain1.astype(jnp.float32)
    gain2_f = gain2.astype(jnp.float32)
    inputs = tokens[0].astype(jnp.float32)
    inv_one = lax.rsqrt(jnp.mean(inputs * inputs, axis=-1, keepdims=True) + EPSILON)
    unit_one = inputs * inv_one
    normed1 = (unit_one * gain1_f).astype(jnp.bfloat16)
    queries = rotate(dot_plain(normed1, wq_full), cos_table, sin_table, H).astype(jnp.bfloat16)
    key_rot = rotate(dot_plain(normed1, wk_full), cos_table, sin_table, KVH).astype(jnp.bfloat16)
    values = dot_plain(normed1, wv_full).astype(jnp.bfloat16)
    grouped = queries.reshape(local_rows, KVH, group_size, HD)
    start_state = (
        jnp.full((local_rows, KVH, group_size), NEGATIVE, jnp.float32),
        jnp.zeros((local_rows, KVH, group_size), jnp.float32),
        jnp.zeros((local_rows, KVH, group_size, HD), jnp.float32),
    )
    running = start_state
    key_piece = lax.all_gather(key_rot, "ctx", axis=0, tiled=True)
    value_piece = lax.all_gather(values, "ctx", axis=0, tiled=True)
    piece_rows = key_piece.shape[0]
    attend_key_width = math.gcd(piece_rows, 512)
    block_count = piece_rows // attend_key_width

    def one_block(carried, index_block):
        block_start = index_block * attend_key_width
        key_blk = lax.dynamic_slice_in_dim(key_piece, block_start, attend_key_width, 0).reshape(
            attend_key_width, KVH, HD
        )
        value_blk = lax.dynamic_slice_in_dim(value_piece, block_start, attend_key_width, 0).reshape(
            attend_key_width, KVH, HD
        )
        key_pos = block_start + jnp.arange(attend_key_width, dtype=jnp.int32)
        key_docs = doc_index(key_pos, starts)
        skip_block = (block_start > last_pos) | (key_docs[attend_key_width - 1] < first_doc)

        def update(current):
            run_max, run_sum, accumulated = current
            scores = (
                jnp.einsum("qkgd,tkd->qkgt", grouped, key_blk, preferred_element_type=jnp.float32)
                * SCORE_SCALE
            )
            allowed = (key_docs[None, :] == doc_ids[:, None]) & (
                key_pos[None, :] <= positions[:, None]
            )
            allowed = allowed[:, None, None, :]
            masked = jnp.where(allowed, scores, NEGATIVE)
            new_max = jnp.maximum(run_max, jnp.max(masked, axis=-1))
            weights_exp = jnp.where(allowed, jnp.exp(masked - new_max[..., None]), 0.0)
            factor = jnp.exp(run_max - new_max)
            new_sum = run_sum * factor + jnp.sum(weights_exp, axis=-1)
            new_acc = accumulated * factor[..., None] + jnp.einsum(
                "qkgt,tkd->qkgd",
                weights_exp.astype(jnp.bfloat16),
                value_blk,
                preferred_element_type=jnp.float32,
            )
            return (new_max, new_sum, new_acc)

        return (lax.cond(skip_block, lambda unchanged: unchanged, update, carried), None)

    running, _ = lax.scan(one_block, running, jnp.arange(block_count))
    run_max, run_sum, accumulated = running
    attended = accumulated / run_sum[..., None]
    log_sum = run_max + jnp.log(run_sum)
    mixed_heads = attended.reshape(local_rows, H * HD).astype(jnp.bfloat16)
    hidden = inputs + RESIDUAL_MULT * dot_plain(mixed_heads, wo_full)
    inv_two = lax.rsqrt(jnp.mean(hidden * hidden, axis=-1, keepdims=True) + EPSILON)
    unit_two = hidden * inv_two
    normed2 = (unit_two * gain2_f).astype(jnp.bfloat16)
    wg_full, wu_full, wd_full = (
        lax.all_gather(w_gate, ("ctx", "fsdp"), axis=0, tiled=True),
        lax.all_gather(w_up, ("ctx", "fsdp"), axis=0, tiled=True),
        lax.all_gather(w_down, ("ctx", "fsdp"), axis=0, tiled=True),
    )
    gate_pre = dot_plain(normed2, wg_full)
    up_pre = dot_plain(normed2, wu_full)
    sig_gate = jax.nn.sigmoid(gate_pre)
    silu_gate = gate_pre * sig_gate
    activ = (silu_gate * up_pre).astype(jnp.bfloat16)
    result = hidden + RESIDUAL_MULT * dot_plain(activ, wd_full)
    output = result.astype(jnp.bfloat16)[None]
    grad_out = cotangent[0].astype(jnp.float32)
    grad_mlp = (RESIDUAL_MULT * grad_out).astype(jnp.bfloat16)
    silu_slope = sig_gate * (1.0 + gate_pre * (1.0 - sig_gate))
    wg_back, wu_back, wd_back = (
        lax.all_gather(w_gate, ("ctx", "fsdp"), axis=0, tiled=True),
        lax.all_gather(w_up, ("ctx", "fsdp"), axis=0, tiled=True),
        lax.all_gather(w_down, ("ctx", "fsdp"), axis=0, tiled=True),
    )
    grad_act = dot_back(grad_mlp, wd_back)
    grad_gate = (grad_act * up_pre * silu_slope).astype(jnp.bfloat16)
    grad_up = (grad_act * silu_gate).astype(jnp.bfloat16)
    grad_norm2 = dot_back(grad_gate, wg_back) + dot_back(grad_up, wu_back)
    left_cols = normed2
    gate_up_shard = lax.psum_scatter(
        jnp.concatenate([dot_outer(left_cols, grad_gate), dot_outer(left_cols, grad_up)], axis=1),
        ("ctx", "fsdp"),
        scatter_dimension=0,
        tiled=True,
    )
    wg_shard = gate_up_shard[:, :FF]
    wu_shard = gate_up_shard[:, FF:]
    left_cols = activ
    wd_shard = lax.psum_scatter(
        dot_outer(left_cols, grad_mlp), ("ctx", "fsdp"), scatter_dimension=0, tiled=True
    )
    grad_g2 = jnp.sum(grad_norm2 * unit_two, axis=0)
    grad_hidden = grad_out + norm_back(grad_norm2, unit_two, inv_two, gain2_f)
    grad_attn = (RESIDUAL_MULT * grad_hidden).astype(jnp.bfloat16)
    wq_back, wk_back, wv_back, wo_back = (
        lax.all_gather(w_query, ("ctx", "fsdp"), axis=0, tiled=True),
        lax.all_gather(w_key, ("ctx", "fsdp"), axis=0, tiled=True),
        lax.all_gather(w_value, ("ctx", "fsdp"), axis=0, tiled=True),
        lax.all_gather(w_output, ("ctx", "fsdp"), axis=0, tiled=True),
    )
    grad_wo = dot_outer(mixed_heads, grad_attn)
    grad_att = (
        dot_back(grad_attn, wo_back).astype(jnp.bfloat16).reshape(local_rows, KVH, group_size, HD)
    )
    row_delta = jnp.sum(grad_att.astype(jnp.float32) * attended, axis=-1)
    key_all, value_all = (
        lax.all_gather(key_rot, "ctx", axis=0, tiled=True),
        lax.all_gather(values, "ctx", axis=0, tiled=True),
    )
    key_width = math.gcd(length, 512)
    block_count = length // key_width

    def back_block(grad_query, index_block):
        block_start = index_block * key_width
        key_blk = lax.dynamic_slice_in_dim(key_all, block_start, key_width, 0).reshape(
            key_width, KVH, HD
        )
        value_blk = lax.dynamic_slice_in_dim(value_all, block_start, key_width, 0).reshape(
            key_width, KVH, HD
        )
        key_pos = block_start + jnp.arange(key_width, dtype=jnp.int32)
        key_docs = doc_index(key_pos, starts)
        skip_block = (block_start > last_pos) | (key_docs[key_width - 1] < first_doc)

        def compute(current):
            scores = (
                jnp.einsum("qkgd,tkd->qkgt", grouped, key_blk, preferred_element_type=jnp.float32)
                * SCORE_SCALE
            )
            allowed = (key_docs[None, :] == doc_ids[:, None]) & (
                key_pos[None, :] <= positions[:, None]
            )
            allowed = allowed[:, None, None, :]
            probs_blk = jnp.where(
                allowed, jnp.exp(jnp.where(allowed, scores, NEGATIVE) - log_sum[..., None]), 0.0
            )
            grad_probs = jnp.einsum(
                "qkgd,tkd->qkgt", grad_att, value_blk, preferred_element_type=jnp.float32
            )
            grad_scores = (probs_blk * (grad_probs - row_delta[..., None])).astype(jnp.bfloat16)
            new_query = (
                current
                + jnp.einsum(
                    "qkgt,tkd->qkgd", grad_scores, key_blk, preferred_element_type=jnp.float32
                )
                * SCORE_SCALE
            )
            grad_key = (
                jnp.einsum(
                    "qkgt,qkgd->tkd", grad_scores, grouped, preferred_element_type=jnp.float32
                )
                * SCORE_SCALE
            )
            grad_value = jnp.einsum(
                "qkgt,qkgd->tkd",
                probs_blk.astype(jnp.bfloat16),
                grad_att,
                preferred_element_type=jnp.float32,
            )
            return (
                new_query,
                (grad_key.reshape(key_width, KVH * HD), grad_value.reshape(key_width, KVH * HD)),
            )

        def nothing(current):
            zero_rows = jnp.zeros((key_width, KVH * HD), jnp.float32)
            return (current, (zero_rows, zero_rows))

        return lax.cond(skip_block, nothing, compute, grad_query)

    grad_query, key_terms = lax.scan(
        back_block,
        jnp.zeros((local_rows, KVH, group_size, HD), jnp.float32),
        jnp.arange(block_count),
    )
    key_term_all = key_terms[0].reshape(length, KVH * HD)
    value_term_all = key_terms[1].reshape(length, KVH * HD)
    grad_keys, grad_values = (
        lax.psum_scatter(
            key_term_all.astype(jnp.bfloat16), "ctx", scatter_dimension=0, tiled=True
        ).astype(jnp.float32),
        lax.psum_scatter(
            value_term_all.astype(jnp.bfloat16), "ctx", scatter_dimension=0, tiled=True
        ).astype(jnp.float32),
    )
    grad_q_pre = rotate(grad_query.reshape(local_rows, H * HD), cos_table, -sin_table, H).astype(
        jnp.bfloat16
    )
    grad_k_pre = rotate(grad_keys, cos_table, -sin_table, KVH).astype(jnp.bfloat16)
    grad_v_pre = grad_values.astype(jnp.bfloat16)
    grad_norm1 = (
        dot_back(grad_q_pre, wq_back)
        + dot_back(grad_k_pre, wk_back)
        + dot_back(grad_v_pre, wv_back)
    )
    grad_wq = dot_outer(normed1, grad_q_pre)
    grad_wk = dot_outer(normed1, grad_k_pre)
    grad_wv = dot_outer(normed1, grad_v_pre)
    grad_g1 = jnp.sum(grad_norm1 * unit_one, axis=0)
    grad_inputs = grad_hidden + norm_back(grad_norm1, unit_one, inv_one, gain1_f)
    g1_shard, g2_shard, wq_shard, wk_shard, wv_shard, wo_shard = (
        lax.psum_scatter(grad_g1, ("ctx", "fsdp"), scatter_dimension=0, tiled=True),
        lax.psum_scatter(grad_g2, ("ctx", "fsdp"), scatter_dimension=0, tiled=True),
        lax.psum_scatter(grad_wq, ("ctx", "fsdp"), scatter_dimension=0, tiled=True),
        lax.psum_scatter(grad_wk, ("ctx", "fsdp"), scatter_dimension=0, tiled=True),
        lax.psum_scatter(grad_wv, ("ctx", "fsdp"), scatter_dimension=0, tiled=True),
        lax.psum_scatter(grad_wo, ("ctx", "fsdp"), scatter_dimension=0, tiled=True),
    )
    return (
        output,
        grad_inputs[None],
        g1_shard,
        wq_shard,
        wk_shard,
        wv_shard,
        wo_shard,
        g2_shard,
        wg_shard,
        wu_shard,
        wd_shard,
    )


def rows_of(blocks):
    return blocks.reshape((-1,) + blocks.shape[2:])


def in_vmem(count):
    return [pl.BlockSpec(memory_space=pltpu.VMEM)] * count


def greet_line(barrier, ctx_at, line_at, line_size, fsdp_size=1):
    for j in range(1, fsdp_size):
        peer = (lax.axis_index("fsdp") + j) % fsdp_size
        pl.semaphore_signal(barrier, inc=1, device_id={"fsdp": peer}, device_id_type=MESH)
    other = ctx_at + 1 - 2 * (ctx_at % PAIR)
    pl.semaphore_signal(barrier, inc=1, device_id={"ctx": other}, device_id_type=MESH)

    @pl.when(line_at > 0)
    def _():
        pl.semaphore_signal(barrier, inc=1, device_id={"ctx": ctx_at - PAIR}, device_id_type=MESH)

    @pl.when(line_at < line_size - 1)
    def _():
        pl.semaphore_signal(barrier, inc=1, device_id={"ctx": ctx_at + PAIR}, device_id_type=MESH)

    last = line_size - 1
    neighbours = fsdp_size + (line_at + last - 1) // last + (2 * last - 1 - line_at) // last
    pl.semaphore_wait(barrier, neighbours)


def greet_all(barrier, me, count, fsdp_size):
    def greet(k, unused):
        target = (me + k) % count
        pl.semaphore_signal(
            barrier, inc=1, device_id=(target // fsdp_size, target % fsdp_size), device_id_type=MESH
        )
        return unused

    lax.fori_loop(1, count, greet, 0)
    pl.semaphore_wait(barrier, count - 1)


def gather_phase(line_size, x_ref, out_ref, send_sem, recv_sem, own_sem):
    me = lax.axis_index("ctx")
    line_at, pair_at = me // PAIR, me % PAIR
    rows = x_ref.shape[0]
    step = rows // CHUNKS

    def piece(block, part):
        return out_ref.at[pl.ds(pl.multiple_of(block * rows + part * step, step), step), :]

    def copy(block, part, way, own):
        slot = block * CHUNKS + part
        return pltpu.make_async_remote_copy(
            src_ref=x_ref.at[pl.ds(part * step, step), :] if own else piece(block, part),
            dst_ref=piece(block, part),
            send_sem=send_sem.at[way, slot],
            recv_sem=recv_sem.at[slot],
            device_id={"ctx": (me + 1 - 2 * pair_at, me + PAIR, me - PAIR)[way]},
            device_id_type=MESH,
        )

    def pass_on(block, part, upward, downward, own, act):
        if upward is not None:
            pl.when(upward)(lambda: act(copy(block, part, 1, own)))
        if downward is not None:
            pl.when(downward)(lambda: act(copy(block, part, 2, own)))
        act(copy(block, part, 0, own))

    def own_part(part, act):
        pass_on(me, part, line_at < line_size - 1, line_at > 0, True, act)

    def others(act, arrive, between):
        for distance in range(1, line_size):
            between(distance)
            for part in range(CHUNKS):

                @pl.when(line_at >= distance)
                def _():
                    block = me - PAIR * distance
                    arrive(block, part)
                    pass_on(block, part, line_at < line_size - 1, None, False, act)

                @pl.when(line_at + distance < line_size)
                def _():
                    block = me + PAIR * distance
                    arrive(block, part)
                    pass_on(block, part, None, line_at > 0, False, act)

    def start_own(part):
        own_part(part, lambda c: c.start())

    def finish(between=lambda distance: None):
        keep = pltpu.make_async_copy(
            x_ref, out_ref.at[pl.ds(pl.multiple_of(me * rows, rows), rows), :], own_sem
        )
        keep.start()
        others(
            lambda c: c.start(),
            lambda block, part: copy(block, part, 0, False).wait_recv(),
            between,
        )
        for place in range(line_size):
            for part in range(CHUNKS):
                copy(place * PAIR + 1 - pair_at, part, 0, False).wait_recv()
        for part in range(CHUNKS):
            own_part(part, lambda c: c.wait_send())
        others(lambda c: c.wait_send(), lambda block, part: None, lambda distance: None)
        keep.wait()

    return start_own, finish


def gather_scratch(ctx_size):
    return [
        pltpu.SemaphoreType.DMA((3, ctx_size * CHUNKS)),
        pltpu.SemaphoreType.DMA((ctx_size * CHUNKS,)),
        pltpu.SemaphoreType.DMA,
    ]


def scatter_phase(line_size, x_ref, sum_ref, near, below, above, near_send, near_sem, line_send, line_sem, emit, midway=lambda: None):
    me = lax.axis_index("ctx")
    line_at, pair_at = me // PAIR, me % PAIR
    rows = sum_ref.shape[0]
    step = rows // CHUNKS
    last = line_size - 1
    low = line_at // (line_size // 2)
    order = [k + (last - 2 * k) * (1 - low) for k in range(line_size // 2)]
    order += [line_at + 1 - 2 * (line_at % 2), line_at]

    def near_copy(place, part):
        start = (place * PAIR + 1 - pair_at) * rows + part * step
        return pltpu.make_async_remote_copy(
            src_ref=x_ref.at[pl.ds(pl.multiple_of(start, step), step), :],
            dst_ref=near.at[place, pl.ds(part * step, step), :],
            send_sem=near_send.at[place, part],
            recv_sem=near_sem.at[place, part],
            device_id={"ctx": me + 1 - 2 * pair_at},
            device_id_type=MESH,
        )

    def line_copy(place, part, up):
        part_rows = pl.ds(part * step, step)
        return pltpu.make_async_remote_copy(
            src_ref=near.at[place, part_rows, :],
            dst_ref=(below if up else above).at[place, part_rows, :],
            send_sem=line_send.at[place, part],
            recv_sem=line_sem.at[0 if up else 1, place, part],
            device_id={"ctx": me + PAIR if up else me - PAIR},
            device_id_type=MESH,
        )

    def mine(place, part):
        start = (place * PAIR + pair_at) * rows + part * step
        return x_ref[pl.ds(pl.multiple_of(start, step), step), :].astype(jnp.float32)

    for place in order:
        for part in range(CHUNKS):
            near_copy(place, part).start()

    for place in order[:-1]:
        for part in range(CHUNKS):
            part_rows = pl.ds(part * step, step)
            near_copy(place, part).wait_recv()

            def send(up, waits, arrived):
                @pl.when(waits)
                def _():
                    line_copy(place, part, up).wait_recv()
                    near[place, part_rows, :] = (
                        mine(place, part)
                        + near[place, part_rows, :].astype(jnp.float32)
                        + arrived[place, part_rows, :].astype(jnp.float32)
                    ).astype(near.dtype)

                @pl.when(jnp.logical_not(waits))
                def _():
                    near[place, part_rows, :] = (
                        mine(place, part) + near[place, part_rows, :].astype(jnp.float32)
                    ).astype(near.dtype)

                line_copy(place, part, up).start()

            pl.when(place > line_at)(lambda: send(True, line_at > 0, below))
            pl.when(place < line_at)(lambda: send(False, line_at < last, above))

    midway()
    for part in range(CHUNKS):
        part_rows = pl.ds(part * step, step)
        near_copy(line_at, part).wait_recv()
        sum_ref[part_rows, :] = mine(line_at, part) + near[line_at, part_rows, :].astype(jnp.float32)

        @pl.when(line_at > 0)
        def _():
            line_copy(line_at, part, True).wait_recv()
            sum_ref[part_rows, :] += below[line_at, part_rows, :].astype(jnp.float32)

        @pl.when(line_at < last)
        def _():
            line_copy(line_at, part, False).wait_recv()
            sum_ref[part_rows, :] += above[line_at, part_rows, :].astype(jnp.float32)

        emit(part, slice(part * step, (part + 1) * step))

    def finish():
        for place in order:
            for part in range(CHUNKS):
                near_copy(place, part).wait_send()
        for place in order[:-1]:
            for part in range(CHUNKS):
                line_copy(place, part, True).wait_send()

    return finish


def scatter_scratch(ctx_size, rows, width):
    line_size = ctx_size // PAIR
    held = pltpu.VMEM((line_size, rows, width), jnp.bfloat16)
    return [
        held,
        held,
        held,
        pltpu.SemaphoreType.DMA((line_size, CHUNKS)),
        pltpu.SemaphoreType.DMA((line_size, CHUNKS)),
        pltpu.SemaphoreType.DMA((line_size, CHUNKS)),
        pltpu.SemaphoreType.DMA((2, line_size, CHUNKS)),
    ]


def swap_lanes(values, outer, inner):
    tile = 128
    half = tile // 2
    low = lax.broadcasted_iota(jnp.int32, (values.shape[0], tile), 1) < half
    placed = [None] * (outer * inner // 2)
    for first in range(0, outer, 2):
        for second in range(0, inner, 2):
            at = (first * inner + second) // 2
            one = values[:, at * tile : (at + 1) * tile]
            at += inner // 2
            two = values[:, at * tile : (at + 1) * tile]
            at = (second * outer + first) // 2
            placed[at] = jnp.where(low, one, pltpu.roll(two, half, 1))
            placed[at + outer // 2] = jnp.where(low, pltpu.roll(one, half, 1), two)
    return jnp.concatenate(placed, axis=1)


def start_kernel(
    ctx_size, fsdp_size, tokens_ref, tile_ref, parts_ref, gate_ref, up_ref, out_ref, gains_ref, weight_ref,
    wide_ref, tiles, normed, tile_send, tile_recv, far_send, far_recv, near_send, near_recv, wide_send,
    wide_recv, kept, wide_kept, *sems
):
    me_ctx, me_fsdp = lax.axis_index("ctx"), lax.axis_index("fsdp")
    count = ctx_size * fsdp_size
    me = me_ctx * fsdp_size + me_fsdp
    greet_all(pltpu.get_barrier_semaphore(), me, count, fsdp_size)

    def tile_copy(k, source):
        target = (me + k) % count
        return pltpu.make_async_remote_copy(
            src_ref=tile_ref,
            dst_ref=tiles.at[source],
            send_sem=tile_send.at[k],
            recv_sem=tile_recv.at[k],
            device_id=(target // fsdp_size, target % fsdp_size),
            device_id_type=MESH,
        )

    def start_tile(k, unused):
        tile_copy(k, me).start()
        return unused

    def finish_tile(k, unused):
        tile_copy(k, (me + count - k) % count).wait_recv()
        return unused

    lax.fori_loop(1, count, start_tile, 0)
    tiles[pl.ds(me, 1)] = tile_ref[...][None]

    def far_copy(k, source):
        target = (me_ctx + k) % ctx_size
        return pltpu.make_async_remote_copy(
            src_ref=parts_ref.at[target],
            dst_ref=weight_ref.at[source * fsdp_size + me_fsdp],
            send_sem=far_send.at[k],
            recv_sem=far_recv.at[k],
            device_id={"ctx": target},
            device_id_type=MESH,
        )

    def near_copy(k, j, fsdp_source):
        block = (me_ctx + ctx_size - k) % ctx_size * fsdp_size + fsdp_source
        return pltpu.make_async_remote_copy(
            src_ref=parts_ref.at[me_ctx] if k == 0 else weight_ref.at[block],
            dst_ref=weight_ref.at[block],
            send_sem=near_send.at[k, j],
            recv_sem=near_recv.at[k, j],
            device_id={"fsdp": (me_fsdp + j) % fsdp_size},
            device_id_type=MESH,
        )

    wide = gate_ref.shape[1] // ctx_size

    def wide_part(which, target, source):
        cols = pl.ds(pl.multiple_of(target * wide, wide), wide)
        return (
            (gate_ref, up_ref)[which].at[:, cols],
            wide_ref.at[source, :, which * wide : (which + 1) * wide],
        )

    def wide_copy(which, k, source):
        target = (me_ctx + k) % ctx_size
        src, dst = wide_part(which, target, source)
        return pltpu.make_async_remote_copy(
            src_ref=src,
            dst_ref=dst,
            send_sem=wide_send.at[which, k],
            recv_sem=wide_recv.at[which, k],
            device_id={"ctx": target},
            device_id_type=MESH,
        )

    def wide_keep(which):
        return pltpu.make_async_copy(*wide_part(which, me_ctx, me_ctx), wide_kept.at[which])

    def wide_start(distance):
        for k in range(2 * distance - 1, min(2 * distance + 1, ctx_size)):
            for which in range(2):
                wide_copy(which, k, me_ctx).start()
        if distance == ctx_size // PAIR - 1:
            for which in range(2):
                wide_copy(which, ctx_size - 1, me_ctx).start()

    for k in range(1, ctx_size):
        far_copy(k, me_ctx).start()
    for j in range(1, fsdp_size):
        near_copy(0, j, me_fsdp).start()
    for which in range(2):
        wide_keep(which).start()
    keep = pltpu.make_async_copy(parts_ref.at[me_ctx], weight_ref.at[me], kept)
    keep.start()

    rows, model = tokens_ref.shape
    lax.fori_loop(1, count, finish_tile, 0)
    held = model // count
    for pair in range(count // 2):
        cols = slice(pair * 2 * held, (pair + 1) * 2 * held)
        gains_ref[:, cols] = tiles[2 * pair] + tiles[2 * pair + 1]
    start_own, finish_gather = gather_phase(ctx_size // PAIR, normed, out_ref, *sems)
    step = rows // CHUNKS
    for part in range(CHUNKS):
        part_rows = slice(part * step, (part + 1) * step)
        values = tokens_ref[part_rows, :].astype(jnp.float32)
        scale = lax.rsqrt(jnp.mean(values * values, axis=-1, keepdims=True) + EPSILON)
        normed[part_rows, :] = (values * scale * gains_ref[0:1, :]).astype(normed.dtype)
        start_own(part)
    for k in range(1, ctx_size):
        far_copy(k, (me_ctx + ctx_size - k) % ctx_size).wait_recv()
        for j in range(1, fsdp_size):
            near_copy(k, j, me_fsdp).start()
    finish_gather(wide_start)
    for which in range(2):
        for k in range(1, ctx_size):
            wide_copy(which, k, (me_ctx + ctx_size - k) % ctx_size).wait_recv()
        for k in range(1, ctx_size):
            wide_copy(which, k, me_ctx).wait_send()
        wide_keep(which).wait()
    for k in range(ctx_size):
        for j in range(1, fsdp_size):
            near_copy(k, j, (me_fsdp + fsdp_size - j) % fsdp_size).wait_recv()
    for k in range(ctx_size):
        for j in range(1, fsdp_size):
            near_copy(k, j, me_fsdp).wait_send()
    for k in range(1, ctx_size):
        far_copy(k, me_ctx).wait_send()

    def sent_tile(k, unused):
        tile_copy(k, me).wait_send()
        return unused

    lax.fori_loop(1, count, sent_tile, 0)
    keep.wait()


def start_layer(tokens, tile, parts, w_gate, w_up):
    ctx_size, fsdp_size = lax.axis_size("ctx"), lax.axis_size("fsdp")
    count = ctx_size * fsdp_size
    rows, model = tokens.shape
    dma = pltpu.SemaphoreType.DMA
    held = w_gate.shape[0]
    normed1, gains, weight, wide = pl.pallas_call(
        functools.partial(start_kernel, ctx_size, fsdp_size),
        out_shape=(
            jax.ShapeDtypeStruct((ctx_size * rows, model), jnp.bfloat16),
            jax.ShapeDtypeStruct((8, model), jnp.float32),
            jax.ShapeDtypeStruct((count,) + parts.shape[1:], parts.dtype),
            jax.ShapeDtypeStruct((ctx_size, held, 2 * w_gate.shape[1] // ctx_size), w_gate.dtype),
        ),
        in_specs=in_vmem(5),
        out_specs=(ANYWHERE, in_vmem(1)[0], ANYWHERE, ANYWHERE),
        scratch_shapes=[
            pltpu.VMEM((count, 8, 128), jnp.float32),
            pltpu.VMEM((rows, model), jnp.bfloat16),
            dma((count,)),
            dma((count,)),
            dma((ctx_size,)),
            dma((ctx_size,)),
            dma((ctx_size, fsdp_size)),
            dma((ctx_size, fsdp_size)),
            dma((2, ctx_size)),
            dma((2, ctx_size)),
            dma,
            dma((2,)),
        ]
        + gather_scratch(ctx_size),
        compiler_params=pltpu.CompilerParams(
            collective_id=0, has_side_effects=True, vmem_limit_bytes=32 * 2**20
        ),
        cost_estimate=LINK_COST,
        name="start_layer",
    )(tokens, tile, parts, w_gate, w_up)
    return normed1, gains, rows_of(weight), rows_of(wide)


def mlp_forward_kernel(
    ctx_size, fsdp_size, x_ref, tokens_ref, gains_ref, hidden_ref, out_ref, sums, normed, *sems
):
    line_size = ctx_size // PAIR
    me = lax.axis_index("ctx")
    greet_line(pltpu.get_barrier_semaphore(), me, me // PAIR, line_size)
    start_own, finish_gather = gather_phase(line_size, normed, out_ref, *sems[7:])

    def emit(part, rows):
        hidden = tokens_ref[rows, :].astype(jnp.float32) + RESIDUAL_MULT * sums[rows, :]
        hidden_ref[rows, :] = hidden
        scale = lax.rsqrt(jnp.mean(hidden * hidden, axis=-1, keepdims=True) + EPSILON)
        scaled = hidden * scale * gains_ref[1:2, :]
        normed[rows, :] = swap_lanes(scaled, ctx_size, fsdp_size).astype(normed.dtype)
        start_own(part)

    finish_scatter = scatter_phase(line_size, x_ref, sums, *sems[:7], emit)
    finish_gather()
    finish_scatter()


def mlp_backward_kernel(
    ctx_size, fsdp_size, x_ref, hidden_ref, grad_ref, gains_ref, terms_ref, grad_hidden_ref, grad_gain_ref,
    total_ref, out_ref, sums, normed, landing, side_send, side_recv, own_sem, *sems
):
    line_size = ctx_size // PAIR
    me, me_fsdp = lax.axis_index("ctx"), lax.axis_index("fsdp")
    greet_line(pltpu.get_barrier_semaphore(), me, me // PAIR, line_size, fsdp_size)

    def side_copy(j):
        target = (me_fsdp + j) % fsdp_size
        return pltpu.make_async_remote_copy(
            src_ref=terms_ref.at[target],
            dst_ref=landing.at[j],
            send_sem=side_send.at[j],
            recv_sem=side_recv.at[j],
            device_id={"fsdp": target},
            device_id_type=MESH,
        )

    own_copy = pltpu.make_async_copy(terms_ref.at[me_fsdp], landing.at[0], own_sem)
    for j in range(1, fsdp_size):
        side_copy(j).start()
    own_copy.start()
    start_own, finish_gather = gather_phase(line_size, normed, out_ref, *sems[7:])

    def emit(part, rows):
        grad_norm = swap_lanes(sums[rows, :], fsdp_size, ctx_size)
        hidden = hidden_ref[rows, :]
        scale = lax.rsqrt(jnp.mean(hidden * hidden, axis=-1, keepdims=True) + EPSILON)
        unit = hidden * scale
        grad_gain_ref[part : part + 1, :] = jnp.sum(grad_norm * unit, axis=0, keepdims=True)
        grad_hidden = grad_ref[rows, :].astype(jnp.float32) + norm_back(
            grad_norm, unit, scale, gains_ref[1:2, :]
        )
        grad_hidden_ref[rows, :] = grad_hidden
        normed[rows, :] = (RESIDUAL_MULT * grad_hidden).astype(normed.dtype)
        start_own(part)

    finish_scatter = scatter_phase(line_size, x_ref, sums, *sems[:7], emit)
    finish_gather()
    own_copy.wait()
    for j in range(1, fsdp_size):
        side_copy(j).wait_recv()
    step = 64

    def add(at, unused):
        rows = pl.ds(pl.multiple_of(at * step, step), step)
        total = landing[0, rows, :].astype(jnp.float32)
        for j in range(1, fsdp_size):
            total += landing[j, rows, :].astype(jnp.float32)
        total_ref[rows, :] = total.astype(total_ref.dtype)
        return unused

    lax.fori_loop(0, total_ref.shape[0] // step, add, 0)
    for j in range(1, fsdp_size):
        side_copy(j).wait_send()
    finish_scatter()


def scatter_gather(kernel, collective_id, extra_shapes, partial, *others, specs=(), scratch=()):
    ctx_size, fsdp_size = lax.axis_size("ctx"), lax.axis_size("fsdp")
    rows, model = partial.shape[0] // ctx_size, partial.shape[1]
    return pl.pallas_call(
        functools.partial(kernel, ctx_size, fsdp_size),
        out_shape=extra_shapes + (jax.ShapeDtypeStruct(partial.shape, jnp.bfloat16),),
        in_specs=in_vmem(1 + len(others) - len(specs)) + list(specs),
        out_specs=tuple(in_vmem(len(extra_shapes))) + (ANYWHERE,),
        scratch_shapes=[pltpu.VMEM((rows, model), jnp.float32), pltpu.VMEM((rows, model), jnp.bfloat16)]
        + list(scratch)
        + scatter_scratch(ctx_size, rows, model)
        + gather_scratch(ctx_size),
        compiler_params=pltpu.CompilerParams(
            collective_id=collective_id, has_side_effects=True, vmem_limit_bytes=48 * 2**20
        ),
        cost_estimate=LINK_COST,
    )(partial, *others)


def mlp_forward(partial, tokens, gains):
    hidden = jax.ShapeDtypeStruct(tokens.shape, jnp.float32)
    return scatter_gather(mlp_forward_kernel, 1, (hidden,), partial, tokens, gains)


def mlp_backward(partial, hidden, grad_out, gains, terms):
    like = jax.ShapeDtypeStruct(hidden.shape, jnp.float32)
    gain = jax.ShapeDtypeStruct((CHUNKS, hidden.shape[1]), jnp.float32)
    return scatter_gather(
        mlp_backward_kernel,
        2,
        (like, gain, jax.ShapeDtypeStruct(terms.shape[1:], terms.dtype)),
        partial,
        hidden,
        grad_out,
        gains,
        terms,
        specs=(ANYWHERE,),
        scratch=(
            pltpu.VMEM(terms.shape, terms.dtype),
            pltpu.SemaphoreType.DMA((terms.shape[0],)),
            pltpu.SemaphoreType.DMA((terms.shape[0],)),
            pltpu.SemaphoreType.DMA,
        ),
    )


def finish_kernel(
    ctx_size, fsdp_size, x_ref, tokens_ref, grad_ref, gains_ref, gain2_ref, wo_ref, qkv_ref,
    grad_tokens_ref, gain_out_ref, wo_out_ref, qkv_out_ref,
    sums, gain1, tiles, arrived, wo_in, qkv_in, qkv_sum, tile_send, tile_recv, near_send, near_recv,
    far_send, far_recv, *sems
):
    line_size = ctx_size // PAIR
    me_ctx, me_fsdp = lax.axis_index("ctx"), lax.axis_index("fsdp")
    count = ctx_size * fsdp_size
    me = me_ctx * fsdp_size + me_fsdp
    greet_all(pltpu.get_barrier_semaphore(), me, count, fsdp_size)

    def near_copy(which, j):
        target = (me_fsdp + j) % fsdp_size
        terms, landing = ((wo_ref, wo_in), (qkv_ref, qkv_in))[which]
        return pltpu.make_async_remote_copy(
            src_ref=terms.at[target],
            dst_ref=landing.at[j],
            send_sem=near_send.at[which, j],
            recv_sem=near_recv.at[which, j],
            device_id={"fsdp": target},
            device_id_type=MESH,
        )

    def far_copy(k, source):
        target = (me_ctx + k) % ctx_size
        return pltpu.make_async_remote_copy(
            src_ref=qkv_sum.at[target],
            dst_ref=qkv_out_ref.at[source],
            send_sem=far_send.at[k],
            recv_sem=far_recv.at[k],
            device_id={"ctx": target},
            device_id_type=MESH,
        )

    def tile_copy(k, source):
        target = (me + k) % count
        return pltpu.make_async_remote_copy(
            src_ref=tiles.at[target // 2],
            dst_ref=arrived.at[source],
            send_sem=tile_send.at[k],
            recv_sem=tile_recv.at[k],
            device_id=(target // fsdp_size, target % fsdp_size),
            device_id_type=MESH,
        )

    def midway():
        for which, own, landing in ((1, qkv_ref, qkv_in), (0, wo_ref, wo_in)):
            for j in range(1, fsdp_size):
                near_copy(which, j).wait_recv()
            total = own[pl.ds(me_fsdp, 1)][0].astype(jnp.float32)
            for j in range(1, fsdp_size):
                total += landing[j].astype(jnp.float32)
            if which:
                qkv_sum[...] = total.astype(qkv_sum.dtype)
                for k in range(1, ctx_size):
                    far_copy(k, me_ctx).start()
                qkv_out_ref[pl.ds(me_ctx, 1)] = qkv_sum[pl.ds(me_ctx, 1)]
            else:
                wo_out_ref[...] = total

    def emit(part, rows):
        grad_norm = sums[rows, :]
        values = tokens_ref[rows, :].astype(jnp.float32)
        scale = lax.rsqrt(jnp.mean(values * values, axis=-1, keepdims=True) + EPSILON)
        unit = values * scale
        gain1[part : part + 1, :] = jnp.sum(grad_norm * unit, axis=0, keepdims=True)
        grad_tokens_ref[rows, :] = grad_ref[rows, :] + norm_back(
            grad_norm, unit, scale, gains_ref[0:1, :]
        )

    for which in (1, 0):
        for j in range(1, fsdp_size):
            near_copy(which, j).start()
    finish_scatter = scatter_phase(line_size, x_ref, sums, *sems, emit, midway)
    row = lax.broadcasted_iota(jnp.int32, (8, 128), 0)
    for pair in range(count // 2):
        cols = slice(pair * 128, (pair + 1) * 128)
        first = jnp.sum(gain1[:, cols], axis=0, keepdims=True)
        second = jnp.sum(gain2_ref[:, cols], axis=0, keepdims=True)
        tiles[pair] = jnp.where(row == 0, first, jnp.where(row == 1, second, 0.0))

    def start_tile(k, unused):
        tile_copy(k, me).start()
        return unused

    def finish_tile(k, unused):
        tile_copy(k, (me + count - k) % count).wait_recv()
        return unused

    def sent_tile(k, unused):
        tile_copy(k, me).wait_send()
        return unused

    lax.fori_loop(1, count, start_tile, 0)
    arrived[pl.ds(me, 1)] = tiles[pl.ds(me // 2, 1)]
    for k in range(1, ctx_size):
        far_copy(k, (me_ctx + ctx_size - k) % ctx_size).wait_recv()
    lax.fori_loop(1, count, finish_tile, 0)
    gain_out_ref[...] = jnp.sum(arrived[...], axis=0)
    finish_scatter()
    for which in range(2):
        for j in range(1, fsdp_size):
            near_copy(which, j).wait_send()
    for k in range(1, ctx_size):
        far_copy(k, me_ctx).wait_send()
    lax.fori_loop(1, count, sent_tile, 0)


def finish_layer(partial, tokens, grad_hidden, gains, grad_gain2, wo_terms, qkv_terms):
    ctx_size, fsdp_size = lax.axis_size("ctx"), lax.axis_size("fsdp")
    count = ctx_size * fsdp_size
    rows, model = tokens.shape
    dma = pltpu.SemaphoreType.DMA
    f32, bf16 = jnp.float32, jnp.bfloat16
    held, width = qkv_terms.shape[2:]
    return pl.pallas_call(
        functools.partial(finish_kernel, ctx_size, fsdp_size),
        out_shape=(
            jax.ShapeDtypeStruct((rows, model), f32),
            jax.ShapeDtypeStruct((8, 128), f32),
            jax.ShapeDtypeStruct(wo_terms.shape[1:], f32),
            jax.ShapeDtypeStruct((ctx_size, held, width), bf16),
        ),
        in_specs=in_vmem(7),
        out_specs=tuple(in_vmem(4)),
        scratch_shapes=[
            pltpu.VMEM((rows, model), f32),
            pltpu.VMEM((CHUNKS, model), f32),
            pltpu.VMEM((count // 2, 8, 128), f32),
            pltpu.VMEM((count, 8, 128), f32),
            pltpu.VMEM(wo_terms.shape, bf16),
            pltpu.VMEM(qkv_terms.shape, bf16),
            pltpu.VMEM((ctx_size, held, width), bf16),
            dma((count,)),
            dma((count,)),
            dma((2, fsdp_size)),
            dma((2, fsdp_size)),
            dma((ctx_size,)),
            dma((ctx_size,)),
        ]
        + scatter_scratch(ctx_size, rows, model),
        compiler_params=pltpu.CompilerParams(
            collective_id=3, has_side_effects=True, vmem_limit_bytes=40 * 2**20
        ),
        cost_estimate=LINK_COST,
        name="finish_layer",
    )(partial, tokens, grad_hidden, gains, grad_gain2, wo_terms, qkv_terms)


def swap_ctx(blocks):
    return lax.all_to_all(blocks, "ctx", split_axis=0, concat_axis=0, tiled=True)


def by_fsdp(grad, ctx_size, fsdp_size):
    parts = grad.reshape(ctx_size, fsdp_size, -1, grad.shape[-1]).transpose(1, 0, 2, 3)
    return rows_of(rows_of(parts))


def return_columns(terms, ctx_size):
    return swap_ctx(terms.reshape(ctx_size, -1, terms.shape[-1]))


def half_turn(values, sign_table):
    lane = lax.broadcasted_iota(jnp.int32, values.shape, 1)
    width = values.shape[1]
    quarter = HD // 2
    ahead = pltpu.roll(values, width - quarter, 1)
    behind = pltpu.roll(values, quarter, 1)
    return jnp.where(lane % HD < quarter, ahead, behind) * sign_table


def turn(values, cos_table, sign_table):
    copies = values.shape[1] // cos_table.shape[1]
    if copies > 1:
        cos_table = jnp.concatenate([cos_table] * copies, axis=1)
        sign_table = jnp.concatenate([sign_table] * copies, axis=1)
    return values * cos_table + half_turn(values, sign_table)


def attention_forward_kernel(
    block_rows, qkv_ref, cos_ref, sin_ref, doc_col_ref, doc_row_ref, q_ref, kv_ref, out_ref, lse_ref
):
    length = qkv_ref.shape[0]
    group = H // KVH
    width = group * HD
    q_ref[...] = turn(qkv_ref[:, :width], cos_ref[...], sin_ref[...]).astype(jnp.bfloat16)
    pair = qkv_ref[:, width:]
    lane = lax.broadcasted_iota(jnp.int32, pair.shape, 1)
    turned = turn(pair, cos_ref[...], sin_ref[...])
    kv_ref[...] = jnp.where(lane < HD, turned, pair).astype(jnp.bfloat16)
    for block in range(length // block_rows):
        rows = slice(block * block_rows, (block + 1) * block_rows)
        reach = (block + 1) * block_rows
        keys = kv_ref[:reach, :HD]
        values = kv_ref[:reach, HD:]
        query_at = block * block_rows + lax.broadcasted_iota(jnp.int32, (block_rows, reach), 0)
        key_at = lax.broadcasted_iota(jnp.int32, (block_rows, reach), 1)
        allowed = (doc_col_ref[rows, :] == doc_row_ref[:, :reach]) & (key_at <= query_at)
        for head in range(group):
            cols = slice(head * HD, (head + 1) * HD)
            scores = dot_back(q_ref[rows, cols], keys) * SCORE_SCALE
            masked = jnp.where(allowed, scores, NEGATIVE)
            top = jnp.max(masked, axis=1, keepdims=True)
            weights = jnp.where(allowed, jnp.exp(masked - top), 0.0)
            total = jnp.sum(weights, axis=1, keepdims=True)
            mixed = dot_plain(weights.astype(jnp.bfloat16), values)
            out_ref[rows, cols] = (mixed / total).astype(jnp.bfloat16)
            lse_ref[rows, head : head + 1] = top + jnp.log(total)


def attention_backward_kernel(
    block_rows, q_ref, kv_ref, do_ref, lse_ref, cos_ref, sin_ref, doc_col_ref, doc_row_ref, grad_ref, dq_ref, dkv_ref
):
    length = q_ref.shape[0]
    group = H // KVH
    width = group * HD
    dkv_ref[...] = jnp.zeros_like(dkv_ref)
    for block in range(length // block_rows):
        rows = slice(block * block_rows, (block + 1) * block_rows)
        reach = (block + 1) * block_rows
        keys = kv_ref[:reach, :HD]
        values = kv_ref[:reach, HD:]
        query_at = block * block_rows + lax.broadcasted_iota(jnp.int32, (block_rows, reach), 0)
        key_at = lax.broadcasted_iota(jnp.int32, (block_rows, reach), 1)
        allowed = (doc_col_ref[rows, :] == doc_row_ref[:, :reach]) & (key_at <= query_at)
        for head in range(group):
            cols = slice(head * HD, (head + 1) * HD)
            query = q_ref[rows, cols]
            grad_out = do_ref[rows, cols]
            scores = dot_back(query, keys) * SCORE_SCALE
            probs = jnp.where(
                allowed,
                jnp.exp(jnp.where(allowed, scores, NEGATIVE) - lse_ref[rows, head : head + 1]),
                0.0,
            )
            grad_probs = dot_back(grad_out, values)
            delta = jnp.sum(probs * grad_probs, axis=1, keepdims=True)
            grad_scores = (probs * (grad_probs - delta)).astype(jnp.bfloat16)
            dq_ref[rows, cols] = dot_plain(grad_scores, keys) * SCORE_SCALE
            dkv_ref[:reach, :HD] += dot_outer(grad_scores, query) * SCORE_SCALE
            dkv_ref[:reach, HD:] += dot_outer(probs.astype(jnp.bfloat16), grad_out)
    grad_ref[:, :width] = turn(dq_ref[...], cos_ref[...], -sin_ref[...]).astype(jnp.bfloat16)
    pair = dkv_ref[...]
    lane = lax.broadcasted_iota(jnp.int32, pair.shape, 1)
    turned = turn(pair, cos_ref[...], -sin_ref[...])
    grad_ref[:, width:] = jnp.where(lane < HD, turned, pair).astype(jnp.bfloat16)


def attention_forward(qkv, tables, block_rows):
    length = qkv.shape[0]
    width = (H // KVH) * HD
    return pl.pallas_call(
        functools.partial(attention_forward_kernel, block_rows),
        out_shape=(
            jax.ShapeDtypeStruct((length, width), jnp.bfloat16),
            jax.ShapeDtypeStruct((length, 2 * HD), jnp.bfloat16),
            jax.ShapeDtypeStruct((length, width), jnp.bfloat16),
            jax.ShapeDtypeStruct((length, H // KVH), jnp.float32),
        ),
        in_specs=in_vmem(5),
        out_specs=tuple(in_vmem(4)),
        compiler_params=pltpu.CompilerParams(vmem_limit_bytes=48 * 2**20),
        name="attend",
    )(qkv, *tables)


def attention_backward(q, kv, grad_out, lse, tables, block_rows):
    length, width = q.shape
    return pl.pallas_call(
        functools.partial(attention_backward_kernel, block_rows),
        out_shape=jax.ShapeDtypeStruct((length, width + 2 * HD), jnp.bfloat16),
        in_specs=in_vmem(8),
        out_specs=in_vmem(1)[0],
        scratch_shapes=[
            pltpu.VMEM((length, width), jnp.float32),
            pltpu.VMEM((length, 2 * HD), jnp.float32),
        ],
        compiler_params=pltpu.CompilerParams(vmem_limit_bytes=48 * 2**20),
        name="attend_back",
    )(q, kv, grad_out, lse, *tables)


def on_device(
    tokens,
    doc_lengths,
    cotangent,
    gain_attn,
    w_query,
    w_key,
    w_value,
    w_output,
    gain_mlp,
    w_gate,
    w_up,
    w_down,
):
    local_rows, model = tokens.shape[1:]
    ctx_size = lax.axis_size("ctx")
    fsdp_size = lax.axis_size("fsdp")
    length = local_rows * ctx_size
    group_width = (H // KVH) * HD
    ff_slice = FF // ctx_size
    held_rows = w_query.shape[0]
    bf16 = jnp.bfloat16

    positions = jnp.arange(length, dtype=jnp.int32)
    seq_lengths = doc_lengths[0]
    starts = jnp.cumsum(seq_lengths) - seq_lengths
    doc_ids = doc_index(positions, starts)
    cos_half, sin_half = rope_tables(positions)
    cos_table = jnp.concatenate([cos_half] * 4, axis=1)
    sin_table = jnp.concatenate([-sin_half, sin_half] * 2, axis=1)
    tables = (cos_table, sin_table, doc_ids[:, None], doc_ids[None, :])


    def by_slice(weight):
        return weight.reshape(held_rows, ctx_size, -1)

    qkv_parts = jnp.concatenate([by_slice(w_query), by_slice(w_key), by_slice(w_value)], axis=2)
    wo_mine = lax.all_gather(w_output, "fsdp", axis=0, tiled=True)
    wd_mine = lax.all_gather(w_down, "fsdp", axis=0, tiled=True)
    gain_rows = jnp.stack([gain_attn, gain_mlp]).astype(jnp.float32)
    odd = lax.axis_index("fsdp") % 2
    gain_tile = jnp.concatenate([gain_rows * (1 - odd), gain_rows * odd], axis=1)
    gain_tile = jnp.pad(gain_tile, ((0, 8 - gain_tile.shape[0]), (0, 128 - gain_tile.shape[1])))
    normed1, gains, w_qkv, gu_mine = start_layer(
        tokens[0], gain_tile, qkv_parts.transpose(1, 0, 2), w_gate, w_up
    )
    w_gu = lax.all_gather(gu_mine, "fsdp", axis=0, tiled=True)
    grad_out = cotangent[0].astype(jnp.float32)
    grad_mlp = (RESIDUAL_MULT * grad_out).astype(bf16)

    block_rows = math.gcd(length, 256)
    qkv = dot_plain(normed1, w_qkv)
    qkv, grad_mlp = lax.optimization_barrier((qkv, grad_mlp))
    grad_mlp = lax.all_gather(grad_mlp, "ctx", axis=0, tiled=True)
    q, kv, mixed_heads, log_sum = attention_forward(qkv, tables, block_rows)
    hidden, normed2 = mlp_forward(dot_plain(mixed_heads, wo_mine).astype(bf16), tokens[0], gains)

    gate_up = dot_plain(normed2, w_gu)
    gate_pre, up_pre = gate_up[:, :ff_slice], gate_up[:, ff_slice:]
    sig_gate = jax.nn.sigmoid(gate_pre)
    silu_gate = gate_pre * sig_gate
    activ = (silu_gate * up_pre).astype(bf16)
    activ, gate_up = lax.optimization_barrier((activ, gate_up))
    gate_pre, up_pre = gate_up[:, :ff_slice], gate_up[:, ff_slice:]
    sig_gate = jax.nn.sigmoid(gate_pre)
    silu_gate = gate_pre * sig_gate
    out_terms, grad_mlp = lax.optimization_barrier(
        (dot_plain(activ, wd_mine).astype(bf16), grad_mlp)
    )
    branch = lax.psum_scatter(out_terms, "ctx", scatter_dimension=0, tiled=True)

    silu_slope = sig_gate * (1.0 + gate_pre * (1.0 - sig_gate))
    grad_act = dot_back(grad_mlp, wd_mine)
    grad_gu = jnp.concatenate(
        [(grad_act * up_pre * silu_slope).astype(bf16), (grad_act * silu_gate).astype(bf16)], axis=1
    )
    partial2, gu_terms, wd_terms = lax.optimization_barrier(
        (
            dot_back(grad_gu, w_gu).astype(bf16),
            dot_outer(normed2, grad_gu).astype(bf16),
            dot_outer(activ, grad_mlp).astype(bf16),
        )
    )
    grad_hidden, grad_g2, gu_back, grad_attn = mlp_backward(
        partial2, hidden, cotangent[0], gains, gu_terms.reshape(fsdp_size, -1, gu_terms.shape[1])
    )
    gu_back = return_columns(gu_back, ctx_size)
    wd_back = lax.psum_scatter(wd_terms, "fsdp", scatter_dimension=0, tiled=True)

    grad_mixed = dot_back(grad_attn, wo_mine).astype(bf16)
    wo_terms = dot_outer(mixed_heads, grad_attn).astype(bf16)
    grad_qkv = attention_backward(q, kv, grad_mixed, log_sum, tables, block_rows)
    partial1 = dot_back(grad_qkv, w_qkv).astype(bf16)
    qkv_terms = by_fsdp(dot_outer(normed1, grad_qkv).astype(bf16), ctx_size, fsdp_size)
    grad_inputs, gain_back, wo_back, qkv_back = finish_layer(
        partial1,
        tokens[0],
        grad_hidden,
        gains,
        grad_g2,
        wo_terms.reshape(fsdp_size, held_rows, model),
        qkv_terms.reshape(fsdp_size, ctx_size, held_rows, -1),
    )
    grad_inputs, wd_back, gu_back, branch = lax.optimization_barrier(
        (grad_inputs, wd_back, gu_back, branch)
    )
    output = (hidden + RESIDUAL_MULT * branch.astype(jnp.float32)).astype(bf16)[None]
    gain_back = jnp.where(odd == 0, gain_back[:2, :held_rows], gain_back[:2, held_rows:])

    def joined(parts):
        return parts.transpose(1, 0, 2).reshape(held_rows, -1).astype(jnp.float32)

    key_end = group_width + HD
    return (
        output,
        grad_inputs[None],
        gain_back[0],
        joined(qkv_back[:, :, :group_width]),
        joined(qkv_back[:, :, group_width:key_end]),
        joined(qkv_back[:, :, key_end:]),
        wo_back,
        gain_back[1],
        joined(gu_back[:, :, :ff_slice]),
        joined(gu_back[:, :, ff_slice:]),
        wd_back.astype(jnp.float32),
    )


def solution(mesh):
    in_specs = (
        P("fsdp", "ctx", None),
        P("fsdp", None),
        P("fsdp", "ctx", None),
        P(("ctx", "fsdp")),
        P(("ctx", "fsdp"), None),
        P(("ctx", "fsdp"), None),
        P(("ctx", "fsdp"), None),
        P(("ctx", "fsdp"), None),
        P(("ctx", "fsdp")),
        P(("ctx", "fsdp"), None),
        P(("ctx", "fsdp"), None),
        P(("ctx", "fsdp"), None),
    )
    out_specs = (
        P("fsdp", "ctx", None),
        P("fsdp", "ctx", None),
        P(("ctx", "fsdp")),
        P(("ctx", "fsdp"), None),
        P(("ctx", "fsdp"), None),
        P(("ctx", "fsdp"), None),
        P(("ctx", "fsdp"), None),
        P(("ctx", "fsdp")),
        P(("ctx", "fsdp"), None),
        P(("ctx", "fsdp"), None),
        P(("ctx", "fsdp"), None),
    )
    if mesh.shape["ctx"] != KVH or KVH != 4 * PAIR:
        return jax.shard_map(
            general_device, mesh=mesh, in_specs=in_specs, out_specs=out_specs, check_vma=False
        )

    return jax.shard_map(
        on_device, mesh=mesh, in_specs=in_specs, out_specs=out_specs, check_vma=False
    )
```

```python
import functools
import math

import jax
import jax.numpy as jnp
from jax import lax
from jax.experimental import pallas as pl
from jax.experimental.pallas import tpu as pltpu
from jax.sharding import PartitionSpec as P

H = 32
KVH = 8
HD = 64
FF = 8192


EPSILON = 1e-05
SCORE_SCALE = 1.0 / 64.0
RESIDUAL_MULT = 0.22
ROPE_BASE = 10000000.0
NEGATIVE = -1e30
MESH = pl.DeviceIdType.MESH
PAIR = 2
CHUNKS = 2
ANYWHERE = pl.BlockSpec(memory_space=pl.ANY)
LINK_COST = pl.CostEstimate(flops=0, bytes_accessed=150_000_000, transcendentals=0)


def doc_index(positions, starts):
    return jnp.sum((positions[:, None] >= starts[None, :]).astype(jnp.int32), axis=1) - 1


def rope_tables(positions):
    half_size = HD // 2
    frequency = ROPE_BASE ** (-(jnp.arange(half_size, dtype=jnp.float32) * 2.0) / HD)
    angles = positions.astype(jnp.float32)[:, None] * frequency[None, :]
    return (jnp.cos(angles), jnp.sin(angles))


def rotate(tensor, cos_table, sin_table, head_count):
    row_count = tensor.shape[0]
    by_head = tensor.reshape(row_count, head_count, HD)
    half_size = HD // 2
    first_half = by_head[..., :half_size]
    second_half = by_head[..., half_size:]
    cos_rows = cos_table[:, None, :]
    sin_rows = sin_table[:, None, :]
    turned = jnp.concatenate(
        [
            first_half * cos_rows - second_half * sin_rows,
            second_half * cos_rows + first_half * sin_rows,
        ],
        axis=-1,
    )
    return turned.reshape(row_count, head_count * HD)


def dot_plain(left, right):
    return jnp.dot(left, right, preferred_element_type=jnp.float32)


def dot_back(left, right):
    return lax.dot_general(
        left, right, (((1,), (1,)), ((), ())), preferred_element_type=jnp.float32
    )


def dot_outer(left, right):
    return lax.dot_general(
        left, right, (((0,), (0,)), ((), ())), preferred_element_type=jnp.float32
    )


def norm_back(grad_normed, unit_rows, inv_scale, gain_full):
    scaled = grad_normed * gain_full
    return inv_scale * (scaled - unit_rows * jnp.mean(scaled * unit_rows, axis=-1, keepdims=True))


def general_device(
    tokens,
    doc_lengths,
    cotangent,
    gain_attn,
    w_query,
    w_key,
    w_value,
    w_output,
    gain_mlp,
    w_gate,
    w_up,
    w_down,
):
    local_rows = tokens.shape[1]
    ctx_size = lax.axis_size("ctx")
    length = local_rows * ctx_size
    group_size = H // KVH
    offset = lax.axis_index("ctx") * local_rows
    positions = offset + jnp.arange(local_rows, dtype=jnp.int32)
    seq_lengths = doc_lengths[0]
    starts = jnp.cumsum(seq_lengths) - seq_lengths
    doc_ids = doc_index(positions, starts)
    last_pos = offset + local_rows - 1
    first_doc = doc_ids[0]
    cos_table, sin_table = rope_tables(positions)
    gain1, gain2, wq_full, wk_full, wv_full, wo_full = (
        lax.all_gather(gain_attn, ("ctx", "fsdp"), axis=0, tiled=True),
        lax.all_gather(gain_mlp, ("ctx", "fsdp"), axis=0, tiled=True),
        lax.all_gather(w_query, ("ctx", "fsdp"), axis=0, tiled=True),
        lax.all_gather(w_key, ("ctx", "fsdp"), axis=0, tiled=True),
        lax.all_gather(w_value, ("ctx", "fsdp"), axis=0, tiled=True),
        lax.all_gather(w_output, ("ctx", "fsdp"), axis=0, tiled=True),
    )
    gain1_f = gain1.astype(jnp.float32)
    gain2_f = gain2.astype(jnp.float32)
    inputs = tokens[0].astype(jnp.float32)
    inv_one = lax.rsqrt(jnp.mean(inputs * inputs, axis=-1, keepdims=True) + EPSILON)
    unit_one = inputs * inv_one
    normed1 = (unit_one * gain1_f).astype(jnp.bfloat16)
    queries = rotate(dot_plain(normed1, wq_full), cos_table, sin_table, H).astype(jnp.bfloat16)
    key_rot = rotate(dot_plain(normed1, wk_full), cos_table, sin_table, KVH).astype(jnp.bfloat16)
    values = dot_plain(normed1, wv_full).astype(jnp.bfloat16)
    grouped = queries.reshape(local_rows, KVH, group_size, HD)
    start_state = (
        jnp.full((local_rows, KVH, group_size), NEGATIVE, jnp.float32),
        jnp.zeros((local_rows, KVH, group_size), jnp.float32),
        jnp.zeros((local_rows, KVH, group_size, HD), jnp.float32),
    )
    running = start_state
    key_piece = lax.all_gather(key_rot, "ctx", axis=0, tiled=True)
    value_piece = lax.all_gather(values, "ctx", axis=0, tiled=True)
    piece_rows = key_piece.shape[0]
    attend_key_width = math.gcd(piece_rows, 512)
    block_count = piece_rows // attend_key_width

    def one_block(carried, index_block):
        block_start = index_block * attend_key_width
        key_blk = lax.dynamic_slice_in_dim(key_piece, block_start, attend_key_width, 0).reshape(
            attend_key_width, KVH, HD
        )
        value_blk = lax.dynamic_slice_in_dim(value_piece, block_start, attend_key_width, 0).reshape(
            attend_key_width, KVH, HD
        )
        key_pos = block_start + jnp.arange(attend_key_width, dtype=jnp.int32)
        key_docs = doc_index(key_pos, starts)
        skip_block = (block_start > last_pos) | (key_docs[attend_key_width - 1] < first_doc)

        def update(current):
            run_max, run_sum, accumulated = current
            scores = (
                jnp.einsum("qkgd,tkd->qkgt", grouped, key_blk, preferred_element_type=jnp.float32)
                * SCORE_SCALE
            )
            allowed = (key_docs[None, :] == doc_ids[:, None]) & (
                key_pos[None, :] <= positions[:, None]
            )
            allowed = allowed[:, None, None, :]
            masked = jnp.where(allowed, scores, NEGATIVE)
            new_max = jnp.maximum(run_max, jnp.max(masked, axis=-1))
            weights_exp = jnp.where(allowed, jnp.exp(masked - new_max[..., None]), 0.0)
            factor = jnp.exp(run_max - new_max)
            new_sum = run_sum * factor + jnp.sum(weights_exp, axis=-1)
            new_acc = accumulated * factor[..., None] + jnp.einsum(
                "qkgt,tkd->qkgd",
                weights_exp.astype(jnp.bfloat16),
                value_blk,
                preferred_element_type=jnp.float32,
            )
            return (new_max, new_sum, new_acc)

        return (lax.cond(skip_block, lambda unchanged: unchanged, update, carried), None)

    running, _ = lax.scan(one_block, running, jnp.arange(block_count))
    run_max, run_sum, accumulated = running
    attended = accumulated / run_sum[..., None]
    log_sum = run_max + jnp.log(run_sum)
    mixed_heads = attended.reshape(local_rows, H * HD).astype(jnp.bfloat16)
    hidden = inputs + RESIDUAL_MULT * dot_plain(mixed_heads, wo_full)
    inv_two = lax.rsqrt(jnp.mean(hidden * hidden, axis=-1, keepdims=True) + EPSILON)
    unit_two = hidden * inv_two
    normed2 = (unit_two * gain2_f).astype(jnp.bfloat16)
    wg_full, wu_full, wd_full = (
        lax.all_gather(w_gate, ("ctx", "fsdp"), axis=0, tiled=True),
        lax.all_gather(w_up, ("ctx", "fsdp"), axis=0, tiled=True),
        lax.all_gather(w_down, ("ctx", "fsdp"), axis=0, tiled=True),
    )
    gate_pre = dot_plain(normed2, wg_full)
    up_pre = dot_plain(normed2, wu_full)
    sig_gate = jax.nn.sigmoid(gate_pre)
    silu_gate = gate_pre * sig_gate
    activ = (silu_gate * up_pre).astype(jnp.bfloat16)
    result = hidden + RESIDUAL_MULT * dot_plain(activ, wd_full)
    output = result.astype(jnp.bfloat16)[None]
    grad_out = cotangent[0].astype(jnp.float32)
    grad_mlp = (RESIDUAL_MULT * grad_out).astype(jnp.bfloat16)
    silu_slope = sig_gate * (1.0 + gate_pre * (1.0 - sig_gate))
    wg_back, wu_back, wd_back = (
        lax.all_gather(w_gate, ("ctx", "fsdp"), axis=0, tiled=True),
        lax.all_gather(w_up, ("ctx", "fsdp"), axis=0, tiled=True),
        lax.all_gather(w_down, ("ctx", "fsdp"), axis=0, tiled=True),
    )
    grad_act = dot_back(grad_mlp, wd_back)
    grad_gate = (grad_act * up_pre * silu_slope).astype(jnp.bfloat16)
    grad_up = (grad_act * silu_gate).astype(jnp.bfloat16)
    grad_norm2 = dot_back(grad_gate, wg_back) + dot_back(grad_up, wu_back)
    left_cols = normed2
    gate_up_shard = lax.psum_scatter(
        jnp.concatenate([dot_outer(left_cols, grad_gate), dot_outer(left_cols, grad_up)], axis=1),
        ("ctx", "fsdp"),
        scatter_dimension=0,
        tiled=True,
    )
    wg_shard = gate_up_shard[:, :FF]
    wu_shard = gate_up_shard[:, FF:]
    left_cols = activ
    wd_shard = lax.psum_scatter(
        dot_outer(left_cols, grad_mlp), ("ctx", "fsdp"), scatter_dimension=0, tiled=True
    )
    grad_g2 = jnp.sum(grad_norm2 * unit_two, axis=0)
    grad_hidden = grad_out + norm_back(grad_norm2, unit_two, inv_two, gain2_f)
    grad_attn = (RESIDUAL_MULT * grad_hidden).astype(jnp.bfloat16)
    wq_back, wk_back, wv_back, wo_back = (
        lax.all_gather(w_query, ("ctx", "fsdp"), axis=0, tiled=True),
        lax.all_gather(w_key, ("ctx", "fsdp"), axis=0, tiled=True),
        lax.all_gather(w_value, ("ctx", "fsdp"), axis=0, tiled=True),
        lax.all_gather(w_output, ("ctx", "fsdp"), axis=0, tiled=True),
    )
    grad_wo = dot_outer(mixed_heads, grad_attn)
    grad_att = (
        dot_back(grad_attn, wo_back).astype(jnp.bfloat16).reshape(local_rows, KVH, group_size, HD)
    )
    row_delta = jnp.sum(grad_att.astype(jnp.float32) * attended, axis=-1)
    key_all, value_all = (
        lax.all_gather(key_rot, "ctx", axis=0, tiled=True),
        lax.all_gather(values, "ctx", axis=0, tiled=True),
    )
    key_width = math.gcd(length, 512)
    block_count = length // key_width

    def back_block(grad_query, index_block):
        block_start = index_block * key_width
        key_blk = lax.dynamic_slice_in_dim(key_all, block_start, key_width, 0).reshape(
            key_width, KVH, HD
        )
        value_blk = lax.dynamic_slice_in_dim(value_all, block_start, key_width, 0).reshape(
            key_width, KVH, HD
        )
        key_pos = block_start + jnp.arange(key_width, dtype=jnp.int32)
        key_docs = doc_index(key_pos, starts)
        skip_block = (block_start > last_pos) | (key_docs[key_width - 1] < first_doc)

        def compute(current):
            scores = (
                jnp.einsum("qkgd,tkd->qkgt", grouped, key_blk, preferred_element_type=jnp.float32)
                * SCORE_SCALE
            )
            allowed = (key_docs[None, :] == doc_ids[:, None]) & (
                key_pos[None, :] <= positions[:, None]
            )
            allowed = allowed[:, None, None, :]
            probs_blk = jnp.where(
                allowed, jnp.exp(jnp.where(allowed, scores, NEGATIVE) - log_sum[..., None]), 0.0
            )
            grad_probs = jnp.einsum(
                "qkgd,tkd->qkgt", grad_att, value_blk, preferred_element_type=jnp.float32
            )
            grad_scores = (probs_blk * (grad_probs - row_delta[..., None])).astype(jnp.bfloat16)
            new_query = (
                current
                + jnp.einsum(
                    "qkgt,tkd->qkgd", grad_scores, key_blk, preferred_element_type=jnp.float32
                )
                * SCORE_SCALE
            )
            grad_key = (
                jnp.einsum(
                    "qkgt,qkgd->tkd", grad_scores, grouped, preferred_element_type=jnp.float32
                )
                * SCORE_SCALE
            )
            grad_value = jnp.einsum(
                "qkgt,qkgd->tkd",
                probs_blk.astype(jnp.bfloat16),
                grad_att,
                preferred_element_type=jnp.float32,
            )
            return (
                new_query,
                (grad_key.reshape(key_width, KVH * HD), grad_value.reshape(key_width, KVH * HD)),
            )

        def nothing(current):
            zero_rows = jnp.zeros((key_width, KVH * HD), jnp.float32)
            return (current, (zero_rows, zero_rows))

        return lax.cond(skip_block, nothing, compute, grad_query)

    grad_query, key_terms = lax.scan(
        back_block,
        jnp.zeros((local_rows, KVH, group_size, HD), jnp.float32),
        jnp.arange(block_count),
    )
    key_term_all = key_terms[0].reshape(length, KVH * HD)
    value_term_all = key_terms[1].reshape(length, KVH * HD)
    grad_keys, grad_values = (
        lax.psum_scatter(
            key_term_all.astype(jnp.bfloat16), "ctx", scatter_dimension=0, tiled=True
        ).astype(jnp.float32),
        lax.psum_scatter(
            value_term_all.astype(jnp.bfloat16), "ctx", scatter_dimension=0, tiled=True
        ).astype(jnp.float32),
    )
    grad_q_pre = rotate(grad_query.reshape(local_rows, H * HD), cos_table, -sin_table, H).astype(
        jnp.bfloat16
    )
    grad_k_pre = rotate(grad_keys, cos_table, -sin_table, KVH).astype(jnp.bfloat16)
    grad_v_pre = grad_values.astype(jnp.bfloat16)
    grad_norm1 = (
        dot_back(grad_q_pre, wq_back)
        + dot_back(grad_k_pre, wk_back)
        + dot_back(grad_v_pre, wv_back)
    )
    grad_wq = dot_outer(normed1, grad_q_pre)
    grad_wk = dot_outer(normed1, grad_k_pre)
    grad_wv = dot_outer(normed1, grad_v_pre)
    grad_g1 = jnp.sum(grad_norm1 * unit_one, axis=0)
    grad_inputs = grad_hidden + norm_back(grad_norm1, unit_one, inv_one, gain1_f)
    g1_shard, g2_shard, wq_shard, wk_shard, wv_shard, wo_shard = (
        lax.psum_scatter(grad_g1, ("ctx", "fsdp"), scatter_dimension=0, tiled=True),
        lax.psum_scatter(grad_g2, ("ctx", "fsdp"), scatter_dimension=0, tiled=True),
        lax.psum_scatter(grad_wq, ("ctx", "fsdp"), scatter_dimension=0, tiled=True),
        lax.psum_scatter(grad_wk, ("ctx", "fsdp"), scatter_dimension=0, tiled=True),
        lax.psum_scatter(grad_wv, ("ctx", "fsdp"), scatter_dimension=0, tiled=True),
        lax.psum_scatter(grad_wo, ("ctx", "fsdp"), scatter_dimension=0, tiled=True),
    )
    return (
        output,
        grad_inputs[None],
        g1_shard,
        wq_shard,
        wk_shard,
        wv_shard,
        wo_shard,
        g2_shard,
        wg_shard,
        wu_shard,
        wd_shard,
    )


def rows_of(blocks):
    return blocks.reshape((-1,) + blocks.shape[2:])


def in_vmem(count):
    return [pl.BlockSpec(memory_space=pltpu.VMEM)] * count


def greet_line(barrier, ctx_at, line_at, line_size, fsdp_size=1):
    for j in range(1, fsdp_size):
        peer = (lax.axis_index("fsdp") + j) % fsdp_size
        pl.semaphore_signal(barrier, inc=1, device_id={"fsdp": peer}, device_id_type=MESH)
    other = ctx_at + 1 - 2 * (ctx_at % PAIR)
    pl.semaphore_signal(barrier, inc=1, device_id={"ctx": other}, device_id_type=MESH)

    @pl.when(line_at > 0)
    def _():
        pl.semaphore_signal(barrier, inc=1, device_id={"ctx": ctx_at - PAIR}, device_id_type=MESH)

    @pl.when(line_at < line_size - 1)
    def _():
        pl.semaphore_signal(barrier, inc=1, device_id={"ctx": ctx_at + PAIR}, device_id_type=MESH)

    last = line_size - 1
    neighbours = fsdp_size + (line_at + last - 1) // last + (2 * last - 1 - line_at) // last
    pl.semaphore_wait(barrier, neighbours)


def greet_all(barrier, me, count, fsdp_size):
    def greet(k, unused):
        target = (me + k) % count
        pl.semaphore_signal(
            barrier, inc=1, device_id=(target // fsdp_size, target % fsdp_size), device_id_type=MESH
        )
        return unused

    lax.fori_loop(1, count, greet, 0)
    pl.semaphore_wait(barrier, count - 1)


def gather_phase(line_size, x_ref, out_ref, send_sem, recv_sem, own_sem):
    me = lax.axis_index("ctx")
    line_at, pair_at = me // PAIR, me % PAIR
    rows = x_ref.shape[0]
    step = rows // CHUNKS

    def piece(block, part):
        return out_ref.at[pl.ds(pl.multiple_of(block * rows + part * step, step), step), :]

    def copy(block, part, way, own):
        slot = block * CHUNKS + part
        return pltpu.make_async_remote_copy(
            src_ref=x_ref.at[pl.ds(part * step, step), :] if own else piece(block, part),
            dst_ref=piece(block, part),
            send_sem=send_sem.at[way, slot],
            recv_sem=recv_sem.at[slot],
            device_id={"ctx": (me + 1 - 2 * pair_at, me + PAIR, me - PAIR)[way]},
            device_id_type=MESH,
        )

    def pass_on(block, part, upward, downward, own, act):
        if upward is not None:
            pl.when(upward)(lambda: act(copy(block, part, 1, own)))
        if downward is not None:
            pl.when(downward)(lambda: act(copy(block, part, 2, own)))
        act(copy(block, part, 0, own))

    def own_part(part, act):
        pass_on(me, part, line_at < line_size - 1, line_at > 0, True, act)

    def others(act, arrive, between):
        for distance in range(1, line_size):
            between(distance)
            for part in range(CHUNKS):

                @pl.when(line_at >= distance)
                def _():
                    block = me - PAIR * distance
                    arrive(block, part)
                    pass_on(block, part, line_at < line_size - 1, None, False, act)

                @pl.when(line_at + distance < line_size)
                def _():
                    block = me + PAIR * distance
                    arrive(block, part)
                    pass_on(block, part, None, line_at > 0, False, act)

    def start_own(part):
        own_part(part, lambda c: c.start())

    def finish(between=lambda distance: None):
        keep = pltpu.make_async_copy(
            x_ref, out_ref.at[pl.ds(pl.multiple_of(me * rows, rows), rows), :], own_sem
        )
        keep.start()
        others(
            lambda c: c.start(),
            lambda block, part: copy(block, part, 0, False).wait_recv(),
            between,
        )
        between(line_size)
        for place in range(line_size):
            for part in range(CHUNKS):
                copy(place * PAIR + 1 - pair_at, part, 0, False).wait_recv()
        for part in range(CHUNKS):
            own_part(part, lambda c: c.wait_send())
        others(lambda c: c.wait_send(), lambda block, part: None, lambda distance: None)
        keep.wait()

    return start_own, finish


def gather_scratch(ctx_size):
    return [
        pltpu.SemaphoreType.DMA((3, ctx_size * CHUNKS)),
        pltpu.SemaphoreType.DMA((ctx_size * CHUNKS,)),
        pltpu.SemaphoreType.DMA,
    ]


def scatter_phase(line_size, x_ref, sum_ref, near, below, above, near_send, near_sem, line_send, line_sem, emit, midway=lambda: None, between=lambda turn: None):
    me = lax.axis_index("ctx")
    line_at, pair_at = me // PAIR, me % PAIR
    rows = sum_ref.shape[0]
    step = rows // CHUNKS
    last = line_size - 1
    low = line_at // (line_size // 2)
    order = [k + (last - 2 * k) * (1 - low) for k in range(line_size // 2)]
    order += [line_at + 1 - 2 * (line_at % 2), line_at]

    def near_copy(place, part):
        start = (place * PAIR + 1 - pair_at) * rows + part * step
        return pltpu.make_async_remote_copy(
            src_ref=x_ref.at[pl.ds(pl.multiple_of(start, step), step), :],
            dst_ref=near.at[place, pl.ds(part * step, step), :],
            send_sem=near_send.at[place, part],
            recv_sem=near_sem.at[place, part],
            device_id={"ctx": me + 1 - 2 * pair_at},
            device_id_type=MESH,
        )

    def line_copy(place, part, up):
        part_rows = pl.ds(part * step, step)
        return pltpu.make_async_remote_copy(
            src_ref=near.at[place, part_rows, :],
            dst_ref=(below if up else above).at[place, part_rows, :],
            send_sem=line_send.at[place, part],
            recv_sem=line_sem.at[0 if up else 1, place, part],
            device_id={"ctx": me + PAIR if up else me - PAIR},
            device_id_type=MESH,
        )

    def mine(place, part):
        start = (place * PAIR + pair_at) * rows + part * step
        return x_ref[pl.ds(pl.multiple_of(start, step), step), :].astype(jnp.float32)

    for place in order:
        for part in range(CHUNKS):
            near_copy(place, part).start()

    for turn, place in enumerate(order[:-1]):
        between(turn)
        for part in range(CHUNKS):
            part_rows = pl.ds(part * step, step)
            near_copy(place, part).wait_recv()

            def send(up, waits, arrived):
                @pl.when(waits)
                def _():
                    line_copy(place, part, up).wait_recv()
                    near[place, part_rows, :] = (
                        mine(place, part)
                        + near[place, part_rows, :].astype(jnp.float32)
                        + arrived[place, part_rows, :].astype(jnp.float32)
                    ).astype(near.dtype)

                @pl.when(jnp.logical_not(waits))
                def _():
                    near[place, part_rows, :] = (
                        mine(place, part) + near[place, part_rows, :].astype(jnp.float32)
                    ).astype(near.dtype)

                line_copy(place, part, up).start()

            pl.when(place > line_at)(lambda: send(True, line_at > 0, below))
            pl.when(place < line_at)(lambda: send(False, line_at < last, above))

    midway()
    for part in range(CHUNKS):
        part_rows = pl.ds(part * step, step)
        near_copy(line_at, part).wait_recv()
        sum_ref[part_rows, :] = mine(line_at, part) + near[line_at, part_rows, :].astype(jnp.float32)

        @pl.when(line_at > 0)
        def _():
            line_copy(line_at, part, True).wait_recv()
            sum_ref[part_rows, :] += below[line_at, part_rows, :].astype(jnp.float32)

        @pl.when(line_at < last)
        def _():
            line_copy(line_at, part, False).wait_recv()
            sum_ref[part_rows, :] += above[line_at, part_rows, :].astype(jnp.float32)

        emit(part, slice(part * step, (part + 1) * step))

    def finish():
        for place in order:
            for part in range(CHUNKS):
                near_copy(place, part).wait_send()
        for place in order[:-1]:
            for part in range(CHUNKS):
                line_copy(place, part, True).wait_send()

    return finish


def scatter_scratch(ctx_size, rows, width):
    line_size = ctx_size // PAIR
    held = pltpu.VMEM((line_size, rows, width), jnp.bfloat16)
    return [
        held,
        held,
        held,
        pltpu.SemaphoreType.DMA((line_size, CHUNKS)),
        pltpu.SemaphoreType.DMA((line_size, CHUNKS)),
        pltpu.SemaphoreType.DMA((line_size, CHUNKS)),
        pltpu.SemaphoreType.DMA((2, line_size, CHUNKS)),
    ]


def swap_lanes(values, outer, inner):
    tile = 128
    half = tile // 2
    low = lax.broadcasted_iota(jnp.int32, (values.shape[0], tile), 1) < half
    placed = [None] * (outer * inner // 2)
    for first in range(0, outer, 2):
        for second in range(0, inner, 2):
            at = (first * inner + second) // 2
            one = values[:, at * tile : (at + 1) * tile]
            at += inner // 2
            two = values[:, at * tile : (at + 1) * tile]
            at = (second * outer + first) // 2
            placed[at] = jnp.where(low, one, pltpu.roll(two, half, 1))
            placed[at + outer // 2] = jnp.where(low, pltpu.roll(one, half, 1), two)
    return jnp.concatenate(placed, axis=1)


def start_kernel(
    ctx_size, fsdp_size, tokens_ref, tile_ref, parts_ref, out_ref, gains_ref, weight_ref,
    tiles, normed, tile_send, tile_recv, far_send, far_recv, near_send, near_recv, kept, *sems
):
    me_ctx, me_fsdp = lax.axis_index("ctx"), lax.axis_index("fsdp")
    count = ctx_size * fsdp_size
    me = me_ctx * fsdp_size + me_fsdp
    greet_all(pltpu.get_barrier_semaphore(), me, count, fsdp_size)

    def tile_copy(k, source):
        target = (me + k) % count
        return pltpu.make_async_remote_copy(
            src_ref=tile_ref,
            dst_ref=tiles.at[source],
            send_sem=tile_send.at[k],
            recv_sem=tile_recv.at[k],
            device_id=(target // fsdp_size, target % fsdp_size),
            device_id_type=MESH,
        )

    def start_tile(k, unused):
        tile_copy(k, me).start()
        return unused

    def finish_tile(k, unused):
        tile_copy(k, (me + count - k) % count).wait_recv()
        return unused

    lax.fori_loop(1, count, start_tile, 0)
    tiles[pl.ds(me, 1)] = tile_ref[...][None]

    def far_copy(k, source):
        target = (me_ctx + k) % ctx_size
        return pltpu.make_async_remote_copy(
            src_ref=parts_ref.at[target],
            dst_ref=weight_ref.at[source * fsdp_size + me_fsdp],
            send_sem=far_send.at[k],
            recv_sem=far_recv.at[k],
            device_id={"ctx": target},
            device_id_type=MESH,
        )

    def near_copy(k, j, fsdp_source):
        block = (me_ctx + ctx_size - k) % ctx_size * fsdp_size + fsdp_source
        return pltpu.make_async_remote_copy(
            src_ref=parts_ref.at[me_ctx] if k == 0 else weight_ref.at[block],
            dst_ref=weight_ref.at[block],
            send_sem=near_send.at[k, j],
            recv_sem=near_recv.at[k, j],
            device_id={"fsdp": (me_fsdp + j) % fsdp_size},
            device_id_type=MESH,
        )

    for k in range(1, ctx_size):
        far_copy(k, me_ctx).start()
    for j in range(1, fsdp_size):
        near_copy(0, j, me_fsdp).start()
    keep = pltpu.make_async_copy(parts_ref.at[me_ctx], weight_ref.at[me], kept)
    keep.start()

    rows, model = tokens_ref.shape
    lax.fori_loop(1, count, finish_tile, 0)
    held = model // count
    for pair in range(count // 2):
        cols = slice(pair * 2 * held, (pair + 1) * 2 * held)
        gains_ref[:, cols] = tiles[2 * pair] + tiles[2 * pair + 1]
    start_own, finish_gather = gather_phase(ctx_size // PAIR, normed, out_ref, *sems)
    step = rows // CHUNKS
    for part in range(CHUNKS):
        part_rows = slice(part * step, (part + 1) * step)
        values = tokens_ref[part_rows, :].astype(jnp.float32)
        scale = lax.rsqrt(jnp.mean(values * values, axis=-1, keepdims=True) + EPSILON)
        normed[part_rows, :] = (values * scale * gains_ref[0:1, :]).astype(normed.dtype)
        start_own(part)
    for k in range(1, ctx_size):
        far_copy(k, (me_ctx + ctx_size - k) % ctx_size).wait_recv()
        for j in range(1, fsdp_size):
            near_copy(k, j, me_fsdp).start()
    finish_gather()
    for k in range(ctx_size):
        for j in range(1, fsdp_size):
            near_copy(k, j, (me_fsdp + fsdp_size - j) % fsdp_size).wait_recv()
    for k in range(ctx_size):
        for j in range(1, fsdp_size):
            near_copy(k, j, me_fsdp).wait_send()
    for k in range(1, ctx_size):
        far_copy(k, me_ctx).wait_send()

    def sent_tile(k, unused):
        tile_copy(k, me).wait_send()
        return unused

    lax.fori_loop(1, count, sent_tile, 0)
    keep.wait()


def start_layer(tokens, tile, parts):
    ctx_size, fsdp_size = lax.axis_size("ctx"), lax.axis_size("fsdp")
    count = ctx_size * fsdp_size
    rows, model = tokens.shape
    dma = pltpu.SemaphoreType.DMA
    normed1, gains, weight = pl.pallas_call(
        functools.partial(start_kernel, ctx_size, fsdp_size),
        out_shape=(
            jax.ShapeDtypeStruct((ctx_size * rows, model), jnp.bfloat16),
            jax.ShapeDtypeStruct((8, model), jnp.float32),
            jax.ShapeDtypeStruct((count,) + parts.shape[1:], parts.dtype),
        ),
        in_specs=in_vmem(3),
        out_specs=(ANYWHERE, in_vmem(1)[0], ANYWHERE),
        scratch_shapes=[
            pltpu.VMEM((count, 8, 128), jnp.float32),
            pltpu.VMEM((rows, model), jnp.bfloat16),
            dma((count,)),
            dma((count,)),
            dma((ctx_size,)),
            dma((ctx_size,)),
            dma((ctx_size, fsdp_size)),
            dma((ctx_size, fsdp_size)),
            dma,
        ]
        + gather_scratch(ctx_size),
        compiler_params=pltpu.CompilerParams(
            collective_id=0, has_side_effects=True, vmem_limit_bytes=32 * 2**20
        ),
        cost_estimate=LINK_COST,
        name="start_layer",
    )(tokens, tile, parts)
    return normed1, gains, rows_of(weight)


def spread_phase(ctx_size, fsdp_size, gate_ref, up_ref, wide_ref, send, recv, side_send, side_recv, kept):
    me, me_fsdp = lax.axis_index("ctx"), lax.axis_index("fsdp")
    along = (me_fsdp + fsdp_size // 2) % fsdp_size
    beside = me_fsdp + 1 - 2 * (me_fsdp % 2)
    diagonal = (beside + fsdp_size // 2) % fsdp_size
    wide = gate_ref.shape[1] // ctx_size

    def part(which, target, source):
        cols = pl.ds(pl.multiple_of(target * wide, wide), wide)
        return (
            (gate_ref, up_ref)[which].at[:, cols],
            wide_ref.at[me_fsdp, source, :, which * wide : (which + 1) * wide],
        )

    def copy(which, k, source):
        target = (me + k) % ctx_size
        src, dst = part(which, target, source)
        return pltpu.make_async_remote_copy(
            src_ref=src,
            dst_ref=dst,
            send_sem=send.at[which, k],
            recv_sem=recv.at[which, k],
            device_id={"ctx": target},
            device_id_type=MESH,
        )

    def keep(which):
        return pltpu.make_async_copy(*part(which, me, me), kept.at[which])

    def side(way, k, rows_of_device):
        block = (rows_of_device, (me + ctx_size - k) % ctx_size)
        return pltpu.make_async_remote_copy(
            src_ref=wide_ref.at[block],
            dst_ref=wide_ref.at[block],
            send_sem=side_send.at[way, k],
            recv_sem=side_recv.at[way, k],
            device_id={"fsdp": along if way == 0 else beside},
            device_id_type=MESH,
        )

    def begin():
        for which in range(2):
            keep(which).start()
        for k in list(range(2, ctx_size, 2)) + list(range(1, ctx_size, 2)):
            for which in range(2):
                copy(which, k, me).start()

    def pass_on(k):
        for which in range(2):
            if k:
                copy(which, k, (me + ctx_size - k) % ctx_size).wait_recv()
            else:
                keep(which).wait()
        side(0, k, me_fsdp).start()
        side(1, k, me_fsdp).start()

    def relay(k):
        side(0, k, along).wait_recv()
        side(2, k, along).start()

    def finish():
        for k in range(ctx_size):
            side(1, k, beside).wait_recv()
            side(2, k, diagonal).wait_recv()
        for k in range(ctx_size):
            for way in range(3):
                side(way, k, me_fsdp).wait_send()
            if k:
                for which in range(2):
                    copy(which, k, me).wait_send()

    return begin, pass_on, relay, finish


def mlp_forward_kernel(
    ctx_size, fsdp_size, x_ref, tokens_ref, gains_ref, gate_ref, up_ref, hidden_ref, wide_ref, out_ref,
    sums, normed, wide_send, wide_recv, side_send, side_recv, kept, *sems
):
    line_size = ctx_size // PAIR
    me, me_fsdp = lax.axis_index("ctx"), lax.axis_index("fsdp")
    barrier = pltpu.get_barrier_semaphore()
    for k in range(1, ctx_size):
        pl.semaphore_signal(barrier, inc=1, device_id={"ctx": (me + k) % ctx_size}, device_id_type=MESH)
    for j in range(1, fsdp_size):
        pl.semaphore_signal(
            barrier, inc=1, device_id={"fsdp": (me_fsdp + j) % fsdp_size}, device_id_type=MESH
        )
    pl.semaphore_wait(barrier, ctx_size + fsdp_size - 2)
    start_own, finish_gather = gather_phase(line_size, normed, out_ref, *sems[7:])
    begin, pass_on, relay, finish_spread = spread_phase(
        ctx_size, fsdp_size, gate_ref, up_ref, wide_ref, wide_send, wide_recv, side_send, side_recv, kept
    )
    even = list(range(0, ctx_size, 2))
    odd = list(range(1, ctx_size, 2))

    def during_scatter(turn):
        if turn == 0:
            begin()
        if turn == 1:
            pass_on(0)
        if turn == 2:
            pass_on(2)

    def midway():
        for k in even[2:]:
            pass_on(k)
        for k in even[:2]:
            relay(k)

    def during_gather(distance):
        if distance == line_size - 2:
            for k in even[2:]:
                relay(k)
            for k in odd[:2]:
                pass_on(k)
        if distance == line_size - 1:
            for k in odd[2:]:
                pass_on(k)
        if distance == line_size:
            for k in odd:
                relay(k)

    def emit(part, rows):
        hidden = tokens_ref[rows, :].astype(jnp.float32) + RESIDUAL_MULT * sums[rows, :]
        hidden_ref[rows, :] = hidden
        scale = lax.rsqrt(jnp.mean(hidden * hidden, axis=-1, keepdims=True) + EPSILON)
        scaled = hidden * scale * gains_ref[1:2, :]
        normed[rows, :] = swap_lanes(scaled, ctx_size, fsdp_size).astype(normed.dtype)
        start_own(part)

    finish_scatter = scatter_phase(
        line_size, x_ref, sums, *sems[:7], emit, midway, during_scatter
    )
    finish_gather(during_gather)
    finish_spread()
    finish_scatter()


def mlp_backward_kernel(
    ctx_size, fsdp_size, x_ref, hidden_ref, grad_ref, gains_ref, terms_ref, grad_hidden_ref, grad_gain_ref,
    total_ref, out_ref, sums, normed, landing, side_send, side_recv, own_sem, *sems
):
    line_size = ctx_size // PAIR
    me, me_fsdp = lax.axis_index("ctx"), lax.axis_index("fsdp")
    greet_line(pltpu.get_barrier_semaphore(), me, me // PAIR, line_size, fsdp_size)

    def side_copy(j):
        target = (me_fsdp + j) % fsdp_size
        return pltpu.make_async_remote_copy(
            src_ref=terms_ref.at[target],
            dst_ref=landing.at[j],
            send_sem=side_send.at[j],
            recv_sem=side_recv.at[j],
            device_id={"fsdp": target},
            device_id_type=MESH,
        )

    own_copy = pltpu.make_async_copy(terms_ref.at[me_fsdp], landing.at[0], own_sem)
    for j in range(1, fsdp_size):
        side_copy(j).start()
    own_copy.start()
    start_own, finish_gather = gather_phase(line_size, normed, out_ref, *sems[7:])

    def emit(part, rows):
        grad_norm = swap_lanes(sums[rows, :], fsdp_size, ctx_size)
        hidden = hidden_ref[rows, :]
        scale = lax.rsqrt(jnp.mean(hidden * hidden, axis=-1, keepdims=True) + EPSILON)
        unit = hidden * scale
        grad_gain_ref[part : part + 1, :] = jnp.sum(grad_norm * unit, axis=0, keepdims=True)
        grad_hidden = grad_ref[rows, :].astype(jnp.float32) + norm_back(
            grad_norm, unit, scale, gains_ref[1:2, :]
        )
        grad_hidden_ref[rows, :] = grad_hidden
        normed[rows, :] = (RESIDUAL_MULT * grad_hidden).astype(normed.dtype)
        start_own(part)

    finish_scatter = scatter_phase(line_size, x_ref, sums, *sems[:7], emit)
    finish_gather()
    own_copy.wait()
    for j in range(1, fsdp_size):
        side_copy(j).wait_recv()
    step = 64

    def add(at, unused):
        rows = pl.ds(pl.multiple_of(at * step, step), step)
        total = landing[0, rows, :].astype(jnp.float32)
        for j in range(1, fsdp_size):
            total += landing[j, rows, :].astype(jnp.float32)
        total_ref[rows, :] = total.astype(total_ref.dtype)
        return unused

    lax.fori_loop(0, total_ref.shape[0] // step, add, 0)
    for j in range(1, fsdp_size):
        side_copy(j).wait_send()
    finish_scatter()


def scatter_gather(kernel, collective_id, extra_shapes, partial, *others, specs=(), out_specs=(), scratch=()):
    ctx_size, fsdp_size = lax.axis_size("ctx"), lax.axis_size("fsdp")
    rows, model = partial.shape[0] // ctx_size, partial.shape[1]
    return pl.pallas_call(
        functools.partial(kernel, ctx_size, fsdp_size),
        out_shape=extra_shapes + (jax.ShapeDtypeStruct(partial.shape, jnp.bfloat16),),
        in_specs=in_vmem(1 + len(others) - len(specs)) + list(specs),
        out_specs=tuple(in_vmem(len(extra_shapes) - len(out_specs))) + tuple(out_specs) + (ANYWHERE,),
        scratch_shapes=[pltpu.VMEM((rows, model), jnp.float32), pltpu.VMEM((rows, model), jnp.bfloat16)]
        + list(scratch)
        + scatter_scratch(ctx_size, rows, model)
        + gather_scratch(ctx_size),
        compiler_params=pltpu.CompilerParams(
            collective_id=collective_id, has_side_effects=True, vmem_limit_bytes=48 * 2**20
        ),
        cost_estimate=LINK_COST,
    )(partial, *others)


def mlp_forward(partial, tokens, gains, w_gate, w_up):
    ctx_size, fsdp_size = lax.axis_size("ctx"), lax.axis_size("fsdp")
    hidden = jax.ShapeDtypeStruct(tokens.shape, jnp.float32)
    slices = (fsdp_size, ctx_size, w_gate.shape[0], 2 * w_gate.shape[1] // ctx_size)
    dma = pltpu.SemaphoreType.DMA
    return scatter_gather(
        mlp_forward_kernel,
        1,
        (hidden, jax.ShapeDtypeStruct(slices, w_gate.dtype)),
        partial,
        tokens,
        gains,
        w_gate,
        w_up,
        out_specs=(ANYWHERE,),
        scratch=(
            dma((2, ctx_size)),
            dma((2, ctx_size)),
            dma((3, ctx_size)),
            dma((3, ctx_size)),
            dma((2,)),
        ),
    )


def mlp_backward(partial, hidden, grad_out, gains, terms):
    like = jax.ShapeDtypeStruct(hidden.shape, jnp.float32)
    gain = jax.ShapeDtypeStruct((CHUNKS, hidden.shape[1]), jnp.float32)
    return scatter_gather(
        mlp_backward_kernel,
        2,
        (like, gain, jax.ShapeDtypeStruct(terms.shape[1:], terms.dtype)),
        partial,
        hidden,
        grad_out,
        gains,
        terms,
        specs=(ANYWHERE,),
        scratch=(
            pltpu.VMEM(terms.shape, terms.dtype),
            pltpu.SemaphoreType.DMA((terms.shape[0],)),
            pltpu.SemaphoreType.DMA((terms.shape[0],)),
            pltpu.SemaphoreType.DMA,
        ),
    )


def finish_kernel(
    ctx_size, fsdp_size, x_ref, tokens_ref, grad_ref, gains_ref, gain2_ref, wo_ref, qkv_ref,
    grad_tokens_ref, gain_out_ref, wo_out_ref, qkv_out_ref,
    sums, gain1, tiles, arrived, wo_in, qkv_in, qkv_sum, tile_send, tile_recv, near_send, near_recv,
    far_send, far_recv, *sems
):
    line_size = ctx_size // PAIR
    me_ctx, me_fsdp = lax.axis_index("ctx"), lax.axis_index("fsdp")
    count = ctx_size * fsdp_size
    me = me_ctx * fsdp_size + me_fsdp
    greet_all(pltpu.get_barrier_semaphore(), me, count, fsdp_size)

    def near_copy(which, j):
        target = (me_fsdp + j) % fsdp_size
        terms, landing = ((wo_ref, wo_in), (qkv_ref, qkv_in))[which]
        return pltpu.make_async_remote_copy(
            src_ref=terms.at[target],
            dst_ref=landing.at[j],
            send_sem=near_send.at[which, j],
            recv_sem=near_recv.at[which, j],
            device_id={"fsdp": target},
            device_id_type=MESH,
        )

    def far_copy(k, source):
        target = (me_ctx + k) % ctx_size
        return pltpu.make_async_remote_copy(
            src_ref=qkv_sum.at[target],
            dst_ref=qkv_out_ref.at[source],
            send_sem=far_send.at[k],
            recv_sem=far_recv.at[k],
            device_id={"ctx": target},
            device_id_type=MESH,
        )

    def tile_copy(k, source):
        target = (me + k) % count
        return pltpu.make_async_remote_copy(
            src_ref=tiles.at[target // 2],
            dst_ref=arrived.at[source],
            send_sem=tile_send.at[k],
            recv_sem=tile_recv.at[k],
            device_id=(target // fsdp_size, target % fsdp_size),
            device_id_type=MESH,
        )

    def midway():
        for which, own, landing in ((1, qkv_ref, qkv_in), (0, wo_ref, wo_in)):
            for j in range(1, fsdp_size):
                near_copy(which, j).wait_recv()
            total = own[pl.ds(me_fsdp, 1)][0].astype(jnp.float32)
            for j in range(1, fsdp_size):
                total += landing[j].astype(jnp.float32)
            if which:
                qkv_sum[...] = total.astype(qkv_sum.dtype)
                for k in range(1, ctx_size):
                    far_copy(k, me_ctx).start()
                qkv_out_ref[pl.ds(me_ctx, 1)] = qkv_sum[pl.ds(me_ctx, 1)]
            else:
                wo_out_ref[...] = total

    def emit(part, rows):
        grad_norm = sums[rows, :]
        values = tokens_ref[rows, :].astype(jnp.float32)
        scale = lax.rsqrt(jnp.mean(values * values, axis=-1, keepdims=True) + EPSILON)
        unit = values * scale
        gain1[part : part + 1, :] = jnp.sum(grad_norm * unit, axis=0, keepdims=True)
        grad_tokens_ref[rows, :] = grad_ref[rows, :] + norm_back(
            grad_norm, unit, scale, gains_ref[0:1, :]
        )

    for which in (1, 0):
        for j in range(1, fsdp_size):
            near_copy(which, j).start()
    finish_scatter = scatter_phase(line_size, x_ref, sums, *sems, emit, midway)
    row = lax.broadcasted_iota(jnp.int32, (8, 128), 0)
    for pair in range(count // 2):
        cols = slice(pair * 128, (pair + 1) * 128)
        first = jnp.sum(gain1[:, cols], axis=0, keepdims=True)
        second = jnp.sum(gain2_ref[:, cols], axis=0, keepdims=True)
        tiles[pair] = jnp.where(row == 0, first, jnp.where(row == 1, second, 0.0))

    def start_tile(k, unused):
        tile_copy(k, me).start()
        return unused

    def finish_tile(k, unused):
        tile_copy(k, (me + count - k) % count).wait_recv()
        return unused

    def sent_tile(k, unused):
        tile_copy(k, me).wait_send()
        return unused

    lax.fori_loop(1, count, start_tile, 0)
    arrived[pl.ds(me, 1)] = tiles[pl.ds(me // 2, 1)]
    for k in range(1, ctx_size):
        far_copy(k, (me_ctx + ctx_size - k) % ctx_size).wait_recv()
    lax.fori_loop(1, count, finish_tile, 0)
    gain_out_ref[...] = jnp.sum(arrived[...], axis=0)
    finish_scatter()
    for which in range(2):
        for j in range(1, fsdp_size):
            near_copy(which, j).wait_send()
    for k in range(1, ctx_size):
        far_copy(k, me_ctx).wait_send()
    lax.fori_loop(1, count, sent_tile, 0)


def finish_layer(partial, tokens, grad_hidden, gains, grad_gain2, wo_terms, qkv_terms):
    ctx_size, fsdp_size = lax.axis_size("ctx"), lax.axis_size("fsdp")
    count = ctx_size * fsdp_size
    rows, model = tokens.shape
    dma = pltpu.SemaphoreType.DMA
    f32, bf16 = jnp.float32, jnp.bfloat16
    held, width = qkv_terms.shape[2:]
    return pl.pallas_call(
        functools.partial(finish_kernel, ctx_size, fsdp_size),
        out_shape=(
            jax.ShapeDtypeStruct((rows, model), f32),
            jax.ShapeDtypeStruct((8, 128), f32),
            jax.ShapeDtypeStruct(wo_terms.shape[1:], f32),
            jax.ShapeDtypeStruct((ctx_size, held, width), bf16),
        ),
        in_specs=in_vmem(7),
        out_specs=tuple(in_vmem(4)),
        scratch_shapes=[
            pltpu.VMEM((rows, model), f32),
            pltpu.VMEM((CHUNKS, model), f32),
            pltpu.VMEM((count // 2, 8, 128), f32),
            pltpu.VMEM((count, 8, 128), f32),
            pltpu.VMEM(wo_terms.shape, bf16),
            pltpu.VMEM(qkv_terms.shape, bf16),
            pltpu.VMEM((ctx_size, held, width), bf16),
            dma((count,)),
            dma((count,)),
            dma((2, fsdp_size)),
            dma((2, fsdp_size)),
            dma((ctx_size,)),
            dma((ctx_size,)),
        ]
        + scatter_scratch(ctx_size, rows, model),
        compiler_params=pltpu.CompilerParams(
            collective_id=3, has_side_effects=True, vmem_limit_bytes=40 * 2**20
        ),
        cost_estimate=LINK_COST,
        name="finish_layer",
    )(partial, tokens, grad_hidden, gains, grad_gain2, wo_terms, qkv_terms)


def swap_ctx(blocks):
    return lax.all_to_all(blocks, "ctx", split_axis=0, concat_axis=0, tiled=True)


def by_fsdp(grad, ctx_size, fsdp_size):
    parts = grad.reshape(ctx_size, fsdp_size, -1, grad.shape[-1]).transpose(1, 0, 2, 3)
    return rows_of(rows_of(parts))


def return_columns(terms, ctx_size):
    return swap_ctx(terms.reshape(ctx_size, -1, terms.shape[-1]))


def half_turn(values, sign_table):
    lane = lax.broadcasted_iota(jnp.int32, values.shape, 1)
    width = values.shape[1]
    quarter = HD // 2
    ahead = pltpu.roll(values, width - quarter, 1)
    behind = pltpu.roll(values, quarter, 1)
    return jnp.where(lane % HD < quarter, ahead, behind) * sign_table


def turn(values, cos_table, sign_table):
    copies = values.shape[1] // cos_table.shape[1]
    if copies > 1:
        cos_table = jnp.concatenate([cos_table] * copies, axis=1)
        sign_table = jnp.concatenate([sign_table] * copies, axis=1)
    return values * cos_table + half_turn(values, sign_table)


def attention_forward_kernel(
    block_rows, qkv_ref, cos_ref, sin_ref, doc_col_ref, doc_row_ref, q_ref, kv_ref, out_ref, lse_ref
):
    length = qkv_ref.shape[0]
    group = H // KVH
    width = group * HD
    q_ref[...] = turn(qkv_ref[:, :width], cos_ref[...], sin_ref[...]).astype(jnp.bfloat16)
    pair = qkv_ref[:, width:]
    lane = lax.broadcasted_iota(jnp.int32, pair.shape, 1)
    turned = turn(pair, cos_ref[...], sin_ref[...])
    kv_ref[...] = jnp.where(lane < HD, turned, pair).astype(jnp.bfloat16)
    for block in range(length // block_rows):
        rows = slice(block * block_rows, (block + 1) * block_rows)
        reach = (block + 1) * block_rows
        keys = kv_ref[:reach, :HD]
        values = kv_ref[:reach, HD:]
        query_at = block * block_rows + lax.broadcasted_iota(jnp.int32, (block_rows, reach), 0)
        key_at = lax.broadcasted_iota(jnp.int32, (block_rows, reach), 1)
        allowed = (doc_col_ref[rows, :] == doc_row_ref[:, :reach]) & (key_at <= query_at)
        for head in range(group):
            cols = slice(head * HD, (head + 1) * HD)
            scores = dot_back(q_ref[rows, cols], keys) * SCORE_SCALE
            masked = jnp.where(allowed, scores, NEGATIVE)
            top = jnp.max(masked, axis=1, keepdims=True)
            weights = jnp.where(allowed, jnp.exp(masked - top), 0.0)
            total = jnp.sum(weights, axis=1, keepdims=True)
            mixed = dot_plain(weights.astype(jnp.bfloat16), values)
            out_ref[rows, cols] = (mixed / total).astype(jnp.bfloat16)
            lse_ref[rows, head : head + 1] = top + jnp.log(total)


def attention_backward_kernel(
    block_rows, q_ref, kv_ref, do_ref, lse_ref, cos_ref, sin_ref, doc_col_ref, doc_row_ref, grad_ref, dq_ref, dkv_ref
):
    length = q_ref.shape[0]
    group = H // KVH
    width = group * HD
    dkv_ref[...] = jnp.zeros_like(dkv_ref)
    for block in range(length // block_rows):
        rows = slice(block * block_rows, (block + 1) * block_rows)
        reach = (block + 1) * block_rows
        keys = kv_ref[:reach, :HD]
        values = kv_ref[:reach, HD:]
        query_at = block * block_rows + lax.broadcasted_iota(jnp.int32, (block_rows, reach), 0)
        key_at = lax.broadcasted_iota(jnp.int32, (block_rows, reach), 1)
        allowed = (doc_col_ref[rows, :] == doc_row_ref[:, :reach]) & (key_at <= query_at)
        for head in range(group):
            cols = slice(head * HD, (head + 1) * HD)
            query = q_ref[rows, cols]
            grad_out = do_ref[rows, cols]
            scores = dot_back(query, keys) * SCORE_SCALE
            probs = jnp.where(
                allowed,
                jnp.exp(jnp.where(allowed, scores, NEGATIVE) - lse_ref[rows, head : head + 1]),
                0.0,
            )
            grad_probs = dot_back(grad_out, values)
            delta = jnp.sum(probs * grad_probs, axis=1, keepdims=True)
            grad_scores = (probs * (grad_probs - delta)).astype(jnp.bfloat16)
            dq_ref[rows, cols] = dot_plain(grad_scores, keys) * SCORE_SCALE
            dkv_ref[:reach, :HD] += dot_outer(grad_scores, query) * SCORE_SCALE
            dkv_ref[:reach, HD:] += dot_outer(probs.astype(jnp.bfloat16), grad_out)
    grad_ref[:, :width] = turn(dq_ref[...], cos_ref[...], -sin_ref[...]).astype(jnp.bfloat16)
    pair = dkv_ref[...]
    lane = lax.broadcasted_iota(jnp.int32, pair.shape, 1)
    turned = turn(pair, cos_ref[...], -sin_ref[...])
    grad_ref[:, width:] = jnp.where(lane < HD, turned, pair).astype(jnp.bfloat16)


def attention_forward(qkv, tables, block_rows):
    length = qkv.shape[0]
    width = (H // KVH) * HD
    return pl.pallas_call(
        functools.partial(attention_forward_kernel, block_rows),
        out_shape=(
            jax.ShapeDtypeStruct((length, width), jnp.bfloat16),
            jax.ShapeDtypeStruct((length, 2 * HD), jnp.bfloat16),
            jax.ShapeDtypeStruct((length, width), jnp.bfloat16),
            jax.ShapeDtypeStruct((length, H // KVH), jnp.float32),
        ),
        in_specs=in_vmem(5),
        out_specs=tuple(in_vmem(4)),
        compiler_params=pltpu.CompilerParams(vmem_limit_bytes=48 * 2**20),
        name="attend",
    )(qkv, *tables)


def attention_backward(q, kv, grad_out, lse, tables, block_rows):
    length, width = q.shape
    return pl.pallas_call(
        functools.partial(attention_backward_kernel, block_rows),
        out_shape=jax.ShapeDtypeStruct((length, width + 2 * HD), jnp.bfloat16),
        in_specs=in_vmem(8),
        out_specs=in_vmem(1)[0],
        scratch_shapes=[
            pltpu.VMEM((length, width), jnp.float32),
            pltpu.VMEM((length, 2 * HD), jnp.float32),
        ],
        compiler_params=pltpu.CompilerParams(vmem_limit_bytes=48 * 2**20),
        name="attend_back",
    )(q, kv, grad_out, lse, *tables)


def on_device(
    tokens,
    doc_lengths,
    cotangent,
    gain_attn,
    w_query,
    w_key,
    w_value,
    w_output,
    gain_mlp,
    w_gate,
    w_up,
    w_down,
):
    local_rows, model = tokens.shape[1:]
    ctx_size = lax.axis_size("ctx")
    fsdp_size = lax.axis_size("fsdp")
    length = local_rows * ctx_size
    group_width = (H // KVH) * HD
    ff_slice = FF // ctx_size
    held_rows = w_query.shape[0]
    bf16 = jnp.bfloat16

    positions = jnp.arange(length, dtype=jnp.int32)
    seq_lengths = doc_lengths[0]
    starts = jnp.cumsum(seq_lengths) - seq_lengths
    doc_ids = doc_index(positions, starts)
    cos_half, sin_half = rope_tables(positions)
    cos_table = jnp.concatenate([cos_half] * 4, axis=1)
    sin_table = jnp.concatenate([-sin_half, sin_half] * 2, axis=1)
    tables = (cos_table, sin_table, doc_ids[:, None], doc_ids[None, :])


    def by_slice(weight):
        return weight.reshape(held_rows, ctx_size, -1)

    qkv_parts = jnp.concatenate([by_slice(w_query), by_slice(w_key), by_slice(w_value)], axis=2)
    wo_mine = lax.all_gather(w_output, "fsdp", axis=0, tiled=True)
    wd_mine = lax.all_gather(w_down, "fsdp", axis=0, tiled=True)
    gain_rows = jnp.stack([gain_attn, gain_mlp]).astype(jnp.float32)
    odd = lax.axis_index("fsdp") % 2
    gain_tile = jnp.concatenate([gain_rows * (1 - odd), gain_rows * odd], axis=1)
    gain_tile = jnp.pad(gain_tile, ((0, 8 - gain_tile.shape[0]), (0, 128 - gain_tile.shape[1])))
    normed1, gains, w_qkv = start_layer(tokens[0], gain_tile, qkv_parts.transpose(1, 0, 2))
    grad_out = cotangent[0].astype(jnp.float32)
    grad_mlp = (RESIDUAL_MULT * grad_out).astype(bf16)

    block_rows = math.gcd(length, 256)
    normed1, grad_mlp = lax.optimization_barrier((normed1, grad_mlp))
    grad_mlp = lax.all_gather(grad_mlp, "ctx", axis=0, tiled=True)
    qkv = dot_plain(normed1, w_qkv)
    q, kv, mixed_heads, log_sum = attention_forward(qkv, tables, block_rows)
    hidden, w_gu, normed2 = mlp_forward(
        dot_plain(mixed_heads, wo_mine).astype(bf16), tokens[0], gains, w_gate, w_up
    )
    w_gu = rows_of(rows_of(w_gu))

    gate_up = dot_plain(normed2, w_gu)
    gate_pre, up_pre = gate_up[:, :ff_slice], gate_up[:, ff_slice:]
    sig_gate = jax.nn.sigmoid(gate_pre)
    silu_gate = gate_pre * sig_gate
    activ = (silu_gate * up_pre).astype(bf16)
    activ, gate_up = lax.optimization_barrier((activ, gate_up))
    gate_pre, up_pre = gate_up[:, :ff_slice], gate_up[:, ff_slice:]
    sig_gate = jax.nn.sigmoid(gate_pre)
    silu_gate = gate_pre * sig_gate
    out_terms, grad_mlp = lax.optimization_barrier(
        (dot_plain(activ, wd_mine).astype(bf16), grad_mlp)
    )
    branch = lax.psum_scatter(out_terms, "ctx", scatter_dimension=0, tiled=True)

    silu_slope = sig_gate * (1.0 + gate_pre * (1.0 - sig_gate))
    grad_act = dot_back(grad_mlp, wd_mine)
    grad_gu = jnp.concatenate(
        [(grad_act * up_pre * silu_slope).astype(bf16), (grad_act * silu_gate).astype(bf16)], axis=1
    )
    partial2, gu_terms, wd_terms = lax.optimization_barrier(
        (
            dot_back(grad_gu, w_gu).astype(bf16),
            dot_outer(normed2, grad_gu).astype(bf16),
            dot_outer(activ, grad_mlp).astype(bf16),
        )
    )
    grad_hidden, grad_g2, gu_back, grad_attn = mlp_backward(
        partial2, hidden, cotangent[0], gains, gu_terms.reshape(fsdp_size, -1, gu_terms.shape[1])
    )
    gu_back = return_columns(gu_back, ctx_size)
    wd_back = lax.psum_scatter(wd_terms, "fsdp", scatter_dimension=0, tiled=True)

    grad_mixed = dot_back(grad_attn, wo_mine).astype(bf16)
    wo_terms = dot_outer(mixed_heads, grad_attn).astype(bf16)
    grad_qkv = attention_backward(q, kv, grad_mixed, log_sum, tables, block_rows)
    partial1 = dot_back(grad_qkv, w_qkv).astype(bf16)
    qkv_terms = by_fsdp(dot_outer(normed1, grad_qkv).astype(bf16), ctx_size, fsdp_size)
    grad_inputs, gain_back, wo_back, qkv_back = finish_layer(
        partial1,
        tokens[0],
        grad_hidden,
        gains,
        grad_g2,
        wo_terms.reshape(fsdp_size, held_rows, model),
        qkv_terms.reshape(fsdp_size, ctx_size, held_rows, -1),
    )
    grad_inputs, wd_back, gu_back, branch = lax.optimization_barrier(
        (grad_inputs, wd_back, gu_back, branch)
    )
    output = (hidden + RESIDUAL_MULT * branch.astype(jnp.float32)).astype(bf16)[None]
    gain_back = jnp.where(odd == 0, gain_back[:2, :held_rows], gain_back[:2, held_rows:])

    def joined(parts):
        return parts.transpose(1, 0, 2).reshape(held_rows, -1).astype(jnp.float32)

    key_end = group_width + HD
    return (
        output,
        grad_inputs[None],
        gain_back[0],
        joined(qkv_back[:, :, :group_width]),
        joined(qkv_back[:, :, group_width:key_end]),
        joined(qkv_back[:, :, key_end:]),
        wo_back,
        gain_back[1],
        joined(gu_back[:, :, :ff_slice]),
        joined(gu_back[:, :, ff_slice:]),
        wd_back.astype(jnp.float32),
    )


def solution(mesh):
    in_specs = (
        P("fsdp", "ctx", None),
        P("fsdp", None),
        P("fsdp", "ctx", None),
        P(("ctx", "fsdp")),
        P(("ctx", "fsdp"), None),
        P(("ctx", "fsdp"), None),
        P(("ctx", "fsdp"), None),
        P(("ctx", "fsdp"), None),
        P(("ctx", "fsdp")),
        P(("ctx", "fsdp"), None),
        P(("ctx", "fsdp"), None),
        P(("ctx", "fsdp"), None),
    )
    out_specs = (
        P("fsdp", "ctx", None),
        P("fsdp", "ctx", None),
        P(("ctx", "fsdp")),
        P(("ctx", "fsdp"), None),
        P(("ctx", "fsdp"), None),
        P(("ctx", "fsdp"), None),
        P(("ctx", "fsdp"), None),
        P(("ctx", "fsdp")),
        P(("ctx", "fsdp"), None),
        P(("ctx", "fsdp"), None),
        P(("ctx", "fsdp"), None),
    )
    if mesh.shape["ctx"] != KVH or KVH != 4 * PAIR:
        return jax.shard_map(
            general_device, mesh=mesh, in_specs=in_specs, out_specs=out_specs, check_vma=False
        )

    return jax.shard_map(
        on_device, mesh=mesh, in_specs=in_specs, out_specs=out_specs, check_vma=False
    )
```

```python
import functools
import math

import jax
import jax.numpy as jnp
from jax import lax
from jax.experimental import pallas as pl
from jax.experimental.pallas import tpu as pltpu
from jax.sharding import PartitionSpec as P

H = 32
KVH = 8
HD = 64
FF = 8192


EPSILON = 1e-05
SCORE_SCALE = 1.0 / 64.0
RESIDUAL_MULT = 0.22
ROPE_BASE = 10000000.0
NEGATIVE = -1e30
MESH = pl.DeviceIdType.MESH
PAIR = 2
CHUNKS = 2
ANYWHERE = pl.BlockSpec(memory_space=pl.ANY)
LINK_COST = pl.CostEstimate(flops=0, bytes_accessed=150_000_000, transcendentals=0)


def doc_index(positions, starts):
    return jnp.sum((positions[:, None] >= starts[None, :]).astype(jnp.int32), axis=1) - 1


def rope_tables(positions):
    half_size = HD // 2
    frequency = ROPE_BASE ** (-(jnp.arange(half_size, dtype=jnp.float32) * 2.0) / HD)
    angles = positions.astype(jnp.float32)[:, None] * frequency[None, :]
    return (jnp.cos(angles), jnp.sin(angles))


def rotate(tensor, cos_table, sin_table, head_count):
    row_count = tensor.shape[0]
    by_head = tensor.reshape(row_count, head_count, HD)
    half_size = HD // 2
    first_half = by_head[..., :half_size]
    second_half = by_head[..., half_size:]
    cos_rows = cos_table[:, None, :]
    sin_rows = sin_table[:, None, :]
    turned = jnp.concatenate(
        [
            first_half * cos_rows - second_half * sin_rows,
            second_half * cos_rows + first_half * sin_rows,
        ],
        axis=-1,
    )
    return turned.reshape(row_count, head_count * HD)


def dot_plain(left, right):
    return jnp.dot(left, right, preferred_element_type=jnp.float32)


def dot_back(left, right):
    return lax.dot_general(
        left, right, (((1,), (1,)), ((), ())), preferred_element_type=jnp.float32
    )


def dot_outer(left, right):
    return lax.dot_general(
        left, right, (((0,), (0,)), ((), ())), preferred_element_type=jnp.float32
    )


def norm_back(grad_normed, unit_rows, inv_scale, gain_full):
    scaled = grad_normed * gain_full
    return inv_scale * (scaled - unit_rows * jnp.mean(scaled * unit_rows, axis=-1, keepdims=True))


def general_device(
    tokens,
    doc_lengths,
    cotangent,
    gain_attn,
    w_query,
    w_key,
    w_value,
    w_output,
    gain_mlp,
    w_gate,
    w_up,
    w_down,
):
    local_rows = tokens.shape[1]
    ctx_size = lax.axis_size("ctx")
    length = local_rows * ctx_size
    group_size = H // KVH
    offset = lax.axis_index("ctx") * local_rows
    positions = offset + jnp.arange(local_rows, dtype=jnp.int32)
    seq_lengths = doc_lengths[0]
    starts = jnp.cumsum(seq_lengths) - seq_lengths
    doc_ids = doc_index(positions, starts)
    last_pos = offset + local_rows - 1
    first_doc = doc_ids[0]
    cos_table, sin_table = rope_tables(positions)
    gain1, gain2, wq_full, wk_full, wv_full, wo_full = (
        lax.all_gather(gain_attn, ("ctx", "fsdp"), axis=0, tiled=True),
        lax.all_gather(gain_mlp, ("ctx", "fsdp"), axis=0, tiled=True),
        lax.all_gather(w_query, ("ctx", "fsdp"), axis=0, tiled=True),
        lax.all_gather(w_key, ("ctx", "fsdp"), axis=0, tiled=True),
        lax.all_gather(w_value, ("ctx", "fsdp"), axis=0, tiled=True),
        lax.all_gather(w_output, ("ctx", "fsdp"), axis=0, tiled=True),
    )
    gain1_f = gain1.astype(jnp.float32)
    gain2_f = gain2.astype(jnp.float32)
    inputs = tokens[0].astype(jnp.float32)
    inv_one = lax.rsqrt(jnp.mean(inputs * inputs, axis=-1, keepdims=True) + EPSILON)
    unit_one = inputs * inv_one
    normed1 = (unit_one * gain1_f).astype(jnp.bfloat16)
    queries = rotate(dot_plain(normed1, wq_full), cos_table, sin_table, H).astype(jnp.bfloat16)
    key_rot = rotate(dot_plain(normed1, wk_full), cos_table, sin_table, KVH).astype(jnp.bfloat16)
    values = dot_plain(normed1, wv_full).astype(jnp.bfloat16)
    grouped = queries.reshape(local_rows, KVH, group_size, HD)
    start_state = (
        jnp.full((local_rows, KVH, group_size), NEGATIVE, jnp.float32),
        jnp.zeros((local_rows, KVH, group_size), jnp.float32),
        jnp.zeros((local_rows, KVH, group_size, HD), jnp.float32),
    )
    running = start_state
    key_piece = lax.all_gather(key_rot, "ctx", axis=0, tiled=True)
    value_piece = lax.all_gather(values, "ctx", axis=0, tiled=True)
    piece_rows = key_piece.shape[0]
    attend_key_width = math.gcd(piece_rows, 512)
    block_count = piece_rows // attend_key_width

    def one_block(carried, index_block):
        block_start = index_block * attend_key_width
        key_blk = lax.dynamic_slice_in_dim(key_piece, block_start, attend_key_width, 0).reshape(
            attend_key_width, KVH, HD
        )
        value_blk = lax.dynamic_slice_in_dim(value_piece, block_start, attend_key_width, 0).reshape(
            attend_key_width, KVH, HD
        )
        key_pos = block_start + jnp.arange(attend_key_width, dtype=jnp.int32)
        key_docs = doc_index(key_pos, starts)
        skip_block = (block_start > last_pos) | (key_docs[attend_key_width - 1] < first_doc)

        def update(current):
            run_max, run_sum, accumulated = current
            scores = (
                jnp.einsum("qkgd,tkd->qkgt", grouped, key_blk, preferred_element_type=jnp.float32)
                * SCORE_SCALE
            )
            allowed = (key_docs[None, :] == doc_ids[:, None]) & (
                key_pos[None, :] <= positions[:, None]
            )
            allowed = allowed[:, None, None, :]
            masked = jnp.where(allowed, scores, NEGATIVE)
            new_max = jnp.maximum(run_max, jnp.max(masked, axis=-1))
            weights_exp = jnp.where(allowed, jnp.exp(masked - new_max[..., None]), 0.0)
            factor = jnp.exp(run_max - new_max)
            new_sum = run_sum * factor + jnp.sum(weights_exp, axis=-1)
            new_acc = accumulated * factor[..., None] + jnp.einsum(
                "qkgt,tkd->qkgd",
                weights_exp.astype(jnp.bfloat16),
                value_blk,
                preferred_element_type=jnp.float32,
            )
            return (new_max, new_sum, new_acc)

        return (lax.cond(skip_block, lambda unchanged: unchanged, update, carried), None)

    running, _ = lax.scan(one_block, running, jnp.arange(block_count))
    run_max, run_sum, accumulated = running
    attended = accumulated / run_sum[..., None]
    log_sum = run_max + jnp.log(run_sum)
    mixed_heads = attended.reshape(local_rows, H * HD).astype(jnp.bfloat16)
    hidden = inputs + RESIDUAL_MULT * dot_plain(mixed_heads, wo_full)
    inv_two = lax.rsqrt(jnp.mean(hidden * hidden, axis=-1, keepdims=True) + EPSILON)
    unit_two = hidden * inv_two
    normed2 = (unit_two * gain2_f).astype(jnp.bfloat16)
    wg_full, wu_full, wd_full = (
        lax.all_gather(w_gate, ("ctx", "fsdp"), axis=0, tiled=True),
        lax.all_gather(w_up, ("ctx", "fsdp"), axis=0, tiled=True),
        lax.all_gather(w_down, ("ctx", "fsdp"), axis=0, tiled=True),
    )
    gate_pre = dot_plain(normed2, wg_full)
    up_pre = dot_plain(normed2, wu_full)
    sig_gate = jax.nn.sigmoid(gate_pre)
    silu_gate = gate_pre * sig_gate
    activ = (silu_gate * up_pre).astype(jnp.bfloat16)
    result = hidden + RESIDUAL_MULT * dot_plain(activ, wd_full)
    output = result.astype(jnp.bfloat16)[None]
    grad_out = cotangent[0].astype(jnp.float32)
    grad_mlp = (RESIDUAL_MULT * grad_out).astype(jnp.bfloat16)
    silu_slope = sig_gate * (1.0 + gate_pre * (1.0 - sig_gate))
    wg_back, wu_back, wd_back = (
        lax.all_gather(w_gate, ("ctx", "fsdp"), axis=0, tiled=True),
        lax.all_gather(w_up, ("ctx", "fsdp"), axis=0, tiled=True),
        lax.all_gather(w_down, ("ctx", "fsdp"), axis=0, tiled=True),
    )
    grad_act = dot_back(grad_mlp, wd_back)
    grad_gate = (grad_act * up_pre * silu_slope).astype(jnp.bfloat16)
    grad_up = (grad_act * silu_gate).astype(jnp.bfloat16)
    grad_norm2 = dot_back(grad_gate, wg_back) + dot_back(grad_up, wu_back)
    left_cols = normed2
    gate_up_shard = lax.psum_scatter(
        jnp.concatenate([dot_outer(left_cols, grad_gate), dot_outer(left_cols, grad_up)], axis=1),
        ("ctx", "fsdp"),
        scatter_dimension=0,
        tiled=True,
    )
    wg_shard = gate_up_shard[:, :FF]
    wu_shard = gate_up_shard[:, FF:]
    left_cols = activ
    wd_shard = lax.psum_scatter(
        dot_outer(left_cols, grad_mlp), ("ctx", "fsdp"), scatter_dimension=0, tiled=True
    )
    grad_g2 = jnp.sum(grad_norm2 * unit_two, axis=0)
    grad_hidden = grad_out + norm_back(grad_norm2, unit_two, inv_two, gain2_f)
    grad_attn = (RESIDUAL_MULT * grad_hidden).astype(jnp.bfloat16)
    wq_back, wk_back, wv_back, wo_back = (
        lax.all_gather(w_query, ("ctx", "fsdp"), axis=0, tiled=True),
        lax.all_gather(w_key, ("ctx", "fsdp"), axis=0, tiled=True),
        lax.all_gather(w_value, ("ctx", "fsdp"), axis=0, tiled=True),
        lax.all_gather(w_output, ("ctx", "fsdp"), axis=0, tiled=True),
    )
    grad_wo = dot_outer(mixed_heads, grad_attn)
    grad_att = (
        dot_back(grad_attn, wo_back).astype(jnp.bfloat16).reshape(local_rows, KVH, group_size, HD)
    )
    row_delta = jnp.sum(grad_att.astype(jnp.float32) * attended, axis=-1)
    key_all, value_all = (
        lax.all_gather(key_rot, "ctx", axis=0, tiled=True),
        lax.all_gather(values, "ctx", axis=0, tiled=True),
    )
    key_width = math.gcd(length, 512)
    block_count = length // key_width

    def back_block(grad_query, index_block):
        block_start = index_block * key_width
        key_blk = lax.dynamic_slice_in_dim(key_all, block_start, key_width, 0).reshape(
            key_width, KVH, HD
        )
        value_blk = lax.dynamic_slice_in_dim(value_all, block_start, key_width, 0).reshape(
            key_width, KVH, HD
        )
        key_pos = block_start + jnp.arange(key_width, dtype=jnp.int32)
        key_docs = doc_index(key_pos, starts)
        skip_block = (block_start > last_pos) | (key_docs[key_width - 1] < first_doc)

        def compute(current):
            scores = (
                jnp.einsum("qkgd,tkd->qkgt", grouped, key_blk, preferred_element_type=jnp.float32)
                * SCORE_SCALE
            )
            allowed = (key_docs[None, :] == doc_ids[:, None]) & (
                key_pos[None, :] <= positions[:, None]
            )
            allowed = allowed[:, None, None, :]
            probs_blk = jnp.where(
                allowed, jnp.exp(jnp.where(allowed, scores, NEGATIVE) - log_sum[..., None]), 0.0
            )
            grad_probs = jnp.einsum(
                "qkgd,tkd->qkgt", grad_att, value_blk, preferred_element_type=jnp.float32
            )
            grad_scores = (probs_blk * (grad_probs - row_delta[..., None])).astype(jnp.bfloat16)
            new_query = (
                current
                + jnp.einsum(
                    "qkgt,tkd->qkgd", grad_scores, key_blk, preferred_element_type=jnp.float32
                )
                * SCORE_SCALE
            )
            grad_key = (
                jnp.einsum(
                    "qkgt,qkgd->tkd", grad_scores, grouped, preferred_element_type=jnp.float32
                )
                * SCORE_SCALE
            )
            grad_value = jnp.einsum(
                "qkgt,qkgd->tkd",
                probs_blk.astype(jnp.bfloat16),
                grad_att,
                preferred_element_type=jnp.float32,
            )
            return (
                new_query,
                (grad_key.reshape(key_width, KVH * HD), grad_value.reshape(key_width, KVH * HD)),
            )

        def nothing(current):
            zero_rows = jnp.zeros((key_width, KVH * HD), jnp.float32)
            return (current, (zero_rows, zero_rows))

        return lax.cond(skip_block, nothing, compute, grad_query)

    grad_query, key_terms = lax.scan(
        back_block,
        jnp.zeros((local_rows, KVH, group_size, HD), jnp.float32),
        jnp.arange(block_count),
    )
    key_term_all = key_terms[0].reshape(length, KVH * HD)
    value_term_all = key_terms[1].reshape(length, KVH * HD)
    grad_keys, grad_values = (
        lax.psum_scatter(
            key_term_all.astype(jnp.bfloat16), "ctx", scatter_dimension=0, tiled=True
        ).astype(jnp.float32),
        lax.psum_scatter(
            value_term_all.astype(jnp.bfloat16), "ctx", scatter_dimension=0, tiled=True
        ).astype(jnp.float32),
    )
    grad_q_pre = rotate(grad_query.reshape(local_rows, H * HD), cos_table, -sin_table, H).astype(
        jnp.bfloat16
    )
    grad_k_pre = rotate(grad_keys, cos_table, -sin_table, KVH).astype(jnp.bfloat16)
    grad_v_pre = grad_values.astype(jnp.bfloat16)
    grad_norm1 = (
        dot_back(grad_q_pre, wq_back)
        + dot_back(grad_k_pre, wk_back)
        + dot_back(grad_v_pre, wv_back)
    )
    grad_wq = dot_outer(normed1, grad_q_pre)
    grad_wk = dot_outer(normed1, grad_k_pre)
    grad_wv = dot_outer(normed1, grad_v_pre)
    grad_g1 = jnp.sum(grad_norm1 * unit_one, axis=0)
    grad_inputs = grad_hidden + norm_back(grad_norm1, unit_one, inv_one, gain1_f)
    g1_shard, g2_shard, wq_shard, wk_shard, wv_shard, wo_shard = (
        lax.psum_scatter(grad_g1, ("ctx", "fsdp"), scatter_dimension=0, tiled=True),
        lax.psum_scatter(grad_g2, ("ctx", "fsdp"), scatter_dimension=0, tiled=True),
        lax.psum_scatter(grad_wq, ("ctx", "fsdp"), scatter_dimension=0, tiled=True),
        lax.psum_scatter(grad_wk, ("ctx", "fsdp"), scatter_dimension=0, tiled=True),
        lax.psum_scatter(grad_wv, ("ctx", "fsdp"), scatter_dimension=0, tiled=True),
        lax.psum_scatter(grad_wo, ("ctx", "fsdp"), scatter_dimension=0, tiled=True),
    )
    return (
        output,
        grad_inputs[None],
        g1_shard,
        wq_shard,
        wk_shard,
        wv_shard,
        wo_shard,
        g2_shard,
        wg_shard,
        wu_shard,
        wd_shard,
    )


def rows_of(blocks):
    return blocks.reshape((-1,) + blocks.shape[2:])


def in_vmem(count):
    return [pl.BlockSpec(memory_space=pltpu.VMEM)] * count


def greet_line(barrier, ctx_at, line_at, line_size, fsdp_size=1):
    for j in range(1, fsdp_size):
        peer = (lax.axis_index("fsdp") + j) % fsdp_size
        pl.semaphore_signal(barrier, inc=1, device_id={"fsdp": peer}, device_id_type=MESH)
    other = ctx_at + 1 - 2 * (ctx_at % PAIR)
    pl.semaphore_signal(barrier, inc=1, device_id={"ctx": other}, device_id_type=MESH)

    @pl.when(line_at > 0)
    def _():
        pl.semaphore_signal(barrier, inc=1, device_id={"ctx": ctx_at - PAIR}, device_id_type=MESH)

    @pl.when(line_at < line_size - 1)
    def _():
        pl.semaphore_signal(barrier, inc=1, device_id={"ctx": ctx_at + PAIR}, device_id_type=MESH)

    last = line_size - 1
    neighbours = fsdp_size + (line_at + last - 1) // last + (2 * last - 1 - line_at) // last
    pl.semaphore_wait(barrier, neighbours)


def greet_all(barrier, me, count, fsdp_size):
    def greet(k, unused):
        target = (me + k) % count
        pl.semaphore_signal(
            barrier, inc=1, device_id=(target // fsdp_size, target % fsdp_size), device_id_type=MESH
        )
        return unused

    lax.fori_loop(1, count, greet, 0)
    pl.semaphore_wait(barrier, count - 1)


def gather_phase(line_size, x_ref, out_ref, send_sem, recv_sem, own_sem):
    me = lax.axis_index("ctx")
    line_at, pair_at = me // PAIR, me % PAIR
    rows = x_ref.shape[0]
    step = rows // CHUNKS

    def piece(block, part):
        return out_ref.at[pl.ds(pl.multiple_of(block * rows + part * step, step), step), :]

    def copy(block, part, way, own):
        slot = block * CHUNKS + part
        return pltpu.make_async_remote_copy(
            src_ref=x_ref.at[pl.ds(part * step, step), :] if own else piece(block, part),
            dst_ref=piece(block, part),
            send_sem=send_sem.at[way, slot],
            recv_sem=recv_sem.at[slot],
            device_id={"ctx": (me + 1 - 2 * pair_at, me + PAIR, me - PAIR)[way]},
            device_id_type=MESH,
        )

    def pass_on(block, part, upward, downward, own, act):
        if upward is not None:
            pl.when(upward)(lambda: act(copy(block, part, 1, own)))
        if downward is not None:
            pl.when(downward)(lambda: act(copy(block, part, 2, own)))
        act(copy(block, part, 0, own))

    def own_part(part, act):
        pass_on(me, part, line_at < line_size - 1, line_at > 0, True, act)

    def others(act, arrive, between):
        for distance in range(1, line_size):
            between(distance)
            for part in range(CHUNKS):

                @pl.when(line_at >= distance)
                def _():
                    block = me - PAIR * distance
                    arrive(block, part)
                    pass_on(block, part, line_at < line_size - 1, None, False, act)

                @pl.when(line_at + distance < line_size)
                def _():
                    block = me + PAIR * distance
                    arrive(block, part)
                    pass_on(block, part, None, line_at > 0, False, act)

    def start_own(part):
        own_part(part, lambda c: c.start())

    def finish(between=lambda distance: None):
        keep = pltpu.make_async_copy(
            x_ref, out_ref.at[pl.ds(pl.multiple_of(me * rows, rows), rows), :], own_sem
        )
        keep.start()
        others(
            lambda c: c.start(),
            lambda block, part: copy(block, part, 0, False).wait_recv(),
            between,
        )
        between(line_size)
        for place in range(line_size):
            for part in range(CHUNKS):
                copy(place * PAIR + 1 - pair_at, part, 0, False).wait_recv()
        for part in range(CHUNKS):
            own_part(part, lambda c: c.wait_send())
        others(lambda c: c.wait_send(), lambda block, part: None, lambda distance: None)
        keep.wait()

    return start_own, finish


def gather_scratch(ctx_size):
    return [
        pltpu.SemaphoreType.DMA((3, ctx_size * CHUNKS)),
        pltpu.SemaphoreType.DMA((ctx_size * CHUNKS,)),
        pltpu.SemaphoreType.DMA,
    ]


def scatter_phase(line_size, x_ref, sum_ref, near, below, above, near_send, near_sem, line_send, line_sem, emit, midway=lambda: None, between=lambda turn: None):
    me = lax.axis_index("ctx")
    line_at, pair_at = me // PAIR, me % PAIR
    rows = sum_ref.shape[0]
    step = rows // CHUNKS
    last = line_size - 1
    low = line_at // (line_size // 2)
    order = [k + (last - 2 * k) * (1 - low) for k in range(line_size // 2)]
    order += [line_at + 1 - 2 * (line_at % 2), line_at]

    def near_copy(place, part):
        start = (place * PAIR + 1 - pair_at) * rows + part * step
        return pltpu.make_async_remote_copy(
            src_ref=x_ref.at[pl.ds(pl.multiple_of(start, step), step), :],
            dst_ref=near.at[place, pl.ds(part * step, step), :],
            send_sem=near_send.at[place, part],
            recv_sem=near_sem.at[place, part],
            device_id={"ctx": me + 1 - 2 * pair_at},
            device_id_type=MESH,
        )

    def line_copy(place, part, up):
        part_rows = pl.ds(part * step, step)
        return pltpu.make_async_remote_copy(
            src_ref=near.at[place, part_rows, :],
            dst_ref=(below if up else above).at[place, part_rows, :],
            send_sem=line_send.at[place, part],
            recv_sem=line_sem.at[0 if up else 1, place, part],
            device_id={"ctx": me + PAIR if up else me - PAIR},
            device_id_type=MESH,
        )

    def mine(place, part):
        start = (place * PAIR + pair_at) * rows + part * step
        return x_ref[pl.ds(pl.multiple_of(start, step), step), :].astype(jnp.float32)

    for place in order:
        for part in range(CHUNKS):
            near_copy(place, part).start()

    for turn, place in enumerate(order[:-1]):
        between(turn)
        for part in range(CHUNKS):
            part_rows = pl.ds(part * step, step)
            near_copy(place, part).wait_recv()

            def send(up, waits, arrived):
                @pl.when(waits)
                def _():
                    line_copy(place, part, up).wait_recv()
                    near[place, part_rows, :] = (
                        mine(place, part)
                        + near[place, part_rows, :].astype(jnp.float32)
                        + arrived[place, part_rows, :].astype(jnp.float32)
                    ).astype(near.dtype)

                @pl.when(jnp.logical_not(waits))
                def _():
                    near[place, part_rows, :] = (
                        mine(place, part) + near[place, part_rows, :].astype(jnp.float32)
                    ).astype(near.dtype)

                line_copy(place, part, up).start()

            pl.when(place > line_at)(lambda: send(True, line_at > 0, below))
            pl.when(place < line_at)(lambda: send(False, line_at < last, above))

    midway()
    for part in range(CHUNKS):
        part_rows = pl.ds(part * step, step)
        near_copy(line_at, part).wait_recv()
        sum_ref[part_rows, :] = mine(line_at, part) + near[line_at, part_rows, :].astype(jnp.float32)

        @pl.when(line_at > 0)
        def _():
            line_copy(line_at, part, True).wait_recv()
            sum_ref[part_rows, :] += below[line_at, part_rows, :].astype(jnp.float32)

        @pl.when(line_at < last)
        def _():
            line_copy(line_at, part, False).wait_recv()
            sum_ref[part_rows, :] += above[line_at, part_rows, :].astype(jnp.float32)

        emit(part, slice(part * step, (part + 1) * step))

    def finish():
        for place in order:
            for part in range(CHUNKS):
                near_copy(place, part).wait_send()
        for place in order[:-1]:
            for part in range(CHUNKS):
                line_copy(place, part, True).wait_send()

    return finish


def scatter_scratch(ctx_size, rows, width):
    line_size = ctx_size // PAIR
    held = pltpu.VMEM((line_size, rows, width), jnp.bfloat16)
    return [
        held,
        held,
        held,
        pltpu.SemaphoreType.DMA((line_size, CHUNKS)),
        pltpu.SemaphoreType.DMA((line_size, CHUNKS)),
        pltpu.SemaphoreType.DMA((line_size, CHUNKS)),
        pltpu.SemaphoreType.DMA((2, line_size, CHUNKS)),
    ]


def swap_lanes(values, outer, inner):
    tile = 128
    half = tile // 2
    low = lax.broadcasted_iota(jnp.int32, (values.shape[0], tile), 1) < half
    placed = [None] * (outer * inner // 2)
    for first in range(0, outer, 2):
        for second in range(0, inner, 2):
            at = (first * inner + second) // 2
            one = values[:, at * tile : (at + 1) * tile]
            at += inner // 2
            two = values[:, at * tile : (at + 1) * tile]
            at = (second * outer + first) // 2
            placed[at] = jnp.where(low, one, pltpu.roll(two, half, 1))
            placed[at + outer // 2] = jnp.where(low, pltpu.roll(one, half, 1), two)
    return jnp.concatenate(placed, axis=1)


def start_kernel(
    ctx_size, fsdp_size, tokens_ref, tile_ref, parts_ref, out_ref, gains_ref, weight_ref,
    tiles, normed, tile_send, tile_recv, far_send, far_recv, near_send, near_recv, kept, *sems
):
    me_ctx, me_fsdp = lax.axis_index("ctx"), lax.axis_index("fsdp")
    count = ctx_size * fsdp_size
    me = me_ctx * fsdp_size + me_fsdp
    greet_all(pltpu.get_barrier_semaphore(), me, count, fsdp_size)

    def tile_copy(k, source):
        target = (me + k) % count
        return pltpu.make_async_remote_copy(
            src_ref=tile_ref,
            dst_ref=tiles.at[source],
            send_sem=tile_send.at[k],
            recv_sem=tile_recv.at[k],
            device_id=(target // fsdp_size, target % fsdp_size),
            device_id_type=MESH,
        )

    def start_tile(k, unused):
        tile_copy(k, me).start()
        return unused

    def finish_tile(k, unused):
        tile_copy(k, (me + count - k) % count).wait_recv()
        return unused

    lax.fori_loop(1, count, start_tile, 0)
    tiles[pl.ds(me, 1)] = tile_ref[...][None]

    def far_copy(k, source):
        target = (me_ctx + k) % ctx_size
        return pltpu.make_async_remote_copy(
            src_ref=parts_ref.at[target],
            dst_ref=weight_ref.at[source * fsdp_size + me_fsdp],
            send_sem=far_send.at[k],
            recv_sem=far_recv.at[k],
            device_id={"ctx": target},
            device_id_type=MESH,
        )

    def near_copy(k, j, fsdp_source):
        block = (me_ctx + ctx_size - k) % ctx_size * fsdp_size + fsdp_source
        return pltpu.make_async_remote_copy(
            src_ref=parts_ref.at[me_ctx] if k == 0 else weight_ref.at[block],
            dst_ref=weight_ref.at[block],
            send_sem=near_send.at[k, j],
            recv_sem=near_recv.at[k, j],
            device_id={"fsdp": (me_fsdp + j) % fsdp_size},
            device_id_type=MESH,
        )

    for k in range(1, ctx_size):
        far_copy(k, me_ctx).start()
    for j in range(1, fsdp_size):
        near_copy(0, j, me_fsdp).start()
    keep = pltpu.make_async_copy(parts_ref.at[me_ctx], weight_ref.at[me], kept)
    keep.start()

    rows, model = tokens_ref.shape
    lax.fori_loop(1, count, finish_tile, 0)
    held = model // count
    for pair in range(count // 2):
        cols = slice(pair * 2 * held, (pair + 1) * 2 * held)
        gains_ref[:, cols] = tiles[2 * pair] + tiles[2 * pair + 1]
    start_own, finish_gather = gather_phase(ctx_size // PAIR, normed, out_ref, *sems)
    step = rows // CHUNKS
    for part in range(CHUNKS):
        part_rows = slice(part * step, (part + 1) * step)
        values = tokens_ref[part_rows, :].astype(jnp.float32)
        scale = lax.rsqrt(jnp.mean(values * values, axis=-1, keepdims=True) + EPSILON)
        normed[part_rows, :] = (values * scale * gains_ref[0:1, :]).astype(normed.dtype)
        start_own(part)
    for k in range(1, ctx_size):
        far_copy(k, (me_ctx + ctx_size - k) % ctx_size).wait_recv()
        for j in range(1, fsdp_size):
            near_copy(k, j, me_fsdp).start()
    finish_gather()
    for k in range(ctx_size):
        for j in range(1, fsdp_size):
            near_copy(k, j, (me_fsdp + fsdp_size - j) % fsdp_size).wait_recv()
    for k in range(ctx_size):
        for j in range(1, fsdp_size):
            near_copy(k, j, me_fsdp).wait_send()
    for k in range(1, ctx_size):
        far_copy(k, me_ctx).wait_send()

    def sent_tile(k, unused):
        tile_copy(k, me).wait_send()
        return unused

    lax.fori_loop(1, count, sent_tile, 0)
    keep.wait()


def start_layer(tokens, tile, parts):
    ctx_size, fsdp_size = lax.axis_size("ctx"), lax.axis_size("fsdp")
    count = ctx_size * fsdp_size
    rows, model = tokens.shape
    dma = pltpu.SemaphoreType.DMA
    normed1, gains, weight = pl.pallas_call(
        functools.partial(start_kernel, ctx_size, fsdp_size),
        out_shape=(
            jax.ShapeDtypeStruct((ctx_size * rows, model), jnp.bfloat16),
            jax.ShapeDtypeStruct((8, model), jnp.float32),
            jax.ShapeDtypeStruct((count,) + parts.shape[1:], parts.dtype),
        ),
        in_specs=in_vmem(3),
        out_specs=(ANYWHERE, in_vmem(1)[0], ANYWHERE),
        scratch_shapes=[
            pltpu.VMEM((count, 8, 128), jnp.float32),
            pltpu.VMEM((rows, model), jnp.bfloat16),
            dma((count,)),
            dma((count,)),
            dma((ctx_size,)),
            dma((ctx_size,)),
            dma((ctx_size, fsdp_size)),
            dma((ctx_size, fsdp_size)),
            dma,
        ]
        + gather_scratch(ctx_size),
        compiler_params=pltpu.CompilerParams(
            collective_id=0, has_side_effects=True, vmem_limit_bytes=10 * 2**20
        ),
        cost_estimate=LINK_COST,
        name="start_layer",
    )(tokens, tile, parts)
    return normed1, gains, rows_of(weight)


def spread_phase(ctx_size, fsdp_size, gate_ref, up_ref, wide_ref, send, recv, side_send, side_recv, kept):
    me, me_fsdp = lax.axis_index("ctx"), lax.axis_index("fsdp")
    along = (me_fsdp + fsdp_size // 2) % fsdp_size
    beside = me_fsdp + 1 - 2 * (me_fsdp % 2)
    diagonal = (beside + fsdp_size // 2) % fsdp_size
    wide = gate_ref.shape[1] // ctx_size

    def part(which, target, source):
        cols = pl.ds(pl.multiple_of(target * wide, wide), wide)
        return (
            (gate_ref, up_ref)[which].at[:, cols],
            wide_ref.at[me_fsdp, source, :, which * wide : (which + 1) * wide],
        )

    def copy(which, k, source):
        target = (me + k) % ctx_size
        src, dst = part(which, target, source)
        return pltpu.make_async_remote_copy(
            src_ref=src,
            dst_ref=dst,
            send_sem=send.at[which, k],
            recv_sem=recv.at[which, k],
            device_id={"ctx": target},
            device_id_type=MESH,
        )

    def keep(which):
        return pltpu.make_async_copy(*part(which, me, me), kept.at[which])

    def side(way, k, rows_of_device):
        block = (rows_of_device, (me + ctx_size - k) % ctx_size)
        return pltpu.make_async_remote_copy(
            src_ref=wide_ref.at[block],
            dst_ref=wide_ref.at[block],
            send_sem=side_send.at[way, k],
            recv_sem=side_recv.at[way, k],
            device_id={"fsdp": along if way == 0 else beside},
            device_id_type=MESH,
        )

    def begin():
        for which in range(2):
            keep(which).start()
        for k in list(range(2, ctx_size, 2)) + list(range(1, ctx_size, 2)):
            for which in range(2):
                copy(which, k, me).start()

    def pass_on(k):
        for which in range(2):
            if k:
                copy(which, k, (me + ctx_size - k) % ctx_size).wait_recv()
            else:
                keep(which).wait()
        side(0, k, me_fsdp).start()
        side(1, k, me_fsdp).start()

    def relay(k):
        side(0, k, along).wait_recv()
        side(2, k, along).start()

    def finish():
        for k in range(ctx_size):
            side(1, k, beside).wait_recv()
            side(2, k, diagonal).wait_recv()
        for k in range(ctx_size):
            for way in range(3):
                side(way, k, me_fsdp).wait_send()
            if k:
                for which in range(2):
                    copy(which, k, me).wait_send()

    return begin, pass_on, relay, finish


def mlp_forward_kernel(
    ctx_size, fsdp_size, x_ref, tokens_ref, gains_ref, gate_ref, up_ref, hidden_ref, wide_ref, out_ref,
    sums, normed, wide_send, wide_recv, side_send, side_recv, kept, *sems
):
    line_size = ctx_size // PAIR
    me, me_fsdp = lax.axis_index("ctx"), lax.axis_index("fsdp")
    barrier = pltpu.get_barrier_semaphore()
    for k in range(1, ctx_size):
        pl.semaphore_signal(barrier, inc=1, device_id={"ctx": (me + k) % ctx_size}, device_id_type=MESH)
    for j in range(1, fsdp_size):
        pl.semaphore_signal(
            barrier, inc=1, device_id={"fsdp": (me_fsdp + j) % fsdp_size}, device_id_type=MESH
        )
    pl.semaphore_wait(barrier, ctx_size + fsdp_size - 2)
    start_own, finish_gather = gather_phase(line_size, normed, out_ref, *sems[7:])
    begin, pass_on, relay, finish_spread = spread_phase(
        ctx_size, fsdp_size, gate_ref, up_ref, wide_ref, wide_send, wide_recv, side_send, side_recv, kept
    )
    even = list(range(0, ctx_size, 2))
    odd = list(range(1, ctx_size, 2))

    def during_scatter(turn):
        if turn == 0:
            begin()
        if turn == 1:
            pass_on(0)
        if turn == 2:
            pass_on(2)

    def midway():
        for k in even[2:]:
            pass_on(k)
        for k in even[:2]:
            relay(k)

    def during_gather(distance):
        if distance == line_size - 2:
            for k in even[2:]:
                relay(k)
            for k in odd[:2]:
                pass_on(k)
        if distance == line_size - 1:
            for k in odd[2:]:
                pass_on(k)
        if distance == line_size:
            for k in odd:
                relay(k)

    def emit(part, rows):
        hidden = tokens_ref[rows, :].astype(jnp.float32) + RESIDUAL_MULT * sums[rows, :]
        hidden_ref[rows, :] = hidden
        scale = lax.rsqrt(jnp.mean(hidden * hidden, axis=-1, keepdims=True) + EPSILON)
        scaled = hidden * scale * gains_ref[1:2, :]
        normed[rows, :] = swap_lanes(scaled, ctx_size, fsdp_size).astype(normed.dtype)
        start_own(part)

    finish_scatter = scatter_phase(
        line_size, x_ref, sums, *sems[:7], emit, midway, during_scatter
    )
    finish_gather(during_gather)
    finish_spread()
    finish_scatter()


def mlp_backward_kernel(
    ctx_size, fsdp_size, x_ref, hidden_ref, grad_ref, gains_ref, terms_ref, grad_hidden_ref, grad_gain_ref,
    total_ref, out_ref, sums, normed, landing, side_send, side_recv, own_sem, *sems
):
    line_size = ctx_size // PAIR
    me, me_fsdp = lax.axis_index("ctx"), lax.axis_index("fsdp")
    greet_line(pltpu.get_barrier_semaphore(), me, me // PAIR, line_size, fsdp_size)

    def side_copy(j):
        target = (me_fsdp + j) % fsdp_size
        return pltpu.make_async_remote_copy(
            src_ref=terms_ref.at[target],
            dst_ref=landing.at[j],
            send_sem=side_send.at[j],
            recv_sem=side_recv.at[j],
            device_id={"fsdp": target},
            device_id_type=MESH,
        )

    own_copy = pltpu.make_async_copy(terms_ref.at[me_fsdp], landing.at[0], own_sem)
    for j in range(1, fsdp_size):
        side_copy(j).start()
    own_copy.start()
    start_own, finish_gather = gather_phase(line_size, normed, out_ref, *sems[7:])

    def emit(part, rows):
        grad_norm = swap_lanes(sums[rows, :], fsdp_size, ctx_size)
        hidden = hidden_ref[rows, :]
        scale = lax.rsqrt(jnp.mean(hidden * hidden, axis=-1, keepdims=True) + EPSILON)
        unit = hidden * scale
        grad_gain_ref[part : part + 1, :] = jnp.sum(grad_norm * unit, axis=0, keepdims=True)
        grad_hidden = grad_ref[rows, :].astype(jnp.float32) + norm_back(
            grad_norm, unit, scale, gains_ref[1:2, :]
        )
        grad_hidden_ref[rows, :] = grad_hidden
        normed[rows, :] = (RESIDUAL_MULT * grad_hidden).astype(normed.dtype)
        start_own(part)

    finish_scatter = scatter_phase(line_size, x_ref, sums, *sems[:7], emit)
    finish_gather()
    own_copy.wait()
    for j in range(1, fsdp_size):
        side_copy(j).wait_recv()
    step = 64

    def add(at, unused):
        rows = pl.ds(pl.multiple_of(at * step, step), step)
        total = landing[0, rows, :].astype(jnp.float32)
        for j in range(1, fsdp_size):
            total += landing[j, rows, :].astype(jnp.float32)
        total_ref[rows, :] = total.astype(total_ref.dtype)
        return unused

    lax.fori_loop(0, total_ref.shape[0] // step, add, 0)
    for j in range(1, fsdp_size):
        side_copy(j).wait_send()
    finish_scatter()


def scatter_gather(kernel, collective_id, extra_shapes, partial, *others, specs=(), out_specs=(), scratch=(), grant=24):
    ctx_size, fsdp_size = lax.axis_size("ctx"), lax.axis_size("fsdp")
    rows, model = partial.shape[0] // ctx_size, partial.shape[1]
    return pl.pallas_call(
        functools.partial(kernel, ctx_size, fsdp_size),
        out_shape=extra_shapes + (jax.ShapeDtypeStruct(partial.shape, jnp.bfloat16),),
        in_specs=in_vmem(1 + len(others) - len(specs)) + list(specs),
        out_specs=tuple(in_vmem(len(extra_shapes) - len(out_specs))) + tuple(out_specs) + (ANYWHERE,),
        scratch_shapes=[pltpu.VMEM((rows, model), jnp.float32), pltpu.VMEM((rows, model), jnp.bfloat16)]
        + list(scratch)
        + scatter_scratch(ctx_size, rows, model)
        + gather_scratch(ctx_size),
        compiler_params=pltpu.CompilerParams(
            collective_id=collective_id, has_side_effects=True, vmem_limit_bytes=grant * 2**20
        ),
        cost_estimate=LINK_COST,
    )(partial, *others)


def mlp_forward(partial, tokens, gains, w_gate, w_up):
    ctx_size, fsdp_size = lax.axis_size("ctx"), lax.axis_size("fsdp")
    hidden = jax.ShapeDtypeStruct(tokens.shape, jnp.float32)
    slices = (fsdp_size, ctx_size, w_gate.shape[0], 2 * w_gate.shape[1] // ctx_size)
    dma = pltpu.SemaphoreType.DMA
    return scatter_gather(
        mlp_forward_kernel,
        1,
        (hidden, jax.ShapeDtypeStruct(slices, w_gate.dtype)),
        partial,
        tokens,
        gains,
        w_gate,
        w_up,
        out_specs=(ANYWHERE,),
        scratch=(
            dma((2, ctx_size)),
            dma((2, ctx_size)),
            dma((3, ctx_size)),
            dma((3, ctx_size)),
            dma((2,)),
        ),
    )


def mlp_backward(partial, hidden, grad_out, gains, terms):
    like = jax.ShapeDtypeStruct(hidden.shape, jnp.float32)
    gain = jax.ShapeDtypeStruct((CHUNKS, hidden.shape[1]), jnp.float32)
    return scatter_gather(
        mlp_backward_kernel,
        2,
        (like, gain, jax.ShapeDtypeStruct(terms.shape[1:], terms.dtype)),
        partial,
        hidden,
        grad_out,
        gains,
        terms,
        grant=36,
        specs=(ANYWHERE,),
        scratch=(
            pltpu.VMEM(terms.shape, terms.dtype),
            pltpu.SemaphoreType.DMA((terms.shape[0],)),
            pltpu.SemaphoreType.DMA((terms.shape[0],)),
            pltpu.SemaphoreType.DMA,
        ),
    )


def finish_kernel(
    ctx_size, fsdp_size, x_ref, tokens_ref, grad_ref, gains_ref, gain2_ref, wo_ref, qkv_ref,
    grad_tokens_ref, gain_out_ref, wo_out_ref, qkv_out_ref,
    sums, gain1, tiles, arrived, wo_in, qkv_in, qkv_sum, tile_send, tile_recv, near_send, near_recv,
    far_send, far_recv, *sems
):
    line_size = ctx_size // PAIR
    me_ctx, me_fsdp = lax.axis_index("ctx"), lax.axis_index("fsdp")
    count = ctx_size * fsdp_size
    me = me_ctx * fsdp_size + me_fsdp
    greet_all(pltpu.get_barrier_semaphore(), me, count, fsdp_size)

    def near_copy(which, j):
        target = (me_fsdp + j) % fsdp_size
        terms, landing = ((wo_ref, wo_in), (qkv_ref, qkv_in))[which]
        return pltpu.make_async_remote_copy(
            src_ref=terms.at[target],
            dst_ref=landing.at[j],
            send_sem=near_send.at[which, j],
            recv_sem=near_recv.at[which, j],
            device_id={"fsdp": target},
            device_id_type=MESH,
        )

    def far_copy(k, source):
        target = (me_ctx + k) % ctx_size
        return pltpu.make_async_remote_copy(
            src_ref=qkv_sum.at[target],
            dst_ref=qkv_out_ref.at[source],
            send_sem=far_send.at[k],
            recv_sem=far_recv.at[k],
            device_id={"ctx": target},
            device_id_type=MESH,
        )

    def tile_copy(k, source):
        target = (me + k) % count
        return pltpu.make_async_remote_copy(
            src_ref=tiles.at[target // 2],
            dst_ref=arrived.at[source],
            send_sem=tile_send.at[k],
            recv_sem=tile_recv.at[k],
            device_id=(target // fsdp_size, target % fsdp_size),
            device_id_type=MESH,
        )

    def midway():
        for which, own, landing in ((1, qkv_ref, qkv_in), (0, wo_ref, wo_in)):
            for j in range(1, fsdp_size):
                near_copy(which, j).wait_recv()
            total = own[pl.ds(me_fsdp, 1)][0].astype(jnp.float32)
            for j in range(1, fsdp_size):
                total += landing[j].astype(jnp.float32)
            if which:
                qkv_sum[...] = total.astype(qkv_sum.dtype)
                for k in range(1, ctx_size):
                    far_copy(k, me_ctx).start()
                qkv_out_ref[pl.ds(me_ctx, 1)] = qkv_sum[pl.ds(me_ctx, 1)]
            else:
                wo_out_ref[...] = total

    def emit(part, rows):
        grad_norm = sums[rows, :]
        values = tokens_ref[rows, :].astype(jnp.float32)
        scale = lax.rsqrt(jnp.mean(values * values, axis=-1, keepdims=True) + EPSILON)
        unit = values * scale
        gain1[part : part + 1, :] = jnp.sum(grad_norm * unit, axis=0, keepdims=True)
        grad_tokens_ref[rows, :] = grad_ref[rows, :] + norm_back(
            grad_norm, unit, scale, gains_ref[0:1, :]
        )

    for which in (1, 0):
        for j in range(1, fsdp_size):
            near_copy(which, j).start()
    finish_scatter = scatter_phase(line_size, x_ref, sums, *sems, emit, midway)
    row = lax.broadcasted_iota(jnp.int32, (8, 128), 0)
    for pair in range(count // 2):
        cols = slice(pair * 128, (pair + 1) * 128)
        first = jnp.sum(gain1[:, cols], axis=0, keepdims=True)
        second = jnp.sum(gain2_ref[:, cols], axis=0, keepdims=True)
        tiles[pair] = jnp.where(row == 0, first, jnp.where(row == 1, second, 0.0))

    def start_tile(k, unused):
        tile_copy(k, me).start()
        return unused

    def finish_tile(k, unused):
        tile_copy(k, (me + count - k) % count).wait_recv()
        return unused

    def sent_tile(k, unused):
        tile_copy(k, me).wait_send()
        return unused

    lax.fori_loop(1, count, start_tile, 0)
    arrived[pl.ds(me, 1)] = tiles[pl.ds(me // 2, 1)]
    for k in range(1, ctx_size):
        far_copy(k, (me_ctx + ctx_size - k) % ctx_size).wait_recv()
    lax.fori_loop(1, count, finish_tile, 0)
    gain_out_ref[...] = jnp.sum(arrived[...], axis=0)
    finish_scatter()
    for which in range(2):
        for j in range(1, fsdp_size):
            near_copy(which, j).wait_send()
    for k in range(1, ctx_size):
        far_copy(k, me_ctx).wait_send()
    lax.fori_loop(1, count, sent_tile, 0)


def finish_layer(partial, tokens, grad_hidden, gains, grad_gain2, wo_terms, qkv_terms):
    ctx_size, fsdp_size = lax.axis_size("ctx"), lax.axis_size("fsdp")
    count = ctx_size * fsdp_size
    rows, model = tokens.shape
    dma = pltpu.SemaphoreType.DMA
    f32, bf16 = jnp.float32, jnp.bfloat16
    held, width = qkv_terms.shape[2:]
    return pl.pallas_call(
        functools.partial(finish_kernel, ctx_size, fsdp_size),
        out_shape=(
            jax.ShapeDtypeStruct((rows, model), f32),
            jax.ShapeDtypeStruct((8, 128), f32),
            jax.ShapeDtypeStruct(wo_terms.shape[1:], f32),
            jax.ShapeDtypeStruct((ctx_size, held, width), bf16),
        ),
        in_specs=in_vmem(7),
        out_specs=tuple(in_vmem(4)),
        scratch_shapes=[
            pltpu.VMEM((rows, model), f32),
            pltpu.VMEM((CHUNKS, model), f32),
            pltpu.VMEM((count // 2, 8, 128), f32),
            pltpu.VMEM((count, 8, 128), f32),
            pltpu.VMEM(wo_terms.shape, bf16),
            pltpu.VMEM(qkv_terms.shape, bf16),
            pltpu.VMEM((ctx_size, held, width), bf16),
            dma((count,)),
            dma((count,)),
            dma((2, fsdp_size)),
            dma((2, fsdp_size)),
            dma((ctx_size,)),
            dma((ctx_size,)),
        ]
        + scatter_scratch(ctx_size, rows, model),
        compiler_params=pltpu.CompilerParams(
            collective_id=3, has_side_effects=True, vmem_limit_bytes=32 * 2**20
        ),
        cost_estimate=LINK_COST,
        name="finish_layer",
    )(partial, tokens, grad_hidden, gains, grad_gain2, wo_terms, qkv_terms)


def swap_ctx(blocks):
    return lax.all_to_all(blocks, "ctx", split_axis=0, concat_axis=0, tiled=True)


def by_fsdp(grad, ctx_size, fsdp_size):
    parts = grad.reshape(ctx_size, fsdp_size, -1, grad.shape[-1]).transpose(1, 0, 2, 3)
    return rows_of(rows_of(parts))


def return_columns(terms, ctx_size):
    return swap_ctx(terms.reshape(ctx_size, -1, terms.shape[-1]))


def half_turn(values, sign_table):
    lane = lax.broadcasted_iota(jnp.int32, values.shape, 1)
    width = values.shape[1]
    quarter = HD // 2
    ahead = pltpu.roll(values, width - quarter, 1)
    behind = pltpu.roll(values, quarter, 1)
    return jnp.where(lane % HD < quarter, ahead, behind) * sign_table


def turn(values, cos_table, sign_table):
    copies = values.shape[1] // cos_table.shape[1]
    if copies > 1:
        cos_table = jnp.concatenate([cos_table] * copies, axis=1)
        sign_table = jnp.concatenate([sign_table] * copies, axis=1)
    return values * cos_table + half_turn(values, sign_table)


def attention_forward_kernel(
    block_rows, qkv_ref, cos_ref, sin_ref, doc_col_ref, doc_row_ref, q_ref, kv_ref, out_ref, lse_ref
):
    length = qkv_ref.shape[0]
    group = H // KVH
    width = group * HD
    q_ref[...] = turn(qkv_ref[:, :width], cos_ref[...], sin_ref[...]).astype(jnp.bfloat16)
    pair = qkv_ref[:, width:]
    lane = lax.broadcasted_iota(jnp.int32, pair.shape, 1)
    turned = turn(pair, cos_ref[...], sin_ref[...])
    kv_ref[...] = jnp.where(lane < HD, turned, pair).astype(jnp.bfloat16)
    for block in range(length // block_rows):
        rows = slice(block * block_rows, (block + 1) * block_rows)
        reach = (block + 1) * block_rows
        keys = kv_ref[:reach, :HD]
        values = kv_ref[:reach, HD:]
        query_at = block * block_rows + lax.broadcasted_iota(jnp.int32, (block_rows, reach), 0)
        key_at = lax.broadcasted_iota(jnp.int32, (block_rows, reach), 1)
        allowed = (doc_col_ref[rows, :] == doc_row_ref[:, :reach]) & (key_at <= query_at)
        for head in range(group):
            cols = slice(head * HD, (head + 1) * HD)
            scores = dot_back(q_ref[rows, cols], keys) * SCORE_SCALE
            masked = jnp.where(allowed, scores, NEGATIVE)
            top = jnp.max(masked, axis=1, keepdims=True)
            weights = jnp.where(allowed, jnp.exp(masked - top), 0.0)
            total = jnp.sum(weights, axis=1, keepdims=True)
            mixed = dot_plain(weights.astype(jnp.bfloat16), values)
            out_ref[rows, cols] = (mixed / total).astype(jnp.bfloat16)
            lse_ref[rows, head : head + 1] = top + jnp.log(total)


def attention_backward_kernel(
    block_rows, q_ref, kv_ref, do_ref, lse_ref, cos_ref, sin_ref, doc_col_ref, doc_row_ref, grad_ref, dq_ref, dkv_ref
):
    length = q_ref.shape[0]
    group = H // KVH
    width = group * HD
    dkv_ref[...] = jnp.zeros_like(dkv_ref)
    for block in range(length // block_rows):
        rows = slice(block * block_rows, (block + 1) * block_rows)
        reach = (block + 1) * block_rows
        keys = kv_ref[:reach, :HD]
        values = kv_ref[:reach, HD:]
        query_at = block * block_rows + lax.broadcasted_iota(jnp.int32, (block_rows, reach), 0)
        key_at = lax.broadcasted_iota(jnp.int32, (block_rows, reach), 1)
        allowed = (doc_col_ref[rows, :] == doc_row_ref[:, :reach]) & (key_at <= query_at)
        for head in range(group):
            cols = slice(head * HD, (head + 1) * HD)
            query = q_ref[rows, cols]
            grad_out = do_ref[rows, cols]
            scores = dot_back(query, keys) * SCORE_SCALE
            probs = jnp.where(
                allowed,
                jnp.exp(jnp.where(allowed, scores, NEGATIVE) - lse_ref[rows, head : head + 1]),
                0.0,
            )
            grad_probs = dot_back(grad_out, values)
            delta = jnp.sum(probs * grad_probs, axis=1, keepdims=True)
            grad_scores = (probs * (grad_probs - delta)).astype(jnp.bfloat16)
            dq_ref[rows, cols] = dot_plain(grad_scores, keys) * SCORE_SCALE
            dkv_ref[:reach, :HD] += dot_outer(grad_scores, query) * SCORE_SCALE
            dkv_ref[:reach, HD:] += dot_outer(probs.astype(jnp.bfloat16), grad_out)
    grad_ref[:, :width] = turn(dq_ref[...], cos_ref[...], -sin_ref[...]).astype(jnp.bfloat16)
    pair = dkv_ref[...]
    lane = lax.broadcasted_iota(jnp.int32, pair.shape, 1)
    turned = turn(pair, cos_ref[...], -sin_ref[...])
    grad_ref[:, width:] = jnp.where(lane < HD, turned, pair).astype(jnp.bfloat16)


def attention_forward(qkv, tables, block_rows):
    length = qkv.shape[0]
    width = (H // KVH) * HD
    return pl.pallas_call(
        functools.partial(attention_forward_kernel, block_rows),
        out_shape=(
            jax.ShapeDtypeStruct((length, width), jnp.bfloat16),
            jax.ShapeDtypeStruct((length, 2 * HD), jnp.bfloat16),
            jax.ShapeDtypeStruct((length, width), jnp.bfloat16),
            jax.ShapeDtypeStruct((length, H // KVH), jnp.float32),
        ),
        in_specs=in_vmem(5),
        out_specs=tuple(in_vmem(4)),
        compiler_params=pltpu.CompilerParams(vmem_limit_bytes=24 * 2**20),
        name="attend",
    )(qkv, *tables)


def attention_backward(q, kv, grad_out, lse, tables, block_rows):
    length, width = q.shape
    return pl.pallas_call(
        functools.partial(attention_backward_kernel, block_rows),
        out_shape=jax.ShapeDtypeStruct((length, width + 2 * HD), jnp.bfloat16),
        in_specs=in_vmem(8),
        out_specs=in_vmem(1)[0],
        scratch_shapes=[
            pltpu.VMEM((length, width), jnp.float32),
            pltpu.VMEM((length, 2 * HD), jnp.float32),
        ],
        compiler_params=pltpu.CompilerParams(vmem_limit_bytes=24 * 2**20),
        name="attend_back",
    )(q, kv, grad_out, lse, *tables)


def on_device(
    tokens,
    doc_lengths,
    cotangent,
    gain_attn,
    w_query,
    w_key,
    w_value,
    w_output,
    gain_mlp,
    w_gate,
    w_up,
    w_down,
):
    local_rows, model = tokens.shape[1:]
    ctx_size = lax.axis_size("ctx")
    fsdp_size = lax.axis_size("fsdp")
    length = local_rows * ctx_size
    group_width = (H // KVH) * HD
    ff_slice = FF // ctx_size
    held_rows = w_query.shape[0]
    bf16 = jnp.bfloat16

    positions = jnp.arange(length, dtype=jnp.int32)
    seq_lengths = doc_lengths[0]
    starts = jnp.cumsum(seq_lengths) - seq_lengths
    doc_ids = doc_index(positions, starts)
    cos_half, sin_half = rope_tables(positions)
    cos_table = jnp.concatenate([cos_half] * 4, axis=1)
    sin_table = jnp.concatenate([-sin_half, sin_half] * 2, axis=1)
    tables = (cos_table, sin_table, doc_ids[:, None], doc_ids[None, :])


    def by_slice(weight):
        return weight.reshape(held_rows, ctx_size, -1)

    qkv_parts = jnp.concatenate([by_slice(w_query), by_slice(w_key), by_slice(w_value)], axis=2)
    wo_mine = lax.all_gather(w_output, "fsdp", axis=0, tiled=True)
    wd_mine = lax.all_gather(w_down, "fsdp", axis=0, tiled=True)
    gain_rows = jnp.stack([gain_attn, gain_mlp]).astype(jnp.float32)
    odd = lax.axis_index("fsdp") % 2
    gain_tile = jnp.concatenate([gain_rows * (1 - odd), gain_rows * odd], axis=1)
    gain_tile = jnp.pad(gain_tile, ((0, 8 - gain_tile.shape[0]), (0, 128 - gain_tile.shape[1])))
    normed1, gains, w_qkv = start_layer(tokens[0], gain_tile, qkv_parts.transpose(1, 0, 2))
    grad_out = cotangent[0].astype(jnp.float32)
    grad_mlp = (RESIDUAL_MULT * grad_out).astype(bf16)

    block_rows = math.gcd(length, 256)
    normed1, grad_mlp = lax.optimization_barrier((normed1, grad_mlp))
    grad_mlp = lax.all_gather(grad_mlp, "ctx", axis=0, tiled=True)
    qkv = dot_plain(normed1, w_qkv)
    q, kv, mixed_heads, log_sum = attention_forward(qkv, tables, block_rows)
    hidden, w_gu, normed2 = mlp_forward(
        dot_plain(mixed_heads, wo_mine).astype(bf16), tokens[0], gains, w_gate, w_up
    )
    w_gu = rows_of(rows_of(w_gu))

    gate_up = dot_plain(normed2, w_gu)
    gate_pre, up_pre = gate_up[:, :ff_slice], gate_up[:, ff_slice:]
    sig_gate = jax.nn.sigmoid(gate_pre)
    silu_gate = gate_pre * sig_gate
    activ = (silu_gate * up_pre).astype(bf16)
    activ, gate_up = lax.optimization_barrier((activ, gate_up))
    gate_pre, up_pre = gate_up[:, :ff_slice], gate_up[:, ff_slice:]
    sig_gate = jax.nn.sigmoid(gate_pre)
    silu_gate = gate_pre * sig_gate
    out_terms, grad_mlp = lax.optimization_barrier(
        (dot_plain(activ, wd_mine).astype(bf16), grad_mlp)
    )
    branch = lax.psum_scatter(out_terms, "ctx", scatter_dimension=0, tiled=True)

    silu_slope = sig_gate * (1.0 + gate_pre * (1.0 - sig_gate))
    grad_act = dot_back(grad_mlp, wd_mine)
    grad_gu = jnp.concatenate(
        [(grad_act * up_pre * silu_slope).astype(bf16), (grad_act * silu_gate).astype(bf16)], axis=1
    )
    partial2, gu_terms, wd_terms = lax.optimization_barrier(
        (
            dot_back(grad_gu, w_gu).astype(bf16),
            dot_outer(normed2, grad_gu).astype(bf16),
            dot_outer(activ, grad_mlp).astype(bf16),
        )
    )
    grad_hidden, grad_g2, gu_back, grad_attn = mlp_backward(
        partial2, hidden, cotangent[0], gains, gu_terms.reshape(fsdp_size, -1, gu_terms.shape[1])
    )
    gu_back = return_columns(gu_back, ctx_size)
    wd_back = lax.psum_scatter(wd_terms, "fsdp", scatter_dimension=0, tiled=True)

    grad_mixed = dot_back(grad_attn, wo_mine).astype(bf16)
    wo_terms = dot_outer(mixed_heads, grad_attn).astype(bf16)
    grad_qkv = attention_backward(q, kv, grad_mixed, log_sum, tables, block_rows)
    partial1 = dot_back(grad_qkv, w_qkv).astype(bf16)
    qkv_terms = by_fsdp(dot_outer(normed1, grad_qkv).astype(bf16), ctx_size, fsdp_size)
    grad_inputs, gain_back, wo_back, qkv_back = finish_layer(
        partial1,
        tokens[0],
        grad_hidden,
        gains,
        grad_g2,
        wo_terms.reshape(fsdp_size, held_rows, model),
        qkv_terms.reshape(fsdp_size, ctx_size, held_rows, -1),
    )
    grad_inputs, wd_back, gu_back, branch = lax.optimization_barrier(
        (grad_inputs, wd_back, gu_back, branch)
    )
    output = (hidden + RESIDUAL_MULT * branch.astype(jnp.float32)).astype(bf16)[None]
    gain_back = jnp.where(odd == 0, gain_back[:2, :held_rows], gain_back[:2, held_rows:])

    def joined(parts):
        return parts.transpose(1, 0, 2).reshape(held_rows, -1).astype(jnp.float32)

    key_end = group_width + HD
    return (
        output,
        grad_inputs[None],
        gain_back[0],
        joined(qkv_back[:, :, :group_width]),
        joined(qkv_back[:, :, group_width:key_end]),
        joined(qkv_back[:, :, key_end:]),
        wo_back,
        gain_back[1],
        joined(gu_back[:, :, :ff_slice]),
        joined(gu_back[:, :, ff_slice:]),
        wd_back.astype(jnp.float32),
    )


def solution(mesh):
    in_specs = (
        P("fsdp", "ctx", None),
        P("fsdp", None),
        P("fsdp", "ctx", None),
        P(("ctx", "fsdp")),
        P(("ctx", "fsdp"), None),
        P(("ctx", "fsdp"), None),
        P(("ctx", "fsdp"), None),
        P(("ctx", "fsdp"), None),
        P(("ctx", "fsdp")),
        P(("ctx", "fsdp"), None),
        P(("ctx", "fsdp"), None),
        P(("ctx", "fsdp"), None),
    )
    out_specs = (
        P("fsdp", "ctx", None),
        P("fsdp", "ctx", None),
        P(("ctx", "fsdp")),
        P(("ctx", "fsdp"), None),
        P(("ctx", "fsdp"), None),
        P(("ctx", "fsdp"), None),
        P(("ctx", "fsdp"), None),
        P(("ctx", "fsdp")),
        P(("ctx", "fsdp"), None),
        P(("ctx", "fsdp"), None),
        P(("ctx", "fsdp"), None),
    )
    if mesh.shape["ctx"] != KVH or KVH != 4 * PAIR:
        return jax.shard_map(
            general_device, mesh=mesh, in_specs=in_specs, out_specs=out_specs, check_vma=False
        )

    return jax.shard_map(
        on_device, mesh=mesh, in_specs=in_specs, out_specs=out_specs, check_vma=False
    )
```

```python
import functools
import math

import jax
import jax.numpy as jnp
from jax import lax
from jax.experimental import pallas as pl
from jax.experimental.pallas import tpu as pltpu
from jax.sharding import PartitionSpec as P

H = 32
KVH = 8
HD = 64
FF = 8192


EPSILON = 1e-05
SCORE_SCALE = 1.0 / 64.0
RESIDUAL_MULT = 0.22
ROPE_BASE = 10000000.0
NEGATIVE = -1e30
MESH = pl.DeviceIdType.MESH
PAIR = 2
CHUNKS = 2
ANYWHERE = pl.BlockSpec(memory_space=pl.ANY)
LINK_COST = pl.CostEstimate(flops=0, bytes_accessed=150_000_000, transcendentals=0)


def doc_index(positions, starts):
    return jnp.sum((positions[:, None] >= starts[None, :]).astype(jnp.int32), axis=1) - 1


def rope_tables(positions):
    half_size = HD // 2
    frequency = ROPE_BASE ** (-(jnp.arange(half_size, dtype=jnp.float32) * 2.0) / HD)
    angles = positions.astype(jnp.float32)[:, None] * frequency[None, :]
    return (jnp.cos(angles), jnp.sin(angles))


def rotate(tensor, cos_table, sin_table, head_count):
    row_count = tensor.shape[0]
    by_head = tensor.reshape(row_count, head_count, HD)
    half_size = HD // 2
    first_half = by_head[..., :half_size]
    second_half = by_head[..., half_size:]
    cos_rows = cos_table[:, None, :]
    sin_rows = sin_table[:, None, :]
    turned = jnp.concatenate(
        [
            first_half * cos_rows - second_half * sin_rows,
            second_half * cos_rows + first_half * sin_rows,
        ],
        axis=-1,
    )
    return turned.reshape(row_count, head_count * HD)


def dot_plain(left, right):
    return jnp.dot(left, right, preferred_element_type=jnp.float32)


def dot_back(left, right):
    return lax.dot_general(
        left, right, (((1,), (1,)), ((), ())), preferred_element_type=jnp.float32
    )


def dot_outer(left, right):
    return lax.dot_general(
        left, right, (((0,), (0,)), ((), ())), preferred_element_type=jnp.float32
    )


def norm_back(grad_normed, unit_rows, inv_scale, gain_full):
    scaled = grad_normed * gain_full
    return inv_scale * (scaled - unit_rows * jnp.mean(scaled * unit_rows, axis=-1, keepdims=True))


def general_device(
    tokens,
    doc_lengths,
    cotangent,
    gain_attn,
    w_query,
    w_key,
    w_value,
    w_output,
    gain_mlp,
    w_gate,
    w_up,
    w_down,
):
    local_rows = tokens.shape[1]
    ctx_size = lax.axis_size("ctx")
    length = local_rows * ctx_size
    group_size = H // KVH
    offset = lax.axis_index("ctx") * local_rows
    positions = offset + jnp.arange(local_rows, dtype=jnp.int32)
    seq_lengths = doc_lengths[0]
    starts = jnp.cumsum(seq_lengths) - seq_lengths
    doc_ids = doc_index(positions, starts)
    last_pos = offset + local_rows - 1
    first_doc = doc_ids[0]
    cos_table, sin_table = rope_tables(positions)
    gain1, gain2, wq_full, wk_full, wv_full, wo_full = (
        lax.all_gather(gain_attn, ("ctx", "fsdp"), axis=0, tiled=True),
        lax.all_gather(gain_mlp, ("ctx", "fsdp"), axis=0, tiled=True),
        lax.all_gather(w_query, ("ctx", "fsdp"), axis=0, tiled=True),
        lax.all_gather(w_key, ("ctx", "fsdp"), axis=0, tiled=True),
        lax.all_gather(w_value, ("ctx", "fsdp"), axis=0, tiled=True),
        lax.all_gather(w_output, ("ctx", "fsdp"), axis=0, tiled=True),
    )
    gain1_f = gain1.astype(jnp.float32)
    gain2_f = gain2.astype(jnp.float32)
    inputs = tokens[0].astype(jnp.float32)
    inv_one = lax.rsqrt(jnp.mean(inputs * inputs, axis=-1, keepdims=True) + EPSILON)
    unit_one = inputs * inv_one
    normed1 = (unit_one * gain1_f).astype(jnp.bfloat16)
    queries = rotate(dot_plain(normed1, wq_full), cos_table, sin_table, H).astype(jnp.bfloat16)
    key_rot = rotate(dot_plain(normed1, wk_full), cos_table, sin_table, KVH).astype(jnp.bfloat16)
    values = dot_plain(normed1, wv_full).astype(jnp.bfloat16)
    grouped = queries.reshape(local_rows, KVH, group_size, HD)
    start_state = (
        jnp.full((local_rows, KVH, group_size), NEGATIVE, jnp.float32),
        jnp.zeros((local_rows, KVH, group_size), jnp.float32),
        jnp.zeros((local_rows, KVH, group_size, HD), jnp.float32),
    )
    running = start_state
    key_piece = lax.all_gather(key_rot, "ctx", axis=0, tiled=True)
    value_piece = lax.all_gather(values, "ctx", axis=0, tiled=True)
    piece_rows = key_piece.shape[0]
    attend_key_width = math.gcd(piece_rows, 512)
    block_count = piece_rows // attend_key_width

    def one_block(carried, index_block):
        block_start = index_block * attend_key_width
        key_blk = lax.dynamic_slice_in_dim(key_piece, block_start, attend_key_width, 0).reshape(
            attend_key_width, KVH, HD
        )
        value_blk = lax.dynamic_slice_in_dim(value_piece, block_start, attend_key_width, 0).reshape(
            attend_key_width, KVH, HD
        )
        key_pos = block_start + jnp.arange(attend_key_width, dtype=jnp.int32)
        key_docs = doc_index(key_pos, starts)
        skip_block = (block_start > last_pos) | (key_docs[attend_key_width - 1] < first_doc)

        def update(current):
            run_max, run_sum, accumulated = current
            scores = (
                jnp.einsum("qkgd,tkd->qkgt", grouped, key_blk, preferred_element_type=jnp.float32)
                * SCORE_SCALE
            )
            allowed = (key_docs[None, :] == doc_ids[:, None]) & (
                key_pos[None, :] <= positions[:, None]
            )
            allowed = allowed[:, None, None, :]
            masked = jnp.where(allowed, scores, NEGATIVE)
            new_max = jnp.maximum(run_max, jnp.max(masked, axis=-1))
            weights_exp = jnp.where(allowed, jnp.exp(masked - new_max[..., None]), 0.0)
            factor = jnp.exp(run_max - new_max)
            new_sum = run_sum * factor + jnp.sum(weights_exp, axis=-1)
            new_acc = accumulated * factor[..., None] + jnp.einsum(
                "qkgt,tkd->qkgd",
                weights_exp.astype(jnp.bfloat16),
                value_blk,
                preferred_element_type=jnp.float32,
            )
            return (new_max, new_sum, new_acc)

        return (lax.cond(skip_block, lambda unchanged: unchanged, update, carried), None)

    running, _ = lax.scan(one_block, running, jnp.arange(block_count))
    run_max, run_sum, accumulated = running
    attended = accumulated / run_sum[..., None]
    log_sum = run_max + jnp.log(run_sum)
    mixed_heads = attended.reshape(local_rows, H * HD).astype(jnp.bfloat16)
    hidden = inputs + RESIDUAL_MULT * dot_plain(mixed_heads, wo_full)
    inv_two = lax.rsqrt(jnp.mean(hidden * hidden, axis=-1, keepdims=True) + EPSILON)
    unit_two = hidden * inv_two
    normed2 = (unit_two * gain2_f).astype(jnp.bfloat16)
    wg_full, wu_full, wd_full = (
        lax.all_gather(w_gate, ("ctx", "fsdp"), axis=0, tiled=True),
        lax.all_gather(w_up, ("ctx", "fsdp"), axis=0, tiled=True),
        lax.all_gather(w_down, ("ctx", "fsdp"), axis=0, tiled=True),
    )
    gate_pre = dot_plain(normed2, wg_full)
    up_pre = dot_plain(normed2, wu_full)
    sig_gate = jax.nn.sigmoid(gate_pre)
    silu_gate = gate_pre * sig_gate
    activ = (silu_gate * up_pre).astype(jnp.bfloat16)
    result = hidden + RESIDUAL_MULT * dot_plain(activ, wd_full)
    output = result.astype(jnp.bfloat16)[None]
    grad_out = cotangent[0].astype(jnp.float32)
    grad_mlp = (RESIDUAL_MULT * grad_out).astype(jnp.bfloat16)
    silu_slope = sig_gate * (1.0 + gate_pre * (1.0 - sig_gate))
    wg_back, wu_back, wd_back = (
        lax.all_gather(w_gate, ("ctx", "fsdp"), axis=0, tiled=True),
        lax.all_gather(w_up, ("ctx", "fsdp"), axis=0, tiled=True),
        lax.all_gather(w_down, ("ctx", "fsdp"), axis=0, tiled=True),
    )
    grad_act = dot_back(grad_mlp, wd_back)
    grad_gate = (grad_act * up_pre * silu_slope).astype(jnp.bfloat16)
    grad_up = (grad_act * silu_gate).astype(jnp.bfloat16)
    grad_norm2 = dot_back(grad_gate, wg_back) + dot_back(grad_up, wu_back)
    left_cols = normed2
    gate_up_shard = lax.psum_scatter(
        jnp.concatenate([dot_outer(left_cols, grad_gate), dot_outer(left_cols, grad_up)], axis=1),
        ("ctx", "fsdp"),
        scatter_dimension=0,
        tiled=True,
    )
    wg_shard = gate_up_shard[:, :FF]
    wu_shard = gate_up_shard[:, FF:]
    left_cols = activ
    wd_shard = lax.psum_scatter(
        dot_outer(left_cols, grad_mlp), ("ctx", "fsdp"), scatter_dimension=0, tiled=True
    )
    grad_g2 = jnp.sum(grad_norm2 * unit_two, axis=0)
    grad_hidden = grad_out + norm_back(grad_norm2, unit_two, inv_two, gain2_f)
    grad_attn = (RESIDUAL_MULT * grad_hidden).astype(jnp.bfloat16)
    wq_back, wk_back, wv_back, wo_back = (
        lax.all_gather(w_query, ("ctx", "fsdp"), axis=0, tiled=True),
        lax.all_gather(w_key, ("ctx", "fsdp"), axis=0, tiled=True),
        lax.all_gather(w_value, ("ctx", "fsdp"), axis=0, tiled=True),
        lax.all_gather(w_output, ("ctx", "fsdp"), axis=0, tiled=True),
    )
    grad_wo = dot_outer(mixed_heads, grad_attn)
    grad_att = (
        dot_back(grad_attn, wo_back).astype(jnp.bfloat16).reshape(local_rows, KVH, group_size, HD)
    )
    row_delta = jnp.sum(grad_att.astype(jnp.float32) * attended, axis=-1)
    key_all, value_all = (
        lax.all_gather(key_rot, "ctx", axis=0, tiled=True),
        lax.all_gather(values, "ctx", axis=0, tiled=True),
    )
    key_width = math.gcd(length, 512)
    block_count = length // key_width

    def back_block(grad_query, index_block):
        block_start = index_block * key_width
        key_blk = lax.dynamic_slice_in_dim(key_all, block_start, key_width, 0).reshape(
            key_width, KVH, HD
        )
        value_blk = lax.dynamic_slice_in_dim(value_all, block_start, key_width, 0).reshape(
            key_width, KVH, HD
        )
        key_pos = block_start + jnp.arange(key_width, dtype=jnp.int32)
        key_docs = doc_index(key_pos, starts)
        skip_block = (block_start > last_pos) | (key_docs[key_width - 1] < first_doc)

        def compute(current):
            scores = (
                jnp.einsum("qkgd,tkd->qkgt", grouped, key_blk, preferred_element_type=jnp.float32)
                * SCORE_SCALE
            )
            allowed = (key_docs[None, :] == doc_ids[:, None]) & (
                key_pos[None, :] <= positions[:, None]
            )
            allowed = allowed[:, None, None, :]
            probs_blk = jnp.where(
                allowed, jnp.exp(jnp.where(allowed, scores, NEGATIVE) - log_sum[..., None]), 0.0
            )
            grad_probs = jnp.einsum(
                "qkgd,tkd->qkgt", grad_att, value_blk, preferred_element_type=jnp.float32
            )
            grad_scores = (probs_blk * (grad_probs - row_delta[..., None])).astype(jnp.bfloat16)
            new_query = (
                current
                + jnp.einsum(
                    "qkgt,tkd->qkgd", grad_scores, key_blk, preferred_element_type=jnp.float32
                )
                * SCORE_SCALE
            )
            grad_key = (
                jnp.einsum(
                    "qkgt,qkgd->tkd", grad_scores, grouped, preferred_element_type=jnp.float32
                )
                * SCORE_SCALE
            )
            grad_value = jnp.einsum(
                "qkgt,qkgd->tkd",
                probs_blk.astype(jnp.bfloat16),
                grad_att,
                preferred_element_type=jnp.float32,
            )
            return (
                new_query,
                (grad_key.reshape(key_width, KVH * HD), grad_value.reshape(key_width, KVH * HD)),
            )

        def nothing(current):
            zero_rows = jnp.zeros((key_width, KVH * HD), jnp.float32)
            return (current, (zero_rows, zero_rows))

        return lax.cond(skip_block, nothing, compute, grad_query)

    grad_query, key_terms = lax.scan(
        back_block,
        jnp.zeros((local_rows, KVH, group_size, HD), jnp.float32),
        jnp.arange(block_count),
    )
    key_term_all = key_terms[0].reshape(length, KVH * HD)
    value_term_all = key_terms[1].reshape(length, KVH * HD)
    grad_keys, grad_values = (
        lax.psum_scatter(
            key_term_all.astype(jnp.bfloat16), "ctx", scatter_dimension=0, tiled=True
        ).astype(jnp.float32),
        lax.psum_scatter(
            value_term_all.astype(jnp.bfloat16), "ctx", scatter_dimension=0, tiled=True
        ).astype(jnp.float32),
    )
    grad_q_pre = rotate(grad_query.reshape(local_rows, H * HD), cos_table, -sin_table, H).astype(
        jnp.bfloat16
    )
    grad_k_pre = rotate(grad_keys, cos_table, -sin_table, KVH).astype(jnp.bfloat16)
    grad_v_pre = grad_values.astype(jnp.bfloat16)
    grad_norm1 = (
        dot_back(grad_q_pre, wq_back)
        + dot_back(grad_k_pre, wk_back)
        + dot_back(grad_v_pre, wv_back)
    )
    grad_wq = dot_outer(normed1, grad_q_pre)
    grad_wk = dot_outer(normed1, grad_k_pre)
    grad_wv = dot_outer(normed1, grad_v_pre)
    grad_g1 = jnp.sum(grad_norm1 * unit_one, axis=0)
    grad_inputs = grad_hidden + norm_back(grad_norm1, unit_one, inv_one, gain1_f)
    g1_shard, g2_shard, wq_shard, wk_shard, wv_shard, wo_shard = (
        lax.psum_scatter(grad_g1, ("ctx", "fsdp"), scatter_dimension=0, tiled=True),
        lax.psum_scatter(grad_g2, ("ctx", "fsdp"), scatter_dimension=0, tiled=True),
        lax.psum_scatter(grad_wq, ("ctx", "fsdp"), scatter_dimension=0, tiled=True),
        lax.psum_scatter(grad_wk, ("ctx", "fsdp"), scatter_dimension=0, tiled=True),
        lax.psum_scatter(grad_wv, ("ctx", "fsdp"), scatter_dimension=0, tiled=True),
        lax.psum_scatter(grad_wo, ("ctx", "fsdp"), scatter_dimension=0, tiled=True),
    )
    return (
        output,
        grad_inputs[None],
        g1_shard,
        wq_shard,
        wk_shard,
        wv_shard,
        wo_shard,
        g2_shard,
        wg_shard,
        wu_shard,
        wd_shard,
    )


def rows_of(blocks):
    return blocks.reshape((-1,) + blocks.shape[2:])


def in_vmem(count):
    return [pl.BlockSpec(memory_space=pltpu.VMEM)] * count


def greet_line(barrier, ctx_at, line_at, line_size, fsdp_size=1):
    for j in range(1, fsdp_size):
        peer = (lax.axis_index("fsdp") + j) % fsdp_size
        pl.semaphore_signal(barrier, inc=1, device_id={"fsdp": peer}, device_id_type=MESH)
    other = ctx_at + 1 - 2 * (ctx_at % PAIR)
    pl.semaphore_signal(barrier, inc=1, device_id={"ctx": other}, device_id_type=MESH)

    @pl.when(line_at > 0)
    def _():
        pl.semaphore_signal(barrier, inc=1, device_id={"ctx": ctx_at - PAIR}, device_id_type=MESH)

    @pl.when(line_at < line_size - 1)
    def _():
        pl.semaphore_signal(barrier, inc=1, device_id={"ctx": ctx_at + PAIR}, device_id_type=MESH)

    last = line_size - 1
    neighbours = fsdp_size + (line_at + last - 1) // last + (2 * last - 1 - line_at) // last
    pl.semaphore_wait(barrier, neighbours)


def greet_all(barrier, me, count, fsdp_size):
    def greet(k, unused):
        target = (me + k) % count
        pl.semaphore_signal(
            barrier, inc=1, device_id=(target // fsdp_size, target % fsdp_size), device_id_type=MESH
        )
        return unused

    lax.fori_loop(1, count, greet, 0)
    pl.semaphore_wait(barrier, count - 1)


def gather_phase(line_size, x_ref, out_ref, send_sem, recv_sem, own_sem):
    me = lax.axis_index("ctx")
    line_at, pair_at = me // PAIR, me % PAIR
    rows = x_ref.shape[0]
    step = rows // CHUNKS

    def piece(block, part):
        return out_ref.at[pl.ds(pl.multiple_of(block * rows + part * step, step), step), :]

    def copy(block, part, way, own):
        slot = block * CHUNKS + part
        return pltpu.make_async_remote_copy(
            src_ref=x_ref.at[pl.ds(part * step, step), :] if own else piece(block, part),
            dst_ref=piece(block, part),
            send_sem=send_sem.at[way, slot],
            recv_sem=recv_sem.at[slot],
            device_id={"ctx": (me + 1 - 2 * pair_at, me + PAIR, me - PAIR)[way]},
            device_id_type=MESH,
        )

    def pass_on(block, part, upward, downward, own, act):
        if upward is not None:
            pl.when(upward)(lambda: act(copy(block, part, 1, own)))
        if downward is not None:
            pl.when(downward)(lambda: act(copy(block, part, 2, own)))
        act(copy(block, part, 0, own))

    def own_part(part, act):
        pass_on(me, part, line_at < line_size - 1, line_at > 0, True, act)

    def others(act, arrive, between):
        for distance in range(1, line_size):
            between(distance)
            for part in range(CHUNKS):

                @pl.when(line_at >= distance)
                def _():
                    block = me - PAIR * distance
                    arrive(block, part)
                    pass_on(block, part, line_at < line_size - 1, None, False, act)

                @pl.when(line_at + distance < line_size)
                def _():
                    block = me + PAIR * distance
                    arrive(block, part)
                    pass_on(block, part, None, line_at > 0, False, act)

    def start_own(part):
        own_part(part, lambda c: c.start())

    def finish(between=lambda distance: None):
        keep = pltpu.make_async_copy(
            x_ref, out_ref.at[pl.ds(pl.multiple_of(me * rows, rows), rows), :], own_sem
        )
        keep.start()
        others(
            lambda c: c.start(),
            lambda block, part: copy(block, part, 0, False).wait_recv(),
            between,
        )
        between(line_size)
        for place in range(line_size):
            for part in range(CHUNKS):
                copy(place * PAIR + 1 - pair_at, part, 0, False).wait_recv()
        for part in range(CHUNKS):
            own_part(part, lambda c: c.wait_send())
        others(lambda c: c.wait_send(), lambda block, part: None, lambda distance: None)
        keep.wait()

    return start_own, finish


def gather_scratch(ctx_size):
    return [
        pltpu.SemaphoreType.DMA((3, ctx_size * CHUNKS)),
        pltpu.SemaphoreType.DMA((ctx_size * CHUNKS,)),
        pltpu.SemaphoreType.DMA,
    ]


def scatter_phase(line_size, x_ref, sum_ref, near, below, above, near_send, near_sem, line_send, line_sem, emit, midway=lambda: None, between=lambda turn: None):
    me = lax.axis_index("ctx")
    line_at, pair_at = me // PAIR, me % PAIR
    rows = sum_ref.shape[0]
    step = rows // CHUNKS
    last = line_size - 1
    low = line_at // (line_size // 2)
    order = [k + (last - 2 * k) * (1 - low) for k in range(line_size // 2)]
    order += [line_at + 1 - 2 * (line_at % 2), line_at]

    def near_copy(place, part):
        start = (place * PAIR + 1 - pair_at) * rows + part * step
        return pltpu.make_async_remote_copy(
            src_ref=x_ref.at[pl.ds(pl.multiple_of(start, step), step), :],
            dst_ref=near.at[place, pl.ds(part * step, step), :],
            send_sem=near_send.at[place, part],
            recv_sem=near_sem.at[place, part],
            device_id={"ctx": me + 1 - 2 * pair_at},
            device_id_type=MESH,
        )

    def line_copy(place, part, up):
        part_rows = pl.ds(part * step, step)
        return pltpu.make_async_remote_copy(
            src_ref=near.at[place, part_rows, :],
            dst_ref=(below if up else above).at[place, part_rows, :],
            send_sem=line_send.at[place, part],
            recv_sem=line_sem.at[0 if up else 1, place, part],
            device_id={"ctx": me + PAIR if up else me - PAIR},
            device_id_type=MESH,
        )

    def mine(place, part):
        start = (place * PAIR + pair_at) * rows + part * step
        return x_ref[pl.ds(pl.multiple_of(start, step), step), :].astype(jnp.float32)

    for place in order:
        for part in range(CHUNKS):
            near_copy(place, part).start()

    for turn, place in enumerate(order[:-1]):
        between(turn)
        for part in range(CHUNKS):
            part_rows = pl.ds(part * step, step)
            near_copy(place, part).wait_recv()

            def send(up, waits, arrived):
                @pl.when(waits)
                def _():
                    line_copy(place, part, up).wait_recv()
                    near[place, part_rows, :] = (
                        mine(place, part)
                        + near[place, part_rows, :].astype(jnp.float32)
                        + arrived[place, part_rows, :].astype(jnp.float32)
                    ).astype(near.dtype)

                @pl.when(jnp.logical_not(waits))
                def _():
                    near[place, part_rows, :] = (
                        mine(place, part) + near[place, part_rows, :].astype(jnp.float32)
                    ).astype(near.dtype)

                line_copy(place, part, up).start()

            pl.when(place > line_at)(lambda: send(True, line_at > 0, below))
            pl.when(place < line_at)(lambda: send(False, line_at < last, above))

    midway()
    for part in range(CHUNKS):
        part_rows = pl.ds(part * step, step)
        near_copy(line_at, part).wait_recv()
        sum_ref[part_rows, :] = mine(line_at, part) + near[line_at, part_rows, :].astype(jnp.float32)

        @pl.when(line_at > 0)
        def _():
            line_copy(line_at, part, True).wait_recv()
            sum_ref[part_rows, :] += below[line_at, part_rows, :].astype(jnp.float32)

        @pl.when(line_at < last)
        def _():
            line_copy(line_at, part, False).wait_recv()
            sum_ref[part_rows, :] += above[line_at, part_rows, :].astype(jnp.float32)

        emit(part, slice(part * step, (part + 1) * step))

    def finish():
        for place in order:
            for part in range(CHUNKS):
                near_copy(place, part).wait_send()
        for place in order[:-1]:
            for part in range(CHUNKS):
                line_copy(place, part, True).wait_send()

    return finish


def scatter_scratch(ctx_size, rows, width):
    line_size = ctx_size // PAIR
    held = pltpu.VMEM((line_size, rows, width), jnp.bfloat16)
    return [
        held,
        held,
        held,
        pltpu.SemaphoreType.DMA((line_size, CHUNKS)),
        pltpu.SemaphoreType.DMA((line_size, CHUNKS)),
        pltpu.SemaphoreType.DMA((line_size, CHUNKS)),
        pltpu.SemaphoreType.DMA((2, line_size, CHUNKS)),
    ]


def swap_lanes(values, outer, inner):
    tile = 128
    half = tile // 2
    low = lax.broadcasted_iota(jnp.int32, (values.shape[0], tile), 1) < half
    placed = [None] * (outer * inner // 2)
    for first in range(0, outer, 2):
        for second in range(0, inner, 2):
            at = (first * inner + second) // 2
            one = values[:, at * tile : (at + 1) * tile]
            at += inner // 2
            two = values[:, at * tile : (at + 1) * tile]
            at = (second * outer + first) // 2
            placed[at] = jnp.where(low, one, pltpu.roll(two, half, 1))
            placed[at + outer // 2] = jnp.where(low, pltpu.roll(one, half, 1), two)
    return jnp.concatenate(placed, axis=1)


def start_kernel(
    ctx_size, fsdp_size, tokens_ref, tile_ref, parts_ref, out_ref, gains_ref, weight_ref,
    tiles, normed, tile_send, tile_recv, far_send, far_recv, near_send, near_recv, kept, *sems
):
    me_ctx, me_fsdp = lax.axis_index("ctx"), lax.axis_index("fsdp")
    count = ctx_size * fsdp_size
    me = me_ctx * fsdp_size + me_fsdp
    greet_all(pltpu.get_barrier_semaphore(), me, count, fsdp_size)

    def tile_copy(k, source):
        target = (me + k) % count
        return pltpu.make_async_remote_copy(
            src_ref=tile_ref,
            dst_ref=tiles.at[source],
            send_sem=tile_send.at[k],
            recv_sem=tile_recv.at[k],
            device_id=(target // fsdp_size, target % fsdp_size),
            device_id_type=MESH,
        )

    def start_tile(k, unused):
        tile_copy(k, me).start()
        return unused

    def finish_tile(k, unused):
        tile_copy(k, (me + count - k) % count).wait_recv()
        return unused

    lax.fori_loop(1, count, start_tile, 0)
    tiles[pl.ds(me, 1)] = tile_ref[...][None]

    def far_copy(k, source):
        target = (me_ctx + k) % ctx_size
        return pltpu.make_async_remote_copy(
            src_ref=parts_ref.at[target],
            dst_ref=weight_ref.at[source * fsdp_size + me_fsdp],
            send_sem=far_send.at[k],
            recv_sem=far_recv.at[k],
            device_id={"ctx": target},
            device_id_type=MESH,
        )

    def near_copy(k, j, fsdp_source):
        block = (me_ctx + ctx_size - k) % ctx_size * fsdp_size + fsdp_source
        return pltpu.make_async_remote_copy(
            src_ref=parts_ref.at[me_ctx] if k == 0 else weight_ref.at[block],
            dst_ref=weight_ref.at[block],
            send_sem=near_send.at[k, j],
            recv_sem=near_recv.at[k, j],
            device_id={"fsdp": (me_fsdp + j) % fsdp_size},
            device_id_type=MESH,
        )

    for k in range(1, ctx_size):
        far_copy(k, me_ctx).start()
    for j in range(1, fsdp_size):
        near_copy(0, j, me_fsdp).start()
    keep = pltpu.make_async_copy(parts_ref.at[me_ctx], weight_ref.at[me], kept)
    keep.start()

    rows, model = tokens_ref.shape
    lax.fori_loop(1, count, finish_tile, 0)
    held = model // count
    for pair in range(count // 2):
        cols = slice(pair * 2 * held, (pair + 1) * 2 * held)
        gains_ref[:, cols] = tiles[2 * pair] + tiles[2 * pair + 1]
    start_own, finish_gather = gather_phase(ctx_size // PAIR, normed, out_ref, *sems)
    step = rows // CHUNKS
    for part in range(CHUNKS):
        part_rows = slice(part * step, (part + 1) * step)
        values = tokens_ref[part_rows, :].astype(jnp.float32)
        scale = lax.rsqrt(jnp.mean(values * values, axis=-1, keepdims=True) + EPSILON)
        normed[part_rows, :] = (values * scale * gains_ref[0:1, :]).astype(normed.dtype)
        start_own(part)
    for k in range(1, ctx_size):
        far_copy(k, (me_ctx + ctx_size - k) % ctx_size).wait_recv()
        for j in range(1, fsdp_size):
            near_copy(k, j, me_fsdp).start()
    finish_gather()
    for k in range(ctx_size):
        for j in range(1, fsdp_size):
            near_copy(k, j, (me_fsdp + fsdp_size - j) % fsdp_size).wait_recv()
    for k in range(ctx_size):
        for j in range(1, fsdp_size):
            near_copy(k, j, me_fsdp).wait_send()
    for k in range(1, ctx_size):
        far_copy(k, me_ctx).wait_send()

    def sent_tile(k, unused):
        tile_copy(k, me).wait_send()
        return unused

    lax.fori_loop(1, count, sent_tile, 0)
    keep.wait()


def start_layer(tokens, tile, parts):
    ctx_size, fsdp_size = lax.axis_size("ctx"), lax.axis_size("fsdp")
    count = ctx_size * fsdp_size
    rows, model = tokens.shape
    dma = pltpu.SemaphoreType.DMA
    normed1, gains, weight = pl.pallas_call(
        functools.partial(start_kernel, ctx_size, fsdp_size),
        out_shape=(
            jax.ShapeDtypeStruct((ctx_size * rows, model), jnp.bfloat16),
            jax.ShapeDtypeStruct((8, model), jnp.float32),
            jax.ShapeDtypeStruct((count,) + parts.shape[1:], parts.dtype),
        ),
        in_specs=in_vmem(3),
        out_specs=(ANYWHERE, in_vmem(1)[0], ANYWHERE),
        scratch_shapes=[
            pltpu.VMEM((count, 8, 128), jnp.float32),
            pltpu.VMEM((rows, model), jnp.bfloat16),
            dma((count,)),
            dma((count,)),
            dma((ctx_size,)),
            dma((ctx_size,)),
            dma((ctx_size, fsdp_size)),
            dma((ctx_size, fsdp_size)),
            dma,
        ]
        + gather_scratch(ctx_size),
        compiler_params=pltpu.CompilerParams(
            collective_id=0, has_side_effects=True, vmem_limit_bytes=10 * 2**20
        ),
        cost_estimate=LINK_COST,
        name="start_layer",
    )(tokens, tile, parts)
    return normed1, gains, rows_of(weight)


def spread_phase(ctx_size, fsdp_size, gate_ref, up_ref, wide_ref, send, recv, side_send, side_recv, kept):
    me, me_fsdp = lax.axis_index("ctx"), lax.axis_index("fsdp")
    along = (me_fsdp + fsdp_size // 2) % fsdp_size
    beside = me_fsdp + 1 - 2 * (me_fsdp % 2)
    diagonal = (beside + fsdp_size // 2) % fsdp_size
    wide = gate_ref.shape[1] // ctx_size

    def part(which, target, source):
        cols = pl.ds(pl.multiple_of(target * wide, wide), wide)
        return (
            (gate_ref, up_ref)[which].at[:, cols],
            wide_ref.at[me_fsdp, source, :, which * wide : (which + 1) * wide],
        )

    def copy(which, k, source):
        target = (me + k) % ctx_size
        src, dst = part(which, target, source)
        return pltpu.make_async_remote_copy(
            src_ref=src,
            dst_ref=dst,
            send_sem=send.at[which, k],
            recv_sem=recv.at[which, k],
            device_id={"ctx": target},
            device_id_type=MESH,
        )

    def keep(which):
        return pltpu.make_async_copy(*part(which, me, me), kept.at[which])

    def side(way, k, rows_of_device):
        block = (rows_of_device, (me + ctx_size - k) % ctx_size)
        return pltpu.make_async_remote_copy(
            src_ref=wide_ref.at[block],
            dst_ref=wide_ref.at[block],
            send_sem=side_send.at[way, k],
            recv_sem=side_recv.at[way, k],
            device_id={"fsdp": along if way == 0 else beside},
            device_id_type=MESH,
        )

    def begin():
        for which in range(2):
            keep(which).start()
        for k in list(range(2, ctx_size, 2)) + list(range(1, ctx_size, 2)):
            for which in range(2):
                copy(which, k, me).start()

    def pass_on(k):
        for which in range(2):
            if k:
                copy(which, k, (me + ctx_size - k) % ctx_size).wait_recv()
            else:
                keep(which).wait()
        side(0, k, me_fsdp).start()
        side(1, k, me_fsdp).start()

    def relay(k):
        side(0, k, along).wait_recv()
        side(2, k, along).start()

    def finish():
        for k in range(ctx_size):
            side(1, k, beside).wait_recv()
            side(2, k, diagonal).wait_recv()
        for k in range(ctx_size):
            for way in range(3):
                side(way, k, me_fsdp).wait_send()
            if k:
                for which in range(2):
                    copy(which, k, me).wait_send()

    return begin, pass_on, relay, finish


def mlp_forward_kernel(
    ctx_size, fsdp_size, x_ref, tokens_ref, gains_ref, gate_ref, up_ref, hidden_ref, wide_ref, out_ref,
    sums, normed, wide_send, wide_recv, side_send, side_recv, kept, *sems
):
    line_size = ctx_size // PAIR
    me, me_fsdp = lax.axis_index("ctx"), lax.axis_index("fsdp")
    barrier = pltpu.get_barrier_semaphore()
    for k in range(1, ctx_size):
        pl.semaphore_signal(barrier, inc=1, device_id={"ctx": (me + k) % ctx_size}, device_id_type=MESH)
    for j in range(1, fsdp_size):
        pl.semaphore_signal(
            barrier, inc=1, device_id={"fsdp": (me_fsdp + j) % fsdp_size}, device_id_type=MESH
        )
    pl.semaphore_wait(barrier, ctx_size + fsdp_size - 2)
    start_own, finish_gather = gather_phase(line_size, normed, out_ref, *sems[7:])
    begin, pass_on, relay, finish_spread = spread_phase(
        ctx_size, fsdp_size, gate_ref, up_ref, wide_ref, wide_send, wide_recv, side_send, side_recv, kept
    )
    even = list(range(0, ctx_size, 2))
    odd = list(range(1, ctx_size, 2))

    def during_scatter(turn):
        if turn == 0:
            begin()
        if turn == 1:
            pass_on(0)
        if turn == 2:
            pass_on(2)

    def midway():
        for k in even[2:]:
            pass_on(k)
        for k in even[:2]:
            relay(k)

    def during_gather(distance):
        if distance == line_size - 2:
            for k in even[2:]:
                relay(k)
            for k in odd[:2]:
                pass_on(k)
        if distance == line_size - 1:
            for k in odd[2:]:
                pass_on(k)
        if distance == line_size:
            for k in odd:
                relay(k)

    def emit(part, rows):
        hidden = tokens_ref[rows, :].astype(jnp.float32) + RESIDUAL_MULT * sums[rows, :]
        hidden_ref[rows, :] = hidden
        scale = lax.rsqrt(jnp.mean(hidden * hidden, axis=-1, keepdims=True) + EPSILON)
        scaled = hidden * scale * gains_ref[1:2, :]
        normed[rows, :] = swap_lanes(scaled, ctx_size, fsdp_size).astype(normed.dtype)
        start_own(part)

    finish_scatter = scatter_phase(
        line_size, x_ref, sums, *sems[:7], emit, midway, during_scatter
    )
    finish_gather(during_gather)
    finish_spread()
    finish_scatter()


def mlp_backward_kernel(
    ctx_size, fsdp_size, x_ref, hidden_ref, grad_ref, gains_ref, terms_ref, grad_hidden_ref, grad_gain_ref,
    total_ref, out_ref, sums, normed, landing, side_send, side_recv, own_sem, *sems
):
    line_size = ctx_size // PAIR
    me, me_fsdp = lax.axis_index("ctx"), lax.axis_index("fsdp")
    greet_line(pltpu.get_barrier_semaphore(), me, me // PAIR, line_size, fsdp_size)

    def side_copy(j):
        target = (me_fsdp + j) % fsdp_size
        return pltpu.make_async_remote_copy(
            src_ref=terms_ref.at[target],
            dst_ref=landing.at[j],
            send_sem=side_send.at[j],
            recv_sem=side_recv.at[j],
            device_id={"fsdp": target},
            device_id_type=MESH,
        )

    own_copy = pltpu.make_async_copy(terms_ref.at[me_fsdp], landing.at[0], own_sem)
    for j in range(1, fsdp_size):
        side_copy(j).start()
    own_copy.start()
    start_own, finish_gather = gather_phase(line_size, normed, out_ref, *sems[7:])

    def emit(part, rows):
        grad_norm = swap_lanes(sums[rows, :], fsdp_size, ctx_size)
        hidden = hidden_ref[rows, :]
        scale = lax.rsqrt(jnp.mean(hidden * hidden, axis=-1, keepdims=True) + EPSILON)
        unit = hidden * scale
        grad_gain_ref[part : part + 1, :] = jnp.sum(grad_norm * unit, axis=0, keepdims=True)
        grad_hidden = grad_ref[rows, :].astype(jnp.float32) + norm_back(
            grad_norm, unit, scale, gains_ref[1:2, :]
        )
        grad_hidden_ref[rows, :] = grad_hidden
        normed[rows, :] = (RESIDUAL_MULT * grad_hidden).astype(normed.dtype)
        start_own(part)

    finish_scatter = scatter_phase(line_size, x_ref, sums, *sems[:7], emit)
    finish_gather()
    own_copy.wait()
    for j in range(1, fsdp_size):
        side_copy(j).wait_recv()
    step = 64

    def add(at, unused):
        rows = pl.ds(pl.multiple_of(at * step, step), step)
        total = landing[0, rows, :].astype(jnp.float32)
        for j in range(1, fsdp_size):
            total += landing[j, rows, :].astype(jnp.float32)
        total_ref[rows, :] = total.astype(total_ref.dtype)
        return unused

    lax.fori_loop(0, total_ref.shape[0] // step, add, 0)
    for j in range(1, fsdp_size):
        side_copy(j).wait_send()
    finish_scatter()


def scatter_gather(kernel, collective_id, extra_shapes, partial, *others, specs=(), out_specs=(), scratch=(), grant=24):
    ctx_size, fsdp_size = lax.axis_size("ctx"), lax.axis_size("fsdp")
    rows, model = partial.shape[0] // ctx_size, partial.shape[1]
    return pl.pallas_call(
        functools.partial(kernel, ctx_size, fsdp_size),
        out_shape=extra_shapes + (jax.ShapeDtypeStruct(partial.shape, jnp.bfloat16),),
        in_specs=in_vmem(1 + len(others) - len(specs)) + list(specs),
        out_specs=tuple(in_vmem(len(extra_shapes) - len(out_specs))) + tuple(out_specs) + (ANYWHERE,),
        scratch_shapes=[pltpu.VMEM((rows, model), jnp.float32), pltpu.VMEM((rows, model), jnp.bfloat16)]
        + list(scratch)
        + scatter_scratch(ctx_size, rows, model)
        + gather_scratch(ctx_size),
        compiler_params=pltpu.CompilerParams(
            collective_id=collective_id, has_side_effects=True, vmem_limit_bytes=grant * 2**20
        ),
        cost_estimate=LINK_COST,
    )(partial, *others)


def mlp_forward(partial, tokens, gains, w_gate, w_up):
    ctx_size, fsdp_size = lax.axis_size("ctx"), lax.axis_size("fsdp")
    hidden = jax.ShapeDtypeStruct(tokens.shape, jnp.float32)
    slices = (fsdp_size, ctx_size, w_gate.shape[0], 2 * w_gate.shape[1] // ctx_size)
    dma = pltpu.SemaphoreType.DMA
    return scatter_gather(
        mlp_forward_kernel,
        1,
        (hidden, jax.ShapeDtypeStruct(slices, w_gate.dtype)),
        partial,
        tokens,
        gains,
        w_gate,
        w_up,
        out_specs=(ANYWHERE,),
        scratch=(
            dma((2, ctx_size)),
            dma((2, ctx_size)),
            dma((3, ctx_size)),
            dma((3, ctx_size)),
            dma((2,)),
        ),
    )


def mlp_backward(partial, hidden, grad_out, gains, terms):
    like = jax.ShapeDtypeStruct(hidden.shape, jnp.float32)
    gain = jax.ShapeDtypeStruct((CHUNKS, hidden.shape[1]), jnp.float32)
    return scatter_gather(
        mlp_backward_kernel,
        2,
        (like, gain, jax.ShapeDtypeStruct(terms.shape[1:], terms.dtype)),
        partial,
        hidden,
        grad_out,
        gains,
        terms,
        grant=36,
        specs=(ANYWHERE,),
        scratch=(
            pltpu.VMEM(terms.shape, terms.dtype),
            pltpu.SemaphoreType.DMA((terms.shape[0],)),
            pltpu.SemaphoreType.DMA((terms.shape[0],)),
            pltpu.SemaphoreType.DMA,
        ),
    )


def finish_kernel(
    ctx_size, fsdp_size, x_ref, tokens_ref, grad_ref, gains_ref, gain2_ref, wo_ref, qkv_ref,
    grad_tokens_ref, gain_out_ref, wo_out_ref, qkv_out_ref,
    sums, gain1, tiles, arrived, wo_in, qkv_in, qkv_sum, tile_send, tile_recv, near_send, near_recv,
    far_send, far_recv, *sems
):
    line_size = ctx_size // PAIR
    me_ctx, me_fsdp = lax.axis_index("ctx"), lax.axis_index("fsdp")
    count = ctx_size * fsdp_size
    me = me_ctx * fsdp_size + me_fsdp
    greet_all(pltpu.get_barrier_semaphore(), me, count, fsdp_size)

    def near_copy(which, j):
        target = (me_fsdp + j) % fsdp_size
        terms, landing = ((wo_ref, wo_in), (qkv_ref, qkv_in))[which]
        return pltpu.make_async_remote_copy(
            src_ref=terms.at[target],
            dst_ref=landing.at[j],
            send_sem=near_send.at[which, j],
            recv_sem=near_recv.at[which, j],
            device_id={"fsdp": target},
            device_id_type=MESH,
        )

    def far_copy(k, source):
        target = (me_ctx + k) % ctx_size
        return pltpu.make_async_remote_copy(
            src_ref=qkv_sum.at[target],
            dst_ref=qkv_out_ref.at[source],
            send_sem=far_send.at[k],
            recv_sem=far_recv.at[k],
            device_id={"ctx": target},
            device_id_type=MESH,
        )

    def tile_copy(k, source):
        target = (me + k) % count
        return pltpu.make_async_remote_copy(
            src_ref=tiles.at[target // 2],
            dst_ref=arrived.at[source],
            send_sem=tile_send.at[k],
            recv_sem=tile_recv.at[k],
            device_id=(target // fsdp_size, target % fsdp_size),
            device_id_type=MESH,
        )

    def midway():
        for which, own, landing in ((1, qkv_ref, qkv_in), (0, wo_ref, wo_in)):
            for j in range(1, fsdp_size):
                near_copy(which, j).wait_recv()
            total = own[pl.ds(me_fsdp, 1)][0].astype(jnp.float32)
            for j in range(1, fsdp_size):
                total += landing[j].astype(jnp.float32)
            if which:
                qkv_sum[...] = total.astype(qkv_sum.dtype)
                for k in range(1, ctx_size):
                    far_copy(k, me_ctx).start()
                qkv_out_ref[pl.ds(me_ctx, 1)] = qkv_sum[pl.ds(me_ctx, 1)]
            else:
                wo_out_ref[...] = total

    def emit(part, rows):
        grad_norm = sums[rows, :]
        values = tokens_ref[rows, :].astype(jnp.float32)
        scale = lax.rsqrt(jnp.mean(values * values, axis=-1, keepdims=True) + EPSILON)
        unit = values * scale
        gain1[part : part + 1, :] = jnp.sum(grad_norm * unit, axis=0, keepdims=True)
        grad_tokens_ref[rows, :] = grad_ref[rows, :] + norm_back(
            grad_norm, unit, scale, gains_ref[0:1, :]
        )

    for which in (1, 0):
        for j in range(1, fsdp_size):
            near_copy(which, j).start()
    finish_scatter = scatter_phase(line_size, x_ref, sums, *sems, emit, midway)
    row = lax.broadcasted_iota(jnp.int32, (8, 128), 0)
    for pair in range(count // 2):
        cols = slice(pair * 128, (pair + 1) * 128)
        first = jnp.sum(gain1[:, cols], axis=0, keepdims=True)
        second = jnp.sum(gain2_ref[:, cols], axis=0, keepdims=True)
        tiles[pair] = jnp.where(row == 0, first, jnp.where(row == 1, second, 0.0))

    def start_tile(k, unused):
        tile_copy(k, me).start()
        return unused

    def finish_tile(k, unused):
        tile_copy(k, (me + count - k) % count).wait_recv()
        return unused

    def sent_tile(k, unused):
        tile_copy(k, me).wait_send()
        return unused

    lax.fori_loop(1, count, start_tile, 0)
    arrived[pl.ds(me, 1)] = tiles[pl.ds(me // 2, 1)]
    for k in range(1, ctx_size):
        far_copy(k, (me_ctx + ctx_size - k) % ctx_size).wait_recv()
    lax.fori_loop(1, count, finish_tile, 0)
    gain_out_ref[...] = jnp.sum(arrived[...], axis=0)
    finish_scatter()
    for which in range(2):
        for j in range(1, fsdp_size):
            near_copy(which, j).wait_send()
    for k in range(1, ctx_size):
        far_copy(k, me_ctx).wait_send()
    lax.fori_loop(1, count, sent_tile, 0)


def finish_layer(partial, tokens, grad_hidden, gains, grad_gain2, wo_terms, qkv_terms):
    ctx_size, fsdp_size = lax.axis_size("ctx"), lax.axis_size("fsdp")
    count = ctx_size * fsdp_size
    rows, model = tokens.shape
    dma = pltpu.SemaphoreType.DMA
    f32, bf16 = jnp.float32, jnp.bfloat16
    held, width = qkv_terms.shape[2:]
    return pl.pallas_call(
        functools.partial(finish_kernel, ctx_size, fsdp_size),
        out_shape=(
            jax.ShapeDtypeStruct((rows, model), f32),
            jax.ShapeDtypeStruct((8, 128), f32),
            jax.ShapeDtypeStruct(wo_terms.shape[1:], f32),
            jax.ShapeDtypeStruct((ctx_size, held, width), bf16),
        ),
        in_specs=in_vmem(7),
        out_specs=tuple(in_vmem(4)),
        scratch_shapes=[
            pltpu.VMEM((rows, model), f32),
            pltpu.VMEM((CHUNKS, model), f32),
            pltpu.VMEM((count // 2, 8, 128), f32),
            pltpu.VMEM((count, 8, 128), f32),
            pltpu.VMEM(wo_terms.shape, bf16),
            pltpu.VMEM(qkv_terms.shape, bf16),
            pltpu.VMEM((ctx_size, held, width), bf16),
            dma((count,)),
            dma((count,)),
            dma((2, fsdp_size)),
            dma((2, fsdp_size)),
            dma((ctx_size,)),
            dma((ctx_size,)),
        ]
        + scatter_scratch(ctx_size, rows, model),
        compiler_params=pltpu.CompilerParams(
            collective_id=3, has_side_effects=True, vmem_limit_bytes=32 * 2**20
        ),
        cost_estimate=LINK_COST,
        name="finish_layer",
    )(partial, tokens, grad_hidden, gains, grad_gain2, wo_terms, qkv_terms)


def swap_ctx(blocks):
    return lax.all_to_all(blocks, "ctx", split_axis=0, concat_axis=0, tiled=True)


def by_fsdp(grad, ctx_size, fsdp_size):
    parts = grad.reshape(ctx_size, fsdp_size, -1, grad.shape[-1]).transpose(1, 0, 2, 3)
    return rows_of(rows_of(parts))


def return_columns(terms, ctx_size):
    return swap_ctx(terms.reshape(ctx_size, -1, terms.shape[-1]))


def half_turn(values, sign_table):
    lane = lax.broadcasted_iota(jnp.int32, values.shape, 1)
    width = values.shape[1]
    quarter = HD // 2
    ahead = pltpu.roll(values, width - quarter, 1)
    behind = pltpu.roll(values, quarter, 1)
    return jnp.where(lane % HD < quarter, ahead, behind) * sign_table


def turn(values, cos_table, sign_table):
    copies = values.shape[1] // cos_table.shape[1]
    if copies > 1:
        cos_table = jnp.concatenate([cos_table] * copies, axis=1)
        sign_table = jnp.concatenate([sign_table] * copies, axis=1)
    return values * cos_table + half_turn(values, sign_table)


def attention_forward_kernel(
    block_rows, qkv_ref, wo_ref, cos_ref, sin_ref, doc_col_ref, doc_row_ref, q_ref, kv_ref, out_ref, lse_ref,
    branch_ref,
):
    length = qkv_ref.shape[0]
    group = H // KVH
    width = group * HD
    q_ref[...] = turn(qkv_ref[:, :width], cos_ref[...], sin_ref[...]).astype(jnp.bfloat16)
    pair = qkv_ref[:, width:]
    lane = lax.broadcasted_iota(jnp.int32, pair.shape, 1)
    turned = turn(pair, cos_ref[...], sin_ref[...])
    kv_ref[...] = jnp.where(lane < HD, turned, pair).astype(jnp.bfloat16)
    for block in range(length // block_rows):
        rows = slice(block * block_rows, (block + 1) * block_rows)
        reach = (block + 1) * block_rows
        keys = kv_ref[:reach, :HD]
        values = kv_ref[:reach, HD:]
        query_at = block * block_rows + lax.broadcasted_iota(jnp.int32, (block_rows, reach), 0)
        key_at = lax.broadcasted_iota(jnp.int32, (block_rows, reach), 1)
        allowed = (doc_col_ref[rows, :] == doc_row_ref[:, :reach]) & (key_at <= query_at)
        for head in range(group):
            cols = slice(head * HD, (head + 1) * HD)
            scores = dot_back(q_ref[rows, cols], keys) * SCORE_SCALE
            masked = jnp.where(allowed, scores, NEGATIVE)
            top = jnp.max(masked, axis=1, keepdims=True)
            weights = jnp.where(allowed, jnp.exp(masked - top), 0.0)
            total = jnp.sum(weights, axis=1, keepdims=True)
            mixed = dot_plain(weights.astype(jnp.bfloat16), values)
            out_ref[rows, cols] = (mixed / total).astype(jnp.bfloat16)
            lse_ref[rows, head : head + 1] = top + jnp.log(total)
        branch_ref[rows, :] = dot_plain(out_ref[rows, :], wo_ref[...]).astype(jnp.bfloat16)


def attention_backward_kernel(
    block_rows, q_ref, kv_ref, do_ref, lse_ref, cos_ref, sin_ref, doc_col_ref, doc_row_ref, grad_ref, dq_ref, dkv_ref
):
    length = q_ref.shape[0]
    group = H // KVH
    width = group * HD
    dkv_ref[...] = jnp.zeros_like(dkv_ref)
    for block in range(length // block_rows):
        rows = slice(block * block_rows, (block + 1) * block_rows)
        reach = (block + 1) * block_rows
        keys = kv_ref[:reach, :HD]
        values = kv_ref[:reach, HD:]
        query_at = block * block_rows + lax.broadcasted_iota(jnp.int32, (block_rows, reach), 0)
        key_at = lax.broadcasted_iota(jnp.int32, (block_rows, reach), 1)
        allowed = (doc_col_ref[rows, :] == doc_row_ref[:, :reach]) & (key_at <= query_at)
        for head in range(group):
            cols = slice(head * HD, (head + 1) * HD)
            query = q_ref[rows, cols]
            grad_out = do_ref[rows, cols]
            scores = dot_back(query, keys) * SCORE_SCALE
            probs = jnp.where(
                allowed,
                jnp.exp(jnp.where(allowed, scores, NEGATIVE) - lse_ref[rows, head : head + 1]),
                0.0,
            )
            grad_probs = dot_back(grad_out, values)
            delta = jnp.sum(probs * grad_probs, axis=1, keepdims=True)
            grad_scores = (probs * (grad_probs - delta)).astype(jnp.bfloat16)
            dq_ref[rows, cols] = dot_plain(grad_scores, keys) * SCORE_SCALE
            dkv_ref[:reach, :HD] += dot_outer(grad_scores, query) * SCORE_SCALE
            dkv_ref[:reach, HD:] += dot_outer(probs.astype(jnp.bfloat16), grad_out)
    grad_ref[:, :width] = turn(dq_ref[...], cos_ref[...], -sin_ref[...]).astype(jnp.bfloat16)
    pair = dkv_ref[...]
    lane = lax.broadcasted_iota(jnp.int32, pair.shape, 1)
    turned = turn(pair, cos_ref[...], -sin_ref[...])
    grad_ref[:, width:] = jnp.where(lane < HD, turned, pair).astype(jnp.bfloat16)


def attention_forward(qkv, w_output, tables, block_rows):
    length = qkv.shape[0]
    width = (H // KVH) * HD
    return pl.pallas_call(
        functools.partial(attention_forward_kernel, block_rows),
        out_shape=(
            jax.ShapeDtypeStruct((length, width), jnp.bfloat16),
            jax.ShapeDtypeStruct((length, 2 * HD), jnp.bfloat16),
            jax.ShapeDtypeStruct((length, width), jnp.bfloat16),
            jax.ShapeDtypeStruct((length, H // KVH), jnp.float32),
            jax.ShapeDtypeStruct((length, w_output.shape[1]), jnp.bfloat16),
        ),
        in_specs=in_vmem(6),
        out_specs=tuple(in_vmem(5)),
        compiler_params=pltpu.CompilerParams(vmem_limit_bytes=24 * 2**20),
        name="attend",
    )(qkv, w_output, *tables)


def attention_backward(q, kv, grad_out, lse, tables, block_rows):
    length, width = q.shape
    return pl.pallas_call(
        functools.partial(attention_backward_kernel, block_rows),
        out_shape=jax.ShapeDtypeStruct((length, width + 2 * HD), jnp.bfloat16),
        in_specs=in_vmem(8),
        out_specs=in_vmem(1)[0],
        scratch_shapes=[
            pltpu.VMEM((length, width), jnp.float32),
            pltpu.VMEM((length, 2 * HD), jnp.float32),
        ],
        compiler_params=pltpu.CompilerParams(vmem_limit_bytes=24 * 2**20),
        name="attend_back",
    )(q, kv, grad_out, lse, *tables)


def on_device(
    tokens,
    doc_lengths,
    cotangent,
    gain_attn,
    w_query,
    w_key,
    w_value,
    w_output,
    gain_mlp,
    w_gate,
    w_up,
    w_down,
):
    local_rows, model = tokens.shape[1:]
    ctx_size = lax.axis_size("ctx")
    fsdp_size = lax.axis_size("fsdp")
    length = local_rows * ctx_size
    group_width = (H // KVH) * HD
    ff_slice = FF // ctx_size
    held_rows = w_query.shape[0]
    bf16 = jnp.bfloat16

    positions = jnp.arange(length, dtype=jnp.int32)
    seq_lengths = doc_lengths[0]
    starts = jnp.cumsum(seq_lengths) - seq_lengths
    doc_ids = doc_index(positions, starts)
    cos_half, sin_half = rope_tables(positions)
    cos_table = jnp.concatenate([cos_half] * 4, axis=1)
    sin_table = jnp.concatenate([-sin_half, sin_half] * 2, axis=1)
    tables = (cos_table, sin_table, doc_ids[:, None], doc_ids[None, :])


    def by_slice(weight):
        return weight.reshape(held_rows, ctx_size, -1)

    qkv_parts = jnp.concatenate([by_slice(w_query), by_slice(w_key), by_slice(w_value)], axis=2)
    wo_mine = lax.all_gather(w_output, "fsdp", axis=0, tiled=True)
    wd_mine = lax.all_gather(w_down, "fsdp", axis=0, tiled=True)
    gain_rows = jnp.stack([gain_attn, gain_mlp]).astype(jnp.float32)
    odd = lax.axis_index("fsdp") % 2
    gain_tile = jnp.concatenate([gain_rows * (1 - odd), gain_rows * odd], axis=1)
    gain_tile = jnp.pad(gain_tile, ((0, 8 - gain_tile.shape[0]), (0, 128 - gain_tile.shape[1])))
    normed1, gains, w_qkv = start_layer(tokens[0], gain_tile, qkv_parts.transpose(1, 0, 2))
    grad_out = cotangent[0].astype(jnp.float32)
    grad_mlp = (RESIDUAL_MULT * grad_out).astype(bf16)

    block_rows = math.gcd(length, 256)
    normed1, grad_mlp = lax.optimization_barrier((normed1, grad_mlp))
    grad_mlp = lax.all_gather(grad_mlp, "ctx", axis=0, tiled=True)
    qkv = dot_plain(normed1, w_qkv)
    q, kv, mixed_heads, log_sum, branch1 = attention_forward(qkv, wo_mine, tables, block_rows)
    hidden, w_gu, normed2 = mlp_forward(branch1, tokens[0], gains, w_gate, w_up)
    w_gu = rows_of(rows_of(w_gu))

    gate_up = dot_plain(normed2, w_gu)
    gate_pre, up_pre = gate_up[:, :ff_slice], gate_up[:, ff_slice:]
    sig_gate = jax.nn.sigmoid(gate_pre)
    silu_gate = gate_pre * sig_gate
    activ = (silu_gate * up_pre).astype(bf16)
    activ, gate_up = lax.optimization_barrier((activ, gate_up))
    gate_pre, up_pre = gate_up[:, :ff_slice], gate_up[:, ff_slice:]
    sig_gate = jax.nn.sigmoid(gate_pre)
    silu_gate = gate_pre * sig_gate
    out_terms, grad_mlp = lax.optimization_barrier(
        (dot_plain(activ, wd_mine).astype(bf16), grad_mlp)
    )
    branch = lax.psum_scatter(out_terms, "ctx", scatter_dimension=0, tiled=True)

    silu_slope = sig_gate * (1.0 + gate_pre * (1.0 - sig_gate))
    grad_act = dot_back(grad_mlp, wd_mine)
    grad_gu = jnp.concatenate(
        [(grad_act * up_pre * silu_slope).astype(bf16), (grad_act * silu_gate).astype(bf16)], axis=1
    )
    partial2, gu_terms, wd_terms = lax.optimization_barrier(
        (
            dot_back(grad_gu, w_gu).astype(bf16),
            dot_outer(normed2, grad_gu).astype(bf16),
            dot_outer(activ, grad_mlp).astype(bf16),
        )
    )
    grad_hidden, grad_g2, gu_back, grad_attn = mlp_backward(
        partial2, hidden, cotangent[0], gains, gu_terms.reshape(fsdp_size, -1, gu_terms.shape[1])
    )
    gu_back = return_columns(gu_back, ctx_size)
    wd_back = lax.psum_scatter(wd_terms, "fsdp", scatter_dimension=0, tiled=True)

    grad_mixed = dot_back(grad_attn, wo_mine).astype(bf16)
    wo_terms = dot_outer(mixed_heads, grad_attn).astype(bf16)
    grad_qkv = attention_backward(q, kv, grad_mixed, log_sum, tables, block_rows)
    partial1 = dot_back(grad_qkv, w_qkv).astype(bf16)
    qkv_terms = by_fsdp(dot_outer(normed1, grad_qkv).astype(bf16), ctx_size, fsdp_size)
    grad_inputs, gain_back, wo_back, qkv_back = finish_layer(
        partial1,
        tokens[0],
        grad_hidden,
        gains,
        grad_g2,
        wo_terms.reshape(fsdp_size, held_rows, model),
        qkv_terms.reshape(fsdp_size, ctx_size, held_rows, -1),
    )
    grad_inputs, wd_back, gu_back, branch = lax.optimization_barrier(
        (grad_inputs, wd_back, gu_back, branch)
    )
    output = (hidden + RESIDUAL_MULT * branch.astype(jnp.float32)).astype(bf16)[None]
    gain_back = jnp.where(odd == 0, gain_back[:2, :held_rows], gain_back[:2, held_rows:])

    def joined(parts):
        return parts.transpose(1, 0, 2).reshape(held_rows, -1).astype(jnp.float32)

    key_end = group_width + HD
    return (
        output,
        grad_inputs[None],
        gain_back[0],
        joined(qkv_back[:, :, :group_width]),
        joined(qkv_back[:, :, group_width:key_end]),
        joined(qkv_back[:, :, key_end:]),
        wo_back,
        gain_back[1],
        joined(gu_back[:, :, :ff_slice]),
        joined(gu_back[:, :, ff_slice:]),
        wd_back.astype(jnp.float32),
    )


def solution(mesh):
    in_specs = (
        P("fsdp", "ctx", None),
        P("fsdp", None),
        P("fsdp", "ctx", None),
        P(("ctx", "fsdp")),
        P(("ctx", "fsdp"), None),
        P(("ctx", "fsdp"), None),
        P(("ctx", "fsdp"), None),
        P(("ctx", "fsdp"), None),
        P(("ctx", "fsdp")),
        P(("ctx", "fsdp"), None),
        P(("ctx", "fsdp"), None),
        P(("ctx", "fsdp"), None),
    )
    out_specs = (
        P("fsdp", "ctx", None),
        P("fsdp", "ctx", None),
        P(("ctx", "fsdp")),
        P(("ctx", "fsdp"), None),
        P(("ctx", "fsdp"), None),
        P(("ctx", "fsdp"), None),
        P(("ctx", "fsdp"), None),
        P(("ctx", "fsdp")),
        P(("ctx", "fsdp"), None),
        P(("ctx", "fsdp"), None),
        P(("ctx", "fsdp"), None),
    )
    if mesh.shape["ctx"] != KVH or KVH != 4 * PAIR:
        return jax.shard_map(
            general_device, mesh=mesh, in_specs=in_specs, out_specs=out_specs, check_vma=False
        )

    return jax.shard_map(
        on_device, mesh=mesh, in_specs=in_specs, out_specs=out_specs, check_vma=False
    )
```

```python
import functools
import math

import jax
import jax.numpy as jnp
from jax import lax
from jax.experimental import pallas as pl
from jax.experimental.pallas import tpu as pltpu
from jax.sharding import PartitionSpec as P

H = 32
KVH = 8
HD = 64
FF = 8192


EPSILON = 1e-05
SCORE_SCALE = 1.0 / 64.0
RESIDUAL_MULT = 0.22
ROPE_BASE = 10000000.0
NEGATIVE = -1e30
MESH = pl.DeviceIdType.MESH
PAIR = 2
CHUNKS = 2
ANYWHERE = pl.BlockSpec(memory_space=pl.ANY)
LINK_COST = pl.CostEstimate(flops=0, bytes_accessed=150_000_000, transcendentals=0)


def doc_index(positions, starts):
    return jnp.sum((positions[:, None] >= starts[None, :]).astype(jnp.int32), axis=1) - 1


def rope_tables(positions):
    half_size = HD // 2
    frequency = ROPE_BASE ** (-(jnp.arange(half_size, dtype=jnp.float32) * 2.0) / HD)
    angles = positions.astype(jnp.float32)[:, None] * frequency[None, :]
    return (jnp.cos(angles), jnp.sin(angles))


def rotate(tensor, cos_table, sin_table, head_count):
    row_count = tensor.shape[0]
    by_head = tensor.reshape(row_count, head_count, HD)
    half_size = HD // 2
    first_half = by_head[..., :half_size]
    second_half = by_head[..., half_size:]
    cos_rows = cos_table[:, None, :]
    sin_rows = sin_table[:, None, :]
    turned = jnp.concatenate(
        [
            first_half * cos_rows - second_half * sin_rows,
            second_half * cos_rows + first_half * sin_rows,
        ],
        axis=-1,
    )
    return turned.reshape(row_count, head_count * HD)


def dot_plain(left, right):
    return jnp.dot(left, right, preferred_element_type=jnp.float32)


def dot_back(left, right):
    return lax.dot_general(
        left, right, (((1,), (1,)), ((), ())), preferred_element_type=jnp.float32
    )


def dot_outer(left, right):
    return lax.dot_general(
        left, right, (((0,), (0,)), ((), ())), preferred_element_type=jnp.float32
    )


def norm_back(grad_normed, unit_rows, inv_scale, gain_full):
    scaled = grad_normed * gain_full
    return inv_scale * (scaled - unit_rows * jnp.mean(scaled * unit_rows, axis=-1, keepdims=True))


def general_device(
    tokens,
    doc_lengths,
    cotangent,
    gain_attn,
    w_query,
    w_key,
    w_value,
    w_output,
    gain_mlp,
    w_gate,
    w_up,
    w_down,
):
    local_rows = tokens.shape[1]
    ctx_size = lax.axis_size("ctx")
    length = local_rows * ctx_size
    group_size = H // KVH
    offset = lax.axis_index("ctx") * local_rows
    positions = offset + jnp.arange(local_rows, dtype=jnp.int32)
    seq_lengths = doc_lengths[0]
    starts = jnp.cumsum(seq_lengths) - seq_lengths
    doc_ids = doc_index(positions, starts)
    last_pos = offset + local_rows - 1
    first_doc = doc_ids[0]
    cos_table, sin_table = rope_tables(positions)
    gain1, gain2, wq_full, wk_full, wv_full, wo_full = (
        lax.all_gather(gain_attn, ("ctx", "fsdp"), axis=0, tiled=True),
        lax.all_gather(gain_mlp, ("ctx", "fsdp"), axis=0, tiled=True),
        lax.all_gather(w_query, ("ctx", "fsdp"), axis=0, tiled=True),
        lax.all_gather(w_key, ("ctx", "fsdp"), axis=0, tiled=True),
        lax.all_gather(w_value, ("ctx", "fsdp"), axis=0, tiled=True),
        lax.all_gather(w_output, ("ctx", "fsdp"), axis=0, tiled=True),
    )
    gain1_f = gain1.astype(jnp.float32)
    gain2_f = gain2.astype(jnp.float32)
    inputs = tokens[0].astype(jnp.float32)
    inv_one = lax.rsqrt(jnp.mean(inputs * inputs, axis=-1, keepdims=True) + EPSILON)
    unit_one = inputs * inv_one
    normed1 = (unit_one * gain1_f).astype(jnp.bfloat16)
    queries = rotate(dot_plain(normed1, wq_full), cos_table, sin_table, H).astype(jnp.bfloat16)
    key_rot = rotate(dot_plain(normed1, wk_full), cos_table, sin_table, KVH).astype(jnp.bfloat16)
    values = dot_plain(normed1, wv_full).astype(jnp.bfloat16)
    grouped = queries.reshape(local_rows, KVH, group_size, HD)
    start_state = (
        jnp.full((local_rows, KVH, group_size), NEGATIVE, jnp.float32),
        jnp.zeros((local_rows, KVH, group_size), jnp.float32),
        jnp.zeros((local_rows, KVH, group_size, HD), jnp.float32),
    )
    running = start_state
    key_piece = lax.all_gather(key_rot, "ctx", axis=0, tiled=True)
    value_piece = lax.all_gather(values, "ctx", axis=0, tiled=True)
    piece_rows = key_piece.shape[0]
    attend_key_width = math.gcd(piece_rows, 512)
    block_count = piece_rows // attend_key_width

    def one_block(carried, index_block):
        block_start = index_block * attend_key_width
        key_blk = lax.dynamic_slice_in_dim(key_piece, block_start, attend_key_width, 0).reshape(
            attend_key_width, KVH, HD
        )
        value_blk = lax.dynamic_slice_in_dim(value_piece, block_start, attend_key_width, 0).reshape(
            attend_key_width, KVH, HD
        )
        key_pos = block_start + jnp.arange(attend_key_width, dtype=jnp.int32)
        key_docs = doc_index(key_pos, starts)
        skip_block = (block_start > last_pos) | (key_docs[attend_key_width - 1] < first_doc)

        def update(current):
            run_max, run_sum, accumulated = current
            scores = (
                jnp.einsum("qkgd,tkd->qkgt", grouped, key_blk, preferred_element_type=jnp.float32)
                * SCORE_SCALE
            )
            allowed = (key_docs[None, :] == doc_ids[:, None]) & (
                key_pos[None, :] <= positions[:, None]
            )
            allowed = allowed[:, None, None, :]
            masked = jnp.where(allowed, scores, NEGATIVE)
            new_max = jnp.maximum(run_max, jnp.max(masked, axis=-1))
            weights_exp = jnp.where(allowed, jnp.exp(masked - new_max[..., None]), 0.0)
            factor = jnp.exp(run_max - new_max)
            new_sum = run_sum * factor + jnp.sum(weights_exp, axis=-1)
            new_acc = accumulated * factor[..., None] + jnp.einsum(
                "qkgt,tkd->qkgd",
                weights_exp.astype(jnp.bfloat16),
                value_blk,
                preferred_element_type=jnp.float32,
            )
            return (new_max, new_sum, new_acc)

        return (lax.cond(skip_block, lambda unchanged: unchanged, update, carried), None)

    running, _ = lax.scan(one_block, running, jnp.arange(block_count))
    run_max, run_sum, accumulated = running
    attended = accumulated / run_sum[..., None]
    log_sum = run_max + jnp.log(run_sum)
    mixed_heads = attended.reshape(local_rows, H * HD).astype(jnp.bfloat16)
    hidden = inputs + RESIDUAL_MULT * dot_plain(mixed_heads, wo_full)
    inv_two = lax.rsqrt(jnp.mean(hidden * hidden, axis=-1, keepdims=True) + EPSILON)
    unit_two = hidden * inv_two
    normed2 = (unit_two * gain2_f).astype(jnp.bfloat16)
    wg_full, wu_full, wd_full = (
        lax.all_gather(w_gate, ("ctx", "fsdp"), axis=0, tiled=True),
        lax.all_gather(w_up, ("ctx", "fsdp"), axis=0, tiled=True),
        lax.all_gather(w_down, ("ctx", "fsdp"), axis=0, tiled=True),
    )
    gate_pre = dot_plain(normed2, wg_full)
    up_pre = dot_plain(normed2, wu_full)
    sig_gate = jax.nn.sigmoid(gate_pre)
    silu_gate = gate_pre * sig_gate
    activ = (silu_gate * up_pre).astype(jnp.bfloat16)
    result = hidden + RESIDUAL_MULT * dot_plain(activ, wd_full)
    output = result.astype(jnp.bfloat16)[None]
    grad_out = cotangent[0].astype(jnp.float32)
    grad_mlp = (RESIDUAL_MULT * grad_out).astype(jnp.bfloat16)
    silu_slope = sig_gate * (1.0 + gate_pre * (1.0 - sig_gate))
    wg_back, wu_back, wd_back = (
        lax.all_gather(w_gate, ("ctx", "fsdp"), axis=0, tiled=True),
        lax.all_gather(w_up, ("ctx", "fsdp"), axis=0, tiled=True),
        lax.all_gather(w_down, ("ctx", "fsdp"), axis=0, tiled=True),
    )
    grad_act = dot_back(grad_mlp, wd_back)
    grad_gate = (grad_act * up_pre * silu_slope).astype(jnp.bfloat16)
    grad_up = (grad_act * silu_gate).astype(jnp.bfloat16)
    grad_norm2 = dot_back(grad_gate, wg_back) + dot_back(grad_up, wu_back)
    left_cols = normed2
    gate_up_shard = lax.psum_scatter(
        jnp.concatenate([dot_outer(left_cols, grad_gate), dot_outer(left_cols, grad_up)], axis=1),
        ("ctx", "fsdp"),
        scatter_dimension=0,
        tiled=True,
    )
    wg_shard = gate_up_shard[:, :FF]
    wu_shard = gate_up_shard[:, FF:]
    left_cols = activ
    wd_shard = lax.psum_scatter(
        dot_outer(left_cols, grad_mlp), ("ctx", "fsdp"), scatter_dimension=0, tiled=True
    )
    grad_g2 = jnp.sum(grad_norm2 * unit_two, axis=0)
    grad_hidden = grad_out + norm_back(grad_norm2, unit_two, inv_two, gain2_f)
    grad_attn = (RESIDUAL_MULT * grad_hidden).astype(jnp.bfloat16)
    wq_back, wk_back, wv_back, wo_back = (
        lax.all_gather(w_query, ("ctx", "fsdp"), axis=0, tiled=True),
        lax.all_gather(w_key, ("ctx", "fsdp"), axis=0, tiled=True),
        lax.all_gather(w_value, ("ctx", "fsdp"), axis=0, tiled=True),
        lax.all_gather(w_output, ("ctx", "fsdp"), axis=0, tiled=True),
    )
    grad_wo = dot_outer(mixed_heads, grad_attn)
    grad_att = (
        dot_back(grad_attn, wo_back).astype(jnp.bfloat16).reshape(local_rows, KVH, group_size, HD)
    )
    row_delta = jnp.sum(grad_att.astype(jnp.float32) * attended, axis=-1)
    key_all, value_all = (
        lax.all_gather(key_rot, "ctx", axis=0, tiled=True),
        lax.all_gather(values, "ctx", axis=0, tiled=True),
    )
    key_width = math.gcd(length, 512)
    block_count = length // key_width

    def back_block(grad_query, index_block):
        block_start = index_block * key_width
        key_blk = lax.dynamic_slice_in_dim(key_all, block_start, key_width, 0).reshape(
            key_width, KVH, HD
        )
        value_blk = lax.dynamic_slice_in_dim(value_all, block_start, key_width, 0).reshape(
            key_width, KVH, HD
        )
        key_pos = block_start + jnp.arange(key_width, dtype=jnp.int32)
        key_docs = doc_index(key_pos, starts)
        skip_block = (block_start > last_pos) | (key_docs[key_width - 1] < first_doc)

        def compute(current):
            scores = (
                jnp.einsum("qkgd,tkd->qkgt", grouped, key_blk, preferred_element_type=jnp.float32)
                * SCORE_SCALE
            )
            allowed = (key_docs[None, :] == doc_ids[:, None]) & (
                key_pos[None, :] <= positions[:, None]
            )
            allowed = allowed[:, None, None, :]
            probs_blk = jnp.where(
                allowed, jnp.exp(jnp.where(allowed, scores, NEGATIVE) - log_sum[..., None]), 0.0
            )
            grad_probs = jnp.einsum(
                "qkgd,tkd->qkgt", grad_att, value_blk, preferred_element_type=jnp.float32
            )
            grad_scores = (probs_blk * (grad_probs - row_delta[..., None])).astype(jnp.bfloat16)
            new_query = (
                current
                + jnp.einsum(
                    "qkgt,tkd->qkgd", grad_scores, key_blk, preferred_element_type=jnp.float32
                )
                * SCORE_SCALE
            )
            grad_key = (
                jnp.einsum(
                    "qkgt,qkgd->tkd", grad_scores, grouped, preferred_element_type=jnp.float32
                )
                * SCORE_SCALE
            )
            grad_value = jnp.einsum(
                "qkgt,qkgd->tkd",
                probs_blk.astype(jnp.bfloat16),
                grad_att,
                preferred_element_type=jnp.float32,
            )
            return (
                new_query,
                (grad_key.reshape(key_width, KVH * HD), grad_value.reshape(key_width, KVH * HD)),
            )

        def nothing(current):
            zero_rows = jnp.zeros((key_width, KVH * HD), jnp.float32)
            return (current, (zero_rows, zero_rows))

        return lax.cond(skip_block, nothing, compute, grad_query)

    grad_query, key_terms = lax.scan(
        back_block,
        jnp.zeros((local_rows, KVH, group_size, HD), jnp.float32),
        jnp.arange(block_count),
    )
    key_term_all = key_terms[0].reshape(length, KVH * HD)
    value_term_all = key_terms[1].reshape(length, KVH * HD)
    grad_keys, grad_values = (
        lax.psum_scatter(
            key_term_all.astype(jnp.bfloat16), "ctx", scatter_dimension=0, tiled=True
        ).astype(jnp.float32),
        lax.psum_scatter(
            value_term_all.astype(jnp.bfloat16), "ctx", scatter_dimension=0, tiled=True
        ).astype(jnp.float32),
    )
    grad_q_pre = rotate(grad_query.reshape(local_rows, H * HD), cos_table, -sin_table, H).astype(
        jnp.bfloat16
    )
    grad_k_pre = rotate(grad_keys, cos_table, -sin_table, KVH).astype(jnp.bfloat16)
    grad_v_pre = grad_values.astype(jnp.bfloat16)
    grad_norm1 = (
        dot_back(grad_q_pre, wq_back)
        + dot_back(grad_k_pre, wk_back)
        + dot_back(grad_v_pre, wv_back)
    )
    grad_wq = dot_outer(normed1, grad_q_pre)
    grad_wk = dot_outer(normed1, grad_k_pre)
    grad_wv = dot_outer(normed1, grad_v_pre)
    grad_g1 = jnp.sum(grad_norm1 * unit_one, axis=0)
    grad_inputs = grad_hidden + norm_back(grad_norm1, unit_one, inv_one, gain1_f)
    g1_shard, g2_shard, wq_shard, wk_shard, wv_shard, wo_shard = (
        lax.psum_scatter(grad_g1, ("ctx", "fsdp"), scatter_dimension=0, tiled=True),
        lax.psum_scatter(grad_g2, ("ctx", "fsdp"), scatter_dimension=0, tiled=True),
        lax.psum_scatter(grad_wq, ("ctx", "fsdp"), scatter_dimension=0, tiled=True),
        lax.psum_scatter(grad_wk, ("ctx", "fsdp"), scatter_dimension=0, tiled=True),
        lax.psum_scatter(grad_wv, ("ctx", "fsdp"), scatter_dimension=0, tiled=True),
        lax.psum_scatter(grad_wo, ("ctx", "fsdp"), scatter_dimension=0, tiled=True),
    )
    return (
        output,
        grad_inputs[None],
        g1_shard,
        wq_shard,
        wk_shard,
        wv_shard,
        wo_shard,
        g2_shard,
        wg_shard,
        wu_shard,
        wd_shard,
    )


def rows_of(blocks):
    return blocks.reshape((-1,) + blocks.shape[2:])


def in_vmem(count):
    return [pl.BlockSpec(memory_space=pltpu.VMEM)] * count


def greet_line(barrier, ctx_at, line_at, line_size, fsdp_size=1):
    for j in range(1, fsdp_size):
        peer = (lax.axis_index("fsdp") + j) % fsdp_size
        pl.semaphore_signal(barrier, inc=1, device_id={"fsdp": peer}, device_id_type=MESH)
    other = ctx_at + 1 - 2 * (ctx_at % PAIR)
    pl.semaphore_signal(barrier, inc=1, device_id={"ctx": other}, device_id_type=MESH)

    @pl.when(line_at > 0)
    def _():
        pl.semaphore_signal(barrier, inc=1, device_id={"ctx": ctx_at - PAIR}, device_id_type=MESH)

    @pl.when(line_at < line_size - 1)
    def _():
        pl.semaphore_signal(barrier, inc=1, device_id={"ctx": ctx_at + PAIR}, device_id_type=MESH)

    last = line_size - 1
    neighbours = fsdp_size + (line_at + last - 1) // last + (2 * last - 1 - line_at) // last
    pl.semaphore_wait(barrier, neighbours)


def greet_all(barrier, me, count, fsdp_size):
    def greet(k, unused):
        target = (me + k) % count
        pl.semaphore_signal(
            barrier, inc=1, device_id=(target // fsdp_size, target % fsdp_size), device_id_type=MESH
        )
        return unused

    lax.fori_loop(1, count, greet, 0)
    pl.semaphore_wait(barrier, count - 1)


def gather_phase(line_size, x_ref, out_ref, send_sem, recv_sem, own_sem):
    me = lax.axis_index("ctx")
    line_at, pair_at = me // PAIR, me % PAIR
    rows = x_ref.shape[0]
    step = rows // CHUNKS

    def piece(block, part):
        return out_ref.at[pl.ds(pl.multiple_of(block * rows + part * step, step), step), :]

    def copy(block, part, way, own):
        slot = block * CHUNKS + part
        return pltpu.make_async_remote_copy(
            src_ref=x_ref.at[pl.ds(part * step, step), :] if own else piece(block, part),
            dst_ref=piece(block, part),
            send_sem=send_sem.at[way, slot],
            recv_sem=recv_sem.at[slot],
            device_id={"ctx": (me + 1 - 2 * pair_at, me + PAIR, me - PAIR)[way]},
            device_id_type=MESH,
        )

    def pass_on(block, part, upward, downward, own, act):
        if upward is not None:
            pl.when(upward)(lambda: act(copy(block, part, 1, own)))
        if downward is not None:
            pl.when(downward)(lambda: act(copy(block, part, 2, own)))
        act(copy(block, part, 0, own))

    def own_part(part, act):
        pass_on(me, part, line_at < line_size - 1, line_at > 0, True, act)

    def others(act, arrive, between):
        for distance in range(1, line_size):
            between(distance)
            for part in range(CHUNKS):

                @pl.when(line_at >= distance)
                def _():
                    block = me - PAIR * distance
                    arrive(block, part)
                    pass_on(block, part, line_at < line_size - 1, None, False, act)

                @pl.when(line_at + distance < line_size)
                def _():
                    block = me + PAIR * distance
                    arrive(block, part)
                    pass_on(block, part, None, line_at > 0, False, act)

    def start_own(part):
        own_part(part, lambda c: c.start())

    def finish(between=lambda distance: None):
        keep = pltpu.make_async_copy(
            x_ref, out_ref.at[pl.ds(pl.multiple_of(me * rows, rows), rows), :], own_sem
        )
        keep.start()
        others(
            lambda c: c.start(),
            lambda block, part: copy(block, part, 0, False).wait_recv(),
            between,
        )
        between(line_size)
        for place in range(line_size):
            for part in range(CHUNKS):
                copy(place * PAIR + 1 - pair_at, part, 0, False).wait_recv()
        for part in range(CHUNKS):
            own_part(part, lambda c: c.wait_send())
        others(lambda c: c.wait_send(), lambda block, part: None, lambda distance: None)
        keep.wait()

    return start_own, finish


def gather_scratch(ctx_size):
    return [
        pltpu.SemaphoreType.DMA((3, ctx_size * CHUNKS)),
        pltpu.SemaphoreType.DMA((ctx_size * CHUNKS,)),
        pltpu.SemaphoreType.DMA,
    ]


def scatter_phase(line_size, x_ref, sum_ref, near, below, above, near_send, near_sem, line_send, line_sem, emit, midway=lambda: None, between=lambda turn: None):
    me = lax.axis_index("ctx")
    line_at, pair_at = me // PAIR, me % PAIR
    rows = sum_ref.shape[0]
    step = rows // CHUNKS
    last = line_size - 1
    low = line_at // (line_size // 2)
    order = [k + (last - 2 * k) * (1 - low) for k in range(line_size // 2)]
    order += [line_at + 1 - 2 * (line_at % 2), line_at]

    def near_copy(place, part):
        start = (place * PAIR + 1 - pair_at) * rows + part * step
        return pltpu.make_async_remote_copy(
            src_ref=x_ref.at[pl.ds(pl.multiple_of(start, step), step), :],
            dst_ref=near.at[place, pl.ds(part * step, step), :],
            send_sem=near_send.at[place, part],
            recv_sem=near_sem.at[place, part],
            device_id={"ctx": me + 1 - 2 * pair_at},
            device_id_type=MESH,
        )

    def line_copy(place, part, up):
        part_rows = pl.ds(part * step, step)
        return pltpu.make_async_remote_copy(
            src_ref=near.at[place, part_rows, :],
            dst_ref=(below if up else above).at[place, part_rows, :],
            send_sem=line_send.at[place, part],
            recv_sem=line_sem.at[0 if up else 1, place, part],
            device_id={"ctx": me + PAIR if up else me - PAIR},
            device_id_type=MESH,
        )

    def mine(place, part):
        start = (place * PAIR + pair_at) * rows + part * step
        return x_ref[pl.ds(pl.multiple_of(start, step), step), :].astype(jnp.float32)

    for place in order:
        for part in range(CHUNKS):
            near_copy(place, part).start()

    for turn, place in enumerate(order[:-1]):
        between(turn)
        for part in range(CHUNKS):
            part_rows = pl.ds(part * step, step)
            near_copy(place, part).wait_recv()

            def send(up, waits, arrived):
                @pl.when(waits)
                def _():
                    line_copy(place, part, up).wait_recv()
                    near[place, part_rows, :] = (
                        mine(place, part)
                        + near[place, part_rows, :].astype(jnp.float32)
                        + arrived[place, part_rows, :].astype(jnp.float32)
                    ).astype(near.dtype)

                @pl.when(jnp.logical_not(waits))
                def _():
                    near[place, part_rows, :] = (
                        mine(place, part) + near[place, part_rows, :].astype(jnp.float32)
                    ).astype(near.dtype)

                line_copy(place, part, up).start()

            pl.when(place > line_at)(lambda: send(True, line_at > 0, below))
            pl.when(place < line_at)(lambda: send(False, line_at < last, above))

    midway()
    for part in range(CHUNKS):
        part_rows = pl.ds(part * step, step)
        near_copy(line_at, part).wait_recv()
        sum_ref[part_rows, :] = mine(line_at, part) + near[line_at, part_rows, :].astype(jnp.float32)

        @pl.when(line_at > 0)
        def _():
            line_copy(line_at, part, True).wait_recv()
            sum_ref[part_rows, :] += below[line_at, part_rows, :].astype(jnp.float32)

        @pl.when(line_at < last)
        def _():
            line_copy(line_at, part, False).wait_recv()
            sum_ref[part_rows, :] += above[line_at, part_rows, :].astype(jnp.float32)

        emit(part, slice(part * step, (part + 1) * step))

    def finish():
        for place in order:
            for part in range(CHUNKS):
                near_copy(place, part).wait_send()
        for place in order[:-1]:
            for part in range(CHUNKS):
                line_copy(place, part, True).wait_send()

    return finish


def scatter_scratch(ctx_size, rows, width):
    line_size = ctx_size // PAIR
    held = pltpu.VMEM((line_size, rows, width), jnp.bfloat16)
    return [
        held,
        held,
        held,
        pltpu.SemaphoreType.DMA((line_size, CHUNKS)),
        pltpu.SemaphoreType.DMA((line_size, CHUNKS)),
        pltpu.SemaphoreType.DMA((line_size, CHUNKS)),
        pltpu.SemaphoreType.DMA((2, line_size, CHUNKS)),
    ]


def swap_lanes(values, outer, inner):
    tile = 128
    half = tile // 2
    low = lax.broadcasted_iota(jnp.int32, (values.shape[0], tile), 1) < half
    placed = [None] * (outer * inner // 2)
    for first in range(0, outer, 2):
        for second in range(0, inner, 2):
            at = (first * inner + second) // 2
            one = values[:, at * tile : (at + 1) * tile]
            at += inner // 2
            two = values[:, at * tile : (at + 1) * tile]
            at = (second * outer + first) // 2
            placed[at] = jnp.where(low, one, pltpu.roll(two, half, 1))
            placed[at + outer // 2] = jnp.where(low, pltpu.roll(one, half, 1), two)
    return jnp.concatenate(placed, axis=1)


def start_kernel(
    ctx_size, fsdp_size, tokens_ref, tile_ref, parts_ref, out_ref, gains_ref, weight_ref,
    tiles, normed, tile_send, tile_recv, far_send, far_recv, near_send, near_recv, kept, *sems
):
    me_ctx, me_fsdp = lax.axis_index("ctx"), lax.axis_index("fsdp")
    count = ctx_size * fsdp_size
    me = me_ctx * fsdp_size + me_fsdp
    greet_all(pltpu.get_barrier_semaphore(), me, count, fsdp_size)

    def tile_copy(k, source):
        target = (me + k) % count
        return pltpu.make_async_remote_copy(
            src_ref=tile_ref,
            dst_ref=tiles.at[source],
            send_sem=tile_send.at[k],
            recv_sem=tile_recv.at[k],
            device_id=(target // fsdp_size, target % fsdp_size),
            device_id_type=MESH,
        )

    def start_tile(k, unused):
        tile_copy(k, me).start()
        return unused

    def finish_tile(k, unused):
        tile_copy(k, (me + count - k) % count).wait_recv()
        return unused

    lax.fori_loop(1, count, start_tile, 0)
    tiles[pl.ds(me, 1)] = tile_ref[...][None]

    def far_copy(k, source):
        target = (me_ctx + k) % ctx_size
        return pltpu.make_async_remote_copy(
            src_ref=parts_ref.at[target],
            dst_ref=weight_ref.at[source * fsdp_size + me_fsdp],
            send_sem=far_send.at[k],
            recv_sem=far_recv.at[k],
            device_id={"ctx": target},
            device_id_type=MESH,
        )

    def near_copy(k, j, fsdp_source):
        block = (me_ctx + ctx_size - k) % ctx_size * fsdp_size + fsdp_source
        return pltpu.make_async_remote_copy(
            src_ref=parts_ref.at[me_ctx] if k == 0 else weight_ref.at[block],
            dst_ref=weight_ref.at[block],
            send_sem=near_send.at[k, j],
            recv_sem=near_recv.at[k, j],
            device_id={"fsdp": (me_fsdp + j) % fsdp_size},
            device_id_type=MESH,
        )

    for k in range(1, ctx_size):
        far_copy(k, me_ctx).start()
    for j in range(1, fsdp_size):
        near_copy(0, j, me_fsdp).start()
    keep = pltpu.make_async_copy(parts_ref.at[me_ctx], weight_ref.at[me], kept)
    keep.start()

    rows, model = tokens_ref.shape
    lax.fori_loop(1, count, finish_tile, 0)
    held = model // count
    for pair in range(count // 2):
        cols = slice(pair * 2 * held, (pair + 1) * 2 * held)
        gains_ref[:, cols] = tiles[2 * pair] + tiles[2 * pair + 1]
    start_own, finish_gather = gather_phase(ctx_size // PAIR, normed, out_ref, *sems)
    step = rows // CHUNKS
    for part in range(CHUNKS):
        part_rows = slice(part * step, (part + 1) * step)
        values = tokens_ref[part_rows, :].astype(jnp.float32)
        scale = lax.rsqrt(jnp.mean(values * values, axis=-1, keepdims=True) + EPSILON)
        normed[part_rows, :] = (values * scale * gains_ref[0:1, :]).astype(normed.dtype)
        start_own(part)
    for k in range(1, ctx_size):
        far_copy(k, (me_ctx + ctx_size - k) % ctx_size).wait_recv()
        for j in range(1, fsdp_size):
            near_copy(k, j, me_fsdp).start()
    finish_gather()
    for k in range(ctx_size):
        for j in range(1, fsdp_size):
            near_copy(k, j, (me_fsdp + fsdp_size - j) % fsdp_size).wait_recv()
    for k in range(ctx_size):
        for j in range(1, fsdp_size):
            near_copy(k, j, me_fsdp).wait_send()
    for k in range(1, ctx_size):
        far_copy(k, me_ctx).wait_send()

    def sent_tile(k, unused):
        tile_copy(k, me).wait_send()
        return unused

    lax.fori_loop(1, count, sent_tile, 0)
    keep.wait()


def start_layer(tokens, tile, parts):
    ctx_size, fsdp_size = lax.axis_size("ctx"), lax.axis_size("fsdp")
    count = ctx_size * fsdp_size
    rows, model = tokens.shape
    dma = pltpu.SemaphoreType.DMA
    normed1, gains, weight = pl.pallas_call(
        functools.partial(start_kernel, ctx_size, fsdp_size),
        out_shape=(
            jax.ShapeDtypeStruct((ctx_size * rows, model), jnp.bfloat16),
            jax.ShapeDtypeStruct((8, model), jnp.float32),
            jax.ShapeDtypeStruct((count,) + parts.shape[1:], parts.dtype),
        ),
        in_specs=in_vmem(3),
        out_specs=(ANYWHERE, in_vmem(1)[0], ANYWHERE),
        scratch_shapes=[
            pltpu.VMEM((count, 8, 128), jnp.float32),
            pltpu.VMEM((rows, model), jnp.bfloat16),
            dma((count,)),
            dma((count,)),
            dma((ctx_size,)),
            dma((ctx_size,)),
            dma((ctx_size, fsdp_size)),
            dma((ctx_size, fsdp_size)),
            dma,
        ]
        + gather_scratch(ctx_size),
        compiler_params=pltpu.CompilerParams(
            collective_id=0, has_side_effects=True, vmem_limit_bytes=10 * 2**20
        ),
        cost_estimate=LINK_COST,
        name="start_layer",
    )(tokens, tile, parts)
    return normed1, gains, rows_of(weight)


def spread_phase(ctx_size, fsdp_size, gate_ref, up_ref, wide_ref, send, recv, side_send, side_recv, kept):
    me, me_fsdp = lax.axis_index("ctx"), lax.axis_index("fsdp")
    along = (me_fsdp + fsdp_size // 2) % fsdp_size
    beside = me_fsdp + 1 - 2 * (me_fsdp % 2)
    diagonal = (beside + fsdp_size // 2) % fsdp_size
    wide = gate_ref.shape[1] // ctx_size

    def part(which, target, source):
        cols = pl.ds(pl.multiple_of(target * wide, wide), wide)
        return (
            (gate_ref, up_ref)[which].at[:, cols],
            wide_ref.at[me_fsdp, source, :, which * wide : (which + 1) * wide],
        )

    def copy(which, k, source):
        target = (me + k) % ctx_size
        src, dst = part(which, target, source)
        return pltpu.make_async_remote_copy(
            src_ref=src,
            dst_ref=dst,
            send_sem=send.at[which, k],
            recv_sem=recv.at[which, k],
            device_id={"ctx": target},
            device_id_type=MESH,
        )

    def keep(which):
        return pltpu.make_async_copy(*part(which, me, me), kept.at[which])

    def side(way, k, rows_of_device):
        block = (rows_of_device, (me + ctx_size - k) % ctx_size)
        return pltpu.make_async_remote_copy(
            src_ref=wide_ref.at[block],
            dst_ref=wide_ref.at[block],
            send_sem=side_send.at[way, k],
            recv_sem=side_recv.at[way, k],
            device_id={"fsdp": along if way == 0 else beside},
            device_id_type=MESH,
        )

    def begin():
        for which in range(2):
            keep(which).start()
        for k in list(range(2, ctx_size, 2)) + list(range(1, ctx_size, 2)):
            for which in range(2):
                copy(which, k, me).start()

    def pass_on(k):
        for which in range(2):
            if k:
                copy(which, k, (me + ctx_size - k) % ctx_size).wait_recv()
            else:
                keep(which).wait()
        side(0, k, me_fsdp).start()
        side(1, k, me_fsdp).start()

    def relay(k):
        side(0, k, along).wait_recv()
        side(2, k, along).start()

    def finish():
        for k in range(ctx_size):
            side(1, k, beside).wait_recv()
            side(2, k, diagonal).wait_recv()
        for k in range(ctx_size):
            for way in range(3):
                side(way, k, me_fsdp).wait_send()
            if k:
                for which in range(2):
                    copy(which, k, me).wait_send()

    return begin, pass_on, relay, finish


def mlp_forward_kernel(
    ctx_size, fsdp_size, x_ref, tokens_ref, gains_ref, gate_ref, up_ref, hidden_ref, wide_ref, out_ref,
    sums, normed, wide_send, wide_recv, side_send, side_recv, kept, *sems
):
    line_size = ctx_size // PAIR
    me, me_fsdp = lax.axis_index("ctx"), lax.axis_index("fsdp")
    barrier = pltpu.get_barrier_semaphore()
    for k in range(1, ctx_size):
        pl.semaphore_signal(barrier, inc=1, device_id={"ctx": (me + k) % ctx_size}, device_id_type=MESH)
    for j in range(1, fsdp_size):
        pl.semaphore_signal(
            barrier, inc=1, device_id={"fsdp": (me_fsdp + j) % fsdp_size}, device_id_type=MESH
        )
    pl.semaphore_wait(barrier, ctx_size + fsdp_size - 2)
    start_own, finish_gather = gather_phase(line_size, normed, out_ref, *sems[7:])
    begin, pass_on, relay, finish_spread = spread_phase(
        ctx_size, fsdp_size, gate_ref, up_ref, wide_ref, wide_send, wide_recv, side_send, side_recv, kept
    )
    even = list(range(0, ctx_size, 2))
    odd = list(range(1, ctx_size, 2))

    def during_scatter(turn):
        if turn == 0:
            begin()
        if turn == 1:
            pass_on(0)
        if turn == 2:
            pass_on(2)

    def midway():
        for k in even[2:]:
            pass_on(k)
        for k in even[:2]:
            relay(k)

    def during_gather(distance):
        if distance == line_size - 2:
            for k in even[2:]:
                relay(k)
            for k in odd[:2]:
                pass_on(k)
        if distance == line_size - 1:
            for k in odd[2:]:
                pass_on(k)
        if distance == line_size:
            for k in odd:
                relay(k)

    def emit(part, rows):
        hidden = tokens_ref[rows, :].astype(jnp.float32) + RESIDUAL_MULT * sums[rows, :]
        hidden_ref[rows, :] = hidden
        scale = lax.rsqrt(jnp.mean(hidden * hidden, axis=-1, keepdims=True) + EPSILON)
        scaled = hidden * scale * gains_ref[1:2, :]
        normed[rows, :] = swap_lanes(scaled, ctx_size, fsdp_size).astype(normed.dtype)
        start_own(part)

    finish_scatter = scatter_phase(
        line_size, x_ref, sums, *sems[:7], emit, midway, during_scatter
    )
    finish_gather(during_gather)
    finish_spread()
    finish_scatter()


def mlp_backward_kernel(
    ctx_size, fsdp_size, x_ref, hidden_ref, grad_ref, gains_ref, terms_ref, grad_hidden_ref, grad_gain_ref,
    total_ref, out_ref, sums, normed, landing, side_send, side_recv, own_sem, *sems
):
    line_size = ctx_size // PAIR
    me, me_fsdp = lax.axis_index("ctx"), lax.axis_index("fsdp")
    greet_line(pltpu.get_barrier_semaphore(), me, me // PAIR, line_size, fsdp_size)

    def side_copy(j):
        target = (me_fsdp + j) % fsdp_size
        return pltpu.make_async_remote_copy(
            src_ref=terms_ref.at[target],
            dst_ref=landing.at[j],
            send_sem=side_send.at[j],
            recv_sem=side_recv.at[j],
            device_id={"fsdp": target},
            device_id_type=MESH,
        )

    own_copy = pltpu.make_async_copy(terms_ref.at[me_fsdp], landing.at[0], own_sem)
    for j in range(1, fsdp_size):
        side_copy(j).start()
    own_copy.start()
    start_own, finish_gather = gather_phase(line_size, normed, out_ref, *sems[7:])

    def emit(part, rows):
        grad_norm = swap_lanes(sums[rows, :], fsdp_size, ctx_size)
        hidden = hidden_ref[rows, :]
        scale = lax.rsqrt(jnp.mean(hidden * hidden, axis=-1, keepdims=True) + EPSILON)
        unit = hidden * scale
        grad_gain_ref[part : part + 1, :] = jnp.sum(grad_norm * unit, axis=0, keepdims=True)
        grad_hidden = grad_ref[rows, :].astype(jnp.float32) + norm_back(
            grad_norm, unit, scale, gains_ref[1:2, :]
        )
        grad_hidden_ref[rows, :] = grad_hidden
        normed[rows, :] = (RESIDUAL_MULT * grad_hidden).astype(normed.dtype)
        start_own(part)

    finish_scatter = scatter_phase(line_size, x_ref, sums, *sems[:7], emit)
    finish_gather()
    own_copy.wait()
    for j in range(1, fsdp_size):
        side_copy(j).wait_recv()
    step = 64

    def add(at, unused):
        rows = pl.ds(pl.multiple_of(at * step, step), step)
        total = landing[0, rows, :].astype(jnp.float32)
        for j in range(1, fsdp_size):
            total += landing[j, rows, :].astype(jnp.float32)
        total_ref[rows, :] = total.astype(total_ref.dtype)
        return unused

    lax.fori_loop(0, total_ref.shape[0] // step, add, 0)
    for j in range(1, fsdp_size):
        side_copy(j).wait_send()
    finish_scatter()


def scatter_gather(kernel, collective_id, extra_shapes, partial, *others, specs=(), out_specs=(), scratch=(), grant=24):
    ctx_size, fsdp_size = lax.axis_size("ctx"), lax.axis_size("fsdp")
    rows, model = partial.shape[0] // ctx_size, partial.shape[1]
    return pl.pallas_call(
        functools.partial(kernel, ctx_size, fsdp_size),
        out_shape=extra_shapes + (jax.ShapeDtypeStruct(partial.shape, jnp.bfloat16),),
        in_specs=in_vmem(1 + len(others) - len(specs)) + list(specs),
        out_specs=tuple(in_vmem(len(extra_shapes) - len(out_specs))) + tuple(out_specs) + (ANYWHERE,),
        scratch_shapes=[pltpu.VMEM((rows, model), jnp.float32), pltpu.VMEM((rows, model), jnp.bfloat16)]
        + list(scratch)
        + scatter_scratch(ctx_size, rows, model)
        + gather_scratch(ctx_size),
        compiler_params=pltpu.CompilerParams(
            collective_id=collective_id, has_side_effects=True, vmem_limit_bytes=grant * 2**20
        ),
        cost_estimate=LINK_COST,
    )(partial, *others)


def mlp_forward(partial, tokens, gains, w_gate, w_up):
    ctx_size, fsdp_size = lax.axis_size("ctx"), lax.axis_size("fsdp")
    hidden = jax.ShapeDtypeStruct(tokens.shape, jnp.float32)
    slices = (fsdp_size, ctx_size, w_gate.shape[0], 2 * w_gate.shape[1] // ctx_size)
    dma = pltpu.SemaphoreType.DMA
    return scatter_gather(
        mlp_forward_kernel,
        1,
        (hidden, jax.ShapeDtypeStruct(slices, w_gate.dtype)),
        partial,
        tokens,
        gains,
        w_gate,
        w_up,
        out_specs=(ANYWHERE,),
        scratch=(
            dma((2, ctx_size)),
            dma((2, ctx_size)),
            dma((3, ctx_size)),
            dma((3, ctx_size)),
            dma((2,)),
        ),
    )


def mlp_backward(partial, hidden, grad_out, gains, terms):
    like = jax.ShapeDtypeStruct(hidden.shape, jnp.float32)
    gain = jax.ShapeDtypeStruct((CHUNKS, hidden.shape[1]), jnp.float32)
    return scatter_gather(
        mlp_backward_kernel,
        2,
        (like, gain, jax.ShapeDtypeStruct(terms.shape[1:], terms.dtype)),
        partial,
        hidden,
        grad_out,
        gains,
        terms,
        grant=36,
        specs=(ANYWHERE,),
        scratch=(
            pltpu.VMEM(terms.shape, terms.dtype),
            pltpu.SemaphoreType.DMA((terms.shape[0],)),
            pltpu.SemaphoreType.DMA((terms.shape[0],)),
            pltpu.SemaphoreType.DMA,
        ),
    )


def finish_kernel(
    ctx_size, fsdp_size, x_ref, tokens_ref, grad_ref, gains_ref, gain2_ref, wo_ref, qkv_ref,
    grad_tokens_ref, gain_out_ref, wo_out_ref, qkv_out_ref,
    sums, gain1, tiles, arrived, wo_in, qkv_in, qkv_sum, tile_send, tile_recv, near_send, near_recv,
    far_send, far_recv, *sems
):
    line_size = ctx_size // PAIR
    me_ctx, me_fsdp = lax.axis_index("ctx"), lax.axis_index("fsdp")
    count = ctx_size * fsdp_size
    me = me_ctx * fsdp_size + me_fsdp
    greet_all(pltpu.get_barrier_semaphore(), me, count, fsdp_size)

    def near_copy(which, j):
        target = (me_fsdp + j) % fsdp_size
        terms, landing = ((wo_ref, wo_in), (qkv_ref, qkv_in))[which]
        return pltpu.make_async_remote_copy(
            src_ref=terms.at[target],
            dst_ref=landing.at[j],
            send_sem=near_send.at[which, j],
            recv_sem=near_recv.at[which, j],
            device_id={"fsdp": target},
            device_id_type=MESH,
        )

    def far_copy(k, source):
        target = (me_ctx + k) % ctx_size
        return pltpu.make_async_remote_copy(
            src_ref=qkv_sum.at[target],
            dst_ref=qkv_out_ref.at[source],
            send_sem=far_send.at[k],
            recv_sem=far_recv.at[k],
            device_id={"ctx": target},
            device_id_type=MESH,
        )

    def tile_copy(k, source):
        target = (me + k) % count
        return pltpu.make_async_remote_copy(
            src_ref=tiles.at[target // 2],
            dst_ref=arrived.at[source],
            send_sem=tile_send.at[k],
            recv_sem=tile_recv.at[k],
            device_id=(target // fsdp_size, target % fsdp_size),
            device_id_type=MESH,
        )

    def midway():
        for which, own, landing in ((1, qkv_ref, qkv_in), (0, wo_ref, wo_in)):
            for j in range(1, fsdp_size):
                near_copy(which, j).wait_recv()
            total = own[pl.ds(me_fsdp, 1)][0].astype(jnp.float32)
            for j in range(1, fsdp_size):
                total += landing[j].astype(jnp.float32)
            if which:
                qkv_sum[...] = total.astype(qkv_sum.dtype)
                for k in range(1, ctx_size):
                    far_copy(k, me_ctx).start()
                qkv_out_ref[pl.ds(me_ctx, 1)] = qkv_sum[pl.ds(me_ctx, 1)]
            else:
                wo_out_ref[...] = total

    def emit(part, rows):
        grad_norm = sums[rows, :]
        values = tokens_ref[rows, :].astype(jnp.float32)
        scale = lax.rsqrt(jnp.mean(values * values, axis=-1, keepdims=True) + EPSILON)
        unit = values * scale
        gain1[part : part + 1, :] = jnp.sum(grad_norm * unit, axis=0, keepdims=True)
        grad_tokens_ref[rows, :] = grad_ref[rows, :] + norm_back(
            grad_norm, unit, scale, gains_ref[0:1, :]
        )

    for which in (1, 0):
        for j in range(1, fsdp_size):
            near_copy(which, j).start()
    finish_scatter = scatter_phase(line_size, x_ref, sums, *sems, emit, midway)
    row = lax.broadcasted_iota(jnp.int32, (8, 128), 0)
    for pair in range(count // 2):
        cols = slice(pair * 128, (pair + 1) * 128)
        first = jnp.sum(gain1[:, cols], axis=0, keepdims=True)
        second = jnp.sum(gain2_ref[:, cols], axis=0, keepdims=True)
        tiles[pair] = jnp.where(row == 0, first, jnp.where(row == 1, second, 0.0))

    def start_tile(k, unused):
        tile_copy(k, me).start()
        return unused

    def finish_tile(k, unused):
        tile_copy(k, (me + count - k) % count).wait_recv()
        return unused

    def sent_tile(k, unused):
        tile_copy(k, me).wait_send()
        return unused

    lax.fori_loop(1, count, start_tile, 0)
    arrived[pl.ds(me, 1)] = tiles[pl.ds(me // 2, 1)]
    for k in range(1, ctx_size):
        far_copy(k, (me_ctx + ctx_size - k) % ctx_size).wait_recv()
    lax.fori_loop(1, count, finish_tile, 0)
    gain_out_ref[...] = jnp.sum(arrived[...], axis=0)
    finish_scatter()
    for which in range(2):
        for j in range(1, fsdp_size):
            near_copy(which, j).wait_send()
    for k in range(1, ctx_size):
        far_copy(k, me_ctx).wait_send()
    lax.fori_loop(1, count, sent_tile, 0)


def finish_layer(partial, tokens, grad_hidden, gains, grad_gain2, wo_terms, qkv_terms):
    ctx_size, fsdp_size = lax.axis_size("ctx"), lax.axis_size("fsdp")
    count = ctx_size * fsdp_size
    rows, model = tokens.shape
    dma = pltpu.SemaphoreType.DMA
    f32, bf16 = jnp.float32, jnp.bfloat16
    held, width = qkv_terms.shape[2:]
    return pl.pallas_call(
        functools.partial(finish_kernel, ctx_size, fsdp_size),
        out_shape=(
            jax.ShapeDtypeStruct((rows, model), f32),
            jax.ShapeDtypeStruct((8, 128), f32),
            jax.ShapeDtypeStruct(wo_terms.shape[1:], f32),
            jax.ShapeDtypeStruct((ctx_size, held, width), bf16),
        ),
        in_specs=in_vmem(7),
        out_specs=tuple(in_vmem(4)),
        scratch_shapes=[
            pltpu.VMEM((rows, model), f32),
            pltpu.VMEM((CHUNKS, model), f32),
            pltpu.VMEM((count // 2, 8, 128), f32),
            pltpu.VMEM((count, 8, 128), f32),
            pltpu.VMEM(wo_terms.shape, bf16),
            pltpu.VMEM(qkv_terms.shape, bf16),
            pltpu.VMEM((ctx_size, held, width), bf16),
            dma((count,)),
            dma((count,)),
            dma((2, fsdp_size)),
            dma((2, fsdp_size)),
            dma((ctx_size,)),
            dma((ctx_size,)),
        ]
        + scatter_scratch(ctx_size, rows, model),
        compiler_params=pltpu.CompilerParams(
            collective_id=3, has_side_effects=True, vmem_limit_bytes=32 * 2**20
        ),
        cost_estimate=LINK_COST,
        name="finish_layer",
    )(partial, tokens, grad_hidden, gains, grad_gain2, wo_terms, qkv_terms)


def swap_ctx(blocks):
    return lax.all_to_all(blocks, "ctx", split_axis=0, concat_axis=0, tiled=True)


def by_fsdp(grad, ctx_size, fsdp_size):
    parts = grad.reshape(ctx_size, fsdp_size, -1, grad.shape[-1]).transpose(1, 0, 2, 3)
    return rows_of(rows_of(parts))


def return_columns(terms, ctx_size):
    return swap_ctx(terms.reshape(ctx_size, -1, terms.shape[-1]))


def half_turn(values, sign_table):
    lane = lax.broadcasted_iota(jnp.int32, values.shape, 1)
    width = values.shape[1]
    quarter = HD // 2
    ahead = pltpu.roll(values, width - quarter, 1)
    behind = pltpu.roll(values, quarter, 1)
    return jnp.where(lane % HD < quarter, ahead, behind) * sign_table


def turn(values, cos_table, sign_table):
    copies = values.shape[1] // cos_table.shape[1]
    if copies > 1:
        cos_table = jnp.concatenate([cos_table] * copies, axis=1)
        sign_table = jnp.concatenate([sign_table] * copies, axis=1)
    return values * cos_table + half_turn(values, sign_table)


def attention_forward_kernel(
    block_rows, qkv_ref, cos_ref, sin_ref, doc_col_ref, doc_row_ref, q_ref, kv_ref, out_ref, lse_ref
):
    length = qkv_ref.shape[0]
    group = H // KVH
    width = group * HD
    q_ref[...] = turn(qkv_ref[:, :width], cos_ref[...], sin_ref[...]).astype(jnp.bfloat16)
    pair = qkv_ref[:, width:]
    lane = lax.broadcasted_iota(jnp.int32, pair.shape, 1)
    turned = turn(pair, cos_ref[...], sin_ref[...])
    kv_ref[...] = jnp.where(lane < HD, turned, pair).astype(jnp.bfloat16)
    for block in range(length // block_rows):
        rows = slice(block * block_rows, (block + 1) * block_rows)
        reach = (block + 1) * block_rows
        keys = kv_ref[:reach, :HD]
        values = kv_ref[:reach, HD:]
        query_at = block * block_rows + lax.broadcasted_iota(jnp.int32, (block_rows, reach), 0)
        key_at = lax.broadcasted_iota(jnp.int32, (block_rows, reach), 1)
        allowed = (doc_col_ref[rows, :] == doc_row_ref[:, :reach]) & (key_at <= query_at)
        for head in range(group):
            cols = slice(head * HD, (head + 1) * HD)
            scores = dot_back(q_ref[rows, cols], keys) * SCORE_SCALE
            masked = jnp.where(allowed, scores, NEGATIVE)
            top = jnp.max(masked, axis=1, keepdims=True)
            weights = jnp.where(allowed, jnp.exp(masked - top), 0.0)
            total = jnp.sum(weights, axis=1, keepdims=True)
            mixed = dot_plain(weights.astype(jnp.bfloat16), values)
            out_ref[rows, cols] = (mixed / total).astype(jnp.bfloat16)
            lse_ref[rows, head : head + 1] = top + jnp.log(total)


def attention_backward_kernel(
    block_rows, q_ref, kv_ref, do_ref, lse_ref, cos_ref, sin_ref, doc_col_ref, doc_row_ref, grad_ref, dq_ref, dkv_ref
):
    length = q_ref.shape[0]
    group = H // KVH
    width = group * HD
    dkv_ref[...] = jnp.zeros_like(dkv_ref)
    for block in range(length // block_rows):
        rows = slice(block * block_rows, (block + 1) * block_rows)
        reach = (block + 1) * block_rows
        keys = kv_ref[:reach, :HD]
        values = kv_ref[:reach, HD:]
        query_at = block * block_rows + lax.broadcasted_iota(jnp.int32, (block_rows, reach), 0)
        key_at = lax.broadcasted_iota(jnp.int32, (block_rows, reach), 1)
        allowed = (doc_col_ref[rows, :] == doc_row_ref[:, :reach]) & (key_at <= query_at)
        for head in range(group):
            cols = slice(head * HD, (head + 1) * HD)
            query = q_ref[rows, cols]
            grad_out = do_ref[rows, cols]
            scores = dot_back(query, keys) * SCORE_SCALE
            probs = jnp.where(
                allowed,
                jnp.exp(jnp.where(allowed, scores, NEGATIVE) - lse_ref[rows, head : head + 1]),
                0.0,
            )
            grad_probs = dot_back(grad_out, values)
            delta = jnp.sum(probs * grad_probs, axis=1, keepdims=True)
            grad_scores = (probs * (grad_probs - delta)).astype(jnp.bfloat16)
            dq_ref[rows, cols] = dot_plain(grad_scores, keys) * SCORE_SCALE
            dkv_ref[:reach, :HD] += dot_outer(grad_scores, query) * SCORE_SCALE
            dkv_ref[:reach, HD:] += dot_outer(probs.astype(jnp.bfloat16), grad_out)
    grad_ref[:, :width] = turn(dq_ref[...], cos_ref[...], -sin_ref[...]).astype(jnp.bfloat16)
    pair = dkv_ref[...]
    lane = lax.broadcasted_iota(jnp.int32, pair.shape, 1)
    turned = turn(pair, cos_ref[...], -sin_ref[...])
    grad_ref[:, width:] = jnp.where(lane < HD, turned, pair).astype(jnp.bfloat16)


def attention_forward(qkv, tables, block_rows):
    length = qkv.shape[0]
    width = (H // KVH) * HD
    return pl.pallas_call(
        functools.partial(attention_forward_kernel, block_rows),
        out_shape=(
            jax.ShapeDtypeStruct((length, width), jnp.bfloat16),
            jax.ShapeDtypeStruct((length, 2 * HD), jnp.bfloat16),
            jax.ShapeDtypeStruct((length, width), jnp.bfloat16),
            jax.ShapeDtypeStruct((length, H // KVH), jnp.float32),
        ),
        in_specs=in_vmem(5),
        out_specs=tuple(in_vmem(4)),
        compiler_params=pltpu.CompilerParams(vmem_limit_bytes=24 * 2**20),
        name="attend",
    )(qkv, *tables)


def attention_backward(q, kv, grad_out, lse, tables, block_rows):
    length, width = q.shape
    return pl.pallas_call(
        functools.partial(attention_backward_kernel, block_rows),
        out_shape=jax.ShapeDtypeStruct((length, width + 2 * HD), jnp.bfloat16),
        in_specs=in_vmem(8),
        out_specs=in_vmem(1)[0],
        scratch_shapes=[
            pltpu.VMEM((length, width), jnp.float32),
            pltpu.VMEM((length, 2 * HD), jnp.float32),
        ],
        compiler_params=pltpu.CompilerParams(vmem_limit_bytes=24 * 2**20),
        name="attend_back",
    )(q, kv, grad_out, lse, *tables)


def mlp_kernel(normed_ref, grad_ref, gu_ref, down_ref, activ_ref, out_ref, grad_gu_ref, back_ref):
    ff = down_ref.shape[0]
    bf16 = jnp.bfloat16
    gate_up = dot_plain(normed_ref[...], gu_ref[...])
    gate, up = gate_up[:, :ff], gate_up[:, ff:]
    sig = jax.nn.sigmoid(gate)
    silu = gate * sig
    activ_ref[...] = (silu * up).astype(bf16)
    grad_act = dot_back(grad_ref[...], down_ref[...])
    grad_gu_ref[:, :ff] = (grad_act * up * (sig * (1.0 + gate * (1.0 - sig)))).astype(bf16)
    grad_gu_ref[:, ff:] = (grad_act * silu).astype(bf16)
    out_ref[...] = dot_plain(activ_ref[...], down_ref[...]).astype(bf16)
    back_ref[...] = dot_back(grad_gu_ref[...], gu_ref[...]).astype(bf16)


def mlp(normed, grad_out, w_gu, w_down):
    rows, model = normed.shape
    ff = w_down.shape[0]
    block_rows = math.gcd(rows, 256)

    def by_rows(width):
        return pl.BlockSpec((block_rows, width), lambda i: (i, 0))

    def whole(shape):
        return pl.BlockSpec(shape, lambda i: (0, 0), pipeline_mode=pl.Buffered(1))

    def like(width):
        return jax.ShapeDtypeStruct((rows, width), jnp.bfloat16)

    return pl.pallas_call(
        mlp_kernel,
        grid=(rows // block_rows,),
        in_specs=[by_rows(model), by_rows(model), whole(w_gu.shape), whole(w_down.shape)],
        out_specs=(by_rows(ff), by_rows(model), by_rows(2 * ff), by_rows(model)),
        out_shape=(like(ff), like(model), like(2 * ff), like(model)),
        compiler_params=pltpu.CompilerParams(vmem_limit_bytes=44 * 2**20),
        cost_estimate=pl.CostEstimate(
            flops=12 * rows * model * ff, bytes_accessed=30_000_000, transcendentals=rows * ff
        ),
        name="mlp",
    )(normed, grad_out, w_gu, w_down)


def on_device(
    tokens,
    doc_lengths,
    cotangent,
    gain_attn,
    w_query,
    w_key,
    w_value,
    w_output,
    gain_mlp,
    w_gate,
    w_up,
    w_down,
):
    local_rows, model = tokens.shape[1:]
    ctx_size = lax.axis_size("ctx")
    fsdp_size = lax.axis_size("fsdp")
    length = local_rows * ctx_size
    group_width = (H // KVH) * HD
    ff_slice = w_gate.shape[1] // ctx_size
    held_rows = w_query.shape[0]
    bf16 = jnp.bfloat16

    positions = jnp.arange(length, dtype=jnp.int32)
    seq_lengths = doc_lengths[0]
    starts = jnp.cumsum(seq_lengths) - seq_lengths
    doc_ids = doc_index(positions, starts)
    cos_half, sin_half = rope_tables(positions)
    cos_table = jnp.concatenate([cos_half] * 4, axis=1)
    sin_table = jnp.concatenate([-sin_half, sin_half] * 2, axis=1)
    tables = (cos_table, sin_table, doc_ids[:, None], doc_ids[None, :])


    def by_slice(weight):
        return weight.reshape(held_rows, ctx_size, -1)

    qkv_parts = jnp.concatenate([by_slice(w_query), by_slice(w_key), by_slice(w_value)], axis=2)
    wo_mine = lax.all_gather(w_output, "fsdp", axis=0, tiled=True)
    wd_mine = lax.all_gather(w_down, "fsdp", axis=0, tiled=True)
    gain_rows = jnp.stack([gain_attn, gain_mlp]).astype(jnp.float32)
    odd = lax.axis_index("fsdp") % 2
    gain_tile = jnp.concatenate([gain_rows * (1 - odd), gain_rows * odd], axis=1)
    gain_tile = jnp.pad(gain_tile, ((0, 8 - gain_tile.shape[0]), (0, 128 - gain_tile.shape[1])))
    normed1, gains, w_qkv = start_layer(tokens[0], gain_tile, qkv_parts.transpose(1, 0, 2))
    grad_out = cotangent[0].astype(jnp.float32)
    grad_mlp = (RESIDUAL_MULT * grad_out).astype(bf16)

    block_rows = math.gcd(length, 256)
    normed1, grad_mlp = lax.optimization_barrier((normed1, grad_mlp))
    grad_mlp = lax.all_gather(grad_mlp, "ctx", axis=0, tiled=True)
    qkv = dot_plain(normed1, w_qkv)
    q, kv, mixed_heads, log_sum = attention_forward(qkv, tables, block_rows)
    hidden, w_gu, normed2 = mlp_forward(
        dot_plain(mixed_heads, wo_mine).astype(bf16), tokens[0], gains, w_gate, w_up
    )
    w_gu = rows_of(rows_of(w_gu))

    activ, out_terms, grad_gu, partial2 = mlp(normed2, grad_mlp, w_gu, wd_mine)
    branch = lax.psum_scatter(out_terms, "ctx", scatter_dimension=0, tiled=True)
    gu_terms = dot_outer(normed2, grad_gu).astype(bf16)
    wd_terms = dot_outer(activ, grad_mlp).astype(bf16)
    partial2, gu_terms, wd_terms = lax.optimization_barrier((partial2, gu_terms, wd_terms))
    grad_hidden, grad_g2, gu_back, grad_attn = mlp_backward(
        partial2, hidden, cotangent[0], gains, gu_terms.reshape(fsdp_size, -1, gu_terms.shape[1])
    )
    gu_back = return_columns(gu_back, ctx_size)
    wd_back = lax.psum_scatter(wd_terms, "fsdp", scatter_dimension=0, tiled=True)

    grad_mixed = dot_back(grad_attn, wo_mine).astype(bf16)
    wo_terms = dot_outer(mixed_heads, grad_attn).astype(bf16)
    grad_qkv = attention_backward(q, kv, grad_mixed, log_sum, tables, block_rows)
    partial1 = dot_back(grad_qkv, w_qkv).astype(bf16)
    qkv_terms = by_fsdp(dot_outer(normed1, grad_qkv).astype(bf16), ctx_size, fsdp_size)
    grad_inputs, gain_back, wo_back, qkv_back = finish_layer(
        partial1,
        tokens[0],
        grad_hidden,
        gains,
        grad_g2,
        wo_terms.reshape(fsdp_size, held_rows, model),
        qkv_terms.reshape(fsdp_size, ctx_size, held_rows, -1),
    )
    grad_inputs, wd_back, gu_back, branch = lax.optimization_barrier(
        (grad_inputs, wd_back, gu_back, branch)
    )
    output = (hidden + RESIDUAL_MULT * branch.astype(jnp.float32)).astype(bf16)[None]
    gain_back = jnp.where(odd == 0, gain_back[:2, :held_rows], gain_back[:2, held_rows:])

    def joined(parts):
        return parts.transpose(1, 0, 2).reshape(held_rows, -1).astype(jnp.float32)

    key_end = group_width + HD
    return (
        output,
        grad_inputs[None],
        gain_back[0],
        joined(qkv_back[:, :, :group_width]),
        joined(qkv_back[:, :, group_width:key_end]),
        joined(qkv_back[:, :, key_end:]),
        wo_back,
        gain_back[1],
        joined(gu_back[:, :, :ff_slice]),
        joined(gu_back[:, :, ff_slice:]),
        wd_back.astype(jnp.float32),
    )


def solution(mesh):
    in_specs = (
        P("fsdp", "ctx", None),
        P("fsdp", None),
        P("fsdp", "ctx", None),
        P(("ctx", "fsdp")),
        P(("ctx", "fsdp"), None),
        P(("ctx", "fsdp"), None),
        P(("ctx", "fsdp"), None),
        P(("ctx", "fsdp"), None),
        P(("ctx", "fsdp")),
        P(("ctx", "fsdp"), None),
        P(("ctx", "fsdp"), None),
        P(("ctx", "fsdp"), None),
    )
    out_specs = (
        P("fsdp", "ctx", None),
        P("fsdp", "ctx", None),
        P(("ctx", "fsdp")),
        P(("ctx", "fsdp"), None),
        P(("ctx", "fsdp"), None),
        P(("ctx", "fsdp"), None),
        P(("ctx", "fsdp"), None),
        P(("ctx", "fsdp")),
        P(("ctx", "fsdp"), None),
        P(("ctx", "fsdp"), None),
        P(("ctx", "fsdp"), None),
    )
    if mesh.shape["ctx"] != KVH or KVH != 4 * PAIR:
        return jax.shard_map(
            general_device, mesh=mesh, in_specs=in_specs, out_specs=out_specs, check_vma=False
        )

    return jax.shard_map(
        on_device, mesh=mesh, in_specs=in_specs, out_specs=out_specs, check_vma=False
    )
```

```python
import functools
import math

import jax
import jax.numpy as jnp
from jax import lax
from jax.experimental import pallas as pl
from jax.experimental.pallas import tpu as pltpu
from jax.sharding import PartitionSpec as P

H = 32
KVH = 8
HD = 64
FF = 8192


EPSILON = 1e-05
SCORE_SCALE = 1.0 / 64.0
RESIDUAL_MULT = 0.22
ROPE_BASE = 10000000.0
NEGATIVE = -1e30
MESH = pl.DeviceIdType.MESH
PAIR = 2
CHUNKS = 2
ANYWHERE = pl.BlockSpec(memory_space=pl.ANY)
LINK_COST = pl.CostEstimate(flops=0, bytes_accessed=150_000_000, transcendentals=0)


def doc_index(positions, starts):
    return jnp.sum((positions[:, None] >= starts[None, :]).astype(jnp.int32), axis=1) - 1


def rope_tables(positions):
    half_size = HD // 2
    frequency = ROPE_BASE ** (-(jnp.arange(half_size, dtype=jnp.float32) * 2.0) / HD)
    angles = positions.astype(jnp.float32)[:, None] * frequency[None, :]
    return (jnp.cos(angles), jnp.sin(angles))


def rotate(tensor, cos_table, sin_table, head_count):
    row_count = tensor.shape[0]
    by_head = tensor.reshape(row_count, head_count, HD)
    half_size = HD // 2
    first_half = by_head[..., :half_size]
    second_half = by_head[..., half_size:]
    cos_rows = cos_table[:, None, :]
    sin_rows = sin_table[:, None, :]
    turned = jnp.concatenate(
        [
            first_half * cos_rows - second_half * sin_rows,
            second_half * cos_rows + first_half * sin_rows,
        ],
        axis=-1,
    )
    return turned.reshape(row_count, head_count * HD)


def dot_plain(left, right):
    return jnp.dot(left, right, preferred_element_type=jnp.float32)


def dot_back(left, right):
    return lax.dot_general(
        left, right, (((1,), (1,)), ((), ())), preferred_element_type=jnp.float32
    )


def dot_outer(left, right):
    return lax.dot_general(
        left, right, (((0,), (0,)), ((), ())), preferred_element_type=jnp.float32
    )


def norm_back(grad_normed, unit_rows, inv_scale, gain_full):
    scaled = grad_normed * gain_full
    return inv_scale * (scaled - unit_rows * jnp.mean(scaled * unit_rows, axis=-1, keepdims=True))


def general_device(
    tokens,
    doc_lengths,
    cotangent,
    gain_attn,
    w_query,
    w_key,
    w_value,
    w_output,
    gain_mlp,
    w_gate,
    w_up,
    w_down,
):
    local_rows = tokens.shape[1]
    ctx_size = lax.axis_size("ctx")
    length = local_rows * ctx_size
    group_size = H // KVH
    offset = lax.axis_index("ctx") * local_rows
    positions = offset + jnp.arange(local_rows, dtype=jnp.int32)
    seq_lengths = doc_lengths[0]
    starts = jnp.cumsum(seq_lengths) - seq_lengths
    doc_ids = doc_index(positions, starts)
    last_pos = offset + local_rows - 1
    first_doc = doc_ids[0]
    cos_table, sin_table = rope_tables(positions)
    gain1, gain2, wq_full, wk_full, wv_full, wo_full = (
        lax.all_gather(gain_attn, ("ctx", "fsdp"), axis=0, tiled=True),
        lax.all_gather(gain_mlp, ("ctx", "fsdp"), axis=0, tiled=True),
        lax.all_gather(w_query, ("ctx", "fsdp"), axis=0, tiled=True),
        lax.all_gather(w_key, ("ctx", "fsdp"), axis=0, tiled=True),
        lax.all_gather(w_value, ("ctx", "fsdp"), axis=0, tiled=True),
        lax.all_gather(w_output, ("ctx", "fsdp"), axis=0, tiled=True),
    )
    gain1_f = gain1.astype(jnp.float32)
    gain2_f = gain2.astype(jnp.float32)
    inputs = tokens[0].astype(jnp.float32)
    inv_one = lax.rsqrt(jnp.mean(inputs * inputs, axis=-1, keepdims=True) + EPSILON)
    unit_one = inputs * inv_one
    normed1 = (unit_one * gain1_f).astype(jnp.bfloat16)
    queries = rotate(dot_plain(normed1, wq_full), cos_table, sin_table, H).astype(jnp.bfloat16)
    key_rot = rotate(dot_plain(normed1, wk_full), cos_table, sin_table, KVH).astype(jnp.bfloat16)
    values = dot_plain(normed1, wv_full).astype(jnp.bfloat16)
    grouped = queries.reshape(local_rows, KVH, group_size, HD)
    start_state = (
        jnp.full((local_rows, KVH, group_size), NEGATIVE, jnp.float32),
        jnp.zeros((local_rows, KVH, group_size), jnp.float32),
        jnp.zeros((local_rows, KVH, group_size, HD), jnp.float32),
    )
    running = start_state
    key_piece = lax.all_gather(key_rot, "ctx", axis=0, tiled=True)
    value_piece = lax.all_gather(values, "ctx", axis=0, tiled=True)
    piece_rows = key_piece.shape[0]
    attend_key_width = math.gcd(piece_rows, 512)
    block_count = piece_rows // attend_key_width

    def one_block(carried, index_block):
        block_start = index_block * attend_key_width
        key_blk = lax.dynamic_slice_in_dim(key_piece, block_start, attend_key_width, 0).reshape(
            attend_key_width, KVH, HD
        )
        value_blk = lax.dynamic_slice_in_dim(value_piece, block_start, attend_key_width, 0).reshape(
            attend_key_width, KVH, HD
        )
        key_pos = block_start + jnp.arange(attend_key_width, dtype=jnp.int32)
        key_docs = doc_index(key_pos, starts)
        skip_block = (block_start > last_pos) | (key_docs[attend_key_width - 1] < first_doc)

        def update(current):
            run_max, run_sum, accumulated = current
            scores = (
                jnp.einsum("qkgd,tkd->qkgt", grouped, key_blk, preferred_element_type=jnp.float32)
                * SCORE_SCALE
            )
            allowed = (key_docs[None, :] == doc_ids[:, None]) & (
                key_pos[None, :] <= positions[:, None]
            )
            allowed = allowed[:, None, None, :]
            masked = jnp.where(allowed, scores, NEGATIVE)
            new_max = jnp.maximum(run_max, jnp.max(masked, axis=-1))
            weights_exp = jnp.where(allowed, jnp.exp(masked - new_max[..., None]), 0.0)
            factor = jnp.exp(run_max - new_max)
            new_sum = run_sum * factor + jnp.sum(weights_exp, axis=-1)
            new_acc = accumulated * factor[..., None] + jnp.einsum(
                "qkgt,tkd->qkgd",
                weights_exp.astype(jnp.bfloat16),
                value_blk,
                preferred_element_type=jnp.float32,
            )
            return (new_max, new_sum, new_acc)

        return (lax.cond(skip_block, lambda unchanged: unchanged, update, carried), None)

    running, _ = lax.scan(one_block, running, jnp.arange(block_count))
    run_max, run_sum, accumulated = running
    attended = accumulated / run_sum[..., None]
    log_sum = run_max + jnp.log(run_sum)
    mixed_heads = attended.reshape(local_rows, H * HD).astype(jnp.bfloat16)
    hidden = inputs + RESIDUAL_MULT * dot_plain(mixed_heads, wo_full)
    inv_two = lax.rsqrt(jnp.mean(hidden * hidden, axis=-1, keepdims=True) + EPSILON)
    unit_two = hidden * inv_two
    normed2 = (unit_two * gain2_f).astype(jnp.bfloat16)
    wg_full, wu_full, wd_full = (
        lax.all_gather(w_gate, ("ctx", "fsdp"), axis=0, tiled=True),
        lax.all_gather(w_up, ("ctx", "fsdp"), axis=0, tiled=True),
        lax.all_gather(w_down, ("ctx", "fsdp"), axis=0, tiled=True),
    )
    gate_pre = dot_plain(normed2, wg_full)
    up_pre = dot_plain(normed2, wu_full)
    sig_gate = jax.nn.sigmoid(gate_pre)
    silu_gate = gate_pre * sig_gate
    activ = (silu_gate * up_pre).astype(jnp.bfloat16)
    result = hidden + RESIDUAL_MULT * dot_plain(activ, wd_full)
    output = result.astype(jnp.bfloat16)[None]
    grad_out = cotangent[0].astype(jnp.float32)
    grad_mlp = (RESIDUAL_MULT * grad_out).astype(jnp.bfloat16)
    silu_slope = sig_gate * (1.0 + gate_pre * (1.0 - sig_gate))
    wg_back, wu_back, wd_back = (
        lax.all_gather(w_gate, ("ctx", "fsdp"), axis=0, tiled=True),
        lax.all_gather(w_up, ("ctx", "fsdp"), axis=0, tiled=True),
        lax.all_gather(w_down, ("ctx", "fsdp"), axis=0, tiled=True),
    )
    grad_act = dot_back(grad_mlp, wd_back)
    grad_gate = (grad_act * up_pre * silu_slope).astype(jnp.bfloat16)
    grad_up = (grad_act * silu_gate).astype(jnp.bfloat16)
    grad_norm2 = dot_back(grad_gate, wg_back) + dot_back(grad_up, wu_back)
    left_cols = normed2
    gate_up_shard = lax.psum_scatter(
        jnp.concatenate([dot_outer(left_cols, grad_gate), dot_outer(left_cols, grad_up)], axis=1),
        ("ctx", "fsdp"),
        scatter_dimension=0,
        tiled=True,
    )
    wg_shard = gate_up_shard[:, :FF]
    wu_shard = gate_up_shard[:, FF:]
    left_cols = activ
    wd_shard = lax.psum_scatter(
        dot_outer(left_cols, grad_mlp), ("ctx", "fsdp"), scatter_dimension=0, tiled=True
    )
    grad_g2 = jnp.sum(grad_norm2 * unit_two, axis=0)
    grad_hidden = grad_out + norm_back(grad_norm2, unit_two, inv_two, gain2_f)
    grad_attn = (RESIDUAL_MULT * grad_hidden).astype(jnp.bfloat16)
    wq_back, wk_back, wv_back, wo_back = (
        lax.all_gather(w_query, ("ctx", "fsdp"), axis=0, tiled=True),
        lax.all_gather(w_key, ("ctx", "fsdp"), axis=0, tiled=True),
        lax.all_gather(w_value, ("ctx", "fsdp"), axis=0, tiled=True),
        lax.all_gather(w_output, ("ctx", "fsdp"), axis=0, tiled=True),
    )
    grad_wo = dot_outer(mixed_heads, grad_attn)
    grad_att = (
        dot_back(grad_attn, wo_back).astype(jnp.bfloat16).reshape(local_rows, KVH, group_size, HD)
    )
    row_delta = jnp.sum(grad_att.astype(jnp.float32) * attended, axis=-1)
    key_all, value_all = (
        lax.all_gather(key_rot, "ctx", axis=0, tiled=True),
        lax.all_gather(values, "ctx", axis=0, tiled=True),
    )
    key_width = math.gcd(length, 512)
    block_count = length // key_width

    def back_block(grad_query, index_block):
        block_start = index_block * key_width
        key_blk = lax.dynamic_slice_in_dim(key_all, block_start, key_width, 0).reshape(
            key_width, KVH, HD
        )
        value_blk = lax.dynamic_slice_in_dim(value_all, block_start, key_width, 0).reshape(
            key_width, KVH, HD
        )
        key_pos = block_start + jnp.arange(key_width, dtype=jnp.int32)
        key_docs = doc_index(key_pos, starts)
        skip_block = (block_start > last_pos) | (key_docs[key_width - 1] < first_doc)

        def compute(current):
            scores = (
                jnp.einsum("qkgd,tkd->qkgt", grouped, key_blk, preferred_element_type=jnp.float32)
                * SCORE_SCALE
            )
            allowed = (key_docs[None, :] == doc_ids[:, None]) & (
                key_pos[None, :] <= positions[:, None]
            )
            allowed = allowed[:, None, None, :]
            probs_blk = jnp.where(
                allowed, jnp.exp(jnp.where(allowed, scores, NEGATIVE) - log_sum[..., None]), 0.0
            )
            grad_probs = jnp.einsum(
                "qkgd,tkd->qkgt", grad_att, value_blk, preferred_element_type=jnp.float32
            )
            grad_scores = (probs_blk * (grad_probs - row_delta[..., None])).astype(jnp.bfloat16)
            new_query = (
                current
                + jnp.einsum(
                    "qkgt,tkd->qkgd", grad_scores, key_blk, preferred_element_type=jnp.float32
                )
                * SCORE_SCALE
            )
            grad_key = (
                jnp.einsum(
                    "qkgt,qkgd->tkd", grad_scores, grouped, preferred_element_type=jnp.float32
                )
                * SCORE_SCALE
            )
            grad_value = jnp.einsum(
                "qkgt,qkgd->tkd",
                probs_blk.astype(jnp.bfloat16),
                grad_att,
                preferred_element_type=jnp.float32,
            )
            return (
                new_query,
                (grad_key.reshape(key_width, KVH * HD), grad_value.reshape(key_width, KVH * HD)),
            )

        def nothing(current):
            zero_rows = jnp.zeros((key_width, KVH * HD), jnp.float32)
            return (current, (zero_rows, zero_rows))

        return lax.cond(skip_block, nothing, compute, grad_query)

    grad_query, key_terms = lax.scan(
        back_block,
        jnp.zeros((local_rows, KVH, group_size, HD), jnp.float32),
        jnp.arange(block_count),
    )
    key_term_all = key_terms[0].reshape(length, KVH * HD)
    value_term_all = key_terms[1].reshape(length, KVH * HD)
    grad_keys, grad_values = (
        lax.psum_scatter(
            key_term_all.astype(jnp.bfloat16), "ctx", scatter_dimension=0, tiled=True
        ).astype(jnp.float32),
        lax.psum_scatter(
            value_term_all.astype(jnp.bfloat16), "ctx", scatter_dimension=0, tiled=True
        ).astype(jnp.float32),
    )
    grad_q_pre = rotate(grad_query.reshape(local_rows, H * HD), cos_table, -sin_table, H).astype(
        jnp.bfloat16
    )
    grad_k_pre = rotate(grad_keys, cos_table, -sin_table, KVH).astype(jnp.bfloat16)
    grad_v_pre = grad_values.astype(jnp.bfloat16)
    grad_norm1 = (
        dot_back(grad_q_pre, wq_back)
        + dot_back(grad_k_pre, wk_back)
        + dot_back(grad_v_pre, wv_back)
    )
    grad_wq = dot_outer(normed1, grad_q_pre)
    grad_wk = dot_outer(normed1, grad_k_pre)
    grad_wv = dot_outer(normed1, grad_v_pre)
    grad_g1 = jnp.sum(grad_norm1 * unit_one, axis=0)
    grad_inputs = grad_hidden + norm_back(grad_norm1, unit_one, inv_one, gain1_f)
    g1_shard, g2_shard, wq_shard, wk_shard, wv_shard, wo_shard = (
        lax.psum_scatter(grad_g1, ("ctx", "fsdp"), scatter_dimension=0, tiled=True),
        lax.psum_scatter(grad_g2, ("ctx", "fsdp"), scatter_dimension=0, tiled=True),
        lax.psum_scatter(grad_wq, ("ctx", "fsdp"), scatter_dimension=0, tiled=True),
        lax.psum_scatter(grad_wk, ("ctx", "fsdp"), scatter_dimension=0, tiled=True),
        lax.psum_scatter(grad_wv, ("ctx", "fsdp"), scatter_dimension=0, tiled=True),
        lax.psum_scatter(grad_wo, ("ctx", "fsdp"), scatter_dimension=0, tiled=True),
    )
    return (
        output,
        grad_inputs[None],
        g1_shard,
        wq_shard,
        wk_shard,
        wv_shard,
        wo_shard,
        g2_shard,
        wg_shard,
        wu_shard,
        wd_shard,
    )


def rows_of(blocks):
    return blocks.reshape((-1,) + blocks.shape[2:])


def in_vmem(count):
    return [pl.BlockSpec(memory_space=pltpu.VMEM)] * count


def greet_line(barrier, ctx_at, line_at, line_size, fsdp_size=1):
    for j in range(1, fsdp_size):
        peer = (lax.axis_index("fsdp") + j) % fsdp_size
        pl.semaphore_signal(barrier, inc=1, device_id={"fsdp": peer}, device_id_type=MESH)
    other = ctx_at + 1 - 2 * (ctx_at % PAIR)
    pl.semaphore_signal(barrier, inc=1, device_id={"ctx": other}, device_id_type=MESH)

    @pl.when(line_at > 0)
    def _():
        pl.semaphore_signal(barrier, inc=1, device_id={"ctx": ctx_at - PAIR}, device_id_type=MESH)

    @pl.when(line_at < line_size - 1)
    def _():
        pl.semaphore_signal(barrier, inc=1, device_id={"ctx": ctx_at + PAIR}, device_id_type=MESH)

    last = line_size - 1
    neighbours = fsdp_size + (line_at + last - 1) // last + (2 * last - 1 - line_at) // last
    pl.semaphore_wait(barrier, neighbours)


def greet_all(barrier, me, count, fsdp_size):
    def greet(k, unused):
        target = (me + k) % count
        pl.semaphore_signal(
            barrier, inc=1, device_id=(target // fsdp_size, target % fsdp_size), device_id_type=MESH
        )
        return unused

    lax.fori_loop(1, count, greet, 0)
    pl.semaphore_wait(barrier, count - 1)


def gather_phase(line_size, x_ref, out_ref, send_sem, recv_sem, own_sem):
    me = lax.axis_index("ctx")
    line_at, pair_at = me // PAIR, me % PAIR
    rows = x_ref.shape[0]
    step = rows // CHUNKS

    def piece(block, part):
        return out_ref.at[pl.ds(pl.multiple_of(block * rows + part * step, step), step), :]

    def copy(block, part, way, own):
        slot = block * CHUNKS + part
        return pltpu.make_async_remote_copy(
            src_ref=x_ref.at[pl.ds(part * step, step), :] if own else piece(block, part),
            dst_ref=piece(block, part),
            send_sem=send_sem.at[way, slot],
            recv_sem=recv_sem.at[slot],
            device_id={"ctx": (me + 1 - 2 * pair_at, me + PAIR, me - PAIR)[way]},
            device_id_type=MESH,
        )

    def pass_on(block, part, upward, downward, own, act):
        if upward is not None:
            pl.when(upward)(lambda: act(copy(block, part, 1, own)))
        if downward is not None:
            pl.when(downward)(lambda: act(copy(block, part, 2, own)))
        act(copy(block, part, 0, own))

    def own_part(part, act):
        pass_on(me, part, line_at < line_size - 1, line_at > 0, True, act)

    def others(act, arrive, between):
        for distance in range(1, line_size):
            between(distance)
            for part in range(CHUNKS):

                @pl.when(line_at >= distance)
                def _():
                    block = me - PAIR * distance
                    arrive(block, part)
                    pass_on(block, part, line_at < line_size - 1, None, False, act)

                @pl.when(line_at + distance < line_size)
                def _():
                    block = me + PAIR * distance
                    arrive(block, part)
                    pass_on(block, part, None, line_at > 0, False, act)

    def start_own(part):
        own_part(part, lambda c: c.start())

    def finish(between=lambda distance: None):
        keep = pltpu.make_async_copy(
            x_ref, out_ref.at[pl.ds(pl.multiple_of(me * rows, rows), rows), :], own_sem
        )
        keep.start()
        others(
            lambda c: c.start(),
            lambda block, part: copy(block, part, 0, False).wait_recv(),
            between,
        )
        between(line_size)
        for place in range(line_size):
            for part in range(CHUNKS):
                copy(place * PAIR + 1 - pair_at, part, 0, False).wait_recv()
        for part in range(CHUNKS):
            own_part(part, lambda c: c.wait_send())
        others(lambda c: c.wait_send(), lambda block, part: None, lambda distance: None)
        keep.wait()

    return start_own, finish


def gather_scratch(ctx_size):
    return [
        pltpu.SemaphoreType.DMA((3, ctx_size * CHUNKS)),
        pltpu.SemaphoreType.DMA((ctx_size * CHUNKS,)),
        pltpu.SemaphoreType.DMA,
    ]


def scatter_phase(line_size, x_ref, sum_ref, near, below, above, near_send, near_sem, line_send, line_sem, emit, midway=lambda: None, between=lambda turn: None):
    me = lax.axis_index("ctx")
    line_at, pair_at = me // PAIR, me % PAIR
    rows = sum_ref.shape[0]
    step = rows // CHUNKS
    last = line_size - 1
    low = line_at // (line_size // 2)
    order = [k + (last - 2 * k) * (1 - low) for k in range(line_size // 2)]
    order += [line_at + 1 - 2 * (line_at % 2), line_at]

    def near_copy(place, part):
        start = (place * PAIR + 1 - pair_at) * rows + part * step
        return pltpu.make_async_remote_copy(
            src_ref=x_ref.at[pl.ds(pl.multiple_of(start, step), step), :],
            dst_ref=near.at[place, pl.ds(part * step, step), :],
            send_sem=near_send.at[place, part],
            recv_sem=near_sem.at[place, part],
            device_id={"ctx": me + 1 - 2 * pair_at},
            device_id_type=MESH,
        )

    def line_copy(place, part, up):
        part_rows = pl.ds(part * step, step)
        return pltpu.make_async_remote_copy(
            src_ref=near.at[place, part_rows, :],
            dst_ref=(below if up else above).at[place, part_rows, :],
            send_sem=line_send.at[place, part],
            recv_sem=line_sem.at[0 if up else 1, place, part],
            device_id={"ctx": me + PAIR if up else me - PAIR},
            device_id_type=MESH,
        )

    def mine(place, part):
        start = (place * PAIR + pair_at) * rows + part * step
        return x_ref[pl.ds(pl.multiple_of(start, step), step), :].astype(jnp.float32)

    for place in order:
        for part in range(CHUNKS):
            near_copy(place, part).start()

    for turn, place in enumerate(order[:-1]):
        between(turn)
        for part in range(CHUNKS):
            part_rows = pl.ds(part * step, step)
            near_copy(place, part).wait_recv()

            def send(up, waits, arrived):
                @pl.when(waits)
                def _():
                    line_copy(place, part, up).wait_recv()
                    near[place, part_rows, :] = (
                        mine(place, part)
                        + near[place, part_rows, :].astype(jnp.float32)
                        + arrived[place, part_rows, :].astype(jnp.float32)
                    ).astype(near.dtype)

                @pl.when(jnp.logical_not(waits))
                def _():
                    near[place, part_rows, :] = (
                        mine(place, part) + near[place, part_rows, :].astype(jnp.float32)
                    ).astype(near.dtype)

                line_copy(place, part, up).start()

            pl.when(place > line_at)(lambda: send(True, line_at > 0, below))
            pl.when(place < line_at)(lambda: send(False, line_at < last, above))

    midway()
    for part in range(CHUNKS):
        part_rows = pl.ds(part * step, step)
        near_copy(line_at, part).wait_recv()
        sum_ref[part_rows, :] = mine(line_at, part) + near[line_at, part_rows, :].astype(jnp.float32)

        @pl.when(line_at > 0)
        def _():
            line_copy(line_at, part, True).wait_recv()
            sum_ref[part_rows, :] += below[line_at, part_rows, :].astype(jnp.float32)

        @pl.when(line_at < last)
        def _():
            line_copy(line_at, part, False).wait_recv()
            sum_ref[part_rows, :] += above[line_at, part_rows, :].astype(jnp.float32)

        emit(part, slice(part * step, (part + 1) * step))

    def finish():
        for place in order:
            for part in range(CHUNKS):
                near_copy(place, part).wait_send()
        for place in order[:-1]:
            for part in range(CHUNKS):
                line_copy(place, part, True).wait_send()

    return finish


def scatter_scratch(ctx_size, rows, width):
    line_size = ctx_size // PAIR
    held = pltpu.VMEM((line_size, rows, width), jnp.bfloat16)
    return [
        held,
        held,
        held,
        pltpu.SemaphoreType.DMA((line_size, CHUNKS)),
        pltpu.SemaphoreType.DMA((line_size, CHUNKS)),
        pltpu.SemaphoreType.DMA((line_size, CHUNKS)),
        pltpu.SemaphoreType.DMA((2, line_size, CHUNKS)),
    ]


def swap_lanes(values, outer, inner):
    tile = 128
    half = tile // 2
    low = lax.broadcasted_iota(jnp.int32, (values.shape[0], tile), 1) < half
    placed = [None] * (outer * inner // 2)
    for first in range(0, outer, 2):
        for second in range(0, inner, 2):
            at = (first * inner + second) // 2
            one = values[:, at * tile : (at + 1) * tile]
            at += inner // 2
            two = values[:, at * tile : (at + 1) * tile]
            at = (second * outer + first) // 2
            placed[at] = jnp.where(low, one, pltpu.roll(two, half, 1))
            placed[at + outer // 2] = jnp.where(low, pltpu.roll(one, half, 1), two)
    return jnp.concatenate(placed, axis=1)


def start_kernel(
    ctx_size, fsdp_size, tokens_ref, tile_ref, parts_ref, out_ref, gains_ref, weight_ref,
    tiles, normed, tile_send, tile_recv, far_send, far_recv, near_send, near_recv, kept, *sems
):
    me_ctx, me_fsdp = lax.axis_index("ctx"), lax.axis_index("fsdp")
    count = ctx_size * fsdp_size
    me = me_ctx * fsdp_size + me_fsdp
    greet_all(pltpu.get_barrier_semaphore(), me, count, fsdp_size)

    def tile_copy(k, source):
        target = (me + k) % count
        return pltpu.make_async_remote_copy(
            src_ref=tile_ref,
            dst_ref=tiles.at[source],
            send_sem=tile_send.at[k],
            recv_sem=tile_recv.at[k],
            device_id=(target // fsdp_size, target % fsdp_size),
            device_id_type=MESH,
        )

    def start_tile(k, unused):
        tile_copy(k, me).start()
        return unused

    def finish_tile(k, unused):
        tile_copy(k, (me + count - k) % count).wait_recv()
        return unused

    lax.fori_loop(1, count, start_tile, 0)
    tiles[pl.ds(me, 1)] = tile_ref[...][None]

    def far_copy(k, source):
        target = (me_ctx + k) % ctx_size
        return pltpu.make_async_remote_copy(
            src_ref=parts_ref.at[target],
            dst_ref=weight_ref.at[source * fsdp_size + me_fsdp],
            send_sem=far_send.at[k],
            recv_sem=far_recv.at[k],
            device_id={"ctx": target},
            device_id_type=MESH,
        )

    def near_copy(k, j, fsdp_source):
        block = (me_ctx + ctx_size - k) % ctx_size * fsdp_size + fsdp_source
        return pltpu.make_async_remote_copy(
            src_ref=parts_ref.at[me_ctx] if k == 0 else weight_ref.at[block],
            dst_ref=weight_ref.at[block],
            send_sem=near_send.at[k, j],
            recv_sem=near_recv.at[k, j],
            device_id={"fsdp": (me_fsdp + j) % fsdp_size},
            device_id_type=MESH,
        )

    for k in range(1, ctx_size):
        far_copy(k, me_ctx).start()
    for j in range(1, fsdp_size):
        near_copy(0, j, me_fsdp).start()
    keep = pltpu.make_async_copy(parts_ref.at[me_ctx], weight_ref.at[me], kept)
    keep.start()

    rows, model = tokens_ref.shape
    lax.fori_loop(1, count, finish_tile, 0)
    held = model // count
    for pair in range(count // 2):
        cols = slice(pair * 2 * held, (pair + 1) * 2 * held)
        gains_ref[:, cols] = tiles[2 * pair] + tiles[2 * pair + 1]
    start_own, finish_gather = gather_phase(ctx_size // PAIR, normed, out_ref, *sems)
    step = rows // CHUNKS
    for part in range(CHUNKS):
        part_rows = slice(part * step, (part + 1) * step)
        values = tokens_ref[part_rows, :].astype(jnp.float32)
        scale = lax.rsqrt(jnp.mean(values * values, axis=-1, keepdims=True) + EPSILON)
        normed[part_rows, :] = (values * scale * gains_ref[0:1, :]).astype(normed.dtype)
        start_own(part)
    for k in range(1, ctx_size):
        far_copy(k, (me_ctx + ctx_size - k) % ctx_size).wait_recv()
        for j in range(1, fsdp_size):
            near_copy(k, j, me_fsdp).start()
    finish_gather()
    for k in range(ctx_size):
        for j in range(1, fsdp_size):
            near_copy(k, j, (me_fsdp + fsdp_size - j) % fsdp_size).wait_recv()
    for k in range(ctx_size):
        for j in range(1, fsdp_size):
            near_copy(k, j, me_fsdp).wait_send()
    for k in range(1, ctx_size):
        far_copy(k, me_ctx).wait_send()

    def sent_tile(k, unused):
        tile_copy(k, me).wait_send()
        return unused

    lax.fori_loop(1, count, sent_tile, 0)
    keep.wait()


def start_layer(tokens, tile, parts):
    ctx_size, fsdp_size = lax.axis_size("ctx"), lax.axis_size("fsdp")
    count = ctx_size * fsdp_size
    rows, model = tokens.shape
    dma = pltpu.SemaphoreType.DMA
    normed1, gains, weight = pl.pallas_call(
        functools.partial(start_kernel, ctx_size, fsdp_size),
        out_shape=(
            jax.ShapeDtypeStruct((ctx_size * rows, model), jnp.bfloat16),
            jax.ShapeDtypeStruct((8, model), jnp.float32),
            jax.ShapeDtypeStruct((count,) + parts.shape[1:], parts.dtype),
        ),
        in_specs=in_vmem(3),
        out_specs=(ANYWHERE, in_vmem(1)[0], ANYWHERE),
        scratch_shapes=[
            pltpu.VMEM((count, 8, 128), jnp.float32),
            pltpu.VMEM((rows, model), jnp.bfloat16),
            dma((count,)),
            dma((count,)),
            dma((ctx_size,)),
            dma((ctx_size,)),
            dma((ctx_size, fsdp_size)),
            dma((ctx_size, fsdp_size)),
            dma,
        ]
        + gather_scratch(ctx_size),
        compiler_params=pltpu.CompilerParams(
            collective_id=0, has_side_effects=True, vmem_limit_bytes=10 * 2**20
        ),
        cost_estimate=LINK_COST,
        name="start_layer",
    )(tokens, tile, parts)
    return normed1, gains, rows_of(weight)


def spread_phase(ctx_size, fsdp_size, gate_ref, up_ref, wide_ref, send, recv, side_send, side_recv, kept):
    me, me_fsdp = lax.axis_index("ctx"), lax.axis_index("fsdp")
    along = (me_fsdp + fsdp_size // 2) % fsdp_size
    beside = me_fsdp + 1 - 2 * (me_fsdp % 2)
    diagonal = (beside + fsdp_size // 2) % fsdp_size
    wide = gate_ref.shape[1] // ctx_size

    def part(which, target, source):
        cols = pl.ds(pl.multiple_of(target * wide, wide), wide)
        return (
            (gate_ref, up_ref)[which].at[:, cols],
            wide_ref.at[me_fsdp, source, :, which * wide : (which + 1) * wide],
        )

    def copy(which, k, source):
        target = (me + k) % ctx_size
        src, dst = part(which, target, source)
        return pltpu.make_async_remote_copy(
            src_ref=src,
            dst_ref=dst,
            send_sem=send.at[which, k],
            recv_sem=recv.at[which, k],
            device_id={"ctx": target},
            device_id_type=MESH,
        )

    def keep(which):
        return pltpu.make_async_copy(*part(which, me, me), kept.at[which])

    def side(way, k, rows_of_device):
        block = (rows_of_device, (me + ctx_size - k) % ctx_size)
        return pltpu.make_async_remote_copy(
            src_ref=wide_ref.at[block],
            dst_ref=wide_ref.at[block],
            send_sem=side_send.at[way, k],
            recv_sem=side_recv.at[way, k],
            device_id={"fsdp": along if way == 0 else beside},
            device_id_type=MESH,
        )

    def begin():
        for which in range(2):
            keep(which).start()
        for k in list(range(2, ctx_size, 2)) + list(range(1, ctx_size, 2)):
            for which in range(2):
                copy(which, k, me).start()

    def pass_on(k):
        for which in range(2):
            if k:
                copy(which, k, (me + ctx_size - k) % ctx_size).wait_recv()
            else:
                keep(which).wait()
        side(0, k, me_fsdp).start()
        side(1, k, me_fsdp).start()

    def relay(k):
        side(0, k, along).wait_recv()
        side(2, k, along).start()

    def finish():
        for k in range(ctx_size):
            side(1, k, beside).wait_recv()
            side(2, k, diagonal).wait_recv()
        for k in range(ctx_size):
            for way in range(3):
                side(way, k, me_fsdp).wait_send()
            if k:
                for which in range(2):
                    copy(which, k, me).wait_send()

    return begin, pass_on, relay, finish


def mlp_forward_kernel(
    ctx_size, fsdp_size, x_ref, tokens_ref, gains_ref, gate_ref, up_ref, hidden_ref, wide_ref, out_ref,
    sums, normed, wide_send, wide_recv, side_send, side_recv, kept, *sems
):
    line_size = ctx_size // PAIR
    me, me_fsdp = lax.axis_index("ctx"), lax.axis_index("fsdp")
    barrier = pltpu.get_barrier_semaphore()
    for k in range(1, ctx_size):
        pl.semaphore_signal(barrier, inc=1, device_id={"ctx": (me + k) % ctx_size}, device_id_type=MESH)
    for j in range(1, fsdp_size):
        pl.semaphore_signal(
            barrier, inc=1, device_id={"fsdp": (me_fsdp + j) % fsdp_size}, device_id_type=MESH
        )
    pl.semaphore_wait(barrier, ctx_size + fsdp_size - 2)
    start_own, finish_gather = gather_phase(line_size, normed, out_ref, *sems[7:])
    begin, pass_on, relay, finish_spread = spread_phase(
        ctx_size, fsdp_size, gate_ref, up_ref, wide_ref, wide_send, wide_recv, side_send, side_recv, kept
    )
    even = list(range(0, ctx_size, 2))
    odd = list(range(1, ctx_size, 2))

    def during_scatter(turn):
        if turn == 0:
            begin()
        if turn == 1:
            pass_on(0)
        if turn == 2:
            pass_on(2)

    def midway():
        for k in even[2:]:
            pass_on(k)
        for k in even[:2]:
            relay(k)

    def during_gather(distance):
        if distance == line_size - 2:
            for k in even[2:]:
                relay(k)
            for k in odd[:2]:
                pass_on(k)
        if distance == line_size - 1:
            for k in odd[2:]:
                pass_on(k)
        if distance == line_size:
            for k in odd:
                relay(k)

    def emit(part, rows):
        hidden = tokens_ref[rows, :].astype(jnp.float32) + RESIDUAL_MULT * sums[rows, :]
        hidden_ref[rows, :] = hidden
        scale = lax.rsqrt(jnp.mean(hidden * hidden, axis=-1, keepdims=True) + EPSILON)
        scaled = hidden * scale * gains_ref[1:2, :]
        normed[rows, :] = swap_lanes(scaled, ctx_size, fsdp_size).astype(normed.dtype)
        start_own(part)

    finish_scatter = scatter_phase(
        line_size, x_ref, sums, *sems[:7], emit, midway, during_scatter
    )
    finish_gather(during_gather)
    finish_spread()
    finish_scatter()


def mlp_backward_kernel(
    ctx_size, fsdp_size, x_ref, hidden_ref, grad_ref, gains_ref, terms_ref, grad_hidden_ref, grad_gain_ref,
    total_ref, out_ref, sums, normed, landing, side_send, side_recv, own_sem, *sems
):
    line_size = ctx_size // PAIR
    me, me_fsdp = lax.axis_index("ctx"), lax.axis_index("fsdp")
    greet_line(pltpu.get_barrier_semaphore(), me, me // PAIR, line_size, fsdp_size)

    def side_copy(j):
        target = (me_fsdp + j) % fsdp_size
        return pltpu.make_async_remote_copy(
            src_ref=terms_ref.at[target],
            dst_ref=landing.at[j],
            send_sem=side_send.at[j],
            recv_sem=side_recv.at[j],
            device_id={"fsdp": target},
            device_id_type=MESH,
        )

    own_copy = pltpu.make_async_copy(terms_ref.at[me_fsdp], landing.at[0], own_sem)
    for j in range(1, fsdp_size):
        side_copy(j).start()
    own_copy.start()
    start_own, finish_gather = gather_phase(line_size, normed, out_ref, *sems[7:])

    def emit(part, rows):
        grad_norm = swap_lanes(sums[rows, :], fsdp_size, ctx_size)
        hidden = hidden_ref[rows, :]
        scale = lax.rsqrt(jnp.mean(hidden * hidden, axis=-1, keepdims=True) + EPSILON)
        unit = hidden * scale
        grad_gain_ref[part : part + 1, :] = jnp.sum(grad_norm * unit, axis=0, keepdims=True)
        grad_hidden = grad_ref[rows, :].astype(jnp.float32) + norm_back(
            grad_norm, unit, scale, gains_ref[1:2, :]
        )
        grad_hidden_ref[rows, :] = grad_hidden
        normed[rows, :] = (RESIDUAL_MULT * grad_hidden).astype(normed.dtype)
        start_own(part)

    finish_scatter = scatter_phase(line_size, x_ref, sums, *sems[:7], emit)
    finish_gather()
    own_copy.wait()
    for j in range(1, fsdp_size):
        side_copy(j).wait_recv()
    step = 64

    def add(at, unused):
        rows = pl.ds(pl.multiple_of(at * step, step), step)
        total = landing[0, rows, :].astype(jnp.float32)
        for j in range(1, fsdp_size):
            total += landing[j, rows, :].astype(jnp.float32)
        total_ref[rows, :] = total.astype(total_ref.dtype)
        return unused

    lax.fori_loop(0, total_ref.shape[0] // step, add, 0)
    for j in range(1, fsdp_size):
        side_copy(j).wait_send()
    finish_scatter()


def scatter_gather(kernel, collective_id, extra_shapes, partial, *others, specs=(), out_specs=(), scratch=(), grant=60):
    ctx_size, fsdp_size = lax.axis_size("ctx"), lax.axis_size("fsdp")
    rows, model = partial.shape[0] // ctx_size, partial.shape[1]
    return pl.pallas_call(
        functools.partial(kernel, ctx_size, fsdp_size),
        out_shape=extra_shapes + (jax.ShapeDtypeStruct(partial.shape, jnp.bfloat16),),
        in_specs=in_vmem(1 + len(others) - len(specs)) + list(specs),
        out_specs=tuple(in_vmem(len(extra_shapes) - len(out_specs))) + tuple(out_specs) + (ANYWHERE,),
        scratch_shapes=[pltpu.VMEM((rows, model), jnp.float32), pltpu.VMEM((rows, model), jnp.bfloat16)]
        + list(scratch)
        + scatter_scratch(ctx_size, rows, model)
        + gather_scratch(ctx_size),
        compiler_params=pltpu.CompilerParams(
            collective_id=collective_id, has_side_effects=True, vmem_limit_bytes=grant * 2**20
        ),
        cost_estimate=LINK_COST,
    )(partial, *others)


def mlp_forward(partial, tokens, gains, w_gate, w_up):
    ctx_size, fsdp_size = lax.axis_size("ctx"), lax.axis_size("fsdp")
    hidden = jax.ShapeDtypeStruct(tokens.shape, jnp.float32)
    slices = (fsdp_size, ctx_size, w_gate.shape[0], 2 * w_gate.shape[1] // ctx_size)
    dma = pltpu.SemaphoreType.DMA
    return scatter_gather(
        mlp_forward_kernel,
        1,
        (hidden, jax.ShapeDtypeStruct(slices, w_gate.dtype)),
        partial,
        tokens,
        gains,
        w_gate,
        w_up,
        out_specs=(ANYWHERE,),
        scratch=(
            dma((2, ctx_size)),
            dma((2, ctx_size)),
            dma((3, ctx_size)),
            dma((3, ctx_size)),
            dma((2,)),
        ),
    )


def mlp_backward(partial, hidden, grad_out, gains, terms):
    like = jax.ShapeDtypeStruct(hidden.shape, jnp.float32)
    gain = jax.ShapeDtypeStruct((CHUNKS, hidden.shape[1]), jnp.float32)
    return scatter_gather(
        mlp_backward_kernel,
        2,
        (like, gain, jax.ShapeDtypeStruct(terms.shape[1:], terms.dtype)),
        partial,
        hidden,
        grad_out,
        gains,
        terms,
        grant=36,
        specs=(ANYWHERE,),
        scratch=(
            pltpu.VMEM(terms.shape, terms.dtype),
            pltpu.SemaphoreType.DMA((terms.shape[0],)),
            pltpu.SemaphoreType.DMA((terms.shape[0],)),
            pltpu.SemaphoreType.DMA,
        ),
    )


def finish_kernel(
    ctx_size, fsdp_size, x_ref, tokens_ref, grad_ref, gains_ref, gain2_ref, wo_ref, qkv_ref,
    grad_tokens_ref, gain_out_ref, wo_out_ref, qkv_out_ref,
    sums, gain1, tiles, arrived, wo_in, qkv_in, qkv_sum, tile_send, tile_recv, near_send, near_recv,
    far_send, far_recv, *sems
):
    line_size = ctx_size // PAIR
    me_ctx, me_fsdp = lax.axis_index("ctx"), lax.axis_index("fsdp")
    count = ctx_size * fsdp_size
    me = me_ctx * fsdp_size + me_fsdp
    greet_all(pltpu.get_barrier_semaphore(), me, count, fsdp_size)

    def near_copy(which, j):
        target = (me_fsdp + j) % fsdp_size
        terms, landing = ((wo_ref, wo_in), (qkv_ref, qkv_in))[which]
        return pltpu.make_async_remote_copy(
            src_ref=terms.at[target],
            dst_ref=landing.at[j],
            send_sem=near_send.at[which, j],
            recv_sem=near_recv.at[which, j],
            device_id={"fsdp": target},
            device_id_type=MESH,
        )

    def far_copy(k, source):
        target = (me_ctx + k) % ctx_size
        return pltpu.make_async_remote_copy(
            src_ref=qkv_sum.at[target],
            dst_ref=qkv_out_ref.at[source],
            send_sem=far_send.at[k],
            recv_sem=far_recv.at[k],
            device_id={"ctx": target},
            device_id_type=MESH,
        )

    def tile_copy(k, source):
        target = (me + k) % count
        return pltpu.make_async_remote_copy(
            src_ref=tiles.at[target // 2],
            dst_ref=arrived.at[source],
            send_sem=tile_send.at[k],
            recv_sem=tile_recv.at[k],
            device_id=(target // fsdp_size, target % fsdp_size),
            device_id_type=MESH,
        )

    def midway():
        for which, own, landing in ((1, qkv_ref, qkv_in), (0, wo_ref, wo_in)):
            for j in range(1, fsdp_size):
                near_copy(which, j).wait_recv()
            total = own[pl.ds(me_fsdp, 1)][0].astype(jnp.float32)
            for j in range(1, fsdp_size):
                total += landing[j].astype(jnp.float32)
            if which:
                qkv_sum[...] = total.astype(qkv_sum.dtype)
                for k in range(1, ctx_size):
                    far_copy(k, me_ctx).start()
                qkv_out_ref[pl.ds(me_ctx, 1)] = qkv_sum[pl.ds(me_ctx, 1)]
            else:
                wo_out_ref[...] = total

    def emit(part, rows):
        grad_norm = sums[rows, :]
        values = tokens_ref[rows, :].astype(jnp.float32)
        scale = lax.rsqrt(jnp.mean(values * values, axis=-1, keepdims=True) + EPSILON)
        unit = values * scale
        gain1[part : part + 1, :] = jnp.sum(grad_norm * unit, axis=0, keepdims=True)
        grad_tokens_ref[rows, :] = grad_ref[rows, :] + norm_back(
            grad_norm, unit, scale, gains_ref[0:1, :]
        )

    for which in (1, 0):
        for j in range(1, fsdp_size):
            near_copy(which, j).start()
    finish_scatter = scatter_phase(line_size, x_ref, sums, *sems, emit, midway)
    row = lax.broadcasted_iota(jnp.int32, (8, 128), 0)
    for pair in range(count // 2):
        cols = slice(pair * 128, (pair + 1) * 128)
        first = jnp.sum(gain1[:, cols], axis=0, keepdims=True)
        second = jnp.sum(gain2_ref[:, cols], axis=0, keepdims=True)
        tiles[pair] = jnp.where(row == 0, first, jnp.where(row == 1, second, 0.0))

    def start_tile(k, unused):
        tile_copy(k, me).start()
        return unused

    def finish_tile(k, unused):
        tile_copy(k, (me + count - k) % count).wait_recv()
        return unused

    def sent_tile(k, unused):
        tile_copy(k, me).wait_send()
        return unused

    lax.fori_loop(1, count, start_tile, 0)
    arrived[pl.ds(me, 1)] = tiles[pl.ds(me // 2, 1)]
    for k in range(1, ctx_size):
        far_copy(k, (me_ctx + ctx_size - k) % ctx_size).wait_recv()
    lax.fori_loop(1, count, finish_tile, 0)
    gain_out_ref[...] = jnp.sum(arrived[...], axis=0)
    finish_scatter()
    for which in range(2):
        for j in range(1, fsdp_size):
            near_copy(which, j).wait_send()
    for k in range(1, ctx_size):
        far_copy(k, me_ctx).wait_send()
    lax.fori_loop(1, count, sent_tile, 0)


def finish_layer(partial, tokens, grad_hidden, gains, grad_gain2, wo_terms, qkv_terms):
    ctx_size, fsdp_size = lax.axis_size("ctx"), lax.axis_size("fsdp")
    count = ctx_size * fsdp_size
    rows, model = tokens.shape
    dma = pltpu.SemaphoreType.DMA
    f32, bf16 = jnp.float32, jnp.bfloat16
    held, width = qkv_terms.shape[2:]
    return pl.pallas_call(
        functools.partial(finish_kernel, ctx_size, fsdp_size),
        out_shape=(
            jax.ShapeDtypeStruct((rows, model), f32),
            jax.ShapeDtypeStruct((8, 128), f32),
            jax.ShapeDtypeStruct(wo_terms.shape[1:], f32),
            jax.ShapeDtypeStruct((ctx_size, held, width), bf16),
        ),
        in_specs=in_vmem(7),
        out_specs=tuple(in_vmem(4)),
        scratch_shapes=[
            pltpu.VMEM((rows, model), f32),
            pltpu.VMEM((CHUNKS, model), f32),
            pltpu.VMEM((count // 2, 8, 128), f32),
            pltpu.VMEM((count, 8, 128), f32),
            pltpu.VMEM(wo_terms.shape, bf16),
            pltpu.VMEM(qkv_terms.shape, bf16),
            pltpu.VMEM((ctx_size, held, width), bf16),
            dma((count,)),
            dma((count,)),
            dma((2, fsdp_size)),
            dma((2, fsdp_size)),
            dma((ctx_size,)),
            dma((ctx_size,)),
        ]
        + scatter_scratch(ctx_size, rows, model),
        compiler_params=pltpu.CompilerParams(
            collective_id=3, has_side_effects=True, vmem_limit_bytes=32 * 2**20
        ),
        cost_estimate=LINK_COST,
        name="finish_layer",
    )(partial, tokens, grad_hidden, gains, grad_gain2, wo_terms, qkv_terms)


def swap_ctx(blocks):
    return lax.all_to_all(blocks, "ctx", split_axis=0, concat_axis=0, tiled=True)


def by_fsdp(grad, ctx_size, fsdp_size):
    parts = grad.reshape(ctx_size, fsdp_size, -1, grad.shape[-1]).transpose(1, 0, 2, 3)
    return rows_of(rows_of(parts))


def return_columns(terms, ctx_size):
    return swap_ctx(terms.reshape(ctx_size, -1, terms.shape[-1]))


def half_turn(values, sign_table):
    lane = lax.broadcasted_iota(jnp.int32, values.shape, 1)
    width = values.shape[1]
    quarter = HD // 2
    ahead = pltpu.roll(values, width - quarter, 1)
    behind = pltpu.roll(values, quarter, 1)
    return jnp.where(lane % HD < quarter, ahead, behind) * sign_table


def turn(values, cos_table, sign_table):
    copies = values.shape[1] // cos_table.shape[1]
    if copies > 1:
        cos_table = jnp.concatenate([cos_table] * copies, axis=1)
        sign_table = jnp.concatenate([sign_table] * copies, axis=1)
    return values * cos_table + half_turn(values, sign_table)


def attention_forward_kernel(
    block_rows, qkv_ref, cos_ref, sin_ref, doc_col_ref, doc_row_ref, q_ref, kv_ref, out_ref, lse_ref
):
    length = qkv_ref.shape[0]
    group = H // KVH
    width = group * HD
    q_ref[...] = turn(qkv_ref[:, :width], cos_ref[...], sin_ref[...]).astype(jnp.bfloat16)
    pair = qkv_ref[:, width:]
    lane = lax.broadcasted_iota(jnp.int32, pair.shape, 1)
    turned = turn(pair, cos_ref[...], sin_ref[...])
    kv_ref[...] = jnp.where(lane < HD, turned, pair).astype(jnp.bfloat16)
    for block in range(length // block_rows):
        rows = slice(block * block_rows, (block + 1) * block_rows)
        reach = (block + 1) * block_rows
        keys = kv_ref[:reach, :HD]
        values = kv_ref[:reach, HD:]
        query_at = block * block_rows + lax.broadcasted_iota(jnp.int32, (block_rows, reach), 0)
        key_at = lax.broadcasted_iota(jnp.int32, (block_rows, reach), 1)
        allowed = (doc_col_ref[rows, :] == doc_row_ref[:, :reach]) & (key_at <= query_at)
        for head in range(group):
            cols = slice(head * HD, (head + 1) * HD)
            scores = dot_back(q_ref[rows, cols], keys) * SCORE_SCALE
            masked = jnp.where(allowed, scores, NEGATIVE)
            top = jnp.max(masked, axis=1, keepdims=True)
            weights = jnp.where(allowed, jnp.exp(masked - top), 0.0)
            total = jnp.sum(weights, axis=1, keepdims=True)
            mixed = dot_plain(weights.astype(jnp.bfloat16), values)
            out_ref[rows, cols] = (mixed / total).astype(jnp.bfloat16)
            lse_ref[rows, head : head + 1] = top + jnp.log(total)


def attention_backward_kernel(
    block_rows, q_ref, kv_ref, do_ref, lse_ref, cos_ref, sin_ref, doc_col_ref, doc_row_ref, grad_ref, dq_ref, dkv_ref
):
    length = q_ref.shape[0]
    group = H // KVH
    width = group * HD
    dkv_ref[...] = jnp.zeros_like(dkv_ref)
    for block in range(length // block_rows):
        rows = slice(block * block_rows, (block + 1) * block_rows)
        reach = (block + 1) * block_rows
        keys = kv_ref[:reach, :HD]
        values = kv_ref[:reach, HD:]
        query_at = block * block_rows + lax.broadcasted_iota(jnp.int32, (block_rows, reach), 0)
        key_at = lax.broadcasted_iota(jnp.int32, (block_rows, reach), 1)
        allowed = (doc_col_ref[rows, :] == doc_row_ref[:, :reach]) & (key_at <= query_at)
        for head in range(group):
            cols = slice(head * HD, (head + 1) * HD)
            query = q_ref[rows, cols]
            grad_out = do_ref[rows, cols]
            scores = dot_back(query, keys) * SCORE_SCALE
            probs = jnp.where(
                allowed,
                jnp.exp(jnp.where(allowed, scores, NEGATIVE) - lse_ref[rows, head : head + 1]),
                0.0,
            )
            grad_probs = dot_back(grad_out, values)
            delta = jnp.sum(probs * grad_probs, axis=1, keepdims=True)
            grad_scores = (probs * (grad_probs - delta)).astype(jnp.bfloat16)
            dq_ref[rows, cols] = dot_plain(grad_scores, keys) * SCORE_SCALE
            dkv_ref[:reach, :HD] += dot_outer(grad_scores, query) * SCORE_SCALE
            dkv_ref[:reach, HD:] += dot_outer(probs.astype(jnp.bfloat16), grad_out)
    grad_ref[:, :width] = turn(dq_ref[...], cos_ref[...], -sin_ref[...]).astype(jnp.bfloat16)
    pair = dkv_ref[...]
    lane = lax.broadcasted_iota(jnp.int32, pair.shape, 1)
    turned = turn(pair, cos_ref[...], -sin_ref[...])
    grad_ref[:, width:] = jnp.where(lane < HD, turned, pair).astype(jnp.bfloat16)


def attention_forward(qkv, tables, block_rows):
    length = qkv.shape[0]
    width = (H // KVH) * HD
    return pl.pallas_call(
        functools.partial(attention_forward_kernel, block_rows),
        out_shape=(
            jax.ShapeDtypeStruct((length, width), jnp.bfloat16),
            jax.ShapeDtypeStruct((length, 2 * HD), jnp.bfloat16),
            jax.ShapeDtypeStruct((length, width), jnp.bfloat16),
            jax.ShapeDtypeStruct((length, H // KVH), jnp.float32),
        ),
        in_specs=in_vmem(5),
        out_specs=tuple(in_vmem(4)),
        compiler_params=pltpu.CompilerParams(vmem_limit_bytes=24 * 2**20),
        name="attend",
    )(qkv, *tables)


def attention_backward(q, kv, grad_out, lse, tables, block_rows):
    length, width = q.shape
    return pl.pallas_call(
        functools.partial(attention_backward_kernel, block_rows),
        out_shape=jax.ShapeDtypeStruct((length, width + 2 * HD), jnp.bfloat16),
        in_specs=in_vmem(8),
        out_specs=in_vmem(1)[0],
        scratch_shapes=[
            pltpu.VMEM((length, width), jnp.float32),
            pltpu.VMEM((length, 2 * HD), jnp.float32),
        ],
        compiler_params=pltpu.CompilerParams(vmem_limit_bytes=24 * 2**20),
        name="attend_back",
    )(q, kv, grad_out, lse, *tables)


def mlp_out_kernel(normed_ref, gu_ref, down_ref, gate_up_ref, activ_ref, out_ref):
    ff = down_ref.shape[0]
    gate_up = dot_plain(normed_ref[...], gu_ref[...])
    gate_up_ref[...] = gate_up
    gate = gate_up[:, :ff]
    activ_ref[...] = (gate * jax.nn.sigmoid(gate) * gate_up[:, ff:]).astype(jnp.bfloat16)
    out_ref[...] = dot_plain(activ_ref[...], down_ref[...]).astype(jnp.bfloat16)


def mlp_grad_kernel(grad_ref, gate_up_ref, gu_ref, down_ref, grad_gu_ref, back_ref):
    ff = down_ref.shape[0]
    bf16 = jnp.bfloat16
    grad_act = dot_back(grad_ref[...], down_ref[...])
    gate, up = gate_up_ref[:, :ff], gate_up_ref[:, ff:]
    sig = jax.nn.sigmoid(gate)
    grad_gu_ref[:, :ff] = (grad_act * up * (sig * (1.0 + gate * (1.0 - sig)))).astype(bf16)
    grad_gu_ref[:, ff:] = (grad_act * (gate * sig)).astype(bf16)
    back_ref[...] = dot_back(grad_gu_ref[...], gu_ref[...]).astype(bf16)


def by_row_blocks(kernel, row_arrays, whole_arrays, outs, flops):
    rows = row_arrays[0].shape[0]
    block_rows = math.gcd(rows, 256)

    def by_rows(width):
        return pl.BlockSpec((block_rows, width), lambda i: (i, 0))

    def whole(shape):
        return pl.BlockSpec(shape, lambda i: (0, 0), pipeline_mode=pl.Buffered(1))

    return pl.pallas_call(
        kernel,
        grid=(rows // block_rows,),
        in_specs=[by_rows(a.shape[1]) for a in row_arrays] + [whole(a.shape) for a in whole_arrays],
        out_specs=tuple(by_rows(width) for width, kind in outs),
        out_shape=tuple(jax.ShapeDtypeStruct((rows, width), kind) for width, kind in outs),
        compiler_params=pltpu.CompilerParams(vmem_limit_bytes=62 * 2**20),
        cost_estimate=pl.CostEstimate(flops=flops, bytes_accessed=30_000_000, transcendentals=0),
    )(*row_arrays, *whole_arrays)


def mlp_out(normed, w_gu, w_down):
    rows, model = normed.shape
    ff = w_down.shape[0]
    outs = ((2 * ff, jnp.float32), (ff, jnp.bfloat16), (model, jnp.bfloat16))
    return by_row_blocks(mlp_out_kernel, (normed,), (w_gu, w_down), outs, 6 * rows * model * ff)


def mlp_grad(grad_out, gate_up, w_gu, w_down):
    rows, model = grad_out.shape
    ff = w_down.shape[0]
    outs = ((2 * ff, jnp.bfloat16), (model, jnp.bfloat16))
    return by_row_blocks(
        mlp_grad_kernel, (grad_out, gate_up), (w_gu, w_down), outs, 6 * rows * model * ff
    )


def on_device(
    tokens,
    doc_lengths,
    cotangent,
    gain_attn,
    w_query,
    w_key,
    w_value,
    w_output,
    gain_mlp,
    w_gate,
    w_up,
    w_down,
):
    local_rows, model = tokens.shape[1:]
    ctx_size = lax.axis_size("ctx")
    fsdp_size = lax.axis_size("fsdp")
    length = local_rows * ctx_size
    group_width = (H // KVH) * HD
    ff_slice = w_gate.shape[1] // ctx_size
    held_rows = w_query.shape[0]
    bf16 = jnp.bfloat16

    positions = jnp.arange(length, dtype=jnp.int32)
    seq_lengths = doc_lengths[0]
    starts = jnp.cumsum(seq_lengths) - seq_lengths
    doc_ids = doc_index(positions, starts)
    cos_half, sin_half = rope_tables(positions)
    cos_table = jnp.concatenate([cos_half] * 4, axis=1)
    sin_table = jnp.concatenate([-sin_half, sin_half] * 2, axis=1)
    tables = (cos_table, sin_table, doc_ids[:, None], doc_ids[None, :])


    def by_slice(weight):
        return weight.reshape(held_rows, ctx_size, -1)

    qkv_parts = jnp.concatenate([by_slice(w_query), by_slice(w_key), by_slice(w_value)], axis=2)
    wo_mine = lax.all_gather(w_output, "fsdp", axis=0, tiled=True)
    wd_mine = lax.all_gather(w_down, "fsdp", axis=0, tiled=True)
    gain_rows = jnp.stack([gain_attn, gain_mlp]).astype(jnp.float32)
    odd = lax.axis_index("fsdp") % 2
    gain_tile = jnp.concatenate([gain_rows * (1 - odd), gain_rows * odd], axis=1)
    gain_tile = jnp.pad(gain_tile, ((0, 8 - gain_tile.shape[0]), (0, 128 - gain_tile.shape[1])))
    normed1, gains, w_qkv = start_layer(tokens[0], gain_tile, qkv_parts.transpose(1, 0, 2))
    grad_out = cotangent[0].astype(jnp.float32)
    grad_mlp = (RESIDUAL_MULT * grad_out).astype(bf16)

    block_rows = math.gcd(length, 256)
    normed1, grad_mlp = lax.optimization_barrier((normed1, grad_mlp))
    grad_mlp = lax.all_gather(grad_mlp, "ctx", axis=0, tiled=True)
    qkv = dot_plain(normed1, w_qkv)
    q, kv, mixed_heads, log_sum = attention_forward(qkv, tables, block_rows)
    hidden, w_gu, normed2 = mlp_forward(
        dot_plain(mixed_heads, wo_mine).astype(bf16), tokens[0], gains, w_gate, w_up
    )
    w_gu = rows_of(rows_of(w_gu))

    gate_up, activ, out_terms = mlp_out(normed2, w_gu, wd_mine)
    branch = lax.psum_scatter(out_terms, "ctx", scatter_dimension=0, tiled=True)
    grad_gu, partial2 = mlp_grad(grad_mlp, gate_up, w_gu, wd_mine)
    gu_terms = dot_outer(normed2, grad_gu).astype(bf16)
    wd_terms = dot_outer(activ, grad_mlp).astype(bf16)
    partial2, gu_terms, wd_terms = lax.optimization_barrier((partial2, gu_terms, wd_terms))
    grad_hidden, grad_g2, gu_back, grad_attn = mlp_backward(
        partial2, hidden, cotangent[0], gains, gu_terms.reshape(fsdp_size, -1, gu_terms.shape[1])
    )
    gu_back = return_columns(gu_back, ctx_size)
    wd_back = lax.psum_scatter(wd_terms, "fsdp", scatter_dimension=0, tiled=True)

    grad_mixed = dot_back(grad_attn, wo_mine).astype(bf16)
    wo_terms = dot_outer(mixed_heads, grad_attn).astype(bf16)
    grad_qkv = attention_backward(q, kv, grad_mixed, log_sum, tables, block_rows)
    partial1 = dot_back(grad_qkv, w_qkv).astype(bf16)
    qkv_terms = by_fsdp(dot_outer(normed1, grad_qkv).astype(bf16), ctx_size, fsdp_size)
    grad_inputs, gain_back, wo_back, qkv_back = finish_layer(
        partial1,
        tokens[0],
        grad_hidden,
        gains,
        grad_g2,
        wo_terms.reshape(fsdp_size, held_rows, model),
        qkv_terms.reshape(fsdp_size, ctx_size, held_rows, -1),
    )
    grad_inputs, wd_back, gu_back, branch = lax.optimization_barrier(
        (grad_inputs, wd_back, gu_back, branch)
    )
    output = (hidden + RESIDUAL_MULT * branch.astype(jnp.float32)).astype(bf16)[None]
    gain_back = jnp.where(odd == 0, gain_back[:2, :held_rows], gain_back[:2, held_rows:])

    def joined(parts):
        return parts.transpose(1, 0, 2).reshape(held_rows, -1).astype(jnp.float32)

    key_end = group_width + HD
    return (
        output,
        grad_inputs[None],
        gain_back[0],
        joined(qkv_back[:, :, :group_width]),
        joined(qkv_back[:, :, group_width:key_end]),
        joined(qkv_back[:, :, key_end:]),
        wo_back,
        gain_back[1],
        joined(gu_back[:, :, :ff_slice]),
        joined(gu_back[:, :, ff_slice:]),
        wd_back.astype(jnp.float32),
    )


def solution(mesh):
    in_specs = (
        P("fsdp", "ctx", None),
        P("fsdp", None),
        P("fsdp", "ctx", None),
        P(("ctx", "fsdp")),
        P(("ctx", "fsdp"), None),
        P(("ctx", "fsdp"), None),
        P(("ctx", "fsdp"), None),
        P(("ctx", "fsdp"), None),
        P(("ctx", "fsdp")),
        P(("ctx", "fsdp"), None),
        P(("ctx", "fsdp"), None),
        P(("ctx", "fsdp"), None),
    )
    out_specs = (
        P("fsdp", "ctx", None),
        P("fsdp", "ctx", None),
        P(("ctx", "fsdp")),
        P(("ctx", "fsdp"), None),
        P(("ctx", "fsdp"), None),
        P(("ctx", "fsdp"), None),
        P(("ctx", "fsdp"), None),
        P(("ctx", "fsdp")),
        P(("ctx", "fsdp"), None),
        P(("ctx", "fsdp"), None),
        P(("ctx", "fsdp"), None),
    )
    if mesh.shape["ctx"] != KVH or KVH != 4 * PAIR:
        return jax.shard_map(
            general_device, mesh=mesh, in_specs=in_specs, out_specs=out_specs, check_vma=False
        )

    return jax.shard_map(
        on_device, mesh=mesh, in_specs=in_specs, out_specs=out_specs, check_vma=False
    )
```
